32 devices in a mesh: expert: 8 (over z, y), tensor: 4 (over x, core).
Axes of the slice: x: 2, y: 2, z: 4, core: 2. Of those that a mesh axis runs over, the one named last changes fastest.
Arguments:
- inputs: bfloat16 [12608, 512], P('expert'), may hold values from -6 to 6
- gain_attend: float32 [512], replicated, may hold values from 0.25 to 1.75
- triple_weight: bfloat16 [512, 3, 512], P(None, None, 'tensor'), may hold values from -0.25 to 0.25
- project_weight: bfloat16 [512, 512], P('tensor'), may hold values from -1.5 to 1.5
- gain_mixture: float32 [512], replicated, may hold values from 0.25 to 1.75
- router_weight: bfloat16 [512, 16], replicated, may hold values from -0.125 to 0.125
- expert_first: bfloat16 [16, 512, 2048], P('expert', None, 'tensor'), may hold values from -0.25 to 0.25
- expert_second: bfloat16 [16, 2048, 512], P('expert', 'tensor'), may hold values from -0.1875 to 0.1875
- triple_down: bfloat16 [512, 128], replicated, may hold values from -0.25 to 0.25
- triple_up: bfloat16 [128, 3, 512], P(None, None, 'tensor'), may hold values from -1.5 to 1.5
- project_down: bfloat16 [512, 128], P('tensor'), may hold values from -1.5 to 1.5
- project_up: bfloat16 [128, 512], replicated, may hold values from -1.5 to 1.5
- router_down: bfloat16 [512, 128], replicated, may hold values from -0.25 to 0.25
- router_up: bfloat16 [128, 16], replicated, may hold values from -0.75 to 0.75
- first_down: bfloat16 [512, 128], replicated, may hold values from -0.25 to 0.25
- first_up: bfloat16 [128, 2048], P(None, 'tensor'), may hold values from -1.5 to 1.5
- second_down: bfloat16 [2048, 128], P('tensor'), may hold values from -0.1875 to 0.1875
- second_up: bfloat16 [128, 512], replicated, may hold values from -1.5 to 1.5
- adapter_index: int32 [64], P('expert'), may hold values from 0 to 7
- routes: int32 [12608, 2], P('expert'), may hold values from 0 to 15, all different within a row
- priority: int32 [8, 1576], P('expert'), may hold values from 0 to 1575, each once within a row
- cotangent: bfloat16 [12608, 512], P('expert'), may hold values from -6 to 6
Outputs:
- block_output: bfloat16 [12608, 512], P('expert')
- input_grad: bfloat16 [12608, 512], P('expert')
- triple_down_grad: float32 [512, 128], replicated
- triple_up_grad: float32 [128, 3, 512], P(None, None, 'tensor')
- project_down_grad: float32 [512, 128], P('tensor')
- project_up_grad: float32 [128, 512], replicated
- router_down_grad: float32 [512, 128], replicated
- router_up_grad: float32 [128, 16], replicated
- first_down_grad: float32 [512, 128], replicated
- first_up_grad: float32 [128, 2048], P(None, 'tensor')
- second_down_grad: float32 [2048, 128], P('tensor')
- second_up_grad: float32 [128, 512], replicated
The draws below stay inside these ranges and needn't reach their ends.
Inputs may be any that keep to these rules, and one draw needn't show every extreme that they name: `routes`: each row names 2 different experts. `priority`: each row holds every token index of its group once.
All inputs are finite; a program needn't handle non-finite values.
Results may differ from the reference program's by a relative error of at most 0.028.
Values may be sent and summed in bfloat16 or wider, within the bound.
A program may use at most 192 MiB of HBM per device.

```python
import jax
import jax.numpy as jnp
from jax import lax

D = 512
HEADS = 8
HEAD_DIM = 64
FF = 2048
TOP = 2
ADAPTERS = 8
RANK = 16
SEQ = 197
TOK_DEV = 1576
IMAGES = 64
TOKENS = 12608
EXPERTS = 16
CAP = 248
N_EXPERT = 8


def plant(entries, own_key, smallest, top_value):
    longest = entries.shape.index(max(entries.shape))
    spots = []
    for shift in (0, 1):
        where = [jax.random.randint(jax.random.fold_in(own_key, axis), (), 0, length) for axis, length in enumerate(entries.shape)]
        where[longest] = (where[longest] + shift) % entries.shape[longest]
        spots.append(tuple(where))
    return entries.at[spots[0]].set(smallest).at[spots[1]].set(top_value)


def level_of(rng, dims, pieces, smallest, top_value):
    level = 1.0
    for axis_at, shards_of in pieces:
        heights = jax.random.uniform(jax.random.fold_in(jax.random.fold_in(rng, 6), axis_at), (shards_of,), jnp.float32, smallest / len(pieces), top_value / len(pieces))
        level = level * jnp.repeat(jnp.exp(heights), dims[axis_at] // shards_of).reshape((-1,) + (1,) * (len(dims) - 1 - axis_at))
    return level


def choose_distinct(own_key, rows, amount, top, lift):
    order = jax.random.permutation(jax.random.fold_in(own_key, 1), amount)
    pull = order
    for power in range(3):
        pull = pull * pull // amount
    pull = pull * lift // amount
    tickets = jax.random.randint(jax.random.fold_in(own_key, 2), (rows, amount), 0, 4096) + pull
    holders = jax.random.permutation(jax.random.fold_in(own_key, 3), rows)[jnp.arange(amount) % rows]
    tickets = jnp.where(jnp.arange(rows)[:, None] == holders[None, :], 1 << 14, tickets)
    merit = tickets * amount + jnp.arange(amount)
    return lax.top_k(merit.astype(jnp.int32), top)[1].astype(jnp.int32)


def noise(stream_key, extent, scale, bound, pieces=(), held_as=jnp.bfloat16):
    values = jax.random.normal(stream_key, extent, jnp.float32) * scale
    if len(pieces) > 0:
        values = level_of(stream_key, extent, pieces, -0.22, 0.18) * values
    return jnp.clip(values, min=-bound, max=bound).astype(held_as)


def setup_inputs(seed: int = 0) -> dict:
    seeds = jax.random.split(jax.random.key(seed), 23)
    return {
        "inputs": noise(seeds[0], (TOKENS, D), 1.0, 6.0, ((0, 8),)),
        "gain_attend": jnp.clip(1.0 + 0.15 * jax.random.normal(seeds[1], (D,), jnp.float32), 0.25, 1.75),
        "triple_weight": noise(seeds[2], (D, 3, D), D ** -0.5, 0.25, ((2, 4),)),
        "project_weight": noise(seeds[3], (D, D), (D // 32) ** -0.5, 1.5, ((0, 4),)),
        "gain_mixture": jnp.clip(1.0 + 0.15 * jax.random.normal(seeds[4], (D,), jnp.float32), 0.25, 1.75),
        "router_weight": noise(seeds[5], (D, EXPERTS), (4 * D) ** -0.5, 0.125),
        "expert_first": noise(seeds[6], (EXPERTS, D, FF), D ** -0.5, 0.25, ((0, 8), (2, 4))),
        "expert_second": noise(seeds[7], (EXPERTS, FF, D), (FF // 2) ** -0.5, 0.1875, ((0, 8), (1, 4))),
        "triple_down": noise(seeds[8], (D, ADAPTERS * RANK), D ** -0.5, 0.25),
        "triple_up": noise(seeds[9], (ADAPTERS * RANK, 3, D), RANK ** -0.5, 1.5, ((2, 4),)),
        "project_down": noise(seeds[10], (D, ADAPTERS * RANK), (D // 32) ** -0.5, 1.5, ((0, 4),)),
        "project_up": noise(seeds[11], (ADAPTERS * RANK, D), RANK ** -0.5, 1.5),
        "router_down": noise(seeds[12], (D, ADAPTERS * RANK), D ** -0.5, 0.25),
        "router_up": noise(seeds[13], (ADAPTERS * RANK, EXPERTS), (4 * RANK) ** -0.5, 0.75),
        "first_down": noise(seeds[14], (D, ADAPTERS * RANK), D ** -0.5, 0.25),
        "first_up": noise(seeds[15], (ADAPTERS * RANK, FF), RANK ** -0.5, 1.5, ((1, 4),)),
        "second_down": noise(seeds[16], (FF, ADAPTERS * RANK), (FF // 2) ** -0.5, 0.1875, ((0, 4),)),
        "second_up": noise(seeds[17], (ADAPTERS * RANK, D), RANK ** -0.5, 1.5),
        "adapter_index": plant(jax.random.randint(seeds[18], (IMAGES,), 0, ADAPTERS), jax.random.fold_in(seeds[18], 1), 0, ADAPTERS - 1).astype(jnp.int32),
        "routes": choose_distinct(seeds[19], TOKENS, EXPERTS, TOP, 1024),
        "priority": jax.vmap(lambda own: jax.random.permutation(own, TOK_DEV))(jax.random.split(seeds[20], N_EXPERT)).reshape((N_EXPERT, TOK_DEV)).astype(jnp.int32),
        "cotangent": noise(seeds[21], (TOKENS, D), 1.0, 6.0, ((0, 8),)),
    }


@jax.custom_vjp
def low(v):
    return lax.optimization_barrier(v.astype(jnp.bfloat16)).astype(jnp.float32)

@jax.custom_vjp
def low_back(v):
    return v

def low_keep(v):
    return (low(v), None)

def low_pass(kept, grad):
    return (grad,)

def back_keep(v):
    return (v, None)

def back_low(kept, grad):
    return (low(grad),)
low.defvjp(low_keep, low_pass)
low_back.defvjp(back_keep, back_low)
highest = lax.Precision.HIGHEST
norm_eps = 1e-06

def norm_rows(values, gain):
    centre = lax.optimization_barrier(jnp.mean(values, axis=-1, keepdims=True))
    shifted = values - centre
    spread = lax.optimization_barrier(jnp.mean(shifted * shifted, axis=-1, keepdims=True))
    return shifted * lax.rsqrt(spread + norm_eps) * gain

def pick_columns(token_ids):
    column = jnp.arange(ADAPTERS * RANK, dtype=jnp.int32) // RANK
    return (token_ids[:, None] == column[None, :]).astype(jnp.float32)

def place_pairs(route_rows, ranking, capacity, experts):
    count = ranking.shape[0]
    ranked = route_rows[ranking]
    pair_expert = jnp.concatenate([ranked[:, 0], ranked[:, 1]])
    pair_token = jnp.concatenate([ranking, ranking])
    onehot = (pair_expert[:, None] == jnp.arange(experts, dtype=jnp.int32)[None, :]).astype(jnp.int32)
    position = lax.optimization_barrier(jnp.sum(jnp.cumsum(onehot, axis=0) * onehot, axis=1)) - 1
    kept_pair = position < capacity
    pair_slot = pair_expert * capacity + jnp.minimum(position, capacity - 1)
    target = jnp.where(kept_pair, pair_slot, experts * capacity)
    slot_token = jnp.full((experts * capacity,), count, jnp.int32).at[target].set(pair_token, mode='drop')
    slot_first = jnp.zeros((count,), jnp.int32).at[ranking].set(pair_slot[:count])
    slot_second = jnp.zeros((count,), jnp.int32).at[ranking].set(pair_slot[count:])
    keep_first = jnp.zeros((count,), jnp.int32).at[ranking].set(kept_pair[:count].astype(jnp.int32))
    keep_second = jnp.zeros((count,), jnp.int32).at[ranking].set(kept_pair[count:].astype(jnp.int32))
    return (slot_token, jnp.stack([slot_first, slot_second], axis=1), jnp.stack([keep_first, keep_second], axis=1))

def take_rows(table, index):
    return table[index]

def reference(inputs, gain_attend, triple_weight, project_weight, gain_mixture, router_weight, expert_first, expert_second, triple_down, triple_up, project_down, project_up, router_down, router_up, first_down, first_up, second_down, second_up, adapter_index, routes, priority, cotangent):
    token_ids = jnp.repeat(adapter_index, SEQ)
    pick_cols = pick_columns(token_ids)
    slot_token, slot_pairs, keep_pairs = jax.vmap(lambda route_rows, ranking: place_pairs(route_rows, ranking, CAP, EXPERTS))(routes.reshape(N_EXPERT, TOK_DEV, TOP), priority)
    id_pad = jnp.concatenate([token_ids.reshape(N_EXPERT, TOK_DEV), jnp.zeros((N_EXPERT, 1), jnp.int32)], axis=1)
    slot_ids = jax.vmap(take_rows)(id_pad, slot_token)
    slot_cols = pick_columns(slot_ids.reshape(-1)).reshape(N_EXPERT, EXPERTS, CAP, ADAPTERS * RANK)
    chosen = (routes[:, :, None] == jnp.arange(EXPERTS, dtype=jnp.int32)[None, None, :]).astype(jnp.float32)
    keep_float = keep_pairs.reshape(TOKENS, TOP).astype(jnp.float32)
    pair_flat = slot_pairs.reshape(N_EXPERT, TOK_DEV * TOP)
    triple_full = triple_weight.astype(jnp.float32).reshape(D, 3 * D)
    project_full = project_weight.astype(jnp.float32)
    router_full = router_weight.astype(jnp.float32)
    first_full = expert_first.astype(jnp.float32)
    second_full = expert_second.astype(jnp.float32)

    def forward(source, triple_low, triple_high, project_low, project_high, router_low, router_high, first_low, first_high, second_low, second_high):
        normed = low(norm_rows(source, gain_attend))
        triple_mid = low(low_back(pick_cols * jnp.dot(normed, triple_low, precision=highest)))
        triple = jnp.dot(normed, triple_full, precision=highest) + jnp.dot(triple_mid, triple_high.reshape(ADAPTERS * RANK, 3 * D), precision=highest)
        triple = low(low_back(triple)).reshape(IMAGES, SEQ, 3, HEADS, HEAD_DIM)
        scores = low_back(jnp.einsum('bqhd,bkhd->bhqk', triple[:, :, 0], triple[:, :, 1], precision=highest) * HEAD_DIM ** (-0.5))
        weights_attn = low(jax.nn.softmax(scores, axis=-1))
        attended = jnp.einsum('bhqk,bkhd->bqhd', weights_attn, triple[:, :, 2], precision=highest).reshape(TOKENS, D)
        attended = low(low_back(attended))
        project_mid = low(low_back(pick_cols * jnp.dot(attended, project_low, precision=highest)))
        branch = jnp.dot(attended, project_full, precision=highest) + jnp.dot(project_mid, project_high, precision=highest)
        middle = source + low_back(branch)
        mixed_in = low(norm_rows(middle, gain_mixture))
        logits = jnp.dot(mixed_in, router_full, precision=highest) + jnp.dot(pick_cols * jnp.dot(mixed_in, router_low, precision=highest), router_high, precision=highest)
        picked = lax.optimization_barrier(jnp.sum(chosen * logits[:, None, :], axis=-1))
        gate_wts = jax.nn.softmax(picked, axis=-1) * keep_float
        padded = jnp.concatenate([mixed_in.reshape(N_EXPERT, TOK_DEV, D), jnp.zeros((N_EXPERT, 1, D), jnp.float32)], axis=1)
        sent = low_back(jax.vmap(take_rows)(padded, slot_token)).reshape(N_EXPERT, EXPERTS, CAP, D)
        first_mid = low(low_back(slot_cols * jnp.einsum('gecd,dr->gecr', sent, first_low, precision=highest)))
        first_pre = jnp.einsum('gecd,edf->gecf', sent, first_full, precision=highest) + jnp.einsum('gecr,rf->gecf', first_mid, first_high, precision=highest)
        hidden = low(jax.nn.gelu(low_back(first_pre), approximate=False))
        second_mid = low(low_back(slot_cols * jnp.einsum('gecf,fr->gecr', hidden, second_low, precision=highest)))
        expert_res = jnp.einsum('gecf,efd->gecd', hidden, second_full, precision=highest) + jnp.einsum('gecr,rd->gecd', second_mid, second_high, precision=highest)
        expert_res = low(low_back(expert_res)).reshape(N_EXPERT, EXPERTS * CAP, D)
        fetched = jax.vmap(take_rows)(expert_res, pair_flat).reshape(TOKENS, TOP, D)
        return middle + lax.optimization_barrier(jnp.sum(gate_wts[:, :, None] * fetched, axis=1))
    adapters = tuple((item.astype(jnp.float32) for item in (triple_down, triple_up, project_down, project_up, router_down, router_up, first_down, first_up, second_down, second_up)))
    result, pullback = jax.vjp(forward, inputs.astype(jnp.float32), *adapters)
    grads = pullback(cotangent.astype(jnp.float32))
    return (result.astype(jnp.bfloat16), grads[0].astype(jnp.bfloat16), grads[1], grads[2], grads[3], grads[4], grads[5], grads[6], grads[7], grads[8], grads[9], grads[10])
```

```python
import functools

import jax
import jax.numpy as jnp
from jax import lax
from jax.experimental import pallas as pl
from jax.experimental.pallas import tpu as pltpu
from jax.sharding import PartitionSpec as P

HEAD_DIM = 64
TOP = 2
ADAPTERS = 8
RANK = 16
ADAPT = ADAPTERS * RANK
EPS = 1e-06

f32 = jnp.float32
bf16 = jnp.bfloat16
i32 = jnp.int32
MESH = pl.DeviceIdType.MESH
VMEM = pltpu.VMEM


def up(a, b):
    return -(-a // b) * b


def dot(a, b):
    return lax.dot_general(a, b, (((1,), (0,)), ((), ())), preferred_element_type=f32)


def dot_nt(a, b):
    return lax.dot_general(a, b, (((1,), (1,)), ((), ())), preferred_element_type=f32)


def dot_tn(a, b):
    return lax.dot_general(a, b, (((0,), (0,)), ((), ())), preferred_element_type=f32)


def split_high_low(a):
    high = a.astype(bf16)
    return high, (a - high.astype(f32)).astype(bf16)


def dot_fine(a, b):
    high, low = split_high_low(a)
    return dot(high, b) + dot(low, b)


def dot_nt_fine(a, b):
    high, low = split_high_low(a)
    return dot_nt(high, b) + dot_nt(low, b)


def iota(shape, axis):
    return lax.broadcasted_iota(i32, shape, axis)


def to_row(col):
    n = col.shape[0]
    return jnp.sum(jnp.where(iota((n, n), 0) == iota((n, n), 1), col, 0.0), axis=0, keepdims=True)


def to_col(row):
    n = row.shape[1]
    return jnp.sum(jnp.where(iota((n, n), 0) == iota((n, n), 1), row, 0.0), axis=1, keepdims=True)


def pick_of(ids):
    return (ids == iota((1, ADAPT), 1) // RANK).astype(f32)


def whole(count):
    return [pl.BlockSpec(memory_space=VMEM) for _ in range(count)]


def norm_stats(x):
    centre = jnp.mean(x, axis=-1, keepdims=True)
    shifted = x - centre
    scale = lax.rsqrt(jnp.mean(shifted * shifted, axis=-1, keepdims=True) + EPS)
    return shifted * scale, scale


def norm_back(grad, gain, unit, scale):
    g = grad * gain
    return scale * (
        g - jnp.mean(g, axis=-1, keepdims=True) - unit * jnp.mean(g * unit, axis=-1, keepdims=True)
    )


def place_kernel(
    dims, tix, prio, rt, idq, cot, slotc, slotr, cots, cot_pad, rank_s, one_s
):
    nt, seq, seqp, images, experts, cap, capq, cp, width = dims
    t = tix[0]
    tok = prio.shape[1]
    rows = images // nt * seqp
    total = nt * rows
    wide = one_s.shape[-1]
    order = iota((seqp, tok), 1).astype(f32)
    lane = iota((seqp, wide), 1)
    for i in range(images):
        at = pl.ds(i * seqp, seqp)
        token = iota((seqp, 1), 0) + i * seqp
        rank_s[at, :] = jnp.sum(jnp.where(prio[...] == token, order, 0.0), axis=1, keepdims=True)
        r = rt[at, :]
        named = jnp.where(lane < experts, r[:, 0:1], jnp.where(r[:, 1:2] < 0, -1, r[:, 1:2] + experts))
        one_s[at, :] = (named == lane).astype(f32).astype(bf16)
    totals = dot(jnp.ones((8, total), bf16), one_s[...])[0:1]
    rank_rows = [to_row(rank_s[pl.ds(q * rows, rows), :]) for q in range(nt)]
    for q in range(nt):
        at = pl.ds(q * rows, rows)
        mine = rank_s[at, :]
        counts = jnp.zeros((rows, wide), f32)
        for p in range(nt):
            before = (rank_rows[p] < mine).astype(f32).astype(bf16)
            counts = counts + dot(before, one_s[pl.ds(p * rows, rows), :])
        lane = iota((rows, wide), 1)
        r = rt[at, :]
        hot = one_s[at, :].astype(f32) * counts
        first = jnp.sum(jnp.where(lane < experts, hot, 0.0), axis=1, keepdims=True)
        second = jnp.sum(
            jnp.where(lane < experts, 0.0, hot)
            + jnp.where((lane < experts) & (r[:, 1:2] == lane), totals, 0.0),
            axis=1,
            keepdims=True,
        )
        for k, pos in ((0, first), (1, second)):
            e = r[:, k : k + 1]
            place = pos.astype(i32)
            kept = (e >= 0) & (place < cap) & (lax.rem(place, nt) == t)
            slot = jnp.where(kept, e * cp + lax.div(place, nt), -1)
            slotc[q, :, k : k + 1] = slot
            slotr[q, k : k + 1, :] = to_row(slot.astype(f32)).astype(i32)
    for i in range(images):
        start = i * seq // 16 * 16
        stop = min(start + up(seq, 16) + 16, tok)
        src = iota((seqp, stop - start), 1) + start
        row = iota((seqp, stop - start), 0)
        sel = ((src == row + i * seq) & (row < seq)).astype(f32).astype(bf16)
        cot_pad[pl.ds(i * seqp, seqp), :] = dot(sel, cot[start:stop, :]).astype(bf16)
    n_out, block = cots.shape[0], cots.shape[1]
    step = max(1, 256 // block)
    ids = [idq[q] for q in range(nt)]

    def send(d, carry):
        s = iota((step * block, 1), 0) + d * (step * block)
        acc = jnp.zeros((step * block, width), f32)
        idc = jnp.zeros((step * block, 1), f32)
        for q in range(nt):
            g = (slotr[q, 0:1, :] == s) | (slotr[q, 1:2, :] == s)
            idc = idc + jnp.sum(jnp.where(g, ids[q], 0.0), axis=1, keepdims=True)
            acc = acc + dot(g.astype(f32).astype(bf16), cot_pad[pl.ds(q * rows, rows), :])
        for b in range(step):
            part = acc[b * block : (b + 1) * block]
            idr = to_row(idc[b * block : (b + 1) * block])
            row = iota((block, block), 0)
            cots[d * step + b, :, 0:block] = jnp.where(row == capq, idr, part[:, 0:block]).astype(bf16)
            cots[d * step + b, :, block:] = part[:, block:].astype(bf16)
        return carry

    lax.fori_loop(0, n_out // step, send, 0)


def attend_kernel(
    dims, tix, x_ref, gain1, wt, tup, tdn, pw, pd, pup, gain2, idq,
    mixed, middle, triple, attended, tlow, plow, attn_in, xs,
):
    nt, seq, seqp, images = dims
    per = images // nt
    rows = per * seqp
    tok = x_ref.shape[0]
    lw = wt.shape[2] // 3
    for li in range(per):
        base = (tix[0] * per + li) * seq
        row = iota((seqp, tok), 0)
        sel = ((iota((seqp, tok), 1) == row + base) & (row < seq)).astype(f32).astype(bf16)
        xs[pl.ds(li * seqp, seqp), :] = dot(sel, x_ref[...])
    pick = pick_of(idq[...])
    unit, _ = norm_stats(xs[...])
    normed = (unit * gain1[...]).astype(bf16)
    attn_in[...] = normed
    low = (dot(normed, tdn[...]) * pick).astype(bf16)
    tlow[...] = low
    head_of = iota((1, lw), 1) // HEAD_DIM
    key_ok = iota((1, seqp), 1) < seq

    def piece(p, carry):
        triple[p] = (dot(normed, wt[p]) + dot(low, tup[p])).astype(bf16)
        for li in range(per):
            at = pl.ds(li * seqp, seqp)
            q = triple[p, at, 0:lw]
            k = triple[p, at, lw : 2 * lw]
            v = triple[p, at, 2 * lw : 3 * lw]
            acc = jnp.zeros((seqp, lw), f32)
            for h in range(lw // HEAD_DIM):
                on = head_of == h
                s = dot_nt(jnp.where(on, q, 0.0).astype(bf16), k) * HEAD_DIM**-0.5
                s = jnp.where(key_ok, s, -jnp.inf)
                e = jnp.exp(s - jnp.max(s, axis=1, keepdims=True))
                probs = (e / jnp.sum(e, axis=1, keepdims=True)).astype(bf16)
                acc = acc + dot(probs, jnp.where(on, v, 0.0).astype(bf16))
            attended[p, at, :] = acc.astype(bf16)
        return carry

    lax.fori_loop(0, nt, piece, 0)
    psum = jnp.zeros((rows, ADAPT), f32)
    branch = jnp.zeros((rows, pup.shape[1]), f32)
    for p in range(nt):
        psum = psum + dot(attended[p], pd[p])
        branch = branch + dot(attended[p], pw[p])
    low2 = (psum * pick).astype(bf16)
    plow[...] = low2
    mid = xs[...] + branch + dot(low2, pup[...])
    middle[...] = mid
    unit2, _ = norm_stats(mid)
    mixed[...] = (unit2 * gain2[...]).astype(bf16)


def gates_of(mixed, rt, ids, rw, rd, ru):
    pick = pick_of(ids)
    low = dot(mixed, rd) * pick
    logits = dot(mixed, rw) + dot_fine(low, ru)
    lane = iota((1, rw.shape[1]), 1)
    first = jnp.sum(jnp.where(rt[:, 0:1] == lane, logits, 0.0), axis=1, keepdims=True)
    second = jnp.sum(jnp.where(rt[:, 1:2] == lane, logits, 0.0), axis=1, keepdims=True)
    top = jnp.maximum(first, second)
    a = jnp.exp(first - top)
    b = jnp.exp(second - top)
    return a / (a + b), b / (a + b), low, pick


def dispatch_kernel(dims, mixed, rt, idc, slotc, slotr, rw, rd, ru, sends, gate_s):
    nt, capq = dims
    rows = mixed.shape[1]
    for q in range(nt):
        at = pl.ds(q * rows, rows)
        a, b, _, _ = gates_of(mixed[q], rt[at, :], idc[at, :], rw[...], rd[...], ru[...])
        gate_s[q, 0] = a
        gate_s[q, 1] = b
    n_out, block, width = sends.shape
    step = max(1, 256 // block)

    def send(d, carry):
        s = iota((step * block, 1), 0) + d * (step * block)
        acc = jnp.zeros((step * block, width), f32)
        for q in range(nt):
            g = (slotr[q, 0:1, :] == s) | (slotr[q, 1:2, :] == s)
            acc = acc + dot(g.astype(f32).astype(bf16), mixed[q])
        sr = iota((1, step * block), 1) + d * (step * block)
        gate = jnp.zeros((1, step * block), f32)
        for q in range(nt):
            for k in range(TOP):
                gate = gate + jnp.sum(
                    jnp.where(slotc[q, :, k : k + 1] == sr, gate_s[q, k], 0.0), axis=0, keepdims=True
                )
        high = gate.astype(bf16).astype(f32)
        low = gate - high
        for b in range(step):
            part = acc[b * block : (b + 1) * block]
            row = iota((block, block), 0)
            head = jnp.where(row == capq, high[:, b * block : (b + 1) * block], part[:, 0:block])
            head = jnp.where(row == capq + 1, low[:, b * block : (b + 1) * block], head)
            sends[d * step + b, :, 0:block] = head.astype(bf16)
            sends[d * step + b, :, block:] = part[:, block:].astype(bf16)
        return carry

    lax.fori_loop(0, n_out // step, send, 0)


def erf_parts(pre):
    cdf = 0.5 * (1.0 + lax.erf(pre * 0.7071067811865476))
    return pre * cdf, cdf + pre * (jnp.exp(-0.5 * pre * pre) * 0.3989422804014327)


def expert_kernel(
    dims, got, cot, w1, w2, fdn, fup, sdn, sup, rets, grads,
    sent_s, sg_s, hid_s, dg_s, low_s, gh_s, acc_fd, acc_fu, acc_sd, acc_su,
):
    nt, local, capq, cp = dims
    n, block, width = got.shape
    ffq = w1.shape[3]
    rows = n * cp
    row_in = iota((rows, 1), 0)
    real = lax.rem(row_in, cp) < capq
    acc_fd[...] = jnp.zeros_like(acc_fd)
    acc_fu[...] = jnp.zeros_like(acc_fu)
    acc_sd[...] = jnp.zeros_like(acc_sd)
    acc_su[...] = jnp.zeros_like(acc_su)
    for e in range(local):
        at = pl.ds(e * cp, cp)
        sent = jnp.where(real, got[:, at, :].reshape(rows, width).astype(f32), 0.0).astype(bf16)
        cots = jnp.where(real, cot[:, at, :].reshape(rows, width).astype(f32), 0.0)
        ids, gates = [], []
        row = iota((cp, block), 0) + e * cp
        diag = row == iota((cp, block), 1)
        for m in range(n):
            idr = cot[m, capq : capq + 1, 0:block].astype(f32)
            gr = got[m, capq : capq + 1, 0:block].astype(f32) + got[
                m, capq + 1 : capq + 2, 0:block
            ].astype(f32)
            ids.append(jnp.sum(jnp.where(diag, idr, 0.0), axis=1, keepdims=True))
            gates.append(jnp.sum(jnp.where(diag, gr, 0.0), axis=1, keepdims=True))
        idc = jnp.concatenate(ids, axis=0).astype(i32)
        gate = jnp.concatenate(gates, axis=0)
        pick = pick_of(idc)
        sent_s[...] = sent
        sgrad = (gate * cots).astype(bf16)
        sg_s[...] = sgrad
        first_low = (dot(sent, fdn[...]) * pick).astype(bf16)
        low_s[0] = first_low
        g2low = (dot_nt(sgrad, sup[...]) * pick).astype(bf16)
        low_s[1] = g2low

        def ahead(c, carry):
            second, res = carry
            pre = dot(sent_s[...], w1[c, e]) + dot(low_s[0], fup[c])
            act, slope = erf_parts(pre)
            hid = act.astype(bf16)
            hid_s[c] = hid
            dg_s[c] = slope
            return second + dot(hid, sdn[c]), res + dot(hid, w2[c, e])

        second, res = lax.fori_loop(
            0, nt, ahead, (jnp.zeros((rows, ADAPT), f32), jnp.zeros((rows, width), f32))
        )
        second_low = (second * pick).astype(bf16)
        res = (res + dot(second_low, sup[...])).astype(bf16).astype(f32)
        grad_gate = jnp.sum(res * cots, axis=1, keepdims=True)
        out = gate * res
        for m in range(n):
            part = out[m * cp : (m + 1) * cp]
            rets[m, 0, at, :] = part.astype(bf16)
            gg = jnp.sum(
                jnp.where(diag, grad_gate[m * cp : (m + 1) * cp], 0.0), axis=0, keepdims=True
            )
            gh_s[m : m + 1, :] = gg if e == 0 else gh_s[m : m + 1, :] + gg
        acc_su[...] += dot_tn(second_low, sgrad)

        def back(c, carry):
            low1, gsent = carry
            ghid = dot_nt(sg_s[...], w2[c, e]) + dot_nt(low_s[1], sdn[c])
            gpre = (ghid * dg_s[c]).astype(bf16)
            acc_fu[c] += dot_tn(low_s[0], gpre)
            acc_sd[c] += dot_tn(low_s[1], hid_s[c])
            return low1 + dot_nt(gpre, fup[c]), gsent + dot_nt(gpre, w1[c, e])

        low1, gsent = lax.fori_loop(
            0, nt, back, (jnp.zeros((rows, ADAPT), f32), jnp.zeros((rows, width), f32))
        )
        g1low = (low1 * pick).astype(bf16)
        gsent = gsent + dot_nt(g1low, fdn[...])
        acc_fd[...] += dot_tn(g1low, sent)
        for m in range(n):
            rets[m, 1, at, :] = gsent[m * cp : (m + 1) * cp].astype(bf16)
    for m in range(n):
        gg = gh_s[m : m + 1, :]
        high = gg.astype(bf16).astype(f32)
        row = iota((16, block), 0)
        base = capq // 16 * 16
        old = rets[m, 0, pl.ds(base, 16), 0:block].astype(f32)
        new = jnp.where(row == capq - base, high, jnp.where(row == capq + 1 - base, gg - high, old))
        rets[m, 0, pl.ds(base, 16), 0:block] = new.astype(bf16)
    quarter = width // nt
    for q in range(nt):
        off = 0
        for c in range(ffq // 128):
            grads[q, off : off + 128, :] = acc_fu[q, :, c * 128 : (c + 1) * 128].astype(bf16)
            off += 128
        grads[q, off : off + ffq, :] = acc_sd[q].T.astype(bf16)
        off += ffq
        grads[q, off : off + quarter, :] = acc_fd[:, q * quarter : (q + 1) * quarter].T.astype(bf16)
        off += quarter
        for c in range(width // 128):
            at = slice(q * (ADAPT // nt), (q + 1) * (ADAPT // nt))
            grads[q, off : off + ADAPT // nt, :] = acc_su[at, c * 128 : (c + 1) * 128].astype(bf16)
            off += ADAPT // nt


def combine_kernel(dims, got, slotc, slotr, res, grad, gg, gcol, rows_s):
    nt, capq = dims
    n, _, block, width = got.shape
    rows = slotc.shape[1]
    for d in range(n):
        gr = got[d, 0, capq : capq + 1, 0:block].astype(f32) + got[
            d, 0, capq + 1 : capq + 2, 0:block
        ].astype(f32)
        gcol[d * block : (d + 1) * block, :] = to_col(gr)
        for j in range(2):
            rows_s[j, d * block : (d + 1) * block, :] = got[d, j]
    slots = n * block
    for q in range(nt):
        s = iota((1, slots), 1)
        g = ((slotc[q, :, 0:1] == s) | (slotc[q, :, 1:2] == s)).astype(f32).astype(bf16)
        grad[q] = dot(g, rows_s[1]).astype(bf16)
        res[q] = dot(g, rows_s[0]).astype(bf16)
        sc = iota((slots, 1), 0)
        for k in range(TOP):
            gg[q, k : k + 1, :] = jnp.sum(
                jnp.where(slotr[q, k : k + 1, :] == sc, gcol[...], 0.0), axis=0, keepdims=True
            )


def back_kernel(
    dims, tix, cot_ref, gmix, ggate, mixed, middle, triple, attended, tlow, plow, attn_in, x_ref,
    gain1, gain2, wt, tup, tdn, pw, pd, pup, rw, rd, ru, rt, idq,
    igrad, grads, xs, gt_s, ga_s, acc_in, acc_low,
):
    nt, seq, seqp, images = dims
    per = images // nt
    tok = x_ref.shape[0]
    width = x_ref.shape[1]
    lw = wt.shape[2] // 3
    rows = per * seqp
    quarter = width // nt
    for li in range(per):
        base = (tix[0] * per + li) * seq
        row = iota((seqp, tok), 0)
        sel = ((iota((seqp, tok), 1) == row + base) & (row < seq)).astype(f32).astype(bf16)
        at = pl.ds(li * seqp, seqp)
        xs[0, at, :] = dot(sel, x_ref[...])
        xs[1, at, :] = dot(sel, cot_ref[...])
    r = rt[...]
    prob0, prob1, rlow, pick = gates_of(mixed[...], r, idq[...], rw[...], rd[...], ru[...])
    gg0 = to_col(ggate[0:1, :])
    gg1 = to_col(ggate[1:2, :])
    inner = prob0 * gg0 + prob1 * gg1
    lane = iota((1, rw.shape[1]), 1)
    glog = jnp.where(r[:, 0:1] == lane, prob0 * (gg0 - inner), 0.0) + jnp.where(
        r[:, 1:2] == lane, prob1 * (gg1 - inner), 0.0
    )
    llow = dot_nt_fine(glog, ru[...]) * pick
    gm = gmix[...].astype(f32) + dot_nt_fine(glog, rw[...]) + dot_nt_fine(llow, rd[...])
    router_up = dot_tn(rlow.astype(bf16), glog.astype(bf16))
    router_down = dot_tn(mixed[...], llow.astype(bf16))
    unit2, scale2 = norm_stats(middle[...])
    gmid = xs[1] + norm_back(gm, gain2[...], unit2, scale2)
    xs[1] = gmid
    gbranch = gmid.astype(bf16)
    project_up = dot_tn(plow[...], gbranch)
    blow = (dot_nt(gbranch, pup[...]) * pick).astype(bf16)
    for p in range(nt):
        ga_s[p] = (dot_nt(gbranch, pw[p]) + dot_nt(blow, pd[p])).astype(bf16)
    head_of = iota((1, lw), 1) // HEAD_DIM
    key_ok = iota((1, seqp), 1) < seq
    acc_in[...] = jnp.zeros_like(acc_in)
    acc_low[...] = jnp.zeros_like(acc_low)

    def piece(p, carry):
        for li in range(per):
            at = pl.ds(li * seqp, seqp)
            q = triple[p, at, 0:lw]
            k = triple[p, at, lw : 2 * lw]
            v = triple[p, at, 2 * lw : 3 * lw]
            ga = ga_s[p, at, :]
            gq = jnp.zeros((seqp, lw), f32)
            gk = jnp.zeros((seqp, lw), f32)
            gv = jnp.zeros((seqp, lw), f32)
            for h in range(lw // HEAD_DIM):
                on = head_of == h
                qm = jnp.where(on, q, 0.0).astype(bf16)
                km = jnp.where(on, k, 0.0).astype(bf16)
                gam = jnp.where(on, ga, 0.0).astype(bf16)
                s = dot_nt(qm, k) * HEAD_DIM**-0.5
                s = jnp.where(key_ok, s, -jnp.inf)
                e = jnp.exp(s - jnp.max(s, axis=1, keepdims=True))
                probs = e / jnp.sum(e, axis=1, keepdims=True)
                gp = dot_nt(gam, v)
                ds = (probs * (gp - jnp.sum(probs * gp, axis=1, keepdims=True))).astype(bf16)
                gq = gq + dot(ds, km)
                gk = gk + dot_tn(ds, qm)
                gv = gv + dot_tn(probs.astype(bf16), gam)
            gt_s[at, 0:lw] = (gq * HEAD_DIM**-0.5).astype(bf16)
            gt_s[at, lw : 2 * lw] = (gk * HEAD_DIM**-0.5).astype(bf16)
            gt_s[at, 2 * lw : 3 * lw] = gv.astype(bf16)
        gt = gt_s[...]
        acc_low[...] += dot_nt(gt, tup[p])
        acc_in[...] += dot_nt(gt, wt[p])
        tu = dot_tn(tlow[...], gt)
        for c in range(3 * lw // 128):
            grads[p, c * 128 : (c + 1) * 128, :] = tu[:, c * 128 : (c + 1) * 128].astype(bf16)
        off = 3 * lw
        grads[p, off : off + lw, :] = dot_tn(attended[p], blow).astype(bf16)
        return carry

    lax.fori_loop(0, nt, piece, 0)
    tglow = (acc_low[...] * pick).astype(bf16)
    gin = acc_in[...] + dot_nt(tglow, tdn[...])
    triple_down = dot_tn(attn_in[...], tglow)
    unit1, scale1 = norm_stats(xs[0])
    igrad[...] = (xs[1] + norm_back(gin, gain1[...], unit1, scale1)).astype(bf16)
    share = ADAPT // nt
    for q in range(nt):
        off = 4 * lw
        at = slice(q * quarter, (q + 1) * quarter)
        grads[q, off : off + quarter, :] = triple_down[at].astype(bf16)
        off += quarter
        grads[q, off : off + quarter, :] = router_down[at].astype(bf16)
        off += quarter
        at = slice(q * share, (q + 1) * share)
        for c in range(width // 128):
            grads[q, off : off + share, :] = project_up[at, c * 128 : (c + 1) * 128].astype(bf16)
            off += share
        ex = rw.shape[1]
        if ex < 128:
            grads[q, off : off + share, :] = jnp.zeros((share, 128), bf16)
        grads[q, off : off + share, 0:ex] = router_up[at].astype(bf16)


def greet(peers):
    barrier = pltpu.get_barrier_semaphore()
    for peer in peers:
        pl.semaphore_signal(barrier, 1, device_id=peer, device_id_type=MESH)
    pl.semaphore_wait(barrier, len(peers))


def remote(src, dst, send, recv, peer):
    return pltpu.make_async_remote_copy(
        src_ref=src, dst_ref=dst, send_sem=send, recv_sem=recv, device_id=peer, device_id_type=MESH
    )


def swap_kernel(n, x_ref, o_ref, send, recv, here):
    e = lax.axis_index("expert")
    t = lax.axis_index("tensor")
    greet([(lax.rem(e + d, n), t) for d in range(1, n)])
    copies = []
    for d in range(1, n):
        p = lax.rem(e + d, n)
        copies.append(remote(x_ref.at[p], o_ref.at[e], send.at[d], recv.at[d], (p, t)))
        copies[-1].start()
    own = pltpu.make_async_copy(x_ref.at[e], o_ref.at[e], here)
    own.start()
    for copy in copies:
        copy.wait()
    own.wait()


def swap(x, n, ident):
    return pl.pallas_call(
        functools.partial(swap_kernel, n),
        out_shape=jax.ShapeDtypeStruct(x.shape, x.dtype),
        in_specs=whole(1),
        out_specs=pl.BlockSpec(memory_space=VMEM),
        scratch_shapes=[
            pltpu.SemaphoreType.DMA((n,)),
            pltpu.SemaphoreType.DMA((n,)),
            pltpu.SemaphoreType.DMA,
        ],
        compiler_params=pltpu.CompilerParams(collective_id=ident, has_side_effects=True),
    )(x)


def gather_kernel(nt, x_ref, o_ref, send, recv, here):
    e = lax.axis_index("expert")
    t = lax.axis_index("tensor")
    far = jnp.bitwise_xor(t, 2)
    near = jnp.bitwise_xor(t, 1)
    greet([(e, far), (e, near)])
    out = remote(x_ref, o_ref.at[t], send.at[0], recv.at[0], (e, far))
    side = remote(x_ref, o_ref.at[t], send.at[1], recv.at[1], (e, near))
    out.start()
    side.start()
    own = pltpu.make_async_copy(x_ref, o_ref.at[t], here)
    own.start()
    out.wait_recv()
    relay = remote(o_ref.at[far], o_ref.at[far], send.at[2], recv.at[2], (e, near))
    relay.start()
    out.wait_send()
    side.wait()
    relay.wait()
    own.wait()


def gather(x, nt, ident):
    return pl.pallas_call(
        functools.partial(gather_kernel, nt),
        out_shape=jax.ShapeDtypeStruct((nt,) + x.shape, x.dtype),
        in_specs=whole(1),
        out_specs=pl.BlockSpec(memory_space=VMEM),
        scratch_shapes=[
            pltpu.SemaphoreType.DMA((3,)),
            pltpu.SemaphoreType.DMA((3,)),
            pltpu.SemaphoreType.DMA,
        ],
        compiler_params=pltpu.CompilerParams(collective_id=ident, has_side_effects=True),
    )(x)


def gather_early(x, nt):
    t = lax.axis_index("tensor")
    near = lax.ppermute(x, "tensor", [(i, i ^ 1) for i in range(nt)])
    far = lax.ppermute(x, "tensor", [(i, i ^ 2) for i in range(nt)])
    cross = lax.ppermute(far, "tensor", [(i, i ^ 1) for i in range(nt)])
    out = jnp.zeros((nt,) + x.shape, x.dtype)
    for mask, part in ((0, x), (1, near), (2, far), (3, cross)):
        out = lax.dynamic_update_index_in_dim(out, part, jnp.bitwise_xor(t, mask), 0)
    return out


def scatter_kernel(nt, grad, res, gg, ograd, ores, ogg, keep_g, keep_r, keep_k, in1, in1r, in1k, in2, in2r, in2k, send, recv):
    e = lax.axis_index("expert")
    t = lax.axis_index("tensor")
    far = jnp.bitwise_xor(t, 2)
    near = jnp.bitwise_xor(t, 1)
    nearfar = jnp.bitwise_xor(t, 3)
    greet([(e, far), (e, near)])
    first = []
    for i, (src, dst) in enumerate(((grad, in1), (gg, in1k), (res, in1r))):
        for j, q in enumerate((nearfar, near)):
            copy = remote(src.at[q], dst.at[j], send.at[2 * i + j], recv.at[2 * i + j], (e, near))
            copy.start()
            first.append(copy)
    second = []
    for i, (src, one, keep, two) in enumerate(
        ((grad, in1, keep_g, in2), (gg, in1k, keep_k, in2k), (res, in1r, keep_r, in2r))
    ):
        first[2 * i].wait()
        keep[...] = (src[far].astype(f32) + one[0].astype(f32)).astype(keep.dtype)
        copy = remote(keep, two, send.at[6 + i], recv.at[6 + i], (e, far))
        copy.start()
        second.append(copy)
    for i, (src, one, two, out) in enumerate(
        ((grad, in1, in2, ograd), (gg, in1k, in2k, ogg), (res, in1r, in2r, ores))
    ):
        first[2 * i + 1].wait()
        mine = src[t].astype(f32) + one[1].astype(f32)
        second[i].wait()
        out[...] = (mine + two[...].astype(f32)).astype(out.dtype)


def scatter_sums(grad, res, gg, nt, ident):
    one = grad.shape[1:]
    small = gg.shape[1:]
    return pl.pallas_call(
        functools.partial(scatter_kernel, nt),
        out_shape=[
            jax.ShapeDtypeStruct(one, f32),
            jax.ShapeDtypeStruct(one, f32),
            jax.ShapeDtypeStruct(small, f32),
        ],
        in_specs=whole(3),
        out_specs=whole(3),
        scratch_shapes=[
            VMEM(one, bf16), VMEM(one, bf16), VMEM(small, f32),
            VMEM((2,) + one, bf16), VMEM((2,) + one, bf16), VMEM((2,) + small, f32),
            VMEM(one, bf16), VMEM(one, bf16), VMEM(small, f32),
            pltpu.SemaphoreType.DMA((9,)),
            pltpu.SemaphoreType.DMA((9,)),
        ],
        compiler_params=pltpu.CompilerParams(collective_id=ident, has_side_effects=True),
    )(grad, res, gg)


def reduce_kernel(nt, ne, first_rows, rep, x_ref, o_ref, rep_ref, in1, keep, in2, mine, parts, total, send, recv):
    e = lax.axis_index("expert")
    t = lax.axis_index("tensor")
    far = jnp.bitwise_xor(t, 2)
    near = jnp.bitwise_xor(t, 1)
    nearfar = jnp.bitwise_xor(t, 3)
    greet([(e, far), (e, near)] + [(lax.rem(e + d, ne), t) for d in range(1, ne)])
    a = remote(x_ref.at[nearfar], in1.at[0], send.at[0], recv.at[0], (e, near))
    b = remote(x_ref.at[near], in1.at[1], send.at[1], recv.at[1], (e, near))
    a.start()
    b.start()
    a.wait()
    keep[...] = (x_ref[far].astype(f32) + in1[0].astype(f32)).astype(bf16)
    c = remote(keep, in2, send.at[2], recv.at[2], (e, far))
    c.start()
    b.wait()
    own = x_ref[t].astype(f32) + in1[1].astype(f32)
    c.wait()
    mine[...] = (own + in2[...].astype(f32)).astype(bf16).reshape(mine.shape)
    out = []
    for d in range(1, ne):
        p = lax.rem(e + d, ne)
        out.append(remote(mine.at[p], parts.at[d - 1], send.at[2 + d], recv.at[2 + d], (p, t)))
        out[-1].start()
    acc = mine[e].astype(f32)
    for d in range(1, ne):
        out[d - 1].wait()
        acc = acc + parts[d - 1].astype(f32)
    total[e] = acc.astype(bf16)
    back = []
    for d in range(1, ne):
        p = lax.rem(e + d, ne)
        k = 1 + ne + d
        back.append(remote(total.at[e], total.at[e], send.at[k], recv.at[k], (p, t)))
        back[-1].start()
    for copy in back:
        copy.wait()
    full = total[...].reshape(o_ref.shape)
    o_ref[...] = full
    rep_ref[t] = full[first_rows : first_rows + rep]
    k = 1 + 2 * ne
    out = remote(rep_ref.at[t], rep_ref.at[t], send.at[k], recv.at[k], (e, far))
    side = remote(rep_ref.at[t], rep_ref.at[t], send.at[k + 1], recv.at[k + 1], (e, near))
    out.start()
    side.start()
    out.wait_recv()
    relay = remote(rep_ref.at[far], rep_ref.at[far], send.at[k + 2], recv.at[k + 2], (e, near))
    relay.start()
    out.wait_send()
    side.wait()
    relay.wait()


def reduce_all(x, nt, ne, first_rows, rep, ident):
    rows = x.shape[1]
    chunk = rows // ne
    return pl.pallas_call(
        functools.partial(reduce_kernel, nt, ne, first_rows, rep),
        out_shape=[
            jax.ShapeDtypeStruct((rows, 128), bf16),
            jax.ShapeDtypeStruct((nt, rep, 128), bf16),
        ],
        in_specs=whole(1),
        out_specs=whole(2),
        scratch_shapes=[
            VMEM((2, rows, 128), bf16),
            VMEM((rows, 128), bf16),
            VMEM((rows, 128), bf16),
            VMEM((ne, chunk, 128), bf16),
            VMEM((ne - 1, chunk, 128), bf16),
            VMEM((ne, chunk, 128), bf16),
            pltpu.SemaphoreType.DMA((4 + 2 * ne,)),
            pltpu.SemaphoreType.DMA((4 + 2 * ne,)),
        ],
        compiler_params=pltpu.CompilerParams(collective_id=ident, has_side_effects=True),
    )(x)


def body(
    inputs, gain_attend, triple_weight, project_weight, gain_mixture, router_weight, expert_first,
    expert_second, triple_down, triple_up, project_down, project_up, router_down, router_up,
    first_down, first_up, second_down, second_up, adapter_index, routes, priority, cotangent,
):
    ne = lax.axis_size("expert")
    nt = lax.axis_size("tensor")
    tok, width = inputs.shape
    images = adapter_index.shape[0]
    seq = tok // images
    seqp = up(seq, 16)
    per = images // nt
    rows = per * seqp
    experts = router_weight.shape[1]
    local = expert_first.shape[0]
    ffq = expert_first.shape[2]
    lw = triple_weight.shape[2]
    cap = nt * ((5 * tok * TOP + 4 * nt * experts - 1) // (4 * nt * experts))
    capq = cap // nt
    cp = up(capq + 2, 16)
    block = local * cp
    t = lax.axis_index("tensor")
    tix = t.astype(i32).reshape(1)
    smem = pl.BlockSpec(memory_space=pltpu.SMEM)

    wt_q = triple_weight.reshape(width, 3 * lw)
    att = jnp.concatenate(
        [wt_q, triple_up.reshape(ADAPT, 3 * lw)], axis=0
    )
    prj = jnp.concatenate([project_weight, project_down], axis=1)
    att_all = gather_early(att, nt)
    prj_all = gather_early(prj, nt)
    w1_all = gather_early(expert_first, nt)
    w2_all = gather_early(expert_second, nt)
    low_all = gather_early(jnp.stack([first_up.reshape(ADAPT, ffq // 128, 128).swapaxes(0, 1).reshape(ffq, 128), second_down]), nt)
    wt_all = att_all[:, :width]
    tup_all = att_all[:, width:]
    pw_all = prj_all[:, :, :width]
    pd_all = prj_all[:, :, width:]
    fup_all = low_all[:, 0].reshape(nt, ffq // 128, ADAPT, 128).swapaxes(1, 2).reshape(nt, ADAPT, ffq)
    sdn_all = low_all[:, 1]

    prio = priority + (seqp - seq) * (priority // seq)
    rt = jnp.pad(
        routes.reshape(images, seq, TOP), ((0, 0), (0, seqp - seq), (0, 0)), constant_values=-1
    ).reshape(images * seqp, TOP)
    ids = jnp.repeat(adapter_index, seqp, total_repeat_length=images * seqp)
    idc = ids.reshape(-1, 1)
    idq = lax.dynamic_slice(idc, (t * rows, 0), (rows, 1))
    rtq = lax.dynamic_slice(rt, (t * rows, 0), (rows, TOP))
    gain1 = gain_attend.reshape(1, width)
    gain2 = gain_mixture.reshape(1, width)

    wide = up(2 * experts, 128)
    slotc, slotr, cots = pl.pallas_call(
        functools.partial(
            place_kernel, (nt, seq, seqp, images, experts, cap, capq, cp, width)
        ),
        out_shape=[
            jax.ShapeDtypeStruct((nt, rows, TOP), i32),
            jax.ShapeDtypeStruct((nt, TOP, rows), i32),
            jax.ShapeDtypeStruct((ne, block, width), bf16),
        ],
        in_specs=[smem] + whole(4),
        out_specs=whole(3),
        scratch_shapes=[
            VMEM((images * seqp, width), bf16),
            VMEM((images * seqp, 1), f32),
            VMEM((images * seqp, wide), bf16),
        ],
        name="place",
    )(tix, prio, rt, ids.astype(f32).reshape(nt, 1, rows), cotangent)
    got_cot = lax.all_to_all(cots, "expert", 0, 0, tiled=True)

    row_f = jax.ShapeDtypeStruct((rows, width), f32)
    row_b = jax.ShapeDtypeStruct((rows, width), bf16)
    low_b = jax.ShapeDtypeStruct((rows, ADAPT), bf16)
    mixed, middle, triple, attended, tlow, plow, attn_in = pl.pallas_call(
        functools.partial(attend_kernel, (nt, seq, seqp, images)),
        out_shape=[
            row_b,
            row_f,
            jax.ShapeDtypeStruct((nt, rows, 3 * lw), bf16),
            jax.ShapeDtypeStruct((nt, rows, lw), bf16),
            low_b,
            low_b,
            row_b,
        ],
        in_specs=[smem] + whole(10),
        out_specs=whole(7),
        scratch_shapes=[VMEM((rows, width), f32)],
        name="attend",
    )(tix, inputs, gain1, wt_all, tup_all, triple_down, pw_all, pd_all, project_up, gain2, idq)

    mixed_all = gather(mixed, nt, 0)
    sends = pl.pallas_call(
        functools.partial(dispatch_kernel, (nt, capq)),
        out_shape=jax.ShapeDtypeStruct((ne, block, width), bf16),
        in_specs=whole(8),
        out_specs=pl.BlockSpec(memory_space=VMEM),
        scratch_shapes=[VMEM((nt, TOP, rows, 1), f32)],
        name="dispatch",
    )(mixed_all, rt, idc, slotc, slotr, router_weight, router_down, router_up)
    got = swap(sends, ne, 1)

    erows = ne * cp
    quarter = width // nt
    grows = 2 * ffq + quarter + (ADAPT // nt) * (width // 128)
    rets, egrads = pl.pallas_call(
        functools.partial(expert_kernel, (nt, local, capq, cp)),
        out_shape=[
            jax.ShapeDtypeStruct((ne, 2, block, width), bf16),
            jax.ShapeDtypeStruct((nt, grows, 128), bf16),
        ],
        in_specs=whole(8),
        out_specs=whole(2),
        scratch_shapes=[
            VMEM((erows, width), bf16),
            VMEM((erows, width), bf16),
            VMEM((nt, erows, ffq), bf16),
            VMEM((nt, erows, ffq), f32),
            VMEM((2, erows, ADAPT), bf16),
            VMEM((ne, block), f32),
            VMEM((ADAPT, width), f32),
            VMEM((nt, ADAPT, ffq), f32),
            VMEM((nt, ADAPT, ffq), f32),
            VMEM((ADAPT, width), f32),
        ],
        name="experts",
    )(got, got_cot, w1_all, w2_all, first_down, fup_all, sdn_all, second_up)
    back = swap(rets, ne, 2)

    part = jax.ShapeDtypeStruct((nt, rows, width), bf16)
    res_part, grad_part, gg_part = pl.pallas_call(
        functools.partial(combine_kernel, (nt, capq)),
        out_shape=[part, part, jax.ShapeDtypeStruct((nt, TOP, rows), f32)],
        in_specs=whole(3),
        out_specs=whole(3),
        scratch_shapes=[VMEM((ne * block, 1), f32), VMEM((2, ne * block, width), bf16)],
        name="combine",
    )(back, slotc, slotr)
    gmix, res_sum, gg = scatter_sums(grad_part, res_part, gg_part, nt, 3)

    arows = 4 * lw + 2 * quarter + (ADAPT // nt) * (width // 128) + ADAPT // nt
    igrad, agrads = pl.pallas_call(
        functools.partial(back_kernel, (nt, seq, seqp, images)),
        out_shape=[row_b, jax.ShapeDtypeStruct((nt, arows, 128), bf16)],
        in_specs=[smem] + whole(24),
        out_specs=whole(2),
        scratch_shapes=[
            VMEM((2, rows, width), f32),
            VMEM((rows, 3 * lw), bf16),
            VMEM((nt, rows, lw), bf16),
            VMEM((rows, width), f32),
            VMEM((rows, ADAPT), f32),
        ],
        name="attend_back",
    )(
        tix, cotangent, gmix, gg, mixed, middle, triple, attended, tlow, plow, attn_in, inputs,
        gain1, gain2, wt_all, tup_all, triple_down, pw_all, pd_all, project_up, router_weight,
        router_down, router_up, rtq, idq,
    )

    out_q = (middle + res_sum).astype(bf16)
    outs = gather(jnp.stack([out_q, igrad]), nt, 4)

    def unpad(x):
        return x.reshape(images, seqp, width)[:, :seq].reshape(tok, width)

    block_output = unpad(outs[:, 0])
    input_grad = unpad(outs[:, 1])

    held = 2 * ffq
    held_a = 4 * lw
    need = grows + arows
    padded = up(need, 16 * ne)
    rep = up(need - held - held_a, 16)
    parts = [egrads[:, :held], agrads[:, :held_a], egrads[:, held:], agrads[:, held_a:]]
    if padded > need:
        parts.append(jnp.zeros((nt, padded - need, 128), bf16))
    total, shared = reduce_all(jnp.concatenate(parts, axis=1), nt, ne, held + held_a, rep, 5)
    total = total.astype(f32)
    shared = shared.astype(f32)

    def widen(x, n):
        return x.reshape(n, -1, 128).swapaxes(0, 1).reshape(-1, n * 128)

    first_up_grad = widen(total[:ffq], ffq // 128)
    second_down_grad = total[ffq : 2 * ffq]
    triple_up_grad = widen(total[held : held + 3 * lw], 3 * lw // 128).reshape(ADAPT, 3, lw)
    project_down_grad = total[held + 3 * lw : held + 4 * lw]
    share = ADAPT // nt
    cut = [quarter, share * (width // 128), quarter, quarter, share * (width // 128), share]
    pieces, off = [], 0
    for size in cut:
        pieces.append(shared[:, off : off + size])
        off += size

    def wide_all(x):
        return x.reshape(nt, width // 128, share, 128).transpose(0, 2, 1, 3).reshape(ADAPT, width)

    first_down_grad = pieces[0].reshape(width, 128)
    second_up_grad = wide_all(pieces[1])
    triple_down_grad = pieces[2].reshape(width, 128)
    router_down_grad = pieces[3].reshape(width, 128)
    project_up_grad = wide_all(pieces[4])
    router_up_grad = pieces[5].reshape(ADAPT, 128)[:, :experts]
    return (
        block_output, input_grad, triple_down_grad, triple_up_grad, project_down_grad,
        project_up_grad, router_down_grad, router_up_grad, first_down_grad, first_up_grad,
        second_down_grad, second_up_grad,
    )


def solution(mesh):
    return jax.shard_map(
        body,
        mesh=mesh,
        in_specs=(
            P("expert", None),
            P(),
            P(None, None, "tensor"),
            P("tensor", None),
            P(),
            P(),
            P("expert", None, "tensor"),
            P("expert", "tensor", None),
            P(),
            P(None, None, "tensor"),
            P("tensor", None),
            P(),
            P(),
            P(),
            P(),
            P(None, "tensor"),
            P("tensor", None),
            P(),
            P("expert"),
            P("expert", None),
            P("expert", None),
            P("expert", None),
        ),
        out_specs=(
            P("expert", None),
            P("expert", None),
            P(),
            P(None, None, "tensor"),
            P("tensor", None),
            P(),
            P(),
            P(),
            P(),
            P(None, "tensor"),
            P("tensor", None),
            P(),
        ),
        check_vma=False,
    )
```

```python
import functools

import jax
import jax.numpy as jnp
from jax import lax
from jax.experimental import pallas as pl
from jax.experimental.pallas import tpu as pltpu
from jax.sharding import PartitionSpec as P

HEAD_DIM = 64
TOP = 2
ADAPTERS = 8
RANK = 16
ADAPT = ADAPTERS * RANK
EPS = 1e-06

f32 = jnp.float32
bf16 = jnp.bfloat16
i32 = jnp.int32
MESH = pl.DeviceIdType.MESH
VMEM = pltpu.VMEM


def up(a, b):
    return -(-a // b) * b


def dot(a, b):
    return lax.dot_general(a, b, (((1,), (0,)), ((), ())), preferred_element_type=f32)


def dot_nt(a, b):
    return lax.dot_general(a, b, (((1,), (1,)), ((), ())), preferred_element_type=f32)


def dot_tn(a, b):
    return lax.dot_general(a, b, (((0,), (0,)), ((), ())), preferred_element_type=f32)


def split_high_low(a):
    high = a.astype(bf16)
    return high, (a - high.astype(f32)).astype(bf16)


def dot_fine(a, b):
    high, low = split_high_low(a)
    return dot(high, b) + dot(low, b)


def dot_nt_fine(a, b):
    high, low = split_high_low(a)
    return dot_nt(high, b) + dot_nt(low, b)


def iota(shape, axis):
    return lax.broadcasted_iota(i32, shape, axis)


def to_row(col):
    n = col.shape[0]
    return jnp.sum(jnp.where(iota((n, n), 0) == iota((n, n), 1), col, 0.0), axis=0, keepdims=True)


def to_col(row):
    n = row.shape[1]
    return jnp.sum(jnp.where(iota((n, n), 0) == iota((n, n), 1), row, 0.0), axis=1, keepdims=True)


def picks_of(adapters, base, per, seqp):
    lane = iota((seqp, ADAPT), 1) // RANK
    return jnp.concatenate(
        [(lane == adapters[base + li]).astype(f32) for li in range(per)], axis=0
    )


def whole(count):
    return [pl.BlockSpec(memory_space=VMEM) for _ in range(count)]


def norm_stats(x):
    centre = jnp.mean(x, axis=-1, keepdims=True)
    shifted = x - centre
    scale = lax.rsqrt(jnp.mean(shifted * shifted, axis=-1, keepdims=True) + EPS)
    return shifted * scale, scale


def norm_back(grad, gain, unit, scale):
    g = grad * gain
    return scale * (
        g - jnp.mean(g, axis=-1, keepdims=True) - unit * jnp.mean(g * unit, axis=-1, keepdims=True)
    )


def greet(peers):
    barrier = pltpu.get_barrier_semaphore()
    for peer in peers:
        pl.semaphore_signal(barrier, 1, device_id=peer, device_id_type=MESH)
    pl.semaphore_wait(barrier, len(peers))


def remote(src, dst, send, recv, peer):
    return pltpu.make_async_remote_copy(
        src_ref=src, dst_ref=dst, send_sem=send, recv_sem=recv, device_id=peer, device_id_type=MESH
    )


def where_am_i():
    e = lax.axis_index("expert")
    t = lax.axis_index("tensor")
    return e, t, jnp.bitwise_xor(t, 1), jnp.bitwise_xor(t, 2), jnp.bitwise_xor(t, 3)


def dma(n):
    return pltpu.SemaphoreType.DMA((n,))


def linked(ident):
    return pltpu.CompilerParams(collective_id=ident, has_side_effects=True)


def place_kernel(dims, *refs):
    nt, seq, seqp, images, experts, cap, capq, cp, width, n_w = dims
    adapters, prio, routes, cot = refs[:4]
    w_in = refs[4 : 4 + n_w]
    slotc, slotr, routec, cots = refs[4 + n_w : 8 + n_w]
    w_out = refs[8 + n_w : 8 + 2 * n_w]
    cot_pad, rank_s, one_s, send, recv, here = refs[8 + 2 * n_w :]
    e, t, near, far, _ = where_am_i()
    greet([(e, far), (e, near)])
    fars, nears, owns = [], [], []
    for i in range(n_w):
        fars.append(remote(w_in[i], w_out[i].at[t], send.at[3 * i], recv.at[3 * i], (e, far)))
        fars[-1].start()
    for i in range(n_w):
        nears.append(
            remote(w_in[i], w_out[i].at[t], send.at[3 * i + 1], recv.at[3 * i + 1], (e, near))
        )
        nears[-1].start()
        owns.append(pltpu.make_async_copy(w_in[i], w_out[i].at[t], here.at[i]))
        owns[-1].start()
    tok = prio.shape[1]
    per = images // nt
    rows = per * seqp
    total = nt * rows
    wide = one_s.shape[-1]
    order = iota((seqp, tok), 1).astype(f32)
    lane = iota((seqp, wide), 1)
    for i in range(images):
        q, at = i // per, pl.ds(i % per * seqp, seqp)
        all_at = pl.ds(i * seqp, seqp)
        token = iota((seqp, 1), 0) + i * seq
        rank_s[all_at, :] = jnp.sum(
            jnp.where(prio[...] == token, order, 0.0), axis=1, keepdims=True
        )
        w0 = i * seq // 128 * 128
        w1 = min(w0 + up(seq + 128, 128), tok)
        here_i = (iota((seqp, w1 - w0), 1) + w0 == token) & (iota((seqp, w1 - w0), 0) < seq)
        r = [
            jnp.sum(
                jnp.where(here_i, routes[k : k + 1, w0:w1].astype(f32) + 1.0, 0.0),
                axis=1,
                keepdims=True,
            ).astype(i32)
            - 1
            for k in range(TOP)
        ]
        for k in range(TOP):
            routec[q, at, k : k + 1] = r[k]
        named = jnp.where(lane < experts, r[0], jnp.where(r[1] < 0, -1, r[1] + experts))
        one_s[all_at, :] = (named == lane).astype(f32).astype(bf16)
    totals = dot(jnp.ones((8, total), bf16), one_s[...])[0:1]
    rank_rows = [to_row(rank_s[pl.ds(q * rows, rows), :]) for q in range(nt)]
    lane = iota((rows, wide), 1)
    for q in range(nt):
        at = pl.ds(q * rows, rows)
        mine = rank_s[at, :]
        counts = jnp.zeros((rows, wide), f32)
        for p in range(nt):
            before = (rank_rows[p] < mine).astype(f32).astype(bf16)
            counts = counts + dot(before, one_s[pl.ds(p * rows, rows), :])
        hot = one_s[at, :].astype(f32) * counts
        first = jnp.sum(jnp.where(lane < experts, hot, 0.0), axis=1, keepdims=True)
        second = jnp.sum(
            jnp.where(lane < experts, 0.0, hot)
            + jnp.where((lane < experts) & (routec[q, :, 1:2] == lane), totals, 0.0),
            axis=1,
            keepdims=True,
        )
        for k, pos in ((0, first), (1, second)):
            named = routec[q, :, k : k + 1]
            place = pos.astype(i32)
            kept = (named >= 0) & (place < cap) & (lax.rem(place, nt) == t)
            slot = jnp.where(kept, named * cp + lax.div(place, nt), -1)
            slotc[q, :, k : k + 1] = slot
            slotr[q, k : k + 1, :] = to_row(slot.astype(f32)).astype(i32)
    relays = []

    def relay(i):
        fars[i].wait_recv()
        copy = remote(
            w_out[i].at[far], w_out[i].at[far], send.at[3 * i + 2], recv.at[3 * i + 2], (e, near)
        )
        copy.start()
        relays.append(copy)

    relay(0)
    for i in range(images):
        start = i * seq // 16 * 16
        stop = min(start + up(seq, 16) + 16, tok)
        src = iota((seqp, stop - start), 1) + start
        row = iota((seqp, stop - start), 0)
        sel = ((src == row + i * seq) & (row < seq)).astype(f32).astype(bf16)
        cot_pad[pl.ds(i * seqp, seqp), :] = dot(sel, cot[start:stop, :]).astype(bf16)
    n_out, block = cots.shape[0], cots.shape[1]
    step = max(1, 512 // block)
    image_of = iota((1, rows), 1) // seqp

    def pack(d, carry):
        s = iota((step * block, 1), 0) + d * (step * block)
        acc = jnp.zeros((step * block, width), f32)
        idc = jnp.zeros((step * block, 1), f32)
        for q in range(nt):
            ids = jnp.zeros((1, rows), f32)
            for li in range(per):
                ids = jnp.where(image_of == li, adapters[q * per + li].astype(f32), ids)
            g = (slotr[q, 0:1, :] == s) | (slotr[q, 1:2, :] == s)
            idc = idc + jnp.sum(jnp.where(g, ids, 0.0), axis=1, keepdims=True)
            acc = acc + dot(g.astype(f32).astype(bf16), cot_pad[pl.ds(q * rows, rows), :])
        row = iota((block, block), 0)
        for b in range(step):
            part = acc[b * block : (b + 1) * block]
            idr = to_row(idc[b * block : (b + 1) * block])
            head = jnp.where(row == capq, idr, part[:, 0:block])
            cots[d * step + b, :, 0:block] = head.astype(bf16)
            cots[d * step + b, :, block:] = part[:, block:].astype(bf16)
        return carry

    lax.fori_loop(0, n_out // step, pack, 0)
    for i in range(1, n_w):
        relay(i)
    for i in range(n_w):
        fars[i].wait_send()
        nears[i].wait()
        owns[i].wait()
        relays[i].wait()


def gates_of(mixed, r0, r1, pick, rw, rd, ru):
    low = dot(mixed, rd) * pick
    logits = dot(mixed, rw) + dot_fine(low, ru)
    lane = iota((1, rw.shape[1]), 1)
    first = jnp.sum(jnp.where(r0 == lane, logits, 0.0), axis=1, keepdims=True)
    second = jnp.sum(jnp.where(r1 == lane, logits, 0.0), axis=1, keepdims=True)
    top = jnp.maximum(first, second)
    a = jnp.exp(first - top)
    b = jnp.exp(second - top)
    return a / (a + b), b / (a + b), low


def attend_kernel(
    dims, adapters, x_ref, gain1, wt, tup, tdn, pw, pd, pup, gain2, routec, slotr, rw, rd, ru, cots,
    got, got_cot, mixed, middle, triple, attended, tlow, plow, attn_in,
    xs, mall, gall, acc_s, gate_s, out_s, send, recv, csend, crecv, tsend, trecv, here,
):
    nt, ne, seq, seqp, images, capq = dims
    e, t, near, far, cross = where_am_i()
    greet([(e, far), (e, near)] + [(lax.rem(e + d, ne), t) for d in range(1, ne)])

    def cot_copy(d):
        p = lax.rem(e + d, ne)
        return remote(cots.at[p], got_cot.at[e], csend.at[d], crecv.at[d], (p, t))

    def cot_start(d, carry):
        cot_copy(d).start()
        return carry

    lax.fori_loop(1, ne, cot_start, 0)
    own_cot = pltpu.make_async_copy(cots.at[e], got_cot.at[e], here.at[0])
    own_cot.start()

    per = images // nt
    rows = per * seqp
    tok = x_ref.shape[0]
    lw = wt.shape[2] // 3
    for li in range(per):
        base = (t * per + li) * seq
        row = iota((seqp, tok), 0)
        sel = ((iota((seqp, tok), 1) == row + base) & (row < seq)).astype(f32).astype(bf16)
        xs[pl.ds(li * seqp, seqp), :] = dot(sel, x_ref[...])
    pick = picks_of(adapters, t * per, per, seqp)
    unit, _ = norm_stats(xs[...])
    normed = (unit * gain1[...]).astype(bf16)
    attn_in[...] = normed
    low = (dot(normed, tdn[...]) * pick).astype(bf16)
    tlow[...] = low
    head_of = iota((1, lw), 1) // HEAD_DIM
    key_ok = iota((1, seqp), 1) < seq

    def piece(p, carry):
        triple[p] = (dot(normed, wt[p]) + dot(low, tup[p])).astype(bf16)
        for li in range(per):
            at = pl.ds(li * seqp, seqp)
            q = triple[p, at, 0:lw]
            k = triple[p, at, lw : 2 * lw]
            v = triple[p, at, 2 * lw : 3 * lw]
            acc = jnp.zeros((seqp, lw), f32)
            for h in range(lw // HEAD_DIM):
                on = head_of == h
                s = dot_nt(jnp.where(on, q, 0.0).astype(bf16), k) * HEAD_DIM**-0.5
                s = jnp.where(key_ok, s, -jnp.inf)
                ex = jnp.exp(s - jnp.max(s, axis=1, keepdims=True))
                probs = (ex / jnp.sum(ex, axis=1, keepdims=True)).astype(bf16)
                acc = acc + dot(probs, jnp.where(on, v, 0.0).astype(bf16))
            attended[p, at, :] = acc.astype(bf16)
        return carry

    lax.fori_loop(0, nt, piece, 0)
    psum = jnp.zeros((rows, ADAPT), f32)
    branch = jnp.zeros((rows, pup.shape[1]), f32)
    for p in range(nt):
        psum = psum + dot(attended[p], pd[p])
        branch = branch + dot(attended[p], pw[p])
    low2 = (psum * pick).astype(bf16)
    plow[...] = low2
    mid = xs[...] + branch + dot(low2, pup[...])
    middle[...] = mid
    unit2, _ = norm_stats(mid)
    mix = (unit2 * gain2[...]).astype(bf16)
    mixed[...] = mix
    mall[t] = mix
    r = routec[t]
    a, b, _ = gates_of(mix, r[:, 0:1], r[:, 1:2], pick, rw[...], rd[...], ru[...])
    gall[t] = jnp.zeros(gall.shape[1:], f32)
    gall[t, 0:1, :] = to_row(a)
    gall[t, 1:2, :] = to_row(b)

    fars = [
        remote(buf.at[t], buf.at[t], tsend.at[i], trecv.at[i], (e, far))
        for i, buf in enumerate((mall, gall))
    ]
    nears = [
        remote(buf.at[t], buf.at[t], tsend.at[2 + i], trecv.at[2 + i], (e, near))
        for i, buf in enumerate((mall, gall))
    ]
    for copy in fars + nears:
        copy.start()

    n_out, block, width = got.shape
    step = max(1, 512 // block)

    def gather_rows(q, s):
        g0 = slotr[q, 0:1, :] == s
        g1 = slotr[q, 1:2, :] == s
        gate = jnp.sum(
            jnp.where(g0, gall[q, 0:1, :], jnp.where(g1, gall[q, 1:2, :], 0.0)), axis=1, keepdims=True
        )
        return dot((g0 | g1).astype(f32).astype(bf16), mall[q]), gate

    def add_quarter(q, fresh):
        def some(d, carry):
            at = pl.ds(pl.multiple_of(d * (step * block), step * block), step * block)
            s = iota((step * block, 1), 0) + d * (step * block)
            part, gate = gather_rows(q, s)
            acc_s[at, :] = part if fresh else acc_s[at, :] + part
            gate_s[at, :] = gate if fresh else gate_s[at, :] + gate
            return carry

        lax.fori_loop(0, n_out // step, some, 0)

    add_quarter(t, True)
    for copy in nears:
        copy.wait_recv()
    add_quarter(near, False)
    for copy in fars:
        copy.wait_recv()
    relays = [
        remote(buf.at[far], buf.at[far], tsend.at[4 + i], trecv.at[4 + i], (e, near))
        for i, buf in enumerate((mall, gall))
    ]
    for copy in relays:
        copy.start()
    add_quarter(far, False)
    for copy in relays:
        copy.wait_recv()

    def finish(p):
        at = pl.ds(pl.multiple_of(p * block, block), block)
        part, gate = gather_rows(cross, iota((block, 1), 0) + p * block)
        part = acc_s[at, :] + part
        gate = to_row(gate_s[at, :] + gate)
        high = gate.astype(bf16).astype(f32)
        row = iota((block, block), 0)
        head = jnp.where(row == capq, high, part[:, 0:block])
        head = jnp.where(row == capq + 1, gate - high, head)
        return head.astype(bf16), part[:, block:].astype(bf16)

    def out_copy(d):
        p = lax.rem(e + d, ne)
        return remote(out_s.at[p], got.at[e], send.at[d], recv.at[d], (p, t))

    def send_one(d, carry):
        p = lax.rem(e + d, ne)
        head, tail = finish(p)
        out_s[p, :, 0:block] = head
        out_s[p, :, block:] = tail
        out_copy(d).start()
        return carry

    lax.fori_loop(1, ne, send_one, 0)
    head, tail = finish(e)
    got[e, :, 0:block] = head
    got[e, :, block:] = tail

    def drain(d, carry):
        cot_copy(d).wait()
        out_copy(d).wait()
        return carry

    lax.fori_loop(1, ne, drain, 0)
    own_cot.wait()
    for copy in fars:
        copy.wait_send()
    for copy in nears:
        copy.wait_send()
    for copy in relays:
        copy.wait_send()


def erf_parts(pre):
    cdf = 0.5 * (1.0 + lax.erf(pre * 0.7071067811865476))
    return pre * cdf, cdf + pre * (jnp.exp(-0.5 * pre * pre) * 0.3989422804014327)


def expert_kernel(
    dims, got, cot, fdn, fup, sdn, sup, w1a, w1b, w1c, w1d, w2a, w2b, w2c, w2d, back, gsum,
    w1, w2, sent_s, sg_s, hid_s, dg_s, low_s, ret_s, acc_fd, acc_fu, acc_sd, acc_su,
    gr_s, in1, keep, in2, send, recv, tsend, trecv, here,
):
    nt, ne, local, capq, cp = dims
    e_i, t, near, far, cross = where_am_i()
    loads = []
    for m, (a, b) in enumerate(((w1a, w2a), (w1b, w2b), (w1c, w2c), (w1d, w2d))):
        q = jnp.bitwise_xor(t, m)
        loads.append(pltpu.make_async_copy(a, w1.at[q], here.at[2 * m]))
        loads.append(pltpu.make_async_copy(b, w2.at[q], here.at[2 * m + 1]))
    for load in loads:
        load.start()
    greet([(e_i, far), (e_i, near)] + [(lax.rem(e_i + d, ne), t) for d in range(1, ne)])
    n, block, width = got.shape
    ffq = w1.shape[3]
    rows = n * cp
    real = lax.rem(iota((rows, 1), 0), cp) < capq
    acc_fd[...] = jnp.zeros_like(acc_fd)
    acc_fu[...] = jnp.zeros_like(acc_fu)
    acc_sd[...] = jnp.zeros_like(acc_sd)
    acc_su[...] = jnp.zeros_like(acc_su)

    def ret_copy(d, e, j):
        p = lax.rem(e_i + d, ne)
        k = (d * local + e) * 2 + j
        return remote(
            ret_s.at[e, j, p], back.at[e_i, j, pl.ds(e * cp, cp)], send.at[k], recv.at[k], (p, t)
        )

    def ret_start(e, j):
        def one(d, carry):
            ret_copy(d, e, j).start()
            return carry

        lax.fori_loop(1, ne, one, 0)
        back[e_i, j, pl.ds(e * cp, cp), :] = ret_s[e, j, e_i]

    for e in range(local):
        at = pl.ds(e * cp, cp)
        sent = jnp.where(real, got[:, at, :].reshape(rows, width).astype(f32), 0.0).astype(bf16)
        cots = jnp.where(real, cot[:, at, :].reshape(rows, width).astype(f32), 0.0)
        diag = iota((cp, block), 0) + e * cp == iota((cp, block), 1)
        ids, gates = [], []
        for m in range(n):
            idr = cot[m, capq : capq + 1, 0:block].astype(f32)
            gr = got[m, capq : capq + 1, 0:block].astype(f32) + got[
                m, capq + 1 : capq + 2, 0:block
            ].astype(f32)
            ids.append(jnp.sum(jnp.where(diag, idr, 0.0), axis=1, keepdims=True))
            gates.append(jnp.sum(jnp.where(diag, gr, 0.0), axis=1, keepdims=True))
        gate = jnp.concatenate(gates, axis=0)
        pick = (jnp.concatenate(ids, axis=0) == (iota((1, ADAPT), 1) // RANK).astype(f32)).astype(f32)
        sent_s[...] = sent
        sgrad = (gate * cots).astype(bf16)
        sg_s[...] = sgrad
        low_s[0] = (dot(sent, fdn[...]) * pick).astype(bf16)
        low_s[1] = (dot_nt(sgrad, sup[...]) * pick).astype(bf16)
        if e == 0:
            for load in loads:
                load.wait()

        def ahead(c, carry):
            second, res = carry
            pre = dot(sent_s[...], w1[c, e]) + dot(low_s[0], fup[c])
            act, slope = erf_parts(pre)
            hid = act.astype(bf16)
            hid_s[c] = hid
            dg_s[c] = slope
            return second + dot(hid, sdn[c]), res + dot(hid, w2[c, e])

        second, res = lax.fori_loop(
            0, nt, ahead, (jnp.zeros((rows, ADAPT), f32), jnp.zeros((rows, width), f32))
        )
        second_low = (second * pick).astype(bf16)
        res = (res + dot(second_low, sup[...])).astype(bf16).astype(f32)
        grad_gate = jnp.sum(res * cots, axis=1, keepdims=True)
        out = gate * res
        row = iota((cp, block), 0)
        for m in range(n):
            part = out[m * cp : (m + 1) * cp]
            gg = jnp.sum(
                jnp.where(diag, grad_gate[m * cp : (m + 1) * cp], 0.0), axis=0, keepdims=True
            )
            high = gg.astype(bf16).astype(f32)
            head = jnp.where(row == capq, high, part[:, 0:block])
            head = jnp.where(row == capq + 1, gg - high, head)
            ret_s[e, 0, m, :, 0:block] = head.astype(bf16)
            ret_s[e, 0, m, :, block:] = part[:, block:].astype(bf16)
        ret_start(e, 0)
        acc_su[...] += dot_tn(second_low, sgrad)

        def behind(c, carry):
            low1, gsent = carry
            ghid = dot_nt(sg_s[...], w2[c, e]) + dot_nt(low_s[1], sdn[c])
            gpre = (ghid * dg_s[c]).astype(bf16)
            acc_fu[c] += dot_tn(low_s[0], gpre)
            acc_sd[c] += dot_tn(low_s[1], hid_s[c])
            return low1 + dot_nt(gpre, fup[c]), gsent + dot_nt(gpre, w1[c, e])

        low1, gsent = lax.fori_loop(
            0, nt, behind, (jnp.zeros((rows, ADAPT), f32), jnp.zeros((rows, width), f32))
        )
        g1low = (low1 * pick).astype(bf16)
        gsent = gsent + dot_nt(g1low, fdn[...])
        ret_s[e, 1] = gsent.astype(bf16).reshape(n, cp, width)
        ret_start(e, 1)
        acc_fd[...] += dot_tn(g1low, sent)
    quarter = width // nt
    share = ADAPT // nt
    for q in range(nt):
        off = 0
        for c in range(ffq // 128):
            gr_s[q, off : off + 128, :] = acc_fu[q, :, c * 128 : (c + 1) * 128].astype(bf16)
            off += 128
        gr_s[q, off : off + ffq, :] = acc_sd[q].T.astype(bf16)
        off += ffq
        gr_s[q, off : off + quarter, :] = acc_fd[:, q * quarter : (q + 1) * quarter].T.astype(bf16)
        off += quarter
        for c in range(width // 128):
            at = slice(q * share, (q + 1) * share)
            gr_s[q, off : off + share, :] = acc_su[at, c * 128 : (c + 1) * 128].astype(bf16)
            off += share
        if off < gr_s.shape[1]:
            gr_s[q, off:, :] = jnp.zeros((gr_s.shape[1] - off, 128), bf16)
    tensor_sum(gr_s, in1, keep, in2, gsum, tsend, trecv, 0)

    def drain(d, carry):
        for e in range(local):
            for j in range(2):
                ret_copy(d, e, j).wait()
        return carry

    lax.fori_loop(1, ne, drain, 0)


def tensor_sum(src, in1, keep, in2, out, send, recv, k):
    e, t, near, far, cross = where_am_i()
    a = remote(src.at[cross], in1.at[0], send.at[k], recv.at[k], (e, near))
    b = remote(src.at[near], in1.at[1], send.at[k + 1], recv.at[k + 1], (e, near))
    a.start()
    b.start()
    a.wait()
    keep[...] = (src[far].astype(f32) + in1[0].astype(f32)).astype(bf16)
    c = remote(keep, in2, send.at[k + 2], recv.at[k + 2], (e, far))
    c.start()
    b.wait()
    mine = src[t].astype(f32) + in1[1].astype(f32)
    c.wait()
    out[...] = (mine + in2[...].astype(f32)).astype(bf16)


def expert_sum_start(ne, src, parts, send, recv):
    e, t = where_am_i()[:2]

    def copy(d):
        p = lax.rem(e + d, ne)
        return remote(src.at[p], parts.at[d - 1], send.at[d], recv.at[d], (p, t))

    def start(d, carry):
        copy(d).start()
        return carry

    lax.fori_loop(1, ne, start, 0)
    return copy


def expert_sum_share(ne, copy, src, parts, total, send, recv):
    e, t = where_am_i()[:2]

    def add(d, acc):
        copy(d).wait()
        return acc + parts[d - 1].astype(f32)

    total[e] = lax.fori_loop(1, ne, add, src[e].astype(f32)).astype(bf16)

    def share(d):
        p = lax.rem(e + d, ne)
        return remote(total.at[e], total.at[e], send.at[ne + d], recv.at[ne + d], (p, t))

    def start(d, carry):
        share(d).start()
        return carry

    lax.fori_loop(1, ne, start, 0)
    return share


def wait_all(ne, copy):
    def wait(d, carry):
        copy(d).wait()
        return carry

    lax.fori_loop(1, ne, wait, 0)


def combine_kernel(
    dims, got, slotc, slotr, eg, ograd, ogg, res_mine, res_far, etot,
    gcol, rows_s, grad_s, res_s, gg_s, in1, in1r, in1k, keep_g, keep_k, in2, in2k, parts,
    send, recv, esend, erecv,
):
    nt, ne, capq, cp = dims
    e, t, near, far, cross = where_am_i()
    greet([(e, far), (e, near)] + [(lax.rem(e + d, ne), t) for d in range(1, ne)])
    first_sum = expert_sum_start(ne, eg, parts, esend, erecv)
    n, _, block, width = got.shape
    for d in range(n):
        gr = jnp.zeros((1, block), f32)
        for le in range(block // cp):
            for k in range(2):
                at = le * cp + capq + k
                gr = gr + got[d, 0, at : at + 1, 0:block].astype(f32)
        gcol[d * block : (d + 1) * block, :] = to_col(gr)
    slots = n * block
    for j in range(2):
        rows_s[j] = got[:, j].reshape(slots, width)

    def tokens(q):
        s = iota((1, slots), 1)
        c = slotc[q]
        g = ((c[:, 0:1] == s) | (c[:, 1:2] == s)).astype(f32).astype(bf16)
        grad_s[q] = dot(g, rows_s[1]).astype(bf16)
        res_s[q] = dot(g, rows_s[0]).astype(bf16)
        sc = iota((slots, 1), 0)
        gg_s[q] = jnp.zeros(gg_s.shape[1:], f32)
        for k in range(TOP):
            gg_s[q, k : k + 1, :] = jnp.sum(
                jnp.where(slotr[q, k : k + 1, :] == sc, gcol[...], 0.0), axis=0, keepdims=True
            )

    stages = ((grad_s, in1), (gg_s, in1k), (res_s, in1r))
    first = {}
    for j, q in enumerate((cross, near)):
        tokens(q)
        for i, (src, dst) in enumerate(stages):
            k = 2 * i + j
            first[i, j] = remote(src.at[q], dst.at[j], send.at[k], recv.at[k], (e, near))
            first[i, j].start()
    tokens(far)
    second = []
    for i, (src, one, keep, two) in enumerate(
        ((grad_s, in1, keep_g, in2), (gg_s, in1k, keep_k, in2k))
    ):
        first[i, 0].wait()
        keep[...] = (src[far].astype(f32) + one[0].astype(f32)).astype(keep.dtype)
        copy = remote(keep, two, send.at[6 + i], recv.at[6 + i], (e, far))
        copy.start()
        second.append(copy)
    first[2, 0].wait()
    res_far[...] = (res_s[far].astype(f32) + in1r[0].astype(f32)).astype(bf16)
    tokens(t)
    second_sum = expert_sum_share(ne, first_sum, eg, parts, etot, esend, erecv)
    first[2, 1].wait()
    res_mine[...] = (res_s[t].astype(f32) + in1r[1].astype(f32)).astype(bf16)
    for i, (src, one, two, out) in enumerate(
        ((grad_s, in1, in2, ograd), (gg_s, in1k, in2k, ogg))
    ):
        first[i, 1].wait()
        mine = src[t].astype(f32) + one[1].astype(f32)
        second[i].wait()
        out[...] = mine + two[...].astype(f32)
    wait_all(ne, second_sum)


def back_kernel(
    dims, place, adapters, cot_ref, gmix, ggate, mixed, middle, triple, attended, tlow, plow, attn_in,
    x_ref, gain1, gain2, wt, tup, tdn, pw, pd, pup, rw, rd, ru, routec,
    igrad, grads, xs, gt_s, ga_s, acc_in, acc_low,
):
    nt, seq, seqp, images = dims
    t = place[0]
    per = images // nt
    tok = x_ref.shape[0]
    width = x_ref.shape[1]
    lw = wt.shape[2] // 3
    rows = per * seqp
    quarter = width // nt
    for li in range(per):
        base = (t * per + li) * seq
        row = iota((seqp, tok), 0)
        sel = ((iota((seqp, tok), 1) == row + base) & (row < seq)).astype(f32).astype(bf16)
        at = pl.ds(li * seqp, seqp)
        xs[0, at, :] = dot(sel, x_ref[...])
        xs[1, at, :] = dot(sel, cot_ref[...])
    r = routec[t]
    pick = picks_of(adapters, t * per, per, seqp)
    prob0, prob1, rlow = gates_of(
        mixed[...], r[:, 0:1], r[:, 1:2], pick, rw[...], rd[...], ru[...]
    )
    gg0 = to_col(ggate[0:1, :])
    gg1 = to_col(ggate[1:2, :])
    inner = prob0 * gg0 + prob1 * gg1
    lane = iota((1, rw.shape[1]), 1)
    glog = jnp.where(r[:, 0:1] == lane, prob0 * (gg0 - inner), 0.0) + jnp.where(
        r[:, 1:2] == lane, prob1 * (gg1 - inner), 0.0
    )
    llow = dot_nt_fine(glog, ru[...]) * pick
    gm = gmix[...].astype(f32) + dot_nt_fine(glog, rw[...]) + dot_nt_fine(llow, rd[...])
    router_up = dot_tn(rlow.astype(bf16), glog.astype(bf16))
    router_down = dot_tn(mixed[...], llow.astype(bf16))
    unit2, scale2 = norm_stats(middle[...])
    gmid = xs[1] + norm_back(gm, gain2[...], unit2, scale2)
    xs[1] = gmid
    gbranch = gmid.astype(bf16)
    project_up = dot_tn(plow[...], gbranch)
    blow = (dot_nt(gbranch, pup[...]) * pick).astype(bf16)
    for p in range(nt):
        ga_s[p] = (dot_nt(gbranch, pw[p]) + dot_nt(blow, pd[p])).astype(bf16)
    head_of = iota((1, lw), 1) // HEAD_DIM
    key_ok = iota((1, seqp), 1) < seq
    acc_in[...] = jnp.zeros_like(acc_in)
    acc_low[...] = jnp.zeros_like(acc_low)

    def piece(p, carry):
        for li in range(per):
            at = pl.ds(li * seqp, seqp)
            q = triple[p, at, 0:lw]
            k = triple[p, at, lw : 2 * lw]
            v = triple[p, at, 2 * lw : 3 * lw]
            ga = ga_s[p, at, :]
            gq = jnp.zeros((seqp, lw), f32)
            gk = jnp.zeros((seqp, lw), f32)
            gv = jnp.zeros((seqp, lw), f32)
            for h in range(lw // HEAD_DIM):
                on = head_of == h
                qm = jnp.where(on, q, 0.0).astype(bf16)
                km = jnp.where(on, k, 0.0).astype(bf16)
                gam = jnp.where(on, ga, 0.0).astype(bf16)
                s = dot_nt(qm, k) * HEAD_DIM**-0.5
                s = jnp.where(key_ok, s, -jnp.inf)
                ex = jnp.exp(s - jnp.max(s, axis=1, keepdims=True))
                probs = ex / jnp.sum(ex, axis=1, keepdims=True)
                gp = dot_nt(gam, v)
                ds = (probs * (gp - jnp.sum(probs * gp, axis=1, keepdims=True))).astype(bf16)
                gq = gq + dot(ds, km)
                gk = gk + dot_tn(ds, qm)
                gv = gv + dot_tn(probs.astype(bf16), gam)
            gt_s[at, 0:lw] = (gq * HEAD_DIM**-0.5).astype(bf16)
            gt_s[at, lw : 2 * lw] = (gk * HEAD_DIM**-0.5).astype(bf16)
            gt_s[at, 2 * lw : 3 * lw] = gv.astype(bf16)
        gt = gt_s[...]
        acc_low[...] += dot_nt(gt, tup[p])
        acc_in[...] += dot_nt(gt, wt[p])
        tu = dot_tn(tlow[...], gt)
        for c in range(3 * lw // 128):
            grads[p, c * 128 : (c + 1) * 128, :] = tu[:, c * 128 : (c + 1) * 128].astype(bf16)
        off = 3 * lw
        grads[p, off : off + lw, :] = dot_tn(attended[p], blow).astype(bf16)
        return carry

    lax.fori_loop(0, nt, piece, 0)
    tglow = (acc_low[...] * pick).astype(bf16)
    gin = acc_in[...] + dot_nt(tglow, tdn[...])
    triple_down = dot_tn(attn_in[...], tglow)
    unit1, scale1 = norm_stats(xs[0])
    igrad[...] = (xs[1] + norm_back(gin, gain1[...], unit1, scale1)).astype(bf16)
    share = ADAPT // nt
    for q in range(nt):
        off = 4 * lw
        at = slice(q * quarter, (q + 1) * quarter)
        grads[q, off : off + quarter, :] = triple_down[at].astype(bf16)
        off += quarter
        grads[q, off : off + quarter, :] = router_down[at].astype(bf16)
        off += quarter
        at = slice(q * share, (q + 1) * share)
        for c in range(width // 128):
            grads[q, off : off + share, :] = project_up[at, c * 128 : (c + 1) * 128].astype(bf16)
            off += share
        grads[q, off:, :] = jnp.zeros((grads.shape[1] - off, 128), bf16)
        grads[q, off : off + share, 0 : rw.shape[1]] = router_up[at].astype(bf16)


def final_kernel(
    dims, ag, igrad, middle, res_mine, res_far, etot, atot, outs, rep,
    in1, keep, in2, mine, parts, send, recv, esend, erecv,
):
    nt, ne, held_e, held_a = dims
    e, t, near, far, cross = where_am_i()
    greet([(e, far), (e, near)] + [(lax.rem(e + d, ne), t) for d in range(1, ne)])
    outs[t, 1] = igrad[...]
    outs[t, 0] = (middle[...] + res_mine[...].astype(f32) + res_far[...].astype(f32)).astype(bf16)
    a = remote(ag.at[cross], in1.at[0], send.at[0], recv.at[0], (e, near))
    b = remote(ag.at[near], in1.at[1], send.at[1], recv.at[1], (e, near))
    a.start()
    b.start()
    a.wait()
    keep[...] = (ag[far].astype(f32) + in1[0].astype(f32)).astype(bf16)
    c = remote(keep, in2, send.at[2], recv.at[2], (e, far))
    c.start()
    out_far = [remote(outs.at[t, j], outs.at[t, j], send.at[3 + j], recv.at[3 + j], (e, far)) for j in range(2)]
    out_near = [remote(outs.at[t, j], outs.at[t, j], send.at[5 + j], recv.at[5 + j], (e, near)) for j in range(2)]
    for copy in out_far + out_near:
        copy.start()
    b.wait()
    own = ag[t].astype(f32) + in1[1].astype(f32)
    c.wait()
    mine[...] = (own + in2[...].astype(f32)).astype(bf16).reshape(mine.shape)
    first_sum = expert_sum_start(ne, mine, parts, esend, erecv)
    second_sum = expert_sum_share(ne, first_sum, mine, parts, atot, esend, erecv)
    relays = []
    for j in range(2):
        out_far[j].wait_recv()
        relays.append(
            remote(outs.at[far, j], outs.at[far, j], send.at[7 + j], recv.at[7 + j], (e, near))
        )
        relays[-1].start()
    wait_all(ne, second_sum)
    e_rows, a_rows = etot.shape[0] * etot.shape[1], atot.shape[0] * atot.shape[1]
    rep[t, 0 : e_rows - held_e, :] = etot[...].reshape(e_rows, 128)[held_e:]
    rep[t, e_rows - held_e :, :] = atot[...].reshape(a_rows, 128)[held_a:]
    out = remote(rep.at[t], rep.at[t], send.at[9], recv.at[9], (e, far))
    side = remote(rep.at[t], rep.at[t], send.at[10], recv.at[10], (e, near))
    out.start()
    side.start()
    out.wait_recv()
    relay = remote(rep.at[far], rep.at[far], send.at[11], recv.at[11], (e, near))
    relay.start()
    for copy in out_far:
        copy.wait_send()
    for copy in out_near + relays:
        copy.wait()
    out.wait_send()
    side.wait()
    relay.wait()


def write_kernel(
    dims, etot, atot, outs, rep, block_output, input_grad, triple_down, triple_up, project_down,
    project_up, router_down, router_up, first_down, first_up, second_down, second_up,
):
    nt, seq, seqp, images, ffq, lw = dims
    per = images // nt
    tok, width = block_output.shape
    flat = outs.shape[2]
    for j, out in enumerate((block_output, input_grad)):
        for a in range(0, tok, seqp):
            b = min(a + seqp, tok)
            i0, i1 = a // seq, (b - 1) // seq
            parts = []
            for i in range(i0, i1 + 1):
                row = iota((b - a, seqp), 0) + a
                sel = (iota((b - a, seqp), 1) == row - i * seq) & (row < (i + 1) * seq)
                src = outs[i // per, j, (i % per) * seqp : (i % per + 1) * seqp, :]
                parts.append(dot(sel.astype(f32).astype(bf16), src))
            whole_part = parts[0]
            for part in parts[1:]:
                whole_part = whole_part + part
            out[a:b, :] = whole_part.astype(bf16)
    e_all = etot[...].reshape(-1, 128)
    a_all = atot[...].reshape(-1, 128)
    for c in range(ffq // 128):
        first_up[:, c * 128 : (c + 1) * 128] = e_all[c * 128 : (c + 1) * 128].astype(f32)
    second_down[...] = e_all[ffq : 2 * ffq].astype(f32)
    for c in range(3):
        triple_up[:, c, :] = a_all[c * lw : (c + 1) * lw].astype(f32)
    project_down[...] = a_all[3 * lw : 4 * lw].astype(f32)
    quarter = width // nt
    share = ADAPT // nt
    e_rep = etot.shape[0] * etot.shape[1] - 2 * ffq
    for q in range(nt):
        at = slice(q * quarter, (q + 1) * quarter)
        up_at = slice(q * share, (q + 1) * share)
        first_down[at, :] = rep[q, 0:quarter, :].astype(f32)
        off = quarter
        for c in range(width // 128):
            second_up[up_at, c * 128 : (c + 1) * 128] = rep[q, off : off + share, :].astype(f32)
            off += share
        off = e_rep
        triple_down[at, :] = rep[q, off : off + quarter, :].astype(f32)
        off += quarter
        router_down[at, :] = rep[q, off : off + quarter, :].astype(f32)
        off += quarter
        for c in range(width // 128):
            project_up[up_at, c * 128 : (c + 1) * 128] = rep[q, off : off + share, :].astype(f32)
            off += share
        router_up[up_at, :] = rep[q, off : off + share, 0 : router_up.shape[1]].astype(f32)


def quarters(x, nt):
    far = lax.ppermute(x, "tensor", [(i, i ^ 2) for i in range(nt)])
    near = lax.ppermute(x, "tensor", [(i, i ^ 1) for i in range(nt)])
    cross = lax.ppermute(far, "tensor", [(i, i ^ 1) for i in range(nt)])
    return x, near, far, cross


def body(
    inputs, gain_attend, triple_weight, project_weight, gain_mixture, router_weight, expert_first,
    expert_second, triple_down, triple_up, project_down, project_up, router_down, router_up,
    first_down, first_up, second_down, second_up, adapter_index, routes, priority, cotangent,
):
    ne = lax.axis_size("expert")
    nt = lax.axis_size("tensor")
    tok, width = inputs.shape
    images = adapter_index.shape[0]
    seq = tok // images
    seqp = up(seq, 16)
    per = images // nt
    rows = per * seqp
    experts = router_weight.shape[1]
    local = expert_first.shape[0]
    ffq = expert_first.shape[2]
    lw = triple_weight.shape[2]
    cap = nt * ((5 * tok * TOP + 4 * nt * experts - 1) // (4 * nt * experts))
    capq = cap // nt
    cp = up(capq + 2, 16)
    block = local * cp
    smem = pl.BlockSpec(memory_space=pltpu.SMEM)
    anywhere = pl.BlockSpec(memory_space=pl.ANY)
    shape = jax.ShapeDtypeStruct

    weights = (
        triple_weight.reshape(width, 3 * lw),
        triple_up.reshape(ADAPT, 3 * lw),
        project_weight,
        project_down,
        first_up,
        second_down,
    )
    n_w = len(weights)
    wide = up(2 * experts, 128)
    placed = pl.pallas_call(
        functools.partial(
            place_kernel, (nt, seq, seqp, images, experts, cap, capq, cp, width, n_w)
        ),
        out_shape=[
            shape((nt, rows, TOP), i32),
            shape((nt, TOP, rows), i32),
            shape((nt, rows, TOP), i32),
            shape((ne, block, width), bf16),
        ]
        + [shape((nt,) + w.shape, bf16) for w in weights],
        in_specs=[smem] + whole(3 + n_w),
        out_specs=whole(4 + n_w),
        scratch_shapes=[
            VMEM((images * seqp, width), bf16),
            VMEM((images * seqp, 1), f32),
            VMEM((images * seqp, wide), bf16),
            dma(3 * n_w),
            dma(3 * n_w),
            dma(n_w),
        ],
        compiler_params=linked(0),
        name="place",
    )(adapter_index, priority, routes.T, cotangent, *weights)
    slotc, slotr, routec, cots, wt_all, tup_all, pw_all, pd_all, fup_all, sdn_all = placed

    w1_own, w2_own, cots = lax.optimization_barrier((expert_first, expert_second, cots))
    w1s = quarters(w1_own, nt)
    w2s = quarters(w2_own, nt)

    gain1 = gain_attend.reshape(1, width)
    gain2 = gain_mixture.reshape(1, width)
    row_f = shape((rows, width), f32)
    row_b = shape((rows, width), bf16)
    low_b = shape((rows, ADAPT), bf16)
    moved = shape((ne, block, width), bf16)
    got, got_cot, mixed, middle, triple, attended, tlow, plow, attn_in = pl.pallas_call(
        functools.partial(attend_kernel, (nt, ne, seq, seqp, images, capq)),
        out_shape=[
            moved,
            moved,
            row_b,
            row_f,
            shape((nt, rows, 3 * lw), bf16),
            shape((nt, rows, lw), bf16),
            low_b,
            low_b,
            row_b,
        ],
        in_specs=[smem] + whole(15),
        out_specs=whole(9),
        scratch_shapes=[
            VMEM((rows, width), f32),
            VMEM((nt, rows, width), bf16),
            VMEM((nt, 8, rows), f32),
            VMEM((ne * block, width), f32),
            VMEM((ne * block, 1), f32),
            VMEM((ne, block, width), bf16),
            dma(ne),
            dma(ne),
            dma(ne),
            dma(ne),
            dma(6),
            dma(6),
            dma(1),
        ],
        compiler_params=linked(1),
        cost_estimate=pl.CostEstimate(flops=10**10, bytes_accessed=10**8, transcendentals=0),
        name="attend",
    )(
        adapter_index, inputs, gain1, wt_all, tup_all, triple_down, pw_all, pd_all, project_up,
        gain2, routec, slotr, router_weight, router_down, router_up, cots,
    )

    erows = ne * cp
    quarter = width // nt
    held_e = 2 * ffq
    grows = up(held_e + quarter + (ADAPT // nt) * (width // 128), 16 * ne)
    echunk = grows // ne
    back, gsum = pl.pallas_call(
        functools.partial(expert_kernel, (nt, ne, local, capq, cp)),
        out_shape=[
            shape((ne, 2, block, width), bf16),
            shape((grows, 128), bf16),
        ],
        in_specs=whole(6) + [anywhere] * 8,
        out_specs=whole(2),
        scratch_shapes=[
            VMEM((nt, local, width, ffq), bf16),
            VMEM((nt, local, ffq, width), bf16),
            VMEM((erows, width), bf16),
            VMEM((erows, width), bf16),
            VMEM((nt, erows, ffq), bf16),
            VMEM((nt, erows, ffq), f32),
            VMEM((2, erows, ADAPT), bf16),
            VMEM((local, 2, ne, cp, width), bf16),
            VMEM((ADAPT, width), f32),
            VMEM((nt, ADAPT, ffq), f32),
            VMEM((nt, ADAPT, ffq), f32),
            VMEM((ADAPT, width), f32),
            VMEM((nt, grows, 128), bf16),
            VMEM((2, grows, 128), bf16),
            VMEM((grows, 128), bf16),
            VMEM((grows, 128), bf16),
            dma(2 * local * ne),
            dma(2 * local * ne),
            dma(3),
            dma(3),
            dma(8),
        ],
        compiler_params=linked(2),
        name="experts",
    )(got, got_cot, first_down, fup_all, sdn_all, second_up, *w1s, *w2s)

    one = (rows, width)
    small = (8, rows)
    gmix, gg, res_mine, res_away, etot = pl.pallas_call(
        functools.partial(combine_kernel, (nt, ne, capq, cp)),
        out_shape=[
            shape(one, f32),
            shape(small, f32),
            shape(one, bf16),
            shape(one, bf16),
            shape((ne, echunk, 128), bf16),
        ],
        in_specs=whole(4),
        out_specs=whole(5),
        scratch_shapes=[
            VMEM((ne * block, 1), f32),
            VMEM((2, ne * block, width), bf16),
            VMEM((nt,) + one, bf16),
            VMEM((nt,) + one, bf16),
            VMEM((nt,) + small, f32),
            VMEM((2,) + one, bf16),
            VMEM((2,) + one, bf16),
            VMEM((2,) + small, f32),
            VMEM(one, bf16),
            VMEM(small, f32),
            VMEM(one, bf16),
            VMEM(small, f32),
            VMEM((ne - 1, echunk, 128), bf16),
            dma(8),
            dma(8),
            dma(2 * ne),
            dma(2 * ne),
        ],
        compiler_params=linked(3),
        name="combine",
    )(back, slotc, slotr, gsum.reshape(ne, echunk, 128))
    res_far = lax.ppermute(res_away, "tensor", [(i, i ^ 2) for i in range(nt)])

    held_a = 4 * lw
    arows = held_a + 2 * quarter + (ADAPT // nt) * (width // 128) + ADAPT // nt
    arows = up(arows, 16 * ne)
    achunk = arows // ne
    igrad, agrads = pl.pallas_call(
        functools.partial(back_kernel, (nt, seq, seqp, images)),
        out_shape=[row_b, shape((nt, arows, 128), bf16)],
        in_specs=[smem, smem] + whole(23),
        out_specs=whole(2),
        scratch_shapes=[
            VMEM((2, rows, width), f32),
            VMEM((rows, 3 * lw), bf16),
            VMEM((nt, rows, lw), bf16),
            VMEM((rows, width), f32),
            VMEM((rows, ADAPT), f32),
        ],
        cost_estimate=pl.CostEstimate(flops=10**10, bytes_accessed=10**8, transcendentals=0),
        name="attend_back",
    )(
        lax.axis_index("tensor").astype(i32).reshape(1), adapter_index, cotangent, gmix, gg, mixed,
        middle, triple, attended, tlow, plow, attn_in, inputs, gain1, gain2, wt_all, tup_all,
        triple_down, pw_all, pd_all, project_up, router_weight, router_down, router_up, routec,
    )

    rep_rows = grows - held_e + arows - held_a
    atot, outs, rep = pl.pallas_call(
        functools.partial(final_kernel, (nt, ne, held_e, held_a)),
        out_shape=[
            shape((ne, achunk, 128), bf16),
            shape((nt, 2) + one, bf16),
            shape((nt, rep_rows, 128), bf16),
        ],
        in_specs=whole(6),
        out_specs=whole(3),
        scratch_shapes=[
            VMEM((2, arows, 128), bf16),
            VMEM((arows, 128), bf16),
            VMEM((arows, 128), bf16),
            VMEM((ne, achunk, 128), bf16),
            VMEM((ne - 1, achunk, 128), bf16),
            dma(12),
            dma(12),
            dma(2 * ne),
            dma(2 * ne),
        ],
        compiler_params=linked(4),
        name="final",
    )(agrads, igrad, middle, res_mine, res_far, etot)

    return tuple(
        pl.pallas_call(
            functools.partial(write_kernel, (nt, seq, seqp, images, ffq, lw)),
            out_shape=[
                shape((tok, width), bf16),
                shape((tok, width), bf16),
                shape((width, ADAPT), f32),
                shape((ADAPT, 3, lw), f32),
                shape((lw, ADAPT), f32),
                shape((ADAPT, width), f32),
                shape((width, ADAPT), f32),
                shape((ADAPT, experts), f32),
                shape((width, ADAPT), f32),
                shape((ADAPT, ffq), f32),
                shape((ffq, ADAPT), f32),
                shape((ADAPT, width), f32),
            ],
            in_specs=whole(4),
            out_specs=whole(12),
            name="write",
        )(etot, atot, outs, rep)
    )


def solution(mesh):
    return jax.shard_map(
        body,
        mesh=mesh,
        in_specs=(
            P("expert", None),
            P(),
            P(None, None, "tensor"),
            P("tensor", None),
            P(),
            P(),
            P("expert", None, "tensor"),
            P("expert", "tensor", None),
            P(),
            P(None, None, "tensor"),
            P("tensor", None),
            P(),
            P(),
            P(),
            P(),
            P(None, "tensor"),
            P("tensor", None),
            P(),
            P("expert"),
            P("expert", None),
            P("expert", None),
            P("expert", None),
        ),
        out_specs=(
            P("expert", None),
            P("expert", None),
            P(),
            P(None, None, "tensor"),
            P("tensor", None),
            P(),
            P(),
            P(),
            P(),
            P(None, "tensor"),
            P("tensor", None),
            P(),
        ),
        check_vma=False,
    )
```

```python
import functools

import jax
import jax.numpy as jnp
from jax import lax
from jax.experimental import pallas as pl
from jax.experimental.pallas import tpu as pltpu
from jax.sharding import PartitionSpec as P

HEAD_DIM = 64
TOP = 2
ADAPTERS = 8
RANK = 16
ADAPT = ADAPTERS * RANK
EPS = 1e-06

f32 = jnp.float32
bf16 = jnp.bfloat16
i32 = jnp.int32
MESH = pl.DeviceIdType.MESH
VMEM = pltpu.VMEM


def up(a, b):
    return -(-a // b) * b


def dot(a, b):
    return lax.dot_general(a, b, (((1,), (0,)), ((), ())), preferred_element_type=f32)


def dot_nt(a, b):
    return lax.dot_general(a, b, (((1,), (1,)), ((), ())), preferred_element_type=f32)


def dot_tn(a, b):
    return lax.dot_general(a, b, (((0,), (0,)), ((), ())), preferred_element_type=f32)


def split_high_low(a):
    high = a.astype(bf16)
    return high, (a - high.astype(f32)).astype(bf16)


def dot_fine(a, b):
    high, low = split_high_low(a)
    return dot(high, b) + dot(low, b)


def dot_nt_fine(a, b):
    high, low = split_high_low(a)
    return dot_nt(high, b) + dot_nt(low, b)


def iota(shape, axis):
    return lax.broadcasted_iota(i32, shape, axis)


def to_row(col):
    n = col.shape[0]
    return jnp.sum(jnp.where(iota((n, n), 0) == iota((n, n), 1), col, 0.0), axis=0, keepdims=True)


def to_col(row):
    n = row.shape[1]
    return jnp.sum(jnp.where(iota((n, n), 0) == iota((n, n), 1), row, 0.0), axis=1, keepdims=True)


def picks_of(adapters, base, per, seqp):
    lane = iota((seqp, ADAPT), 1) // RANK
    return jnp.concatenate(
        [(lane == adapters[base + li]).astype(f32) for li in range(per)], axis=0
    )


def whole(count):
    return [pl.BlockSpec(memory_space=VMEM) for _ in range(count)]


def norm_stats(x):
    centre = jnp.mean(x, axis=-1, keepdims=True)
    shifted = x - centre
    scale = lax.rsqrt(jnp.mean(shifted * shifted, axis=-1, keepdims=True) + EPS)
    return shifted * scale, scale


def norm_back(grad, gain, unit, scale):
    g = grad * gain
    return scale * (
        g - jnp.mean(g, axis=-1, keepdims=True) - unit * jnp.mean(g * unit, axis=-1, keepdims=True)
    )


def greet(peers):
    barrier = pltpu.get_barrier_semaphore()
    for peer in peers:
        pl.semaphore_signal(barrier, 1, device_id=peer, device_id_type=MESH)
    pl.semaphore_wait(barrier, len(peers))


def remote(src, dst, send, recv, peer):
    return pltpu.make_async_remote_copy(
        src_ref=src, dst_ref=dst, send_sem=send, recv_sem=recv, device_id=peer, device_id_type=MESH
    )


def where_am_i():
    e = lax.axis_index("expert")
    t = lax.axis_index("tensor")
    return e, t, jnp.bitwise_xor(t, 1), jnp.bitwise_xor(t, 2), jnp.bitwise_xor(t, 3)


def dma(n):
    return pltpu.SemaphoreType.DMA((n,))


def linked(ident):
    return pltpu.CompilerParams(collective_id=ident, has_side_effects=True)


def gates_of(mixed, r0, r1, pick, rw, rd, ru):
    low = dot(mixed, rd) * pick
    logits = dot_nt(mixed, rw) + dot_nt_fine(low, ru)
    lane = iota((1, rw.shape[0]), 1)
    first = jnp.sum(jnp.where(r0 == lane, logits, 0.0), axis=1, keepdims=True)
    second = jnp.sum(jnp.where(r1 == lane, logits, 0.0), axis=1, keepdims=True)
    top = jnp.maximum(first, second)
    a = jnp.exp(first - top)
    b = jnp.exp(second - top)
    return a / (a + b), b / (a + b), low


def own_images(ref, first, per, seq, seqp, put):
    tok = ref.shape[0]
    for li in range(per):
        row = iota((seqp, tok), 0)
        sel = (iota((seqp, tok), 1) == row + (first + li) * seq) & (row < seq)
        put(pl.ds(li * seqp, seqp), dot(sel.astype(f32).astype(bf16), ref[...]))


def front_kernel(
    dims, adapters, prio, routes, cot, x_ref, gain1, gain2, wt_in, tup_in, pw_in, pd_in,
    tdn, pup, rw, rd, ru, w1_in, w2_in, fup_in, sdn_in,
    slotc, slotr, routec, got, got_cot, mixed, middle, triple, attended, tlow, plow, attn_in,
    wt, tup, pw, pd, w1_out, w2_out, fup_out, sdn_out,
    cot_pad, rank_s, one_s, cots, xs, mall, gall, acc_s, gate_s, out_s,
    wsend, wrecv, bsend, brecv, csend, crecv, tsend, trecv, send, recv, here,
):
    nt, ne, seq, seqp, images, experts, cap, capq, cp = dims
    e, t, near, far, cross = where_am_i()
    lw = pw_in.shape[0]
    width = x_ref.shape[1]
    greet([(e, far), (e, near)] + [(lax.rem(e + d, ne), t) for d in range(1, ne)])

    moves = []
    for c in range(3):
        lanes = pl.ds(c * lw, lw)
        moves.append((wt_in.at[c], lambda q, lanes=lanes: wt.at[q, :, lanes]))
        moves.append((tup_in.at[c], lambda q, lanes=lanes: tup.at[q, :, lanes]))
    moves.append((pw_in, lambda q: pw.at[q]))
    moves.append((pd_in, lambda q: pd.at[q]))
    n_w = len(moves)
    fars = [
        remote(src, at(t), wsend.at[3 * i], wrecv.at[3 * i], (e, far))
        for i, (src, at) in enumerate(moves)
    ]
    nears = [
        remote(src, at(t), wsend.at[3 * i + 1], wrecv.at[3 * i + 1], (e, near))
        for i, (src, at) in enumerate(moves)
    ]
    owns = [
        pltpu.make_async_copy(src, at(t), here.at[i]) for i, (src, at) in enumerate(moves)
    ]
    for copy in fars + nears + owns:
        copy.start()
    big = ((w1_in, w1_out), (fup_in, fup_out), (sdn_in, sdn_out), (w2_in, w2_out))
    big_far = [
        remote(src, dst.at[1], bsend.at[3 * i], brecv.at[3 * i], (e, far))
        for i, (src, dst) in enumerate(big)
    ]
    big_near = [
        remote(src, dst.at[0], bsend.at[3 * i + 1], brecv.at[3 * i + 1], (e, near))
        for i, (src, dst) in enumerate(big)
    ]
    big_relay = [
        remote(dst.at[1], dst.at[2], bsend.at[3 * i + 2], brecv.at[3 * i + 2], (e, near))
        for i, (src, dst) in enumerate(big)
    ]

    tok = prio.shape[1]
    per = images // nt
    rows = per * seqp
    total = nt * rows
    wide = one_s.shape[-1]
    order = iota((seqp, tok), 1).astype(f32)
    lane = iota((seqp, wide), 1)
    for i in range(images):
        q, at = i // per, pl.ds(i % per * seqp, seqp)
        all_at = pl.ds(i * seqp, seqp)
        token = iota((seqp, 1), 0) + i * seq
        rank_s[all_at, :] = jnp.sum(
            jnp.where(prio[...] == token, order, 0.0), axis=1, keepdims=True
        )
        w0 = i * seq // 128 * 128
        w1 = min(w0 + up(seq + 128, 128), tok)
        here_i = (iota((seqp, w1 - w0), 1) + w0 == token) & (iota((seqp, w1 - w0), 0) < seq)
        r = [
            jnp.sum(
                jnp.where(here_i, routes[k : k + 1, w0:w1].astype(f32) + 1.0, 0.0),
                axis=1,
                keepdims=True,
            ).astype(i32)
            - 1
            for k in range(TOP)
        ]
        for k in range(TOP):
            routec[q, at, k : k + 1] = r[k]
        named = jnp.where(lane < experts, r[0], jnp.where(r[1] < 0, -1, r[1] + experts))
        one_s[all_at, :] = (named == lane).astype(f32).astype(bf16)
    totals = dot(jnp.ones((8, total), bf16), one_s[...])[0:1]
    rank_rows = [to_row(rank_s[pl.ds(q * rows, rows), :]) for q in range(nt)]
    lane = iota((rows, wide), 1)
    for q in range(nt):
        at = pl.ds(q * rows, rows)
        mine = rank_s[at, :]
        counts = jnp.zeros((rows, wide), f32)
        for p in range(nt):
            before = (rank_rows[p] < mine).astype(f32).astype(bf16)
            counts = counts + dot(before, one_s[pl.ds(p * rows, rows), :])
        hot = one_s[at, :].astype(f32) * counts
        first = jnp.sum(jnp.where(lane < experts, hot, 0.0), axis=1, keepdims=True)
        second = jnp.sum(
            jnp.where(lane < experts, 0.0, hot)
            + jnp.where((lane < experts) & (routec[q, :, 1:2] == lane), totals, 0.0),
            axis=1,
            keepdims=True,
        )
        for k, pos in ((0, first), (1, second)):
            named = routec[q, :, k : k + 1]
            place = pos.astype(i32)
            kept = (named >= 0) & (place < cap) & (lax.rem(place, nt) == t)
            slot = jnp.where(kept, named * cp + lax.div(place, nt), -1)
            slotc[q, :, k : k + 1] = slot
            slotr[q, k : k + 1, :] = to_row(slot.astype(f32)).astype(i32)

    for i in range(images):
        start = i * seq // 16 * 16
        stop = min(start + up(seq, 16) + 16, tok)
        src = iota((seqp, stop - start), 1) + start
        row = iota((seqp, stop - start), 0)
        sel = ((src == row + i * seq) & (row < seq)).astype(f32).astype(bf16)
        cot_pad[pl.ds(i * seqp, seqp), :] = dot(sel, cot[start:stop, :]).astype(bf16)
    n_out, block = cots.shape[0], cots.shape[1]
    step = max(1, 512 // block)
    image_of = iota((1, rows), 1) // seqp

    def pack(d, carry):
        s = iota((step * block, 1), 0) + d * (step * block)
        acc = jnp.zeros((step * block, width), f32)
        idc = jnp.zeros((step * block, 1), f32)
        for q in range(nt):
            ids = jnp.zeros((1, rows), f32)
            for li in range(per):
                ids = jnp.where(image_of == li, adapters[q * per + li].astype(f32), ids)
            g = (slotr[q, 0:1, :] == s) | (slotr[q, 1:2, :] == s)
            idc = idc + jnp.sum(jnp.where(g, ids, 0.0), axis=1, keepdims=True)
            acc = acc + dot(g.astype(f32).astype(bf16), cot_pad[pl.ds(q * rows, rows), :])
        row = iota((block, block), 0)
        for b in range(step):
            part = acc[b * block : (b + 1) * block]
            idr = to_row(idc[b * block : (b + 1) * block])
            head = jnp.where(row == capq, idr, part[:, 0:block])
            cots[d * step + b, :, 0:block] = head.astype(bf16)
            cots[d * step + b, :, block:] = part[:, block:].astype(bf16)
        return carry

    lax.fori_loop(0, n_out // step, pack, 0)

    def cot_copy(d):
        p = lax.rem(e + d, ne)
        return remote(cots.at[p], got_cot.at[e], csend.at[d], crecv.at[d], (p, t))

    def cot_start(d, carry):
        cot_copy(d).start()
        return carry

    lax.fori_loop(1, ne, cot_start, 0)
    own_cot = pltpu.make_async_copy(cots.at[e], got_cot.at[e], here.at[n_w])
    own_cot.start()

    def put_x(at, value):
        xs[at, :] = value

    own_images(x_ref, t * per, per, seq, seqp, put_x)
    pick = picks_of(adapters, t * per, per, seqp)
    unit, _ = norm_stats(xs[...])
    normed = (unit * gain1[...]).astype(bf16)
    attn_in[...] = normed
    low = (dot(normed, tdn[...]) * pick).astype(bf16)
    tlow[...] = low
    relays = []
    for i, (_, at) in enumerate(moves):
        fars[i].wait_recv()
        relays.append(
            remote(at(far), at(far), wsend.at[3 * i + 2], wrecv.at[3 * i + 2], (e, near))
        )
        relays[-1].start()
    for copy in big_far[:3]:
        copy.start()
    for copy in nears + owns + relays:
        copy.wait()
    for copy in big_near:
        copy.start()
    head_of = iota((1, lw), 1) // HEAD_DIM
    key_ok = iota((1, seqp), 1) < seq

    def piece(p, carry):
        triple[p] = (dot(normed, wt[p]) + dot(low, tup[p])).astype(bf16)
        for li in range(per):
            at = pl.ds(li * seqp, seqp)
            q = triple[p, at, 0:lw]
            k = triple[p, at, lw : 2 * lw]
            v = triple[p, at, 2 * lw : 3 * lw]
            acc = jnp.zeros((seqp, lw), f32)
            for h in range(lw // HEAD_DIM):
                on = head_of == h
                s = dot_nt(jnp.where(on, q, 0.0).astype(bf16), k) * HEAD_DIM**-0.5
                s = jnp.where(key_ok, s, -jnp.inf)
                ex = jnp.exp(s - jnp.max(s, axis=1, keepdims=True))
                probs = (ex / jnp.sum(ex, axis=1, keepdims=True)).astype(bf16)
                acc = acc + dot(probs, jnp.where(on, v, 0.0).astype(bf16))
            attended[p, at, :] = acc.astype(bf16)
        return carry

    lax.fori_loop(0, nt, piece, 0)
    psum = jnp.zeros((rows, ADAPT), f32)
    branch = jnp.zeros((rows, width), f32)
    for p in range(nt):
        psum = psum + dot(attended[p], pd[p])
        branch = branch + dot(attended[p], pw[p])
    low2 = (psum * pick).astype(bf16)
    plow[...] = low2
    mid = xs[...] + branch + dot(low2, pup[...])
    middle[...] = mid
    unit2, _ = norm_stats(mid)
    mix = (unit2 * gain2[...]).astype(bf16)
    mixed[...] = mix
    mall[t] = mix
    r = routec[t]
    a, b, _ = gates_of(mix, r[:, 0:1], r[:, 1:2], pick, rw[...], rd[...], ru[...])
    gall[t] = jnp.zeros(gall.shape[1:], f32)
    gall[t, 0:1, :] = to_row(a)
    gall[t, 1:2, :] = to_row(b)

    mix_far = [
        remote(buf.at[t], buf.at[t], tsend.at[i], trecv.at[i], (e, far))
        for i, buf in enumerate((mall, gall))
    ]
    mix_near = [
        remote(buf.at[t], buf.at[t], tsend.at[2 + i], trecv.at[2 + i], (e, near))
        for i, buf in enumerate((mall, gall))
    ]
    mix_relay = [
        remote(buf.at[far], buf.at[far], tsend.at[4 + i], trecv.at[4 + i], (e, near))
        for i, buf in enumerate((mall, gall))
    ]
    for copy in mix_far + mix_near:
        copy.start()

    def gather_rows(q, s):
        g0 = slotr[q, 0:1, :] == s
        g1 = slotr[q, 1:2, :] == s
        gate = jnp.sum(
            jnp.where(g0, gall[q, 0:1, :], jnp.where(g1, gall[q, 1:2, :], 0.0)), axis=1, keepdims=True
        )
        return dot((g0 | g1).astype(f32).astype(bf16), mall[q]), gate

    def add_quarter(q, fresh):
        def some(d, carry):
            at = pl.ds(pl.multiple_of(d * (step * block), step * block), step * block)
            s = iota((step * block, 1), 0) + d * (step * block)
            part, gate = gather_rows(q, s)
            acc_s[at, :] = part if fresh else acc_s[at, :] + part
            gate_s[at, :] = gate if fresh else gate_s[at, :] + gate
            return carry

        lax.fori_loop(0, n_out // step, some, 0)

    add_quarter(t, True)
    for copy in mix_near:
        copy.wait_recv()
    add_quarter(near, False)
    for copy in mix_far:
        copy.wait_recv()
    big_far[3].start()
    for copy in mix_relay:
        copy.start()
    add_quarter(far, False)
    for copy in mix_relay:
        copy.wait_recv()

    def finish(p):
        at = pl.ds(pl.multiple_of(p * block, block), block)
        part, gate = gather_rows(cross, iota((block, 1), 0) + p * block)
        part = acc_s[at, :] + part
        gate = to_row(gate_s[at, :] + gate)
        high = gate.astype(bf16).astype(f32)
        row = iota((block, block), 0)
        head = jnp.where(row == capq, high, part[:, 0:block])
        head = jnp.where(row == capq + 1, gate - high, head)
        return head.astype(bf16), part[:, block:].astype(bf16)

    def out_copy(d):
        p = lax.rem(e + d, ne)
        return remote(out_s.at[p], got.at[e], send.at[d], recv.at[d], (p, t))

    def send_one(d, carry):
        p = lax.rem(e + d, ne)
        head, tail = finish(p)
        out_s[p, :, 0:block] = head
        out_s[p, :, block:] = tail
        out_copy(d).start()
        return carry

    lax.fori_loop(1, ne, send_one, 0)
    head, tail = finish(e)
    got[e, :, 0:block] = head
    got[e, :, block:] = tail
    for i in range(4):
        big_far[i].wait_recv()
        big_relay[i].start()

    def drain(d, carry):
        cot_copy(d).wait()
        out_copy(d).wait()
        return carry

    lax.fori_loop(1, ne, drain, 0)
    own_cot.wait()
    for copy in fars + mix_far + mix_near + mix_relay + big_far:
        copy.wait_send()
    for copy in big_near + big_relay:
        copy.wait()


def erf_parts(pre):
    cdf = 0.5 * (1.0 + lax.erf(pre * 0.7071067811865476))
    return pre * cdf, cdf + pre * (jnp.exp(-0.5 * pre * pre) * 0.3989422804014327)


def expert_kernel(
    dims, got, cot, fdn, sup, w1_own, w2_own, fup_own, sdn_own, w1_all, w2_all, fup_all, sdn_all,
    back, ret_res, gsum,
    w1, w2, fup, sdn, sent_s, sg_s, hid_s, dg_s, low_s, ret_s, acc_fd, acc_fu, acc_sd, acc_su,
    gr_s, in1, keep, in2, send, recv, tsend, trecv, here,
):
    nt, ne, local, capq, cp = dims
    e_i, t, near, far, cross = where_am_i()
    loads = []
    for i, (own, rest, dst) in enumerate(
        ((w1_own, w1_all, w1), (w2_own, w2_all, w2), (fup_own, fup_all, fup), (sdn_own, sdn_all, sdn))
    ):
        for m in range(nt):
            src = rest.at[m - 1] if m else own
            loads.append(
                pltpu.make_async_copy(src, dst.at[jnp.bitwise_xor(t, m)], here.at[nt * i + m])
            )
    for load in loads:
        load.start()
    greet([(e_i, far), (e_i, near)] + [(lax.rem(e_i + d, ne), t) for d in range(1, ne)])
    n, block, width = got.shape
    ffq = w1.shape[3]
    rows = n * cp
    real = lax.rem(iota((rows, 1), 0), cp) < capq
    acc_fd[...] = jnp.zeros_like(acc_fd)
    acc_fu[...] = jnp.zeros_like(acc_fu)
    acc_sd[...] = jnp.zeros_like(acc_sd)
    acc_su[...] = jnp.zeros_like(acc_su)

    def ret_copy(d, e):
        p = lax.rem(e_i + d, ne)
        k = d * local + e
        return remote(ret_s.at[e, p], back.at[e_i, pl.ds(e * cp, cp)], send.at[k], recv.at[k], (p, t))

    def ret_start(e):
        def one(d, carry):
            ret_copy(d, e).start()
            return carry

        lax.fori_loop(1, ne, one, 0)
        back[e_i, pl.ds(e * cp, cp), :] = ret_s[e, e_i]

    for e in range(local):
        at = pl.ds(e * cp, cp)
        sent = jnp.where(real, got[:, at, :].reshape(rows, width).astype(f32), 0.0).astype(bf16)
        cots = jnp.where(real, cot[:, at, :].reshape(rows, width).astype(f32), 0.0)
        diag = iota((cp, block), 0) + e * cp == iota((cp, block), 1)
        ids, gates = [], []
        for m in range(n):
            idr = cot[m, capq : capq + 1, 0:block].astype(f32)
            gr = got[m, capq : capq + 1, 0:block].astype(f32) + got[
                m, capq + 1 : capq + 2, 0:block
            ].astype(f32)
            ids.append(jnp.sum(jnp.where(diag, idr, 0.0), axis=1, keepdims=True))
            gates.append(jnp.sum(jnp.where(diag, gr, 0.0), axis=1, keepdims=True))
        gate = jnp.concatenate(gates, axis=0)
        pick = (jnp.concatenate(ids, axis=0) == (iota((1, ADAPT), 1) // RANK).astype(f32)).astype(f32)
        sent_s[...] = sent
        sgrad = (gate * cots).astype(bf16)
        sg_s[...] = sgrad
        low_s[0] = (dot(sent, fdn[...]) * pick).astype(bf16)
        low_s[1] = (dot_nt(sgrad, sup[...]) * pick).astype(bf16)
        if e == 0:
            for load in loads:
                load.wait()

        def ahead(c, carry):
            second, res = carry
            pre = dot(sent_s[...], w1[c, e]) + dot(low_s[0], fup[c])
            act, slope = erf_parts(pre)
            hid = act.astype(bf16)
            hid_s[c] = hid
            dg_s[c] = slope
            return second + dot(hid, sdn[c]), res + dot(hid, w2[c, e])

        second, res = lax.fori_loop(
            0, nt, ahead, (jnp.zeros((rows, ADAPT), f32), jnp.zeros((rows, width), f32))
        )
        second_low = (second * pick).astype(bf16)
        res = (res + dot(second_low, sup[...])).astype(bf16).astype(f32)
        grad_gate = jnp.sum(res * cots, axis=1, keepdims=True)
        ret_res[e] = (gate * res).astype(bf16).reshape(n, cp, width)
        acc_su[...] += dot_tn(second_low, sgrad)

        def behind(c, carry):
            low1, gsent = carry
            ghid = dot_nt(sg_s[...], w2[c, e]) + dot_nt(low_s[1], sdn[c])
            gpre = (ghid * dg_s[c]).astype(bf16)
            acc_fu[c] += dot_tn(low_s[0], gpre)
            acc_sd[c] += dot_tn(low_s[1], hid_s[c])
            return low1 + dot_nt(gpre, fup[c]), gsent + dot_nt(gpre, w1[c, e])

        low1, gsent = lax.fori_loop(
            0, nt, behind, (jnp.zeros((rows, ADAPT), f32), jnp.zeros((rows, width), f32))
        )
        g1low = (low1 * pick).astype(bf16)
        gsent = gsent + dot_nt(g1low, fdn[...])
        row = iota((cp, block), 0)
        for m in range(n):
            part = gsent[m * cp : (m + 1) * cp]
            gg = jnp.sum(
                jnp.where(diag, grad_gate[m * cp : (m + 1) * cp], 0.0), axis=0, keepdims=True
            )
            high = gg.astype(bf16).astype(f32)
            head = jnp.where(row == capq, high, part[:, 0:block])
            head = jnp.where(row == capq + 1, gg - high, head)
            ret_s[e, m, :, 0:block] = head.astype(bf16)
            ret_s[e, m, :, block:] = part[:, block:].astype(bf16)
        ret_start(e)
        acc_fd[...] += dot_tn(g1low, sent)
    quarter = width // nt
    share = ADAPT // nt
    for q in range(nt):
        off = 0
        for c in range(ffq // 128):
            gr_s[q, off : off + 128, :] = acc_fu[q, :, c * 128 : (c + 1) * 128].astype(bf16)
            off += 128
        gr_s[q, off : off + ffq, :] = acc_sd[q].T.astype(bf16)
        off += ffq
        gr_s[q, off : off + quarter, :] = acc_fd[:, q * quarter : (q + 1) * quarter].T.astype(bf16)
        off += quarter
        for c in range(width // 128):
            at = slice(q * share, (q + 1) * share)
            gr_s[q, off : off + share, :] = acc_su[at, c * 128 : (c + 1) * 128].astype(bf16)
            off += share
        if off < gr_s.shape[1]:
            gr_s[q, off:, :] = jnp.zeros((gr_s.shape[1] - off, 128), bf16)
    tensor_sum(gr_s, in1, keep, in2, gsum, tsend, trecv, 0)

    def drain(d, carry):
        for e in range(local):
            ret_copy(d, e).wait()
        return carry

    lax.fori_loop(1, ne, drain, 0)


def tensor_sum(src, in1, keep, in2, out, send, recv, k):
    e, t, near, far, cross = where_am_i()
    a = remote(src.at[cross], in1.at[0], send.at[k], recv.at[k], (e, near))
    b = remote(src.at[near], in1.at[1], send.at[k + 1], recv.at[k + 1], (e, near))
    a.start()
    b.start()
    a.wait()
    keep[...] = (src[far].astype(f32) + in1[0].astype(f32)).astype(bf16)
    c = remote(keep, in2, send.at[k + 2], recv.at[k + 2], (e, far))
    c.start()
    b.wait()
    mine = src[t].astype(f32) + in1[1].astype(f32)
    c.wait()
    out[...] = (mine + in2[...].astype(f32)).astype(bf16)


def expert_sum_start(ne, src, parts, send, recv):
    e, t = where_am_i()[:2]

    def copy(d):
        p = lax.rem(e + d, ne)
        return remote(src.at[p], parts.at[d - 1], send.at[d], recv.at[d], (p, t))

    def start(d, carry):
        copy(d).start()
        return carry

    lax.fori_loop(1, ne, start, 0)
    return copy


def expert_sum_share(ne, copy, src, parts, total, send, recv):
    e, t = where_am_i()[:2]

    def add(d, acc):
        copy(d).wait()
        return acc + parts[d - 1].astype(f32)

    total[e] = lax.fori_loop(1, ne, add, src[e].astype(f32)).astype(bf16)

    def share(d):
        p = lax.rem(e + d, ne)
        return remote(total.at[e], total.at[e], send.at[ne + d], recv.at[ne + d], (p, t))

    def start(d, carry):
        share(d).start()
        return carry

    lax.fori_loop(1, ne, start, 0)
    return share


def wait_all(ne, copy):
    def wait(d, carry):
        copy(d).wait()
        return carry

    lax.fori_loop(1, ne, wait, 0)


def tail_kernel(
    dims, adapters, back, ret_res, eg, slotc, slotr, routec, cot_ref, x_ref, mixed, middle, triple,
    attended, tlow, plow, attn_in, gain1, gain2, wt, tup, tdn, pw, pd, pup, rw, rd, ru,
    etot, atot, outs, rep,
    got_res, gcol, res_rows, grad_s, res_s, gg_s, in1, in1r, in1k, keep_g, keep_k, keep_r, in2, in2k, in2r,
    eparts, xs, gt_s, ga_s, acc_in, acc_low, ag, ain1, akeep, ain2, mine, aparts,
    send, recv, rsend, rrecv, esend, erecv, asend, arecv, osend, orecv, here,
):
    nt, ne, seq, seqp, images, capq, cp, held_e, held_a = dims
    e, t, near, far, cross = where_am_i()
    greet(
        [(e, far), (e, near), (e, cross)] + [(lax.rem(e + d, ne), t) for d in range(1, ne)]
    )
    n, block, width = back.shape
    local = block // cp

    def res_copy(d, le):
        p = lax.rem(e + d, ne)
        k = d * local + le
        return remote(
            ret_res.at[le, p], got_res.at[e, pl.ds(le * cp, cp)], rsend.at[k], rrecv.at[k], (p, t)
        )

    def res_start(d, carry):
        for le in range(local):
            res_copy(d, le).start()
        return carry

    lax.fori_loop(1, ne, res_start, 0)
    own_res = [
        pltpu.make_async_copy(ret_res.at[le, e], got_res.at[e, pl.ds(le * cp, cp)], here.at[le])
        for le in range(local)
    ]
    for copy in own_res:
        copy.start()
    first_sum = expert_sum_start(ne, eg, eparts, esend, erecv)

    for d in range(n):
        gr = jnp.zeros((1, block), f32)
        for le in range(local):
            for k in range(2):
                at = le * cp + capq + k
                gr = gr + back[d, at : at + 1, 0:block].astype(f32)
        gcol[d * block : (d + 1) * block, :] = to_col(gr)
    slots = n * block

    def hot(q):
        s = iota((1, slots), 1)
        c = slotc[q]
        return ((c[:, 0:1] == s) | (c[:, 1:2] == s)).astype(f32).astype(bf16)

    def grad_tokens(q):
        grad_s[q] = dot(hot(q), back[...].reshape(slots, width)).astype(bf16)
        sc = iota((slots, 1), 0)
        gg_s[q] = jnp.zeros(gg_s.shape[1:], f32)
        for k in range(TOP):
            gg_s[q, k : k + 1, :] = jnp.sum(
                jnp.where(slotr[q, k : k + 1, :] == sc, gcol[...], 0.0), axis=0, keepdims=True
            )

    stages = ((grad_s, in1, keep_g, in2), (gg_s, in1k, keep_k, in2k))
    first = {}
    for j, q in enumerate((cross, near)):
        grad_tokens(q)
        for i, (src, dst, _, _) in enumerate(stages):
            k = 3 * i + j
            first[i, j] = remote(src.at[q], dst.at[j], send.at[k], recv.at[k], (e, near))
            first[i, j].start()
    grad_tokens(far)
    second = []
    for i, (src, one, keep, two) in enumerate(stages):
        first[i, 0].wait()
        keep[...] = (src[far].astype(f32) + one[0].astype(f32)).astype(keep.dtype)
        copy = remote(keep, two, send.at[3 * i + 2], recv.at[3 * i + 2], (e, far))
        copy.start()
        second.append(copy)
    grad_tokens(t)

    per = images // nt
    rows = per * seqp
    lw = wt.shape[2] // 3
    quarter = width // nt

    def put_x(at, value):
        xs[0, at, :] = value

    def put_c(at, value):
        xs[1, at, :] = value

    own_images(x_ref, t * per, per, seq, seqp, put_x)
    own_images(cot_ref, t * per, per, seq, seqp, put_c)
    r = routec[t]
    pick = picks_of(adapters, t * per, per, seqp)
    prob0, prob1, rlow = gates_of(
        mixed[...], r[:, 0:1], r[:, 1:2], pick, rw[...], rd[...], ru[...]
    )
    unit2, scale2 = norm_stats(middle[...])

    sums = []
    for i, (src, one, _, two) in enumerate(stages):
        first[i, 1].wait()
        mine_i = src[t].astype(f32) + one[1].astype(f32)
        second[i].wait()
        sums.append(mine_i + two[...].astype(f32))
    gmix, ggate = sums
    gg0 = to_col(ggate[0:1, :])
    gg1 = to_col(ggate[1:2, :])
    inner = prob0 * gg0 + prob1 * gg1
    lane = iota((1, rw.shape[0]), 1)
    glog = jnp.where(r[:, 0:1] == lane, prob0 * (gg0 - inner), 0.0) + jnp.where(
        r[:, 1:2] == lane, prob1 * (gg1 - inner), 0.0
    )
    llow = dot_fine(glog, ru[...]) * pick
    gm = gmix + dot_fine(glog, rw[...]) + dot_nt_fine(llow, rd[...])
    router_up = dot_tn(glog.astype(bf16), rlow.astype(bf16))
    router_down = dot_tn(mixed[...], llow.astype(bf16))
    gmid = xs[1] + norm_back(gm, gain2[...], unit2, scale2)
    xs[1] = gmid
    gbranch = gmid.astype(bf16)
    project_up = dot_tn(plow[...], gbranch)
    blow = (dot_nt(gbranch, pup[...]) * pick).astype(bf16)
    for p in range(nt):
        ga_s[p] = (dot_nt(gbranch, pw[p]) + dot_nt(blow, pd[p])).astype(bf16)
    share = ADAPT // nt
    ex = rw.shape[0]
    for q in range(nt):
        off = 4 * lw + quarter
        at = slice(q * quarter, (q + 1) * quarter)
        ag[q, off : off + quarter, :] = router_down[at].astype(bf16)
        off += quarter
        at = slice(q * share, (q + 1) * share)
        for c in range(width // 128):
            ag[q, off : off + share, :] = project_up[at, c * 128 : (c + 1) * 128].astype(bf16)
            off += share
        ag[q, off:, :] = jnp.zeros((ag.shape[1] - off, 128), bf16)
    off = 4 * lw + 2 * quarter + share * (width // 128)
    ag[0, off : off + ex, :] = router_up.astype(bf16)
    head_of = iota((1, lw), 1) // HEAD_DIM
    key_ok = iota((1, seqp), 1) < seq
    acc_in[...] = jnp.zeros_like(acc_in)
    acc_low[...] = jnp.zeros_like(acc_low)

    def piece(p, carry):
        for li in range(per):
            at = pl.ds(li * seqp, seqp)
            q = triple[p, at, 0:lw]
            k = triple[p, at, lw : 2 * lw]
            v = triple[p, at, 2 * lw : 3 * lw]
            ga = ga_s[p, at, :]
            gq = jnp.zeros((seqp, lw), f32)
            gk = jnp.zeros((seqp, lw), f32)
            gv = jnp.zeros((seqp, lw), f32)
            for h in range(lw // HEAD_DIM):
                on = head_of == h
                qm = jnp.where(on, q, 0.0).astype(bf16)
                km = jnp.where(on, k, 0.0).astype(bf16)
                gam = jnp.where(on, ga, 0.0).astype(bf16)
                s = dot_nt(qm, k) * HEAD_DIM**-0.5
                s = jnp.where(key_ok, s, -jnp.inf)
                exps = jnp.exp(s - jnp.max(s, axis=1, keepdims=True))
                probs = exps / jnp.sum(exps, axis=1, keepdims=True)
                gp = dot_nt(gam, v)
                ds = (probs * (gp - jnp.sum(probs * gp, axis=1, keepdims=True))).astype(bf16)
                gq = gq + dot(ds, km)
                gk = gk + dot_tn(ds, qm)
                gv = gv + dot_tn(probs.astype(bf16), gam)
            gt_s[at, 0:lw] = (gq * HEAD_DIM**-0.5).astype(bf16)
            gt_s[at, lw : 2 * lw] = (gk * HEAD_DIM**-0.5).astype(bf16)
            gt_s[at, 2 * lw : 3 * lw] = gv.astype(bf16)
        gt = gt_s[...]
        acc_low[...] += dot_nt(gt, tup[p])
        acc_in[...] += dot_nt(gt, wt[p])
        tu = dot_tn(tlow[...], gt)
        for c in range(3 * lw // 128):
            ag[p, c * 128 : (c + 1) * 128, :] = tu[:, c * 128 : (c + 1) * 128].astype(bf16)
        off = 3 * lw
        ag[p, off : off + lw, :] = dot_tn(attended[p], blow).astype(bf16)
        return carry

    half = nt // 2
    lax.fori_loop(0, half, piece, 0)

    def res_wait(d, carry):
        for le in range(local):
            res_copy(d, le).wait()
        return carry

    lax.fori_loop(1, ne, res_wait, 0)
    for copy in own_res:
        copy.wait()
    res_rows[...] = got_res[...].reshape(slots, width)
    res_first = []
    for j, q in enumerate((cross, near)):
        res_s[q] = dot(hot(q), res_rows[...]).astype(bf16)
        res_first.append(remote(res_s.at[q], in1r.at[j], send.at[6 + j], recv.at[6 + j], (e, near)))
        res_first[-1].start()
    res_s[far] = dot(hot(far), res_rows[...]).astype(bf16)
    res_first[0].wait()
    keep_r[...] = (res_s[far].astype(f32) + in1r[0].astype(f32)).astype(bf16)
    res_second = remote(keep_r, in2r, send.at[8], recv.at[8], (e, far))
    res_second.start()
    res_s[t] = dot(hot(t), res_rows[...]).astype(bf16)
    second_sum = expert_sum_share(ne, first_sum, eg, eparts, etot, esend, erecv)
    lax.fori_loop(half, nt, piece, 0)

    tglow = (acc_low[...] * pick).astype(bf16)
    triple_down = dot_tn(attn_in[...], tglow)
    for q in range(nt):
        off = 4 * lw
        ag[q, off : off + quarter, :] = triple_down[q * quarter : (q + 1) * quarter].astype(bf16)
    sum_a = remote(ag.at[cross], ain1.at[0], osend.at[0], orecv.at[0], (e, near))
    sum_b = remote(ag.at[near], ain1.at[1], osend.at[1], orecv.at[1], (e, near))
    sum_a.start()
    sum_b.start()
    gin = acc_in[...] + dot_nt(tglow, tdn[...])
    unit1, scale1 = norm_stats(xs[0])
    sum_a.wait()
    akeep[...] = (ag[far].astype(f32) + ain1[0].astype(f32)).astype(bf16)
    sum_c = remote(akeep, ain2, osend.at[2], orecv.at[2], (e, far))
    sum_c.start()
    outs[t, 1] = (xs[1] + norm_back(gin, gain1[...], unit1, scale1)).astype(bf16)
    res_first[1].wait()
    res_second.wait()
    outs[t, 0] = (
        middle[...] + (res_s[t].astype(f32) + in1r[1].astype(f32)) + in2r[...].astype(f32)
    ).astype(bf16)
    out_far = [
        remote(outs.at[t, j], outs.at[t, j], osend.at[3 + j], orecv.at[3 + j], (e, far))
        for j in range(2)
    ]
    out_near = [
        remote(outs.at[t, j], outs.at[t, j], osend.at[5 + j], orecv.at[5 + j], (e, near))
        for j in range(2)
    ]
    for copy in out_far + out_near:
        copy.start()
    sum_b.wait()
    own = ag[t].astype(f32) + ain1[1].astype(f32)
    sum_c.wait()
    mine[...] = (own + ain2[...].astype(f32)).astype(bf16).reshape(mine.shape)
    a_first = expert_sum_start(ne, mine, aparts, asend, arecv)
    a_second = expert_sum_share(ne, a_first, mine, aparts, atot, asend, arecv)
    wait_all(ne, second_sum)
    wait_all(ne, a_second)
    e_rows, a_rows = etot.shape[0] * etot.shape[1], atot.shape[0] * atot.shape[1]
    rep[t, 0 : e_rows - held_e, :] = etot[...].reshape(e_rows, 128)[held_e:]
    rep[t, e_rows - held_e :, :] = atot[...].reshape(a_rows, 128)[held_a:]
    reps = [
        remote(rep.at[t], rep.at[t], osend.at[9 + i], orecv.at[9 + i], (e, peer))
        for i, peer in enumerate((far, cross, near))
    ]
    for copy in reps:
        copy.start()
    relays = []
    for j in range(2):
        out_far[j].wait_recv()
        relays.append(
            remote(outs.at[far, j], outs.at[far, j], osend.at[7 + j], orecv.at[7 + j], (e, near))
        )
        relays[-1].start()
    for copy in out_far:
        copy.wait_send()
    for copy in out_near + relays + reps:
        copy.wait()


def write_kernel(
    dims, etot, atot, outs, rep, block_output, input_grad, triple_down, triple_up, project_down,
    project_up, router_down, router_up, first_down, first_up, second_down, second_up,
):
    nt, seq, seqp, images, ffq, lw = dims
    per = images // nt
    tok, width = block_output.shape
    flat = outs.shape[2]
    for j, out in enumerate((block_output, input_grad)):
        for a in range(0, tok, seqp):
            b = min(a + seqp, tok)
            i0, i1 = a // seq, (b - 1) // seq
            parts = []
            for i in range(i0, i1 + 1):
                row = iota((b - a, seqp), 0) + a
                sel = (iota((b - a, seqp), 1) == row - i * seq) & (row < (i + 1) * seq)
                src = outs[i // per, j, (i % per) * seqp : (i % per + 1) * seqp, :]
                parts.append(dot(sel.astype(f32).astype(bf16), src))
            whole_part = parts[0]
            for part in parts[1:]:
                whole_part = whole_part + part
            out[a:b, :] = whole_part.astype(bf16)
    e_all = etot[...].reshape(-1, 128)
    a_all = atot[...].reshape(-1, 128)
    for c in range(ffq // 128):
        first_up[:, c * 128 : (c + 1) * 128] = e_all[c * 128 : (c + 1) * 128].astype(f32)
    second_down[...] = e_all[ffq : 2 * ffq].astype(f32)
    for c in range(3):
        triple_up[c] = a_all[c * lw : (c + 1) * lw].astype(f32)
    project_down[...] = a_all[3 * lw : 4 * lw].astype(f32)
    quarter = width // nt
    share = ADAPT // nt
    e_rep = etot.shape[0] * etot.shape[1] - 2 * ffq
    for q in range(nt):
        at = slice(q * quarter, (q + 1) * quarter)
        up_at = slice(q * share, (q + 1) * share)
        first_down[at, :] = rep[q, 0:quarter, :].astype(f32)
        off = quarter
        for c in range(width // 128):
            second_up[up_at, c * 128 : (c + 1) * 128] = rep[q, off : off + share, :].astype(f32)
            off += share
        off = e_rep
        triple_down[at, :] = rep[q, off : off + quarter, :].astype(f32)
        off += quarter
        router_down[at, :] = rep[q, off : off + quarter, :].astype(f32)
        off += quarter
        for c in range(width // 128):
            project_up[up_at, c * 128 : (c + 1) * 128] = rep[q, off : off + share, :].astype(f32)
            off += share
    router_up[...] = rep[0, off : off + router_up.shape[0], :].astype(f32)


def body(
    inputs, gain_attend, triple_weight, project_weight, gain_mixture, router_weight, expert_first,
    expert_second, triple_down, triple_up, project_down, project_up, router_down, router_up,
    first_down, first_up, second_down, second_up, adapter_index, routes, priority, cotangent,
):
    ne = lax.axis_size("expert")
    nt = lax.axis_size("tensor")
    tok, width = inputs.shape
    images = adapter_index.shape[0]
    seq = tok // images
    seqp = up(seq, 16)
    per = images // nt
    rows = per * seqp
    experts = router_weight.shape[1]
    local = expert_first.shape[0]
    ffq = expert_first.shape[2]
    lw = triple_weight.shape[2]
    cap = nt * ((5 * tok * TOP + 4 * nt * experts - 1) // (4 * nt * experts))
    capq = cap // nt
    cp = up(capq + 2, 16)
    block = local * cp
    smem = pl.BlockSpec(memory_space=pltpu.SMEM)
    anywhere = pl.BlockSpec(memory_space=pl.ANY)
    shape = jax.ShapeDtypeStruct
    wide = up(2 * experts, 128)
    gain1 = gain_attend.reshape(1, width)
    gain2 = gain_mixture.reshape(1, width)
    rw = router_weight.T
    ru = router_up.T
    row_f = shape((rows, width), f32)
    row_b = shape((rows, width), bf16)
    low_b = shape((rows, ADAPT), bf16)
    moved = shape((ne, block, width), bf16)
    big = (expert_first, expert_second, first_up, second_down)
    n_w = 8

    (
        slotc, slotr, routec, got, got_cot, mixed, middle, triple, attended, tlow, plow, attn_in,
        wt, tup, pw, pd, *big_all,
    ) = pl.pallas_call(
        functools.partial(
            front_kernel, (nt, ne, seq, seqp, images, experts, cap, capq, cp)
        ),
        out_shape=[
            shape((nt, rows, TOP), i32),
            shape((nt, TOP, rows), i32),
            shape((nt, rows, TOP), i32),
            moved,
            moved,
            row_b,
            row_f,
            shape((nt, rows, 3 * lw), bf16),
            shape((nt, rows, lw), bf16),
            low_b,
            low_b,
            row_b,
            shape((nt, width, 3 * lw), bf16),
            shape((nt, ADAPT, 3 * lw), bf16),
            shape((nt, lw, width), bf16),
            shape((nt, lw, ADAPT), bf16),
        ]
        + [shape((nt - 1,) + w.shape, bf16) for w in big],
        in_specs=[smem] + whole(15) + [anywhere] * 4,
        out_specs=whole(16) + [anywhere] * 4,
        scratch_shapes=[
            VMEM((images * seqp, width), bf16),
            VMEM((images * seqp, 1), f32),
            VMEM((images * seqp, wide), bf16),
            VMEM((ne, block, width), bf16),
            VMEM((rows, width), f32),
            VMEM((nt, rows, width), bf16),
            VMEM((nt, 8, rows), f32),
            VMEM((ne * block, width), f32),
            VMEM((ne * block, 1), f32),
            VMEM((ne, block, width), bf16),
            dma(3 * n_w),
            dma(3 * n_w),
            dma(12),
            dma(12),
            dma(ne),
            dma(ne),
            dma(6),
            dma(6),
            dma(ne),
            dma(ne),
            dma(n_w + 1),
        ],
        compiler_params=linked(0),
        name="front",
    )(
        adapter_index, priority, routes.T, cotangent, inputs, gain1, gain2,
        triple_weight.transpose(1, 0, 2), triple_up.transpose(1, 0, 2), project_weight,
        project_down, triple_down, project_up, rw, router_down, ru, *big,
    )

    erows = ne * cp
    quarter = width // nt
    held_e = 2 * ffq
    grows = up(held_e + quarter + (ADAPT // nt) * (width // 128), 16 * ne)
    echunk = grows // ne
    back, ret_res, gsum = pl.pallas_call(
        functools.partial(expert_kernel, (nt, ne, local, capq, cp)),
        out_shape=[
            moved,
            shape((local, ne, cp, width), bf16),
            shape((grows, 128), bf16),
        ],
        in_specs=whole(4) + [anywhere] * 8,
        out_specs=whole(3),
        scratch_shapes=[
            VMEM((nt, local, width, ffq), bf16),
            VMEM((nt, local, ffq, width), bf16),
            VMEM((nt, ADAPT, ffq), bf16),
            VMEM((nt, ffq, ADAPT), bf16),
            VMEM((erows, width), bf16),
            VMEM((erows, width), bf16),
            VMEM((nt, erows, ffq), bf16),
            VMEM((nt, erows, ffq), f32),
            VMEM((2, erows, ADAPT), bf16),
            VMEM((local, ne, cp, width), bf16),
            VMEM((ADAPT, width), f32),
            VMEM((nt, ADAPT, ffq), f32),
            VMEM((nt, ADAPT, ffq), f32),
            VMEM((ADAPT, width), f32),
            VMEM((nt, grows, 128), bf16),
            VMEM((2, grows, 128), bf16),
            VMEM((grows, 128), bf16),
            VMEM((grows, 128), bf16),
            dma(local * ne),
            dma(local * ne),
            dma(3),
            dma(3),
            dma(4 * nt),
        ],
        compiler_params=linked(1),
        name="experts",
    )(got, got_cot, first_down, second_up, *big, *big_all)

    one = (rows, width)
    small = (8, rows)
    held_a = 4 * lw
    arows = held_a + 2 * quarter + (ADAPT // nt) * (width // 128) + experts
    arows = up(arows, 16 * ne)
    achunk = arows // ne
    rep_rows = grows - held_e + arows - held_a
    finals = pl.pallas_call(
        functools.partial(
            tail_kernel, (nt, ne, seq, seqp, images, capq, cp, held_e, held_a)
        ),
        out_shape=[
            shape((ne, echunk, 128), bf16),
            shape((ne, achunk, 128), bf16),
            shape((nt, 2) + one, bf16),
            shape((nt, rep_rows, 128), bf16),
        ],
        in_specs=[smem] + whole(26),
        out_specs=whole(4),
        scratch_shapes=[
            VMEM((ne, block, width), bf16),
            VMEM((ne * block, 1), f32),
            VMEM((ne * block, width), bf16),
            VMEM((nt,) + one, bf16),
            VMEM((nt,) + one, bf16),
            VMEM((nt,) + small, f32),
            VMEM((2,) + one, bf16),
            VMEM((2,) + one, bf16),
            VMEM((2,) + small, f32),
            VMEM(one, bf16),
            VMEM(small, f32),
            VMEM(one, bf16),
            VMEM(one, bf16),
            VMEM(small, f32),
            VMEM(one, bf16),
            VMEM((ne - 1, echunk, 128), bf16),
            VMEM((2,) + one, f32),
            VMEM((rows, 3 * lw), bf16),
            VMEM((nt, rows, lw), bf16),
            VMEM(one, f32),
            VMEM((rows, ADAPT), f32),
            VMEM((nt, arows, 128), bf16),
            VMEM((2, arows, 128), bf16),
            VMEM((arows, 128), bf16),
            VMEM((arows, 128), bf16),
            VMEM((ne, achunk, 128), bf16),
            VMEM((ne - 1, achunk, 128), bf16),
            dma(9),
            dma(9),
            dma(local * ne),
            dma(local * ne),
            dma(2 * ne),
            dma(2 * ne),
            dma(2 * ne),
            dma(2 * ne),
            dma(12),
            dma(12),
            dma(local),
        ],
        compiler_params=linked(2),
        name="tail",
    )(
        adapter_index, back, ret_res, gsum.reshape(ne, echunk, 128), slotc, slotr, routec,
        cotangent, inputs, mixed, middle, triple, attended, tlow, plow, attn_in, gain1, gain2, wt,
        tup, triple_down, pw, pd, project_up, rw, router_down, ru,
    )

    outs = pl.pallas_call(
        functools.partial(write_kernel, (nt, seq, seqp, images, ffq, lw)),
        out_shape=[
            shape((tok, width), bf16),
            shape((tok, width), bf16),
            shape((width, ADAPT), f32),
            shape((3, ADAPT, lw), f32),
            shape((lw, ADAPT), f32),
            shape((ADAPT, width), f32),
            shape((width, ADAPT), f32),
            shape((experts, ADAPT), f32),
            shape((width, ADAPT), f32),
            shape((ADAPT, ffq), f32),
            shape((ffq, ADAPT), f32),
            shape((ADAPT, width), f32),
        ],
        in_specs=whole(4),
        out_specs=whole(12),
        name="write",
    )(*finals)
    outs = list(outs)
    outs[3] = outs[3].transpose(1, 0, 2)
    outs[7] = outs[7].T
    return tuple(outs)


def solution(mesh):
    return jax.shard_map(
        body,
        mesh=mesh,
        in_specs=(
            P("expert", None),
            P(),
            P(None, None, "tensor"),
            P("tensor", None),
            P(),
            P(),
            P("expert", None, "tensor"),
            P("expert", "tensor", None),
            P(),
            P(None, None, "tensor"),
            P("tensor", None),
            P(),
            P(),
            P(),
            P(),
            P(None, "tensor"),
            P("tensor", None),
            P(),
            P("expert"),
            P("expert", None),
            P("expert", None),
            P("expert", None),
        ),
        out_specs=(
            P("expert", None),
            P("expert", None),
            P(),
            P(None, None, "tensor"),
            P("tensor", None),
            P(),
            P(),
            P(),
            P(),
            P(None, "tensor"),
            P("tensor", None),
            P(),
        ),
        check_vma=False,
    )
```

```python
import functools

import jax
import jax.numpy as jnp
from jax import lax
from jax.experimental import pallas as pl
from jax.experimental.pallas import tpu as pltpu
from jax.sharding import PartitionSpec as P

HEAD_DIM = 64
TOP = 2
ADAPTERS = 8
RANK = 16
ADAPT = ADAPTERS * RANK
EPS = 1e-06

f32 = jnp.float32
bf16 = jnp.bfloat16
i32 = jnp.int32
MESH = pl.DeviceIdType.MESH
VMEM = pltpu.VMEM


def up(a, b):
    return -(-a // b) * b


def dot(a, b):
    return lax.dot_general(a, b, (((1,), (0,)), ((), ())), preferred_element_type=f32)


def dot_nt(a, b):
    return lax.dot_general(a, b, (((1,), (1,)), ((), ())), preferred_element_type=f32)


def dot_tn(a, b):
    return lax.dot_general(a, b, (((0,), (0,)), ((), ())), preferred_element_type=f32)


def split_high_low(a):
    high = a.astype(bf16)
    return high, (a - high.astype(f32)).astype(bf16)


def dot_fine(a, b):
    high, low = split_high_low(a)
    return dot(high, b) + dot(low, b)


def dot_nt_fine(a, b):
    high, low = split_high_low(a)
    return dot_nt(high, b) + dot_nt(low, b)


def iota(shape, axis):
    return lax.broadcasted_iota(i32, shape, axis)


def to_row(col):
    n = col.shape[0]
    return jnp.sum(jnp.where(iota((n, n), 0) == iota((n, n), 1), col, 0.0), axis=0, keepdims=True)


def to_col(row):
    n = row.shape[1]
    return jnp.sum(jnp.where(iota((n, n), 0) == iota((n, n), 1), row, 0.0), axis=1, keepdims=True)


def picks_of(adapters, base, per, seqp):
    lane = iota((seqp, ADAPT), 1) // RANK
    return jnp.concatenate(
        [(lane == adapters[base + li]).astype(f32) for li in range(per)], axis=0
    )


def whole(count):
    return [pl.BlockSpec(memory_space=VMEM) for _ in range(count)]


def norm_stats(x):
    centre = jnp.mean(x, axis=-1, keepdims=True)
    shifted = x - centre
    scale = lax.rsqrt(jnp.mean(shifted * shifted, axis=-1, keepdims=True) + EPS)
    return shifted * scale, scale


def norm_back(grad, gain, unit, scale):
    g = grad * gain
    return scale * (
        g - jnp.mean(g, axis=-1, keepdims=True) - unit * jnp.mean(g * unit, axis=-1, keepdims=True)
    )


def greet(peers):
    barrier = pltpu.get_barrier_semaphore()
    for peer in peers:
        pl.semaphore_signal(barrier, 1, device_id=peer, device_id_type=MESH)
    pl.semaphore_wait(barrier, len(peers))


def remote(src, dst, send, recv, peer):
    return pltpu.make_async_remote_copy(
        src_ref=src, dst_ref=dst, send_sem=send, recv_sem=recv, device_id=peer, device_id_type=MESH
    )


def where_am_i():
    e = lax.axis_index("expert")
    t = lax.axis_index("tensor")
    return e, t, jnp.bitwise_xor(t, 1), jnp.bitwise_xor(t, 2), jnp.bitwise_xor(t, 3)


def dma(n):
    return pltpu.SemaphoreType.DMA((n,))


def linked(ident):
    return pltpu.CompilerParams(collective_id=ident, has_side_effects=True)


def gates_of(mixed, r0, r1, pick, rw, rd, ru):
    low = dot(mixed, rd) * pick
    logits = dot_nt(mixed, rw) + dot_nt_fine(low, ru)
    lane = iota((1, rw.shape[0]), 1)
    first = jnp.sum(jnp.where(r0 == lane, logits, 0.0), axis=1, keepdims=True)
    second = jnp.sum(jnp.where(r1 == lane, logits, 0.0), axis=1, keepdims=True)
    top = jnp.maximum(first, second)
    a = jnp.exp(first - top)
    b = jnp.exp(second - top)
    return a / (a + b), b / (a + b), low


def own_images(ref, first, per, seq, seqp, put):
    tok = ref.shape[0]
    for li in range(per):
        row = iota((seqp, tok), 0)
        sel = (iota((seqp, tok), 1) == row + (first + li) * seq) & (row < seq)
        put(pl.ds(li * seqp, seqp), dot(sel.astype(f32).astype(bf16), ref[...]))


def erf_parts(pre):
    cdf = 0.5 * (1.0 + lax.erf(pre * 0.7071067811865476))
    return pre * cdf, cdf + pre * (jnp.exp(-0.5 * pre * pre) * 0.3989422804014327)


def chunk_of(ref, ne, p):
    size = ref.shape[0] // ne
    return pl.ds(pl.multiple_of(p * size, size), size)


def sum_start(ne, src, parts, send, recv):
    e, t = where_am_i()[:2]

    def copy(d):
        p = lax.rem(e + d, ne)
        return remote(src.at[chunk_of(src, ne, p)], parts.at[d - 1], send.at[d], recv.at[d], (p, t))

    def start(d, carry):
        copy(d).start()
        return carry

    lax.fori_loop(1, ne, start, 0)
    return copy


def sum_share(ne, copy, src, parts, total, send, recv):
    e, t = where_am_i()[:2]
    mine = chunk_of(src, ne, e)

    def add(d, acc):
        copy(d).wait()
        return acc + parts[d - 1].astype(f32)

    total[mine, :] = lax.fori_loop(1, ne, add, src[mine, :].astype(f32)).astype(bf16)

    def share(d):
        p = lax.rem(e + d, ne)
        return remote(total.at[mine], total.at[mine], send.at[ne + d], recv.at[ne + d], (p, t))

    def start(d, carry):
        share(d).start()
        return carry

    lax.fori_loop(1, ne, start, 0)
    return share


def wait_all(ne, copy):
    def wait(d, carry):
        copy(d).wait()
        return carry

    lax.fori_loop(1, ne, wait, 0)


def block_kernel(
    dims, adapters, prio, routes, cot_in, x_in, gain1, gain2, wt_in, tup_in, pw_in, pd_in,
    tdn, pup, rw, rd, ru, fdn, sup, w1_in, w2_in, fup_in, sdn_in,
    etot, atot, outs, rep_e, rep_a, back_out, res_out, *rest,
):
    nt, ne, seq, seqp, images, experts, cap, capq, cp, held_e, grows, la, lb, roomy = dims
    (
        slotc, slotr, routec, xs, cot_own, mixed, middle, triple, attended, tlow, plow, attn_in,
        wt, tup, pw, pd, got, got_cot, cot_pad, one_s, cots, mall, gall, acc_s, gate_s, out_s,
        w1, w2, fup, sdn, sent_s, sg_s, low_s, pick_s, gcol_s, acc_low,
        acc_fd, acc_fu, acc_sd, acc_su, gr_s, gin1, keep, gin2, cot, x_own,
        back_s, res_s, tin1, tin1k, tin1r, keep_g, keep_k, tin2, tin2k, tin2r,
        bin1, bin2, ain1, ain2, ebuf, eparts, aparts, gt_s, ga_s, back_low,
        wsend, wrecv, bsend, brecv, csend, crecv, tsend, trecv, send, recv, gsend, grecv, rsend, rrecv,
        ssend, srecv, usend, urecv, esend, erecv, asend, arecv, osend, orecv,
        here, own_sem, load_sem, ret_sem,
    ) = rest
    back = back_s if roomy else back_out
    got_res = res_s if roomy else res_out
    e, t, near, far, cross = where_am_i()
    lw = pw_in.shape[0]
    width = x_in.shape[1]
    local = w1_in.shape[0]
    parts = nt // local
    n_out, block = cots.shape[0], cots.shape[1]
    peers = [(e, far), (e, near)] + [(lax.rem(e + d, ne), t) for d in range(1, ne)]
    barrier = pltpu.get_barrier_semaphore()
    for peer in peers:
        pl.semaphore_signal(barrier, 1, device_id=peer, device_id_type=MESH)

    def big_ref(k, to):
        return (fup_in, sdn_in)[k] if k < 2 else (w1_in, w2_in)[k - 2].at[lax.div(to, parts)]

    big = (fup, sdn, w1, w2)
    n_big = len(big)
    big_own = [
        pltpu.make_async_copy(big_ref(k, t), big[k].at[t], load_sem.at[k]) for k in range(n_big)
    ]
    big_far = [
        remote(big_ref(k, far), big[k].at[t], bsend.at[3 * k], brecv.at[3 * k], (e, far))
        for k in range(n_big)
    ]
    big_near = [
        remote(big_ref(k, near), big[k].at[t], bsend.at[3 * k + 1], brecv.at[3 * k + 1], (e, near))
        for k in range(n_big)
    ]
    big_relay = [
        remote(big[k].at[far], big[k].at[far], bsend.at[3 * k + 2], brecv.at[3 * k + 2], (e, near))
        for k in range(n_big)
    ]
    load_cot = pltpu.make_async_copy(cot_in, cot, load_sem.at[n_big])
    x_ref = x_own if roomy else cot
    load_x = pltpu.make_async_copy(x_in, x_ref, load_sem.at[n_big + 1])
    for copy in [load_cot] + big_own:
        copy.start()
    if roomy:
        load_x.start()

    moves = []
    for c in range(3):
        lanes = pl.ds(c * lw, lw)
        moves.append((wt_in.at[c], lambda q, lanes=lanes: wt.at[q, :, lanes]))
        moves.append((tup_in.at[c], lambda q, lanes=lanes: tup.at[q, :, lanes]))
    moves.append((pw_in, lambda q: pw.at[q]))
    moves.append((pd_in, lambda q: pd.at[q]))
    n_w = len(moves)
    fars = [
        remote(src, at(t), wsend.at[3 * i], wrecv.at[3 * i], (e, far))
        for i, (src, at) in enumerate(moves)
    ]
    nears = [
        remote(src, at(t), wsend.at[3 * i + 1], wrecv.at[3 * i + 1], (e, near))
        for i, (src, at) in enumerate(moves)
    ]
    relays = [
        remote(at(far), at(far), wsend.at[3 * i + 2], wrecv.at[3 * i + 2], (e, near))
        for i, (src, at) in enumerate(moves)
    ]
    owns = [
        pltpu.make_async_copy(src, at(t), own_sem.at[i]) for i, (src, at) in enumerate(moves)
    ]
    for copy in owns:
        copy.start()

    tok = prio.shape[1]
    per = images // nt
    rows = per * seqp
    total = nt * rows
    wide = one_s.shape[-1]
    order = iota((seqp, tok), 1).astype(f32)
    lane = iota((seqp, wide), 1)
    for i in range(images):
        q, at = i // per, pl.ds(i % per * seqp, seqp)
        all_at = pl.ds(i * seqp, seqp)
        token = iota((seqp, 1), 0) + i * seq
        gate_s[all_at, :] = jnp.sum(
            jnp.where(prio[...] == token, order, 0.0), axis=1, keepdims=True
        )
        lane0 = i * seq // 128 * 128
        lane1 = min(lane0 + up(seq + 128, 128), tok)
        here_i = (iota((seqp, lane1 - lane0), 1) + lane0 == token) & (iota((seqp, lane1 - lane0), 0) < seq)
        r = [
            jnp.sum(
                jnp.where(here_i, routes[k : k + 1, lane0:lane1].astype(f32) + 1.0, 0.0),
                axis=1,
                keepdims=True,
            ).astype(i32)
            - 1
            for k in range(TOP)
        ]
        for k in range(TOP):
            routec[q, at, k : k + 1] = r[k]
        named = jnp.where(lane < experts, r[0], jnp.where(r[1] < 0, -1, r[1] + experts))
        one_s[all_at, :] = (named == lane).astype(f32).astype(bf16)
    pl.semaphore_wait(barrier, len(peers))
    for copy in fars + nears:
        copy.start()
    totals = dot(jnp.ones((8, total), bf16), one_s[...])[0:1]
    rank_rows = [to_row(gate_s[pl.ds(q * rows, rows), :]) for q in range(nt)]
    lane = iota((rows, wide), 1)
    for q in range(nt):
        at = pl.ds(q * rows, rows)
        mine = gate_s[at, :]
        counts = jnp.zeros((rows, wide), f32)
        for p in range(nt):
            before = (rank_rows[p] < mine).astype(f32).astype(bf16)
            counts = counts + dot(before, one_s[pl.ds(p * rows, rows), :])
        hot = one_s[at, :].astype(f32) * counts
        first = jnp.sum(jnp.where(lane < experts, hot, 0.0), axis=1, keepdims=True)
        second = jnp.sum(
            jnp.where(lane < experts, 0.0, hot)
            + jnp.where((lane < experts) & (routec[q, :, 1:2] == lane), totals, 0.0),
            axis=1,
            keepdims=True,
        )
        for k, pos in ((0, first), (1, second)):
            named = routec[q, :, k : k + 1]
            place = pos.astype(i32)
            kept = (named >= 0) & (place < cap)
            kept = kept & (lax.rem(named, local) == lax.div(t, parts))
            kept = kept & (lax.rem(place, parts) == lax.rem(t, parts))
            index = lax.div(place, parts)
            index = lax.div(index, capq) * cp + lax.rem(index, capq)
            slot = jnp.where(kept, lax.div(named, local) * block + index, -1)
            slotc[q, :, k : k + 1] = slot
            slotr[q, k : k + 1, :] = to_row(slot.astype(f32)).astype(i32)

    load_cot.wait()
    for i in range(images):
        start = i * seq // 16 * 16
        stop = min(start + up(seq, 16) + 16, tok)
        src = iota((seqp, stop - start), 1) + start
        row = iota((seqp, stop - start), 0)
        sel = ((src == row + i * seq) & (row < seq)).astype(f32).astype(bf16)
        cot_pad[i // per, pl.ds(i % per * seqp, seqp), :] = dot(sel, cot[start:stop, :]).astype(bf16)
    step = max(1, 512 // block)
    image_of = iota((1, rows), 1) // seqp

    def pack(d, carry):
        s = iota((step * block, 1), 0) + d * (step * block)
        acc = jnp.zeros((step * block, width), f32)
        idc = jnp.zeros((step * block, 1), f32)
        for q in range(nt):
            ids = jnp.zeros((1, rows), f32)
            for li in range(per):
                ids = jnp.where(image_of == li, adapters[q * per + li].astype(f32), ids)
            g = (slotr[q, 0:1, :] == s) | (slotr[q, 1:2, :] == s)
            idc = idc + jnp.sum(jnp.where(g, ids, 0.0), axis=1, keepdims=True)
            acc = acc + dot(g.astype(f32).astype(bf16), cot_pad[q])
        row = iota((block, block), 0)
        for b in range(step):
            part = acc[b * block : (b + 1) * block]
            idr = to_row(idc[b * block : (b + 1) * block])
            head = jnp.where(row == capq, idr, part[:, 0:block])
            cots[d * step + b, :, 0:block] = head.astype(bf16)
            cots[d * step + b, :, block:] = part[:, block:].astype(bf16)
        return carry

    lax.fori_loop(0, n_out // step, pack, 0)

    def cot_copy(d):
        p = lax.rem(e + d, ne)
        return remote(cots.at[p], got_cot.at[e], csend.at[d], crecv.at[d], (p, t))

    def cot_start(d, carry):
        cot_copy(d).start()
        return carry

    lax.fori_loop(1, ne, cot_start, 0)
    own_cot = pltpu.make_async_copy(cots.at[e], got_cot.at[e], here.at[0])
    own_cot.start()

    def put_x(at, value):
        xs[at, :] = value

    def put_cot(at, value):
        cot_own[at, :] = value.astype(bf16)

    if not roomy:
        own_images(cot, t * per, per, seq, seqp, put_cot)
        load_x.start()
    load_x.wait()
    own_images(x_ref, t * per, per, seq, seqp, put_x)
    pick = picks_of(adapters, t * per, per, seqp)
    unit, _ = norm_stats(xs[...])
    normed = (unit * gain1[...]).astype(bf16)
    attn_in[...] = normed
    low = (dot(normed, tdn[...]) * pick).astype(bf16)
    tlow[...] = low
    head_of = iota((1, lw), 1) // HEAD_DIM
    key_ok = iota((1, seqp), 1) < seq

    def piece(m, carry):
        p = jnp.bitwise_xor(t, m)

        @pl.when(m == 0)
        def _():
            for copy in owns:
                copy.wait()

        @pl.when(m == 1)
        def _():
            for copy in nears:
                copy.wait()

        @pl.when(m == 2)
        def _():
            for i in range(6):
                fars[i].wait_recv()
                relays[i].start()

        @pl.when(m == 3)
        def _():
            for i in range(6):
                relays[i].wait_recv()

        triple[p] = (dot(attn_in[...], wt[p]) + dot(tlow[...], tup[p])).astype(bf16)
        for li in range(per):
            at = pl.ds(li * seqp, seqp)
            q = triple[p, at, 0:lw]
            k = triple[p, at, lw : 2 * lw]
            v = triple[p, at, 2 * lw : 3 * lw]
            acc = jnp.zeros((seqp, lw), f32)
            for h in range(lw // HEAD_DIM):
                on = head_of == h
                s = dot_nt(jnp.where(on, q, 0.0).astype(bf16), k) * HEAD_DIM**-0.5
                s = jnp.where(key_ok, s, -jnp.inf)
                ex = jnp.exp(s - jnp.max(s, axis=1, keepdims=True))
                probs = (ex / jnp.sum(ex, axis=1, keepdims=True)).astype(bf16)
                acc = acc + dot(probs, jnp.where(on, v, 0.0).astype(bf16))
            attended[p, at, :] = acc.astype(bf16)
        return carry

    lax.fori_loop(0, nt, piece, 0)
    for copy in big_near:
        copy.start()
    for i in range(6, n_w):
        fars[i].wait_recv()
        relays[i].start()
    for i in range(6, n_w):
        relays[i].wait_recv()
    psum = jnp.zeros((rows, ADAPT), f32)
    branch = jnp.zeros((rows, width), f32)
    for p in range(nt):
        psum = psum + dot(attended[p], pd[p])
        branch = branch + dot(attended[p], pw[p])
    low2 = (psum * pick).astype(bf16)
    plow[...] = low2
    mid = xs[...] + branch + dot(low2, pup[...])
    middle[...] = mid
    unit2, _ = norm_stats(mid)
    mix = (unit2 * gain2[...]).astype(bf16)
    mixed[...] = mix
    mall[t] = mix
    r = routec[t]
    a, b, _ = gates_of(mix, r[:, 0:1], r[:, 1:2], pick, rw[...], rd[...], ru[...])
    gall[t] = jnp.zeros(gall.shape[1:], f32)
    gall[t, 0:1, :] = to_row(a)
    gall[t, 1:2, :] = to_row(b)

    mix_far = [
        remote(buf.at[t], buf.at[t], tsend.at[i], trecv.at[i], (e, far))
        for i, buf in enumerate((mall, gall))
    ]
    mix_near = [
        remote(buf.at[t], buf.at[t], tsend.at[2 + i], trecv.at[2 + i], (e, near))
        for i, buf in enumerate((mall, gall))
    ]
    mix_relay = [
        remote(buf.at[far], buf.at[far], tsend.at[4 + i], trecv.at[4 + i], (e, near))
        for i, buf in enumerate((mall, gall))
    ]
    for copy in mix_far + mix_near:
        copy.start()
    for copy in big_far:
        copy.start()
    step = max(1, 512 // block)

    def gather_rows(q, s):
        g0 = slotr[q, 0:1, :] == s
        g1 = slotr[q, 1:2, :] == s
        gate = jnp.sum(
            jnp.where(g0, gall[q, 0:1, :], jnp.where(g1, gall[q, 1:2, :], 0.0)), axis=1, keepdims=True
        )
        return dot((g0 | g1).astype(f32).astype(bf16), mall[q]), gate

    def add_quarter(q, fresh):
        def some(d, carry):
            at = pl.ds(pl.multiple_of(d * (step * block), step * block), step * block)
            s = iota((step * block, 1), 0) + d * (step * block)
            part, gate = gather_rows(q, s)
            acc_s[at, :] = part if fresh else acc_s[at, :] + part
            gate_s[at, :] = gate if fresh else gate_s[at, :] + gate
            return carry

        lax.fori_loop(0, n_out // step, some, 0)

    add_quarter(t, True)
    for copy in mix_near:
        copy.wait_recv()
    add_quarter(near, False)
    if roomy:
        own_images(cot, t * per, per, seq, seqp, put_cot)
    for copy in mix_far:
        copy.wait_recv()
    for copy in mix_relay:
        copy.start()
    add_quarter(far, False)
    for copy in mix_relay:
        copy.wait_recv()

    def finish(p):
        at = pl.ds(pl.multiple_of(p * block, block), block)
        part, gate = gather_rows(cross, iota((block, 1), 0) + p * block)
        part = acc_s[at, :] + part
        gate = to_row(gate_s[at, :] + gate)
        high = gate.astype(bf16).astype(f32)
        row = iota((block, block), 0)
        head = jnp.where(row == capq, high, part[:, 0:block])
        head = jnp.where(row == capq + 1, gate - high, head)
        return head.astype(bf16), part[:, block:].astype(bf16)

    def out_copy(d, le):
        p = lax.rem(e + d, ne)
        at = pl.ds(le * cp, cp)
        k = d * local + le
        return remote(out_s.at[p, at], got.at[e, at], send.at[k], recv.at[k], (p, t))

    def send_one(d, carry):
        p = lax.rem(e + d, ne)
        head, tail = finish(p)
        out_s[p, :, 0:block] = head
        out_s[p, :, block:] = tail
        out_copy(d, 0).start()
        return carry

    lax.fori_loop(1, ne, send_one, 0)

    def send_more(d, carry):
        for le in range(1, local):
            out_copy(d, le).start()
        return carry

    lax.fori_loop(1, ne, send_more, 0)
    head, tail = finish(e)
    got[e, :, 0:block] = head
    got[e, :, block:] = tail

    n = ne
    erows = n * cp
    real = lax.rem(iota((erows, 1), 0), cp) < capq
    res_at, gsent_at = pl.ds(0, erows), pl.ds(erows, erows)
    for buf in (acc_fd, acc_fu, acc_sd, acc_su):
        buf[...] = jnp.zeros_like(buf)
    for copy in big_own + big_near:
        copy.wait()

    def cot_wait(d, carry):
        cot_copy(d).wait()
        return carry

    lax.fori_loop(1, ne, cot_wait, 0)
    own_cot.wait()

    def grad_copy(d, le):
        p = lax.rem(e + d, ne)
        k = d * local + le
        at = pl.ds(le * cp, cp)
        return remote(cots.at[p, at], back.at[e, at], gsend.at[k], grecv.at[k], (p, t))

    def res_copy(d, le):
        p = lax.rem(e + d, ne)
        k = d * local + le
        at = pl.ds(le * cp, cp)
        return remote(out_s.at[p, at], got_res.at[e, at], rsend.at[k], rrecv.at[k], (p, t))

    locals_ = []
    for le in range(local):
        at = pl.ds(le * cp, cp)

        def rows_wait(d, carry, le=le):
            out_copy(d, le).wait_recv()
            return carry

        lax.fori_loop(1, ne, rows_wait, 0)
        diag = iota((cp, block), 0) + le * cp == iota((cp, block), 1)

        def headers(m, carry, le=le, diag=diag):
            idr = got_cot[m, capq : capq + 1, 0:block].astype(f32)
            gr = got[m, capq : capq + 1, 0:block].astype(f32) + got[
                m, capq + 1 : capq + 2, 0:block
            ].astype(f32)
            to = pl.ds(pl.multiple_of(m * cp, cp), cp)
            gcol_s[to, 0:1] = jnp.sum(jnp.where(diag, idr, 0.0), axis=1, keepdims=True)
            gcol_s[to, 1:2] = jnp.sum(jnp.where(diag, gr, 0.0), axis=1, keepdims=True)
            return carry

        lax.fori_loop(0, n, headers, 0)
        sent = jnp.where(real, got[:, at, :].reshape(erows, width).astype(f32), 0.0).astype(bf16)
        cotf = jnp.where(real, got_cot[:, at, :].reshape(erows, width).astype(f32), 0.0)
        pick_e = (gcol_s[:, 0:1] == (iota((1, ADAPT), 1) // RANK).astype(f32)).astype(f32)
        pick_s[...] = pick_e
        sent_s[...] = sent
        sgrad = (gcol_s[:, 1:2] * cotf).astype(bf16)
        sg_s[...] = sgrad
        low_s[0] = (dot(sent, fdn[...]) * pick_e).astype(bf16)
        low_s[1] = (dot_nt(sgrad, sup[...]) * pick_e).astype(bf16)
        acc_low[...] = jnp.zeros_like(acc_low)
        acc_s[...] = jnp.zeros_like(acc_s)

        def through(m, carry, le=le):
            c = jnp.bitwise_xor(t, m)
            if le == 0:

                @pl.when(m == 2)
                def _():
                    for far_copy, relay in zip(big_far, big_relay):
                        far_copy.wait_recv()
                        relay.start()

                @pl.when(m == 3)
                def _():
                    for relay in big_relay:
                        relay.wait_recv()

            span = min(erows, 512)
            for r0 in range(0, erows, span):
                rs = slice(r0, r0 + span)
                gs = slice(erows + r0, erows + r0 + span)
                pre = dot(sent_s[rs, :], w1[c]) + dot(low_s[0, rs, :], fup[c])
                act, slope = erf_parts(pre)
                hid = act.astype(bf16)
                acc_low[0, rs, :] += dot(hid, sdn[c])
                acc_s[rs, :] += dot(hid, w2[c])
                ghid = dot_nt(sg_s[rs, :], w2[c]) + dot_nt(low_s[1, rs, :], sdn[c])
                gpre = (ghid * slope).astype(bf16)
                acc_fu[c] += dot_tn(low_s[0, rs, :], gpre)
                acc_sd[c] += dot_tn(low_s[1, rs, :], hid)
                acc_low[1, rs, :] += dot_nt(gpre, fup[c])
                acc_s[gs, :] += dot_nt(gpre, w1[c])
            return carry

        lax.fori_loop(0, nt, through, 0)
        if le == 0:

            def sent_wait(d, carry):
                for other in range(local):
                    out_copy(d, other).wait_send()
                return carry

            lax.fori_loop(1, ne, sent_wait, 0)
        second_low = (acc_low[0] * pick_s[...]).astype(bf16)
        res = (acc_s[res_at, :] + dot(second_low, sup[...])).astype(bf16).astype(f32)
        cotf = got_cot[:, at, :].reshape(erows, width).astype(f32)
        grad_gate = jnp.sum(res * cotf, axis=1, keepdims=True)
        g1low = (acc_low[1] * pick_s[...]).astype(bf16)
        gsent = acc_s[gsent_at, :] + dot_nt(g1low, fdn[...])
        cots[:, at, :] = gsent.astype(bf16).reshape(n, cp, width)
        acc_low[0, :, 0:1] = grad_gate

        def footers(m, carry, le=le, diag=diag):
            gg = jnp.sum(
                jnp.where(diag, acc_low[0, pl.ds(pl.multiple_of(m * cp, cp), cp), 0:1], 0.0),
                axis=0,
                keepdims=True,
            )
            high = gg.astype(bf16).astype(f32)
            base = capq // 16 * 16
            row = iota((16, block), 0) + base
            to = pl.ds(le * cp + base, 16)
            old = cots[m, to, 0:block].astype(f32)
            old = jnp.where(row == capq, high, jnp.where(row == capq + 1, gg - high, old))
            cots[m, to, 0:block] = old.astype(bf16)
            return carry

        lax.fori_loop(0, n, footers, 0)

        def grad_start(d, carry, le=le):
            grad_copy(d, le).start()
            return carry

        lax.fori_loop(1, ne, grad_start, 0)
        locals_.append(
            pltpu.make_async_copy(cots.at[e, at], back.at[e, at], ret_sem.at[2 * le])
        )
        out_s[:, at, :] = (gcol_s[:, 1:2] * res).astype(bf16).reshape(n, cp, width)
        locals_.append(
            pltpu.make_async_copy(out_s.at[e, at], got_res.at[e, at], ret_sem.at[2 * le + 1])
        )
        for copy in locals_[-2:]:
            copy.start()
        acc_su[...] += dot_tn(second_low, sg_s[...])
        acc_fd[...] += dot_tn(g1low, sent_s[...])

    def res_start(d, carry):
        for le in range(local):
            res_copy(d, le).start()
        return carry

    lax.fori_loop(1, ne, res_start, 0)

    ffq = w1.shape[2]
    quarter = width // nt
    share = ADAPT // nt
    for q in range(nt):
        off = 0
        for c in range(ffq // 128):
            gr_s[q, off : off + 128, :] = acc_fu[q, :, c * 128 : (c + 1) * 128].astype(bf16)
            off += 128
        gr_s[q, off : off + ffq, :] = acc_sd[q].T.astype(bf16)
        off += ffq
        gr_s[q, off : off + quarter, :] = acc_fd[:, q * quarter : (q + 1) * quarter].T.astype(bf16)
        off += quarter
        for c in range(width // 128):
            at = slice(q * share, (q + 1) * share)
            gr_s[q, off : off + share, :] = acc_su[at, c * 128 : (c + 1) * 128].astype(bf16)
            off += share
        if off < grows:
            gr_s[q, off:grows, :] = jnp.zeros((grows - off, 128), bf16)

    def tensor_sum(rows_at, in1, in2, k):
        a = remote(gr_s.at[cross, rows_at], in1.at[0], ssend.at[k], srecv.at[k], (e, near))
        b = remote(gr_s.at[near, rows_at], in1.at[1], ssend.at[k + 1], srecv.at[k + 1], (e, near))
        held = keep.at[rows_at]
        c = remote(held, in2, ssend.at[k + 2], srecv.at[k + 2], (e, far))

        def start():
            a.start()
            b.start()

        def cross_over():
            a.wait()
            held[...] = (gr_s[far, rows_at, :].astype(f32) + in1[0].astype(f32)).astype(bf16)
            c.start()

        def result():
            b.wait()
            c.wait()
            mine = gr_s[t, rows_at, :].astype(f32) + in1[1].astype(f32)
            return (mine + in2[...].astype(f32)).astype(bf16)

        return start, cross_over, result

    g_start, g_cross, g_result = tensor_sum(pl.ds(0, grows), gin1, gin2, 0)
    g_start()

    r = routec[t]
    prob0, prob1, rlow = gates_of(
        mixed[...], r[:, 0:1], r[:, 1:2], pick, rw[...], rd[...], ru[...]
    )
    g_cross()

    def back_wait(d, carry):
        for le in range(local):
            grad_copy(d, le).wait()
        return carry

    lax.fori_loop(1, ne, back_wait, 0)
    for copy in locals_:
        copy.wait()
    for copy in mix_far + mix_near + mix_relay:
        copy.wait_send()
    if not roomy:
        load = pltpu.make_async_copy(back, got, here.at[0])
        load.start()
        load.wait()
    rows_back = back if roomy else got
    for d in range(n):
        gr = jnp.zeros((1, block), f32)
        for le in range(local):
            for k in range(2):
                at = le * cp + capq + k
                gr = gr + rows_back[d, at : at + 1, 0:block].astype(f32)
        gate_s[d * block : (d + 1) * block, :] = to_col(gr)
    slots = n * block
    grad_s, gg_s, tok_s = cot_pad, gall, mall

    def hot(q):
        s = iota((1, slots), 1)
        c = slotc[q]
        return ((c[:, 0:1] == s) | (c[:, 1:2] == s)).astype(f32).astype(bf16)

    def grad_tokens(q):
        grad_s[q] = dot(hot(q), rows_back[...].reshape(slots, width)).astype(bf16)
        sc = iota((slots, 1), 0)
        gg_s[q] = jnp.zeros(gg_s.shape[1:], f32)
        for k in range(TOP):
            gg_s[q, k : k + 1, :] = jnp.sum(
                jnp.where(slotr[q, k : k + 1, :] == sc, gate_s[0:slots, :], 0.0), axis=0, keepdims=True
            )

    stages = ((grad_s, tin1, keep_g, tin2), (gg_s, tin1k, keep_k, tin2k))
    first = {}
    for j, q in enumerate((cross, near)):
        grad_tokens(q)
        for i, (src, dst, _, _) in enumerate(stages):
            k = 3 * i + j
            first[i, j] = remote(src.at[q], dst.at[j], usend.at[k], urecv.at[k], (e, near))
            first[i, j].start()
    grad_tokens(far)
    second = []
    for i, (src, one, held, two) in enumerate(stages):
        first[i, 0].wait()
        held[...] = (src[far].astype(f32) + one[0].astype(f32)).astype(held.dtype)
        copy = remote(held, two, usend.at[3 * i + 2], urecv.at[3 * i + 2], (e, far))
        copy.start()
        second.append(copy)
    grad_tokens(t)
    ebuf[0:grows, :] = g_result()
    unit2, scale2 = norm_stats(middle[...])
    sums = []
    for i, (src, one, _, two) in enumerate(stages):
        first[i, 1].wait()
        mine = src[t].astype(f32) + one[1].astype(f32)
        second[i].wait()
        sums.append(mine + two[...].astype(f32))
    gmix, ggate = sums
    gg0 = to_col(ggate[0:1, :])
    gg1 = to_col(ggate[1:2, :])
    inner = prob0 * gg0 + prob1 * gg1
    lane = iota((1, rw.shape[0]), 1)
    glog = jnp.where(r[:, 0:1] == lane, prob0 * (gg0 - inner), 0.0) + jnp.where(
        r[:, 1:2] == lane, prob1 * (gg1 - inner), 0.0
    )
    llow = dot_fine(glog, ru[...]) * pick
    gm = gmix + dot_fine(glog, rw[...]) + dot_nt_fine(llow, rd[...])
    router_up = dot_tn(glog.astype(bf16), rlow.astype(bf16))
    router_down = dot_tn(mixed[...], llow.astype(bf16))
    gmid = cot_own[...].astype(f32) + norm_back(gm, gain2[...], unit2, scale2)
    mid_at, in_at = pl.ds(0, rows), pl.ds(rows, rows)
    acc_s[mid_at, :] = gmid
    gbranch = gmid.astype(bf16)
    project_up = dot_tn(plow[...], gbranch)
    blow = (dot_nt(gbranch, pup[...]) * pick).astype(bf16)
    for p in range(nt):
        ga_s[p] = (dot_nt(gbranch, pw[p]) + dot_nt(blow, pd[p])).astype(bf16)

    for q in range(nt):
        off = la
        at = slice(q * share, (q + 1) * share)
        for c in range(width // 128):
            gr_s[q, off : off + share, :] = project_up[at, c * 128 : (c + 1) * 128].astype(bf16)
            off += share
        at = slice(q * quarter, (q + 1) * quarter)
        gr_s[q, off : off + quarter, :] = router_down[at].astype(bf16)
        off += quarter
        gr_s[q, off : la + lb - lw, :] = jnp.zeros((la + lb - lw - off, 128), bf16)
        gr_s[q, la + lb - lw : la + lb, :] = dot_tn(attended[q], blow).astype(bf16)
    off = la + ADAPT + quarter
    gr_s[0, off : off + experts, :] = router_up.astype(bf16)
    b_start, b_cross, b_result = tensor_sum(pl.ds(la, lb), bin1, bin2, 3)
    b_start()

    acc_s[in_at, :] = jnp.zeros((rows, width), f32)
    back_low[...] = jnp.zeros_like(back_low)

    def piece_back(p, carry):
        for li in range(per):
            at = pl.ds(li * seqp, seqp)
            q = triple[p, at, 0:lw]
            k = triple[p, at, lw : 2 * lw]
            v = triple[p, at, 2 * lw : 3 * lw]
            ga = ga_s[p, at, :]
            gq = jnp.zeros((seqp, lw), f32)
            gk = jnp.zeros((seqp, lw), f32)
            gv = jnp.zeros((seqp, lw), f32)
            for h in range(lw // HEAD_DIM):
                on = head_of == h
                qm = jnp.where(on, q, 0.0).astype(bf16)
                km = jnp.where(on, k, 0.0).astype(bf16)
                gam = jnp.where(on, ga, 0.0).astype(bf16)
                s = dot_nt(qm, k) * HEAD_DIM**-0.5
                s = jnp.where(key_ok, s, -jnp.inf)
                ex = jnp.exp(s - jnp.max(s, axis=1, keepdims=True))
                probs = ex / jnp.sum(ex, axis=1, keepdims=True)
                gp = dot_nt(gam, v)
                ds = (probs * (gp - jnp.sum(probs * gp, axis=1, keepdims=True))).astype(bf16)
                gq = gq + dot(ds, km)
                gk = gk + dot_tn(ds, qm)
                gv = gv + dot_tn(probs.astype(bf16), gam)
            gt_s[at, 0:lw] = (gq * HEAD_DIM**-0.5).astype(bf16)
            gt_s[at, lw : 2 * lw] = (gk * HEAD_DIM**-0.5).astype(bf16)
            gt_s[at, 2 * lw : 3 * lw] = gv.astype(bf16)
        gt = gt_s[...]
        back_low[...] += dot_nt(gt, tup[p])
        acc_s[in_at, :] += dot_nt(gt, wt[p])
        tu = dot_tn(tlow[...], gt)
        for c in range(3 * lw // 128):
            gr_s[p, c * 128 : (c + 1) * 128, :] = tu[:, c * 128 : (c + 1) * 128].astype(bf16)
        return carry

    half = nt // 2
    lax.fori_loop(0, half, piece_back, 0)
    b_cross()

    def res_wait(d, carry):
        for le in range(local):
            res_copy(d, le).wait()
        return carry

    lax.fori_loop(1, ne, res_wait, 0)
    if not roomy:
        load = pltpu.make_async_copy(got_res, got_cot, here.at[0])
        load.start()
        load.wait()
    res_rows = got_res if roomy else got_cot

    def res_tokens(q):
        tok_s[q] = dot(hot(q), res_rows[...].reshape(slots, width)).astype(bf16)

    res_first = []
    for j, q in enumerate((cross, near)):
        res_tokens(q)
        res_first.append(remote(tok_s.at[q], tin1r.at[j], usend.at[6 + j], urecv.at[6 + j], (e, near)))
        res_first[-1].start()
    res_tokens(far)
    res_first[0].wait()
    keep_g[...] = (tok_s[far].astype(f32) + tin1r[0].astype(f32)).astype(bf16)
    res_second = remote(keep_g, tin2r, usend.at[8], urecv.at[8], (e, far))
    res_second.start()
    res_tokens(t)
    ebuf[grows:, :] = b_result()
    e_first = sum_start(ne, ebuf, eparts, esend, erecv)
    lax.fori_loop(half, nt, piece_back, 0)

    tglow = (back_low[...] * pick).astype(bf16)
    triple_down = dot_tn(attn_in[...], tglow)
    for q in range(nt):
        off = 3 * lw
        gr_s[q, off : off + quarter, :] = triple_down[q * quarter : (q + 1) * quarter].astype(bf16)
        if off + quarter < la:
            gr_s[q, off + quarter : la, :] = jnp.zeros((la - off - quarter, 128), bf16)
    a_start, a_cross, a_result = tensor_sum(pl.ds(0, la), ain1, ain2, 6)
    a_start()
    gin = acc_s[in_at, :] + dot_nt(tglow, tdn[...])
    a_cross()
    unit1, scale1 = norm_stats(xs[...])
    attn_in[...] = (acc_s[mid_at, :] + norm_back(gin, gain1[...], unit1, scale1)).astype(bf16)

    def share_out(j, src, k):
        return [
            remote(src, outs.at[t, j], osend.at[k], orecv.at[k], (e, far)),
            remote(src, outs.at[t, j], osend.at[k + 1], orecv.at[k + 1], (e, near)),
            remote(outs.at[far, j], outs.at[far, j], osend.at[k + 2], orecv.at[k + 2], (e, near)),
            pltpu.make_async_copy(src, outs.at[t, j], here.at[1 + j]),
        ]

    igrad_out = share_out(1, attn_in, 0)
    for i in (0, 1, 3):
        igrad_out[i].start()
    e_second = sum_share(ne, e_first, ebuf, eparts, etot, esend, erecv)
    res_first[1].wait()
    res_second.wait()
    mixed[...] = (
        middle[...] + (tok_s[t].astype(f32) + tin1r[1].astype(f32)) + tin2r[...].astype(f32)
    ).astype(bf16)
    block_out = share_out(0, mixed, 3)
    for i in (0, 1, 3):
        block_out[i].start()
    abuf = keep.at[pl.ds(la, la)]
    abuf[...] = a_result()
    a_first = sum_start(ne, abuf, aparts, asend, arecv)
    wait_all(ne, e_second)
    re = rep_e.shape[1]
    rep_e[t] = etot[held_e : held_e + re, :]

    def share_rows(buf, k):
        return [
            remote(buf.at[t], buf.at[t], osend.at[k], orecv.at[k], (e, far)),
            remote(buf.at[t], buf.at[t], osend.at[k + 1], orecv.at[k + 1], (e, near)),
            remote(buf.at[far], buf.at[far], osend.at[k + 2], orecv.at[k + 2], (e, near)),
        ]

    rep_out = share_rows(rep_e, 6)
    for i in (0, 1):
        rep_out[i].start()
    a_second = sum_share(ne, a_first, abuf, aparts, atot, asend, arecv)
    igrad_out[0].wait_recv()
    igrad_out[2].start()
    wait_all(ne, a_second)
    rep_a[t] = atot[3 * lw : 3 * lw + quarter, :]
    last_out = share_rows(rep_a, 9)
    for i in (0, 1):
        last_out[i].start()
    for group in (block_out, rep_out, last_out):
        group[0].wait_recv()
        group[2].start()
    for group in (igrad_out, block_out, rep_out, last_out):
        group[0].wait_send()
        for copy in group[1:]:
            copy.wait()
    for copy in fars + relays + big_far + big_relay:
        copy.wait_send()


def write_kernel(
    dims, e_all, a_all, outs, rep_e, rep_a, block_output, input_grad, triple_down, triple_up, project_down,
    project_up, router_down, router_up, first_down, first_up, second_down, second_up,
):
    nt, seq, seqp, images, ffq, lw, grows = dims
    per = images // nt
    tok, width = block_output.shape
    flat = outs.shape[2]
    for j, out in enumerate((block_output, input_grad)):
        for a in range(0, tok, seqp):
            b = min(a + seqp, tok)
            i0, i1 = a // seq, (b - 1) // seq
            parts = []
            for i in range(i0, i1 + 1):
                row = iota((b - a, seqp), 0) + a
                sel = (iota((b - a, seqp), 1) == row - i * seq) & (row < (i + 1) * seq)
                src = outs[i // per, j, (i % per) * seqp : (i % per + 1) * seqp, :]
                parts.append(dot(sel.astype(f32).astype(bf16), src))
            whole_part = parts[0]
            for part in parts[1:]:
                whole_part = whole_part + part
            out[a:b, :] = whole_part.astype(bf16)
    for c in range(ffq // 128):
        first_up[:, c * 128 : (c + 1) * 128] = e_all[c * 128 : (c + 1) * 128].astype(f32)
    second_down[...] = e_all[ffq : 2 * ffq].astype(f32)
    for c in range(3):
        triple_up[c] = a_all[c * lw : (c + 1) * lw].astype(f32)
    last = e_all.shape[0]
    project_down[...] = e_all[last - lw : last].astype(f32)
    quarter = width // nt
    share = ADAPT // nt
    for q in range(nt):
        at = slice(q * quarter, (q + 1) * quarter)
        up_at = slice(q * share, (q + 1) * share)
        triple_down[at, :] = rep_a[q].astype(f32)
        first_down[at, :] = rep_e[q, 0:quarter, :].astype(f32)
        off = quarter
        for c in range(width // 128):
            second_up[up_at, c * 128 : (c + 1) * 128] = rep_e[q, off : off + share, :].astype(f32)
            off += share
        off = grows - 2 * ffq
        for c in range(width // 128):
            project_up[up_at, c * 128 : (c + 1) * 128] = rep_e[q, off : off + share, :].astype(f32)
            off += share
        router_down[at, :] = rep_e[q, off : off + quarter, :].astype(f32)
        off += quarter
    router_up[...] = rep_e[0, off : off + router_up.shape[0], :].astype(f32)


def body(
    inputs, gain_attend, triple_weight, project_weight, gain_mixture, router_weight, expert_first,
    expert_second, triple_down, triple_up, project_down, project_up, router_down, router_up,
    first_down, first_up, second_down, second_up, adapter_index, routes, priority, cotangent,
):
    ne = lax.axis_size("expert")
    nt = lax.axis_size("tensor")
    tok, width = inputs.shape
    images = adapter_index.shape[0]
    seq = tok // images
    seqp = up(seq, 16)
    per = images // nt
    rows = per * seqp
    experts = router_weight.shape[1]
    local = expert_first.shape[0]
    ffq = expert_first.shape[2]
    lw = triple_weight.shape[2]
    cap = nt * ((5 * tok * TOP + 4 * nt * experts - 1) // (4 * nt * experts))
    capq = cap // nt
    cp = up(capq + 2, 16)
    block = local * cp
    smem = pl.BlockSpec(memory_space=pltpu.SMEM)
    anywhere = pl.BlockSpec(memory_space=pl.ANY)
    shape = jax.ShapeDtypeStruct
    wide = up(2 * experts, 128)
    gain1 = gain_attend.reshape(1, width)
    gain2 = gain_mixture.reshape(1, width)
    rw = router_weight.T
    ru = router_up.T
    big = (expert_first, expert_second, first_up, second_down)
    n_w = 8
    erows = ne * cp
    quarter = width // nt
    held_e = 2 * ffq
    grows = up(held_e + quarter + (ADAPT // nt) * (width // 128), 16 * ne)
    one = (rows, width)
    small = (8, rows)
    la = up(3 * lw + quarter, 16 * ne)
    lb = up(ADAPT + quarter + experts + lw, 16 * ne)
    re = grows + lb - lw - held_e
    n_big = len(big)
    slots = (ne, block, width)
    roomy = ne * block <= 1024
    spare = slots if roomy else (8, 128)
    finals = pl.pallas_call(
        functools.partial(
            block_kernel,
            (nt, ne, seq, seqp, images, experts, cap, capq, cp, held_e, grows, la, lb, roomy),
        ),
        out_shape=[
            shape((grows + lb, 128), bf16),
            shape((la, 128), bf16),
            shape((nt, 2) + one, bf16),
            shape((nt, re, 128), bf16),
            shape((nt, quarter, 128), bf16),
            shape((8, 128) if roomy else slots, bf16),
            shape((8, 128) if roomy else slots, bf16),
        ],
        in_specs=[smem] + whole(2) + [anywhere] * 2 + whole(13) + [anywhere] * 4,
        out_specs=whole(2) + [anywhere] + whole(2) + [anywhere] * 2,
        scratch_shapes=[
            VMEM((nt, rows, TOP), i32),
            VMEM((nt, TOP, rows), i32),
            VMEM((nt, rows, TOP), i32),
            VMEM(one, f32),
            VMEM(one, bf16),
            VMEM(one, bf16),
            VMEM(one, f32),
            VMEM((nt, rows, 3 * lw), bf16),
            VMEM((nt, rows, lw), bf16),
            VMEM((rows, ADAPT), bf16),
            VMEM((rows, ADAPT), bf16),
            VMEM(one, bf16),
            VMEM((nt, width, 3 * lw), bf16),
            VMEM((nt, ADAPT, 3 * lw), bf16),
            VMEM((nt, lw, width), bf16),
            VMEM((nt, lw, ADAPT), bf16),
            VMEM(slots, bf16),
            VMEM(slots, bf16),
            VMEM((nt,) + one, bf16),
            VMEM((images * seqp, wide), bf16),
            VMEM(slots, bf16),
            VMEM((nt,) + one, bf16),
            VMEM((nt,) + small, f32),
            VMEM((max(2 * erows, 2 * rows), width), f32),
            VMEM((max(ne * block, images * seqp), 1), f32),
            VMEM(slots, bf16),
            VMEM((nt, width, ffq), bf16),
            VMEM((nt, ffq, width), bf16),
            VMEM((nt, ADAPT, ffq), bf16),
            VMEM((nt, ffq, ADAPT), bf16),
            VMEM((erows, width), bf16),
            VMEM((erows, width), bf16),
            VMEM((2, erows, ADAPT), bf16),
            VMEM((erows, ADAPT), f32),
            VMEM((erows, 2), f32),
            VMEM((2, erows, ADAPT), f32),
            VMEM((ADAPT, width), f32),
            VMEM((nt, ADAPT, ffq), f32),
            VMEM((nt, ADAPT, ffq), f32),
            VMEM((ADAPT, width), f32),
            VMEM((nt, max(grows, la + lb), 128), bf16),
            VMEM((2, grows, 128), bf16),
            VMEM((max(grows, la + lb, 2 * la), 128), bf16),
            VMEM((grows, 128), bf16),
            VMEM((tok, width), bf16),
            VMEM((tok, width) if roomy else (8, 128), bf16),
            VMEM(spare, bf16),
            VMEM(spare, bf16),
            VMEM((2,) + one, bf16),
            VMEM((2,) + small, f32),
            VMEM((2,) + one, bf16),
            VMEM(one, bf16),
            VMEM(small, f32),
            VMEM(one, bf16),
            VMEM(small, f32),
            VMEM(one, bf16),
            VMEM((2, lb, 128), bf16),
            VMEM((lb, 128), bf16),
            VMEM((2, la, 128), bf16),
            VMEM((la, 128), bf16),
            VMEM((grows + lb, 128), bf16),
            VMEM((ne - 1, (grows + lb) // ne, 128), bf16),
            VMEM((ne - 1, la // ne, 128), bf16),
            VMEM((rows, 3 * lw), bf16),
            VMEM((nt, rows, lw), bf16),
            VMEM((rows, ADAPT), f32),
            dma(3 * n_w),
            dma(3 * n_w),
            dma(3 * n_big),
            dma(3 * n_big),
            dma(ne),
            dma(ne),
            dma(6),
            dma(6),
            dma(local * ne),
            dma(local * ne),
            dma(local * ne),
            dma(local * ne),
            dma(local * ne),
            dma(local * ne),
            dma(9),
            dma(9),
            dma(9),
            dma(9),
            dma(2 * ne),
            dma(2 * ne),
            dma(2 * ne),
            dma(2 * ne),
            dma(12),
            dma(12),
            dma(3),
            dma(n_w),
            dma(n_big + 2),
            dma(2 * local),
        ],
        compiler_params=pltpu.CompilerParams(
            collective_id=0, has_side_effects=True, vmem_limit_bytes=67000000
        ),
        name="block",
    )(
        adapter_index, priority, routes.T, cotangent, inputs, gain1, gain2,
        triple_weight.transpose(1, 0, 2), triple_up.transpose(1, 0, 2), project_weight,
        project_down, triple_down, project_up, rw, router_down, ru, first_down, second_up, *big,
    )

    outs = pl.pallas_call(
        functools.partial(write_kernel, (nt, seq, seqp, images, ffq, lw, grows)),
        out_shape=[
            shape((tok, width), bf16),
            shape((tok, width), bf16),
            shape((width, ADAPT), f32),
            shape((3, ADAPT, lw), f32),
            shape((lw, ADAPT), f32),
            shape((ADAPT, width), f32),
            shape((width, ADAPT), f32),
            shape((experts, ADAPT), f32),
            shape((width, ADAPT), f32),
            shape((ADAPT, ffq), f32),
            shape((ffq, ADAPT), f32),
            shape((ADAPT, width), f32),
        ],
        in_specs=whole(5),
        out_specs=whole(12),
        name="write",
    )(*finals[:5])
    outs = list(outs)
    outs[3] = outs[3].transpose(1, 0, 2)
    outs[7] = outs[7].T
    return tuple(outs)


def solution(mesh):
    return jax.shard_map(
        body,
        mesh=mesh,
        in_specs=(
            P("expert", None),
            P(),
            P(None, None, "tensor"),
            P("tensor", None),
            P(),
            P(),
            P("expert", None, "tensor"),
            P("expert", "tensor", None),
            P(),
            P(None, None, "tensor"),
            P("tensor", None),
            P(),
            P(),
            P(),
            P(),
            P(None, "tensor"),
            P("tensor", None),
            P(),
            P("expert"),
            P("expert", None),
            P("expert", None),
            P("expert", None),
        ),
        out_specs=(
            P("expert", None),
            P("expert", None),
            P(),
            P(None, None, "tensor"),
            P("tensor", None),
            P(),
            P(),
            P(),
            P(),
            P(None, "tensor"),
            P("tensor", None),
            P(),
        ),
        check_vma=False,
    )
```

```python
import functools

import jax
import jax.numpy as jnp
from jax import lax
from jax.experimental import pallas as pl
from jax.experimental.pallas import tpu as pltpu
from jax.sharding import PartitionSpec as P

HEAD_DIM = 64
TOP = 2
ADAPTERS = 8
RANK = 16
ADAPT = ADAPTERS * RANK
EPS = 1e-06

f32 = jnp.float32
bf16 = jnp.bfloat16
i32 = jnp.int32
MESH = pl.DeviceIdType.MESH
VMEM = pltpu.VMEM


def up(a, b):
    return -(-a // b) * b


def dot(a, b):
    return lax.dot_general(a, b, (((1,), (0,)), ((), ())), preferred_element_type=f32)


def dot_nt(a, b):
    return lax.dot_general(a, b, (((1,), (1,)), ((), ())), preferred_element_type=f32)


def dot_tn(a, b):
    return lax.dot_general(a, b, (((0,), (0,)), ((), ())), preferred_element_type=f32)


def split_high_low(a):
    high = a.astype(bf16)
    return high, (a - high.astype(f32)).astype(bf16)


def dot_fine(a, b):
    high, low = split_high_low(a)
    return dot(high, b) + dot(low, b)


def dot_nt_fine(a, b):
    high, low = split_high_low(a)
    return dot_nt(high, b) + dot_nt(low, b)


def iota(shape, axis):
    return lax.broadcasted_iota(i32, shape, axis)


def to_row(col):
    n = col.shape[0]
    return jnp.sum(jnp.where(iota((n, n), 0) == iota((n, n), 1), col, 0.0), axis=0, keepdims=True)


def to_col(row):
    n = row.shape[1]
    return jnp.sum(jnp.where(iota((n, n), 0) == iota((n, n), 1), row, 0.0), axis=1, keepdims=True)


def picks_of(adapters, base, per, seqp):
    lane = iota((seqp, ADAPT), 1) // RANK
    return jnp.concatenate(
        [(lane == adapters[base + li]).astype(f32) for li in range(per)], axis=0
    )


def whole(count):
    return [pl.BlockSpec(memory_space=VMEM) for _ in range(count)]


def norm_stats(x):
    centre = jnp.mean(x, axis=-1, keepdims=True)
    shifted = x - centre
    scale = lax.rsqrt(jnp.mean(shifted * shifted, axis=-1, keepdims=True) + EPS)
    return shifted * scale, scale


def norm_back(grad, gain, unit, scale):
    g = grad * gain
    return scale * (
        g - jnp.mean(g, axis=-1, keepdims=True) - unit * jnp.mean(g * unit, axis=-1, keepdims=True)
    )


def greet(peers):
    barrier = pltpu.get_barrier_semaphore()
    for peer in peers:
        pl.semaphore_signal(barrier, 1, device_id=peer, device_id_type=MESH)
    pl.semaphore_wait(barrier, len(peers))


def remote(src, dst, send, recv, peer):
    return pltpu.make_async_remote_copy(
        src_ref=src, dst_ref=dst, send_sem=send, recv_sem=recv, device_id=peer, device_id_type=MESH
    )


def where_am_i():
    e = lax.axis_index("expert")
    t = lax.axis_index("tensor")
    return e, t, jnp.bitwise_xor(t, 1), jnp.bitwise_xor(t, 2), jnp.bitwise_xor(t, 3)


def dma(n):
    return pltpu.SemaphoreType.DMA((n,))


def linked(ident):
    return pltpu.CompilerParams(collective_id=ident, has_side_effects=True)


def gates_of(mixed, r0, r1, pick, rw, rd, ru):
    low = dot(mixed, rd) * pick
    logits = dot_nt(mixed, rw) + dot_nt_fine(low, ru)
    lane = iota((1, rw.shape[0]), 1)
    first = jnp.sum(jnp.where(r0 == lane, logits, 0.0), axis=1, keepdims=True)
    second = jnp.sum(jnp.where(r1 == lane, logits, 0.0), axis=1, keepdims=True)
    top = jnp.maximum(first, second)
    a = jnp.exp(first - top)
    b = jnp.exp(second - top)
    return a / (a + b), b / (a + b), low


def own_images(ref, first, per, seq, seqp, put):
    tok = ref.shape[0]
    for li in range(per):
        row = iota((seqp, tok), 0)
        sel = (iota((seqp, tok), 1) == row + (first + li) * seq) & (row < seq)
        put(pl.ds(li * seqp, seqp), dot(sel.astype(f32).astype(bf16), ref[...]))


def erf_parts(pre):
    cdf = 0.5 * (1.0 + lax.erf(pre * 0.7071067811865476))
    return pre * cdf, cdf + pre * (jnp.exp(-0.5 * pre * pre) * 0.3989422804014327)


def chunk_of(ref, ne, p):
    size = ref.shape[0] // ne
    return pl.ds(pl.multiple_of(p * size, size), size)


def sum_copy(ne, src, parts, send, recv):
    e, t = where_am_i()[:2]

    def copy(d):
        p = lax.rem(e + d, ne)
        return remote(src.at[chunk_of(src, ne, p)], parts.at[d - 1], send.at[d], recv.at[d], (p, t))

    return copy


def start_all(ne, copy):
    def start(d, carry):
        copy(d).start()
        return carry

    lax.fori_loop(1, ne, start, 0)


def sum_share(ne, copy, src, parts, total, send, recv):
    e, t = where_am_i()[:2]
    mine = chunk_of(src, ne, e)

    def add(d, acc):
        copy(d).wait()
        return acc + parts[d - 1].astype(f32)

    total[mine, :] = lax.fori_loop(1, ne, add, src[mine, :].astype(f32)).astype(bf16)

    def share(d):
        p = lax.rem(e + d, ne)
        return remote(total.at[mine], total.at[mine], send.at[ne + d], recv.at[ne + d], (p, t))

    def start(d, carry):
        share(d).start()
        return carry

    lax.fori_loop(1, ne, start, 0)
    return share


def wait_all(ne, copy):
    def wait(d, carry):
        copy(d).wait()
        return carry

    lax.fori_loop(1, ne, wait, 0)


def block_kernel(
    dims, adapters, prio, routes, cot_in, x_in, gain1, gain2, wt_in, tup_in, pw_in, pd_in,
    tdn, pup, rw, rd, ru, fdn, sup, w1_in, w2_in, fup_in, sdn_in,
    etot, btot, atot, outs, rep_e, rep_a, back_out, res_out, *rest,
):
    nt, ne, seq, seqp, images, experts, cap, chunks, cp, held_e, grows, la, lb, roomy = dims
    (
        slotc, slotr, routec, xs, cot_own, mixed, middle, triple, attended, tlow, plow, attn_in,
        wt, tup, pw, pd, got, got_cot, cot_pad, one_s, cots, mall, gall, acc_s, gate_s, out_s,
        w1, w2, fup, sdn, sent_s, sg_s, low_s, gcol_s, gg_rows, acc_low,
        acc_fd, acc_fu, acc_sd, acc_su, gr_s, gin1, keep, gin2, cot, x_own,
        back_s, res_s, tin1, tin1k, tin1r, keep_g, keep_k, tin2, tin2k, tin2r,
        bin1, bin2, ain1, ain2, eparts, bparts, aparts, gt_s, ga_s, back_low,
        wsend, wrecv, bsend, brecv, csend, crecv, tsend, trecv, send, recv, gsend, grecv, rsend, rrecv,
        ssend, srecv, usend, urecv, esend, erecv, b2send, b2recv, asend, arecv, osend, orecv,
        here, own_sem, load_sem, ret_sem,
    ) = rest
    back = back_s if roomy else back_out
    ebuf, bbuf = gin1.at[0], bin1.at[0]
    got_res = res_s if roomy else res_out
    e, t, near, far, cross = where_am_i()
    lw = pw_in.shape[0]
    width = x_in.shape[1]
    local = w1_in.shape[0]
    parts = nt // local
    n_out, block = cots.shape[0], cots.shape[1]
    peers = [(e, far), (e, near)] + [(lax.rem(e + d, ne), t) for d in range(1, ne)]
    barrier = pltpu.get_barrier_semaphore()
    for peer in peers:
        pl.semaphore_signal(barrier, 1, device_id=peer, device_id_type=MESH)

    def big_ref(k, to):
        return (fup_in, sdn_in)[k] if k < 2 else (w1_in, w2_in)[k - 2].at[lax.div(to, parts)]

    big = (fup, sdn, w1, w2)
    n_big = len(big)
    big_own = [
        pltpu.make_async_copy(big_ref(k, t), big[k].at[t], load_sem.at[k]) for k in range(n_big)
    ]
    big_far = [
        remote(big_ref(k, far), big[k].at[t], bsend.at[3 * k], brecv.at[3 * k], (e, far))
        for k in range(n_big)
    ]
    big_near = [
        remote(big_ref(k, near), big[k].at[t], bsend.at[3 * k + 1], brecv.at[3 * k + 1], (e, near))
        for k in range(n_big)
    ]
    big_relay = [
        remote(big[k].at[far], big[k].at[far], bsend.at[3 * k + 2], brecv.at[3 * k + 2], (e, near))
        for k in range(n_big)
    ]
    load_cot = pltpu.make_async_copy(cot_in, cot, load_sem.at[n_big])
    x_ref = x_own if roomy else cot
    load_x = pltpu.make_async_copy(x_in, x_ref, load_sem.at[n_big + 1])
    for copy in [load_cot] + big_own:
        copy.start()
    if roomy:
        load_x.start()

    moves = []
    for c in range(3):
        lanes = pl.ds(c * lw, lw)
        moves.append((wt_in.at[c], lambda q, lanes=lanes: wt.at[q, :, lanes]))
        moves.append((tup_in.at[c], lambda q, lanes=lanes: tup.at[q, :, lanes]))
    moves.append((pw_in, lambda q: pw.at[q]))
    moves.append((pd_in, lambda q: pd.at[q]))
    n_w = len(moves)
    fars = [
        remote(src, at(t), wsend.at[3 * i], wrecv.at[3 * i], (e, far))
        for i, (src, at) in enumerate(moves)
    ]
    nears = [
        remote(src, at(t), wsend.at[3 * i + 1], wrecv.at[3 * i + 1], (e, near))
        for i, (src, at) in enumerate(moves)
    ]
    relays = [
        remote(at(far), at(far), wsend.at[3 * i + 2], wrecv.at[3 * i + 2], (e, near))
        for i, (src, at) in enumerate(moves)
    ]
    owns = [
        pltpu.make_async_copy(src, at(t), own_sem.at[i]) for i, (src, at) in enumerate(moves)
    ]
    for copy in owns:
        copy.start()

    tok = prio.shape[1]
    per = images // nt
    rows = per * seqp
    total = nt * rows
    wide = one_s.shape[-1]
    order = iota((seqp, tok), 1).astype(f32)
    lane = iota((seqp, wide), 1)
    for i in range(images):
        q, at = i // per, pl.ds(i % per * seqp, seqp)
        all_at = pl.ds(i * seqp, seqp)
        token = iota((seqp, 1), 0) + i * seq
        gate_s[all_at, :] = jnp.sum(
            jnp.where(prio[...] == token, order, 0.0), axis=1, keepdims=True
        )
        lane0 = i * seq // 128 * 128
        lane1 = min(lane0 + up(seq + 128, 128), tok)
        here_i = (iota((seqp, lane1 - lane0), 1) + lane0 == token) & (iota((seqp, lane1 - lane0), 0) < seq)
        r = [
            jnp.sum(
                jnp.where(here_i, routes[k : k + 1, lane0:lane1].astype(f32) + 1.0, 0.0),
                axis=1,
                keepdims=True,
            ).astype(i32)
            - 1
            for k in range(TOP)
        ]
        for k in range(TOP):
            routec[q, at, k : k + 1] = r[k]
        named = jnp.where(lane < experts, r[0], jnp.where(r[1] < 0, -1, r[1] + experts))
        one_s[all_at, :] = (named == lane).astype(f32).astype(bf16)
    pl.semaphore_wait(barrier, len(peers))
    for copy in fars + nears:
        copy.start()
    totals = dot(jnp.ones((8, total), bf16), one_s[...])[0:1]
    rank_rows = [to_row(gate_s[pl.ds(q * rows, rows), :]) for q in range(nt)]
    lane = iota((rows, wide), 1)
    for q in range(nt):
        at = pl.ds(q * rows, rows)
        mine = gate_s[at, :]
        counts = jnp.zeros((rows, wide), f32)
        for p in range(nt):
            before = (rank_rows[p] < mine).astype(f32).astype(bf16)
            counts = counts + dot(before, one_s[pl.ds(p * rows, rows), :])
        hot = one_s[at, :].astype(f32) * counts
        first = jnp.sum(jnp.where(lane < experts, hot, 0.0), axis=1, keepdims=True)
        second = jnp.sum(
            jnp.where(lane < experts, 0.0, hot)
            + jnp.where((lane < experts) & (routec[q, :, 1:2] == lane), totals, 0.0),
            axis=1,
            keepdims=True,
        )
        for k, pos in ((0, first), (1, second)):
            named = routec[q, :, k : k + 1]
            place = pos.astype(i32)
            kept = (named >= 0) & (place < cap)
            kept = kept & (lax.rem(named, local) == lax.div(t, parts))
            kept = kept & (lax.rem(place, parts) == lax.rem(t, parts))
            index = lax.div(place, parts)
            index = jnp.where(index < cp - 2, index, index + 2)
            slot = jnp.where(kept, lax.div(named, local) * block + index, -1)
            slotc[q, :, k : k + 1] = slot
            slotr[q, k : k + 1, :] = to_row(slot.astype(f32)).astype(i32)

    load_cot.wait()
    for i in range(images):
        start = i * seq // 16 * 16
        stop = min(start + up(seq, 16) + 16, tok)
        src = iota((seqp, stop - start), 1) + start
        row = iota((seqp, stop - start), 0)
        sel = ((src == row + i * seq) & (row < seq)).astype(f32).astype(bf16)
        cot_pad[i // per, pl.ds(i % per * seqp, seqp), :] = dot(sel, cot[start:stop, :]).astype(bf16)
    step = max(1, 512 // block)
    image_of = iota((1, rows), 1) // seqp

    def pack(d, carry):
        s = iota((step * block, 1), 0) + d * (step * block)
        acc = jnp.zeros((step * block, width), f32)
        idc = jnp.zeros((step * block, 1), f32)
        for q in range(nt):
            ids = jnp.zeros((1, rows), f32)
            for li in range(per):
                ids = jnp.where(image_of == li, adapters[q * per + li].astype(f32), ids)
            g = (slotr[q, 0:1, :] == s) | (slotr[q, 1:2, :] == s)
            idc = idc + jnp.sum(jnp.where(g, ids, 0.0), axis=1, keepdims=True)
            acc = acc + dot(g.astype(f32).astype(bf16), cot_pad[q])
        row = iota((block, block), 0)
        for b in range(step):
            part = acc[b * block : (b + 1) * block]
            idr = to_row(idc[b * block : (b + 1) * block])
            head = jnp.where(row == cp - 2, idr, part[:, 0:block])
            cots[d * step + b, :, 0:block] = head.astype(bf16)
            cots[d * step + b, :, block:] = part[:, block:].astype(bf16)
        return carry

    lax.fori_loop(0, n_out // step, pack, 0)

    def cot_copy(d):
        p = lax.rem(e + d, ne)
        return remote(cots.at[p], got_cot.at[e], csend.at[d], crecv.at[d], (p, t))

    def cot_start(d, carry):
        cot_copy(d).start()
        return carry

    lax.fori_loop(1, ne, cot_start, 0)
    own_cot = pltpu.make_async_copy(cots.at[e], got_cot.at[e], here.at[0])
    own_cot.start()

    def put_x(at, value):
        xs[at, :] = value

    def put_cot(at, value):
        cot_own[at, :] = value.astype(bf16)

    if not roomy:
        own_images(cot, t * per, per, seq, seqp, put_cot)
        load_x.start()
    load_x.wait()
    own_images(x_ref, t * per, per, seq, seqp, put_x)
    pick = picks_of(adapters, t * per, per, seqp)
    unit, _ = norm_stats(xs[...])
    normed = (unit * gain1[...]).astype(bf16)
    attn_in[...] = normed
    low = (dot(normed, tdn[...]) * pick).astype(bf16)
    tlow[...] = low
    head_of = iota((1, lw), 1) // HEAD_DIM
    key_ok = iota((1, seqp), 1) < seq

    def piece(m, carry):
        p = jnp.bitwise_xor(t, m)

        @pl.when(m == 0)
        def _():
            for copy in owns:
                copy.wait()

        @pl.when(m == 1)
        def _():
            for copy in nears:
                copy.wait()

        @pl.when(m == 2)
        def _():
            for i in range(6):
                fars[i].wait_recv()
                relays[i].start()

        @pl.when(m == 3)
        def _():
            for i in range(6):
                relays[i].wait_recv()

        triple[p] = (dot(attn_in[...], wt[p]) + dot(tlow[...], tup[p])).astype(bf16)
        for li in range(per):
            at = pl.ds(li * seqp, seqp)
            q = triple[p, at, 0:lw]
            k = triple[p, at, lw : 2 * lw]
            v = triple[p, at, 2 * lw : 3 * lw]
            acc = jnp.zeros((seqp, lw), f32)
            for h in range(lw // HEAD_DIM):
                on = head_of == h
                s = dot_nt(jnp.where(on, q, 0.0).astype(bf16), k) * HEAD_DIM**-0.5
                s = jnp.where(key_ok, s, -jnp.inf)
                ex = jnp.exp(s - jnp.max(s, axis=1, keepdims=True))
                probs = (ex / jnp.sum(ex, axis=1, keepdims=True)).astype(bf16)
                acc = acc + dot(probs, jnp.where(on, v, 0.0).astype(bf16))
            attended[p, at, :] = acc.astype(bf16)
        return carry

    lax.fori_loop(0, nt, piece, 0)
    for copy in big_near:
        copy.start()
    for i in range(6, n_w):
        fars[i].wait_recv()
        relays[i].start()
    for i in range(6, n_w):
        relays[i].wait_recv()
    psum = jnp.zeros((rows, ADAPT), f32)
    branch = jnp.zeros((rows, width), f32)
    for p in range(nt):
        psum = psum + dot(attended[p], pd[p])
        branch = branch + dot(attended[p], pw[p])
    low2 = (psum * pick).astype(bf16)
    plow[...] = low2
    mid = xs[...] + branch + dot(low2, pup[...])
    middle[...] = mid
    unit2, _ = norm_stats(mid)
    mix = (unit2 * gain2[...]).astype(bf16)
    mixed[...] = mix
    mall[t] = mix
    r = routec[t]
    a, b, _ = gates_of(mix, r[:, 0:1], r[:, 1:2], pick, rw[...], rd[...], ru[...])
    gall[t] = jnp.zeros(gall.shape[1:], f32)
    gall[t, 0:1, :] = to_row(a)
    gall[t, 1:2, :] = to_row(b)

    mix_far = [
        remote(buf.at[t], buf.at[t], tsend.at[i], trecv.at[i], (e, far))
        for i, buf in enumerate((mall, gall))
    ]
    mix_near = [
        remote(buf.at[t], buf.at[t], tsend.at[2 + i], trecv.at[2 + i], (e, near))
        for i, buf in enumerate((mall, gall))
    ]
    mix_relay = [
        remote(buf.at[far], buf.at[far], tsend.at[4 + i], trecv.at[4 + i], (e, near))
        for i, buf in enumerate((mall, gall))
    ]
    for copy in mix_far + mix_near:
        copy.start()
    for copy in big_far:
        copy.start()
    step = max(1, 512 // block)

    def gather_rows(q, s):
        g0 = slotr[q, 0:1, :] == s
        g1 = slotr[q, 1:2, :] == s
        gate = jnp.sum(
            jnp.where(g0, gall[q, 0:1, :], jnp.where(g1, gall[q, 1:2, :], 0.0)), axis=1, keepdims=True
        )
        return dot((g0 | g1).astype(f32).astype(bf16), mall[q]), gate

    def add_quarter(q, fresh):
        def some(d, carry):
            at = pl.ds(pl.multiple_of(d * (step * block), step * block), step * block)
            s = iota((step * block, 1), 0) + d * (step * block)
            part, gate = gather_rows(q, s)
            acc_s[at, :] = part if fresh else acc_s[at, :] + part
            gate_s[at, :] = gate if fresh else gate_s[at, :] + gate
            return carry

        lax.fori_loop(0, n_out // step, some, 0)

    add_quarter(t, True)
    for copy in mix_near:
        copy.wait_recv()
    add_quarter(near, False)
    if roomy:
        own_images(cot, t * per, per, seq, seqp, put_cot)
    for copy in mix_far:
        copy.wait_recv()
    for copy in mix_relay:
        copy.start()
    add_quarter(far, False)
    for copy in mix_relay:
        copy.wait_recv()

    def finish(p):
        at = pl.ds(pl.multiple_of(p * block, block), block)
        part, gate = gather_rows(cross, iota((block, 1), 0) + p * block)
        part = acc_s[at, :] + part
        gate = to_row(gate_s[at, :] + gate)
        high = gate.astype(bf16).astype(f32)
        row = iota((block, block), 0)
        head = jnp.where(row == cp - 2, high, part[:, 0:block])
        head = jnp.where(row == cp - 1, gate - high, head)
        return head.astype(bf16), part[:, block:].astype(bf16)

    def chunk(h):
        return pl.ds(pl.multiple_of(h * cp, cp), cp)

    def out_copy(d, h):
        p = lax.rem(e + d, ne)
        k = d * chunks + h
        return remote(out_s.at[p, chunk(h)], got.at[e, chunk(h)], send.at[k], recv.at[k], (p, t))

    def send_one(d, carry):
        p = lax.rem(e + d, ne)
        head, tail = finish(p)
        out_s[p, :, 0:block] = head
        out_s[p, :, block:] = tail
        out_copy(d, 0).start()
        return carry

    lax.fori_loop(1, ne, send_one, 0)

    for h in range(1, chunks):

        def send_more(d, carry, h=h):
            out_copy(d, h).start()
            return carry

        lax.fori_loop(1, ne, send_more, 0)
    head, tail = finish(e)
    got[e, :, 0:block] = head
    got[e, :, block:] = tail

    n = ne
    erows = n * cp
    row_at = lax.rem(iota((erows, 1), 0), cp)
    res_at, gsent_at = pl.ds(0, erows), pl.ds(erows, erows)
    for buf in (acc_fd, acc_fu, acc_sd, acc_su):
        buf[...] = jnp.zeros_like(buf)
    for copy in big_own + big_near:
        copy.wait()

    def cot_wait(d, carry):
        cot_copy(d).wait()
        return carry

    lax.fori_loop(1, ne, cot_wait, 0)
    own_cot.wait()

    def grad_copy(d, h):
        p = lax.rem(e + d, ne)
        k = d * chunks + h
        return remote(cots.at[p, chunk(h)], back.at[e, chunk(h)], gsend.at[k], grecv.at[k], (p, t))

    def res_copy(d):
        p = lax.rem(e + d, ne)
        return remote(out_s.at[p], got_res.at[e], rsend.at[d], rrecv.at[d], (p, t))

    def experts_chunk(h, carry):
        at = chunk(h)

        def rows_wait(d, carry):
            out_copy(d, h).wait_recv()
            return carry

        lax.fori_loop(1, ne, rows_wait, 0)

        @pl.when(h == 0)
        def _():
            diag = iota((block, block), 0) == iota((block, block), 1)

            def headers(m, carry):
                idr = got_cot[m, cp - 2 : cp - 1, 0:block].astype(f32)
                gr = got[m, cp - 2 : cp - 1, 0:block].astype(f32) + got[
                    m, cp - 1 : cp, 0:block
                ].astype(f32)
                gcol_s[m, :, 0:1] = jnp.sum(jnp.where(diag, idr, 0.0), axis=1, keepdims=True)
                gcol_s[m, :, 1:2] = jnp.sum(jnp.where(diag, gr, 0.0), axis=1, keepdims=True)
                return carry

            lax.fori_loop(0, n, headers, 0)

        spare = jnp.where((h == 0) | (h == chunks - 1), cp - 2, cp)
        real = row_at < spare
        cols = gcol_s[:, at, :].reshape(erows, 2)
        sent = jnp.where(real, got[:, at, :].reshape(erows, width).astype(f32), 0.0).astype(bf16)
        cotf = jnp.where(real, got_cot[:, at, :].reshape(erows, width).astype(f32), 0.0)
        pick_e = (cols[:, 0:1] == (iota((1, ADAPT), 1) // RANK).astype(f32)).astype(f32)
        sent_s[...] = sent
        sgrad = (cols[:, 1:2] * cotf).astype(bf16)
        sg_s[...] = sgrad
        low_s[0] = (dot(sent, fdn[...]) * pick_e).astype(bf16)
        low_s[1] = (dot_nt(sgrad, sup[...]) * pick_e).astype(bf16)
        acc_low[...] = jnp.zeros_like(acc_low)
        acc_s[pl.ds(0, 2 * erows), :] = jnp.zeros((2 * erows, width), f32)

        def through(m, carry):
            c = jnp.bitwise_xor(t, m)

            @pl.when((h == 0) & (m == 2))
            def _():
                for far_copy, relay in zip(big_far, big_relay):
                    far_copy.wait_recv()
                    relay.start()

            @pl.when((h == 0) & (m == 3))
            def _():
                for relay in big_relay:
                    relay.wait_recv()

            span = min(erows, 512)
            for r0 in range(0, erows, span):
                rs = slice(r0, r0 + span)
                gs = slice(erows + r0, erows + r0 + span)
                pre = dot(sent_s[rs, :], w1[c]) + dot(low_s[0, rs, :], fup[c])
                act, slope = erf_parts(pre)
                hid = act.astype(bf16)
                acc_low[0, rs, :] += dot(hid, sdn[c])
                acc_s[rs, :] += dot(hid, w2[c])
                ghid = dot_nt(sg_s[rs, :], w2[c]) + dot_nt(low_s[1, rs, :], sdn[c])
                gpre = (ghid * slope).astype(bf16)
                acc_fu[c] += dot_tn(low_s[0, rs, :], gpre)
                acc_sd[c] += dot_tn(low_s[1, rs, :], hid)
                acc_low[1, rs, :] += dot_nt(gpre, fup[c])
                acc_s[gs, :] += dot_nt(gpre, w1[c])
            return carry

        lax.fori_loop(0, nt, through, 0)

        def sent_wait(d, carry):
            out_copy(d, h).wait_send()
            return carry

        lax.fori_loop(1, ne, sent_wait, 0)
        cols = gcol_s[:, at, :].reshape(erows, 2)
        pick_e = (cols[:, 0:1] == (iota((1, ADAPT), 1) // RANK).astype(f32)).astype(f32)
        second_low = (acc_low[0] * pick_e).astype(bf16)
        res = (acc_s[res_at, :] + dot(second_low, sup[...])).astype(bf16).astype(f32)
        cotf = got_cot[:, at, :].reshape(erows, width).astype(f32)
        acc_low[0, :, 0:1] = jnp.sum(res * cotf, axis=1, keepdims=True)
        g1low = (acc_low[1] * pick_e).astype(bf16)
        gsent = acc_s[gsent_at, :] + dot_nt(g1low, fdn[...])
        cots[:, at, :] = gsent.astype(bf16).reshape(n, cp, width)
        diag = iota((cp, block), 0) + h * cp == iota((cp, block), 1)

        def footers(m, carry):
            gg = jnp.sum(
                jnp.where(diag, acc_low[0, pl.ds(pl.multiple_of(m * cp, cp), cp), 0:1], 0.0),
                axis=0,
                keepdims=True,
            )
            total = jnp.where(h == 0, gg, gg_rows[pl.ds(m, 1), :] + gg)
            gg_rows[pl.ds(m, 1), :] = total

            @pl.when(h == chunks - 1)
            def _():
                high = total.astype(bf16).astype(f32)
                row = iota((16, block), 0)
                to = pl.ds(block - 16, 16)
                old = cots[m, to, 0:block].astype(f32)
                old = jnp.where(row == 14, high, jnp.where(row == 15, total - high, old))
                cots[m, to, 0:block] = old.astype(bf16)

            return carry

        lax.fori_loop(0, n, footers, 0)

        def grad_start(d, carry):
            grad_copy(d, h).start()
            return carry

        lax.fori_loop(1, ne, grad_start, 0)
        out_s[:, at, :] = (cols[:, 1:2] * res).astype(bf16).reshape(n, cp, width)
        acc_su[...] += dot_tn(second_low, sg_s[...])
        acc_fd[...] += dot_tn(g1low, sent_s[...])
        return carry

    gg_rows[...] = jnp.zeros_like(gg_rows)
    lax.fori_loop(0, chunks, experts_chunk, 0)
    locals_ = [
        pltpu.make_async_copy(cots.at[e], back.at[e], ret_sem.at[0]),
        pltpu.make_async_copy(out_s.at[e], got_res.at[e], ret_sem.at[1]),
    ]
    for copy in locals_:
        copy.start()

    def res_start(d, carry):
        res_copy(d).start()
        return carry

    ffq = w1.shape[2]
    quarter = width // nt
    share = ADAPT // nt
    for q in range(nt):
        off = 0
        for c in range(ffq // 128):
            gr_s[q, off : off + 128, :] = acc_fu[q, :, c * 128 : (c + 1) * 128].astype(bf16)
            off += 128
        gr_s[q, off : off + ffq, :] = acc_sd[q].T.astype(bf16)
        off += ffq
        gr_s[q, off : off + quarter, :] = acc_fd[:, q * quarter : (q + 1) * quarter].T.astype(bf16)
        off += quarter
        for c in range(width // 128):
            at = slice(q * share, (q + 1) * share)
            gr_s[q, off : off + share, :] = acc_su[at, c * 128 : (c + 1) * 128].astype(bf16)
            off += share
        if off < grows:
            gr_s[q, off:grows, :] = jnp.zeros((grows - off, 128), bf16)

    def tensor_sum(rows_at, in1, in2, k):
        a = remote(gr_s.at[cross, rows_at], in1.at[0], ssend.at[k], srecv.at[k], (e, near))
        b = remote(gr_s.at[near, rows_at], in1.at[1], ssend.at[k + 1], srecv.at[k + 1], (e, near))
        held = keep.at[rows_at]
        c = remote(held, in2, ssend.at[k + 2], srecv.at[k + 2], (e, far))

        def start():
            a.start()
            b.start()

        def cross_over():
            a.wait()
            held[...] = (gr_s[far, rows_at, :].astype(f32) + in1[0].astype(f32)).astype(bf16)
            c.start()

        def result():
            b.wait()
            c.wait()
            mine = gr_s[t, rows_at, :].astype(f32) + in1[1].astype(f32)
            return (mine + in2[...].astype(f32)).astype(bf16)

        return start, cross_over, result

    g_start, g_cross, g_result = tensor_sum(pl.ds(0, grows), gin1, gin2, 0)
    g_start()

    r = routec[t]
    prob0, prob1, rlow = gates_of(
        mixed[...], r[:, 0:1], r[:, 1:2], pick, rw[...], rd[...], ru[...]
    )
    g_cross()

    def softmax_of(qm, k):
        s = jnp.where(key_ok, dot_nt(qm, k) * HEAD_DIM**-0.5, -jnp.inf)
        ex = jnp.exp(s - jnp.max(s, axis=1, keepdims=True))
        return ex / jnp.sum(ex, axis=1, keepdims=True)

    def back_wait(d, carry):
        for h in range(chunks):
            grad_copy(d, h).wait()
        return carry

    lax.fori_loop(1, ne, back_wait, 0)
    lax.fori_loop(1, ne, res_start, 0)
    for copy in locals_:
        copy.wait()
    for copy in mix_far + mix_near + mix_relay:
        copy.wait_send()
    if not roomy:
        load = pltpu.make_async_copy(back, got, here.at[0])
        load.start()
        load.wait()
    rows_back = back if roomy else got
    slots = n * block
    grad_s, gg_s, tok_s = cot_pad, gall, mall

    def hot(q):
        s = iota((1, slots), 1)
        c = slotc[q]
        return ((c[:, 0:1] == s) | (c[:, 1:2] == s)).astype(f32).astype(bf16)

    def grad_tokens(q):
        grad_s[q] = dot(hot(q), rows_back[...].reshape(slots, width)).astype(bf16)

    def gate_tokens(q):
        sc = iota((slots, 1), 0)
        gg_s[q] = jnp.zeros(gg_s.shape[1:], f32)
        for k in range(TOP):
            gg_s[q, k : k + 1, :] = jnp.sum(
                jnp.where(slotr[q, k : k + 1, :] == sc, gate_s[0:slots, :], 0.0), axis=0, keepdims=True
            )

    stages = ((grad_s, tin1, keep_g, tin2), (gg_s, tin1k, keep_k, tin2k))
    first = {}
    for i, (src, dst, _, _) in enumerate(stages):
        if i == 1:
            for d in range(n):
                gr = rows_back[d, block - 2 : block - 1, 0:block].astype(f32)
                gr = gr + rows_back[d, block - 1 : block, 0:block].astype(f32)
                gate_s[d * block : (d + 1) * block, :] = to_col(gr)
        for j, q in enumerate((cross, near)):
            (grad_tokens, gate_tokens)[i](q)
            k = 3 * i + j
            first[i, j] = remote(src.at[q], dst.at[j], usend.at[k], urecv.at[k], (e, near))
            first[i, j].start()
        (grad_tokens, gate_tokens)[i](far)
    second = []
    for i, (src, one, held, two) in enumerate(stages):
        first[i, 0].wait()
        held[...] = (src[far].astype(f32) + one[0].astype(f32)).astype(held.dtype)
        copy = remote(held, two, usend.at[3 * i + 2], urecv.at[3 * i + 2], (e, far))
        copy.start()
        second.append(copy)
    grad_tokens(t)
    gate_tokens(t)
    ebuf[...] = g_result()
    e_first = sum_copy(ne, ebuf, eparts, esend, erecv)
    start_all(ne, e_first)
    unit2, scale2 = norm_stats(middle[...])
    sums = []
    for i, (src, one, _, two) in enumerate(stages):
        first[i, 1].wait()
        mine = src[t].astype(f32) + one[1].astype(f32)
        second[i].wait()
        sums.append(mine + two[...].astype(f32))
    gmix, ggate = sums
    gg0 = to_col(ggate[0:1, :])
    gg1 = to_col(ggate[1:2, :])
    inner = prob0 * gg0 + prob1 * gg1
    lane = iota((1, rw.shape[0]), 1)
    glog = jnp.where(r[:, 0:1] == lane, prob0 * (gg0 - inner), 0.0) + jnp.where(
        r[:, 1:2] == lane, prob1 * (gg1 - inner), 0.0
    )
    llow = dot_fine(glog, ru[...]) * pick
    gm = gmix + dot_fine(glog, rw[...]) + dot_nt_fine(llow, rd[...])
    router_up = dot_tn(glog.astype(bf16), rlow.astype(bf16))
    router_down = dot_tn(mixed[...], llow.astype(bf16))
    gmid = cot_own[...].astype(f32) + norm_back(gm, gain2[...], unit2, scale2)
    mid_at, in_at = pl.ds(0, rows), pl.ds(rows, rows)
    acc_s[mid_at, :] = gmid
    gbranch = gmid.astype(bf16)
    project_up = dot_tn(plow[...], gbranch)
    blow = (dot_nt(gbranch, pup[...]) * pick).astype(bf16)
    for p in range(nt):
        ga_s[p] = (dot_nt(gbranch, pw[p]) + dot_nt(blow, pd[p])).astype(bf16)

    for q in range(nt):
        off = la
        at = slice(q * share, (q + 1) * share)
        for c in range(width // 128):
            gr_s[q, off : off + share, :] = project_up[at, c * 128 : (c + 1) * 128].astype(bf16)
            off += share
        at = slice(q * quarter, (q + 1) * quarter)
        gr_s[q, off : off + quarter, :] = router_down[at].astype(bf16)
        off += quarter
        gr_s[q, off : la + lb - lw, :] = jnp.zeros((la + lb - lw - off, 128), bf16)
        gr_s[q, la + lb - lw : la + lb, :] = dot_tn(attended[q], blow).astype(bf16)
    off = la + ADAPT + quarter
    gr_s[0, off : off + experts, :] = router_up.astype(bf16)
    b_start, b_cross, b_result = tensor_sum(pl.ds(la, lb), bin1, bin2, 3)
    b_start()
    b_first = sum_copy(ne, bbuf, bparts, b2send, b2recv)

    acc_s[in_at, :] = jnp.zeros((rows, width), f32)
    back_low[...] = jnp.zeros_like(back_low)

    def piece_back(p, carry):
        for li in range(per):
            at = pl.ds(li * seqp, seqp)
            q = triple[p, at, 0:lw]
            k = triple[p, at, lw : 2 * lw]
            v = triple[p, at, 2 * lw : 3 * lw]
            ga = ga_s[p, at, :]
            gq = jnp.zeros((seqp, lw), f32)
            gk = jnp.zeros((seqp, lw), f32)
            gv = jnp.zeros((seqp, lw), f32)
            for h in range(lw // HEAD_DIM):
                on = head_of == h
                qm = jnp.where(on, q, 0.0).astype(bf16)
                km = jnp.where(on, k, 0.0).astype(bf16)
                gam = jnp.where(on, ga, 0.0).astype(bf16)
                probs = softmax_of(qm, k)
                gp = dot_nt(gam, v)
                ds = (probs * (gp - jnp.sum(probs * gp, axis=1, keepdims=True))).astype(bf16)
                gq = gq + dot(ds, km)
                gk = gk + dot_tn(ds, qm)
                gv = gv + dot_tn(probs.astype(bf16), gam)
            gt_s[at, 0:lw] = (gq * HEAD_DIM**-0.5).astype(bf16)
            gt_s[at, lw : 2 * lw] = (gk * HEAD_DIM**-0.5).astype(bf16)
            gt_s[at, 2 * lw : 3 * lw] = gv.astype(bf16)
        gt = gt_s[...]
        back_low[...] += dot_nt(gt, tup[p])
        acc_s[in_at, :] += dot_nt(gt, wt[p])
        tu = dot_tn(tlow[...], gt)
        for c in range(3 * lw // 128):
            gr_s[p, c * 128 : (c + 1) * 128, :] = tu[:, c * 128 : (c + 1) * 128].astype(bf16)

        @pl.when(p == 0)
        def _():
            b_cross()

        @pl.when(p == 2)
        def _():
            bbuf[...] = b_result()
            start_all(ne, b_first)

        return carry

    lax.fori_loop(0, nt, piece_back, 0)

    tglow = (back_low[...] * pick).astype(bf16)
    triple_down = dot_tn(attn_in[...], tglow)
    for q in range(nt):
        off = 3 * lw
        gr_s[q, off : off + quarter, :] = triple_down[q * quarter : (q + 1) * quarter].astype(bf16)
        if off + quarter < la:
            gr_s[q, off + quarter : la, :] = jnp.zeros((la - off - quarter, 128), bf16)
    a_start, a_cross, a_result = tensor_sum(pl.ds(0, la), ain1, ain2, 6)
    a_start()
    gin = acc_s[in_at, :] + dot_nt(tglow, tdn[...])
    a_cross()
    unit1, scale1 = norm_stats(xs[...])
    attn_in[...] = (acc_s[mid_at, :] + norm_back(gin, gain1[...], unit1, scale1)).astype(bf16)

    def share_out(j, src, k):
        return [
            remote(src, outs.at[t, j], osend.at[k], orecv.at[k], (e, far)),
            remote(src, outs.at[t, j], osend.at[k + 1], orecv.at[k + 1], (e, near)),
            remote(outs.at[far, j], outs.at[far, j], osend.at[k + 2], orecv.at[k + 2], (e, near)),
            pltpu.make_async_copy(src, outs.at[t, j], here.at[1 + j]),
        ]

    def share_rows(buf, k):
        return [
            remote(buf.at[t], buf.at[t], osend.at[k], orecv.at[k], (e, far)),
            remote(buf.at[t], buf.at[t], osend.at[k + 1], orecv.at[k + 1], (e, near)),
            remote(buf.at[far], buf.at[far], osend.at[k + 2], orecv.at[k + 2], (e, near)),
        ]

    igrad_out = share_out(1, attn_in, 0)
    for i in (0, 1, 3):
        igrad_out[i].start()
    def res_wait(d, carry):
        res_copy(d).wait()
        return carry

    lax.fori_loop(1, ne, res_wait, 0)
    if not roomy:
        load = pltpu.make_async_copy(got_res, got_cot, here.at[0])
        load.start()
        load.wait()
    res_rows = got_res if roomy else got_cot

    def res_tokens(q):
        tok_s[q] = dot(hot(q), res_rows[...].reshape(slots, width)).astype(bf16)

    res_first = []
    for j, q in enumerate((cross, near)):
        res_tokens(q)
        res_first.append(remote(tok_s.at[q], tin1r.at[j], usend.at[6 + j], urecv.at[6 + j], (e, near)))
        res_first[-1].start()
    res_tokens(far)
    res_first[0].wait()
    keep_g[...] = (tok_s[far].astype(f32) + tin1r[0].astype(f32)).astype(bf16)
    res_second = remote(keep_g, tin2r, usend.at[8], urecv.at[8], (e, far))
    res_second.start()
    res_tokens(t)
    abuf = keep.at[pl.ds(la, la)]
    abuf[...] = a_result()
    a_first = sum_copy(ne, abuf, aparts, asend, arecv)
    start_all(ne, a_first)
    e_second = sum_share(ne, e_first, ebuf, eparts, etot, esend, erecv)
    b_second = sum_share(ne, b_first, bbuf, bparts, btot, b2send, b2recv)
    a_second = sum_share(ne, a_first, abuf, aparts, atot, asend, arecv)
    wait_all(ne, e_second)
    wait_all(ne, b_second)
    ra = grows - held_e
    rep_e[t, 0:ra, :] = etot[held_e:grows, :]
    rep_e[t, ra:, :] = btot[0 : lb - lw, :]
    rep_out = share_rows(rep_e, 6)
    for i in (0, 1):
        rep_out[i].start()
    wait_all(ne, a_second)
    rep_a[t] = atot[3 * lw : 3 * lw + quarter, :]
    last_out = share_rows(rep_a, 9)
    for i in (0, 1):
        last_out[i].start()
    res_first[1].wait()
    res_second.wait()
    mixed[...] = (
        middle[...] + (tok_s[t].astype(f32) + tin1r[1].astype(f32)) + tin2r[...].astype(f32)
    ).astype(bf16)
    block_out = share_out(0, mixed, 3)
    for i in (0, 1, 3):
        block_out[i].start()
    igrad_out[0].wait_recv()
    igrad_out[2].start()
    for group in (block_out, rep_out, last_out):
        group[0].wait_recv()
        group[2].start()
    for group in (igrad_out, block_out, rep_out, last_out):
        group[0].wait_send()
        for copy in group[1:]:
            copy.wait()
    for copy in fars + relays + big_far + big_relay:
        copy.wait_send()


def write_kernel(
    dims, e_all, b_all, a_all, outs, rep_e, rep_a, block_output, input_grad, triple_down, triple_up, project_down,
    project_up, router_down, router_up, first_down, first_up, second_down, second_up,
):
    nt, seq, seqp, images, ffq, lw, grows = dims
    per = images // nt
    tok, width = block_output.shape
    flat = outs.shape[2]
    for j, out in enumerate((block_output, input_grad)):
        for a in range(0, tok, seqp):
            b = min(a + seqp, tok)
            i0, i1 = a // seq, (b - 1) // seq
            parts = []
            for i in range(i0, i1 + 1):
                row = iota((b - a, seqp), 0) + a
                sel = (iota((b - a, seqp), 1) == row - i * seq) & (row < (i + 1) * seq)
                src = outs[i // per, j, (i % per) * seqp : (i % per + 1) * seqp, :]
                parts.append(dot(sel.astype(f32).astype(bf16), src))
            whole_part = parts[0]
            for part in parts[1:]:
                whole_part = whole_part + part
            out[a:b, :] = whole_part.astype(bf16)
    for c in range(ffq // 128):
        first_up[:, c * 128 : (c + 1) * 128] = e_all[c * 128 : (c + 1) * 128].astype(f32)
    second_down[...] = e_all[ffq : 2 * ffq].astype(f32)
    for c in range(3):
        triple_up[c] = a_all[c * lw : (c + 1) * lw].astype(f32)
    last = b_all.shape[0]
    project_down[...] = b_all[last - lw : last].astype(f32)
    quarter = width // nt
    share = ADAPT // nt
    for q in range(nt):
        at = slice(q * quarter, (q + 1) * quarter)
        up_at = slice(q * share, (q + 1) * share)
        triple_down[at, :] = rep_a[q].astype(f32)
        first_down[at, :] = rep_e[q, 0:quarter, :].astype(f32)
        off = quarter
        for c in range(width // 128):
            second_up[up_at, c * 128 : (c + 1) * 128] = rep_e[q, off : off + share, :].astype(f32)
            off += share
        off = grows - 2 * ffq
        for c in range(width // 128):
            project_up[up_at, c * 128 : (c + 1) * 128] = rep_e[q, off : off + share, :].astype(f32)
            off += share
        router_down[at, :] = rep_e[q, off : off + quarter, :].astype(f32)
        off += quarter
    router_up[...] = rep_e[0, off : off + router_up.shape[0], :].astype(f32)


def body(
    inputs, gain_attend, triple_weight, project_weight, gain_mixture, router_weight, expert_first,
    expert_second, triple_down, triple_up, project_down, project_up, router_down, router_up,
    first_down, first_up, second_down, second_up, adapter_index, routes, priority, cotangent,
):
    ne = lax.axis_size("expert")
    nt = lax.axis_size("tensor")
    tok, width = inputs.shape
    images = adapter_index.shape[0]
    seq = tok // images
    seqp = up(seq, 16)
    per = images // nt
    rows = per * seqp
    experts = router_weight.shape[1]
    local = expert_first.shape[0]
    ffq = expert_first.shape[2]
    lw = triple_weight.shape[2]
    cap = nt * ((5 * tok * TOP + 4 * nt * experts - 1) // (4 * nt * experts))
    used = cap * local // nt
    chunks = 2
    block = up(used + 4, 16 * chunks)
    cp = block // chunks
    smem = pl.BlockSpec(memory_space=pltpu.SMEM)
    anywhere = pl.BlockSpec(memory_space=pl.ANY)
    shape = jax.ShapeDtypeStruct
    wide = up(2 * experts, 128)
    gain1 = gain_attend.reshape(1, width)
    gain2 = gain_mixture.reshape(1, width)
    rw = router_weight.T
    ru = router_up.T
    big = (expert_first, expert_second, first_up, second_down)
    n_w = 8
    erows = ne * cp
    quarter = width // nt
    held_e = 2 * ffq
    grows = up(held_e + quarter + (ADAPT // nt) * (width // 128), 16 * ne)
    one = (rows, width)
    small = (8, rows)
    la = up(3 * lw + quarter, 16 * ne)
    lb = up(ADAPT + quarter + experts + lw, 16 * ne)
    re = grows + lb - lw - held_e
    n_big = len(big)
    slots = (ne, block, width)
    roomy = ne * block <= 1024
    spare = slots if roomy else (8, 128)
    finals = pl.pallas_call(
        functools.partial(
            block_kernel,
            (nt, ne, seq, seqp, images, experts, cap, chunks, cp, held_e, grows, la, lb, roomy),
        ),
        out_shape=[
            shape((grows, 128), bf16),
            shape((lb, 128), bf16),
            shape((la, 128), bf16),
            shape((nt, 2) + one, bf16),
            shape((nt, re, 128), bf16),
            shape((nt, quarter, 128), bf16),
            shape((8, 128) if roomy else slots, bf16),
            shape((8, 128) if roomy else slots, bf16),
        ],
        in_specs=[smem] + whole(2) + [anywhere] * 2 + whole(13) + [anywhere] * 4,
        out_specs=whole(3) + [anywhere] + whole(2) + [anywhere] * 2,
        scratch_shapes=[
            VMEM((nt, rows, TOP), i32),
            VMEM((nt, TOP, rows), i32),
            VMEM((nt, rows, TOP), i32),
            VMEM(one, f32),
            VMEM(one, bf16),
            VMEM(one, bf16),
            VMEM(one, f32),
            VMEM((nt, rows, 3 * lw), bf16),
            VMEM((nt, rows, lw), bf16),
            VMEM((rows, ADAPT), bf16),
            VMEM((rows, ADAPT), bf16),
            VMEM(one, bf16),
            VMEM((nt, width, 3 * lw), bf16),
            VMEM((nt, ADAPT, 3 * lw), bf16),
            VMEM((nt, lw, width), bf16),
            VMEM((nt, lw, ADAPT), bf16),
            VMEM(slots, bf16),
            VMEM(slots, bf16),
            VMEM((nt,) + one, bf16),
            VMEM((images * seqp, wide), bf16),
            VMEM(slots, bf16),
            VMEM((nt,) + one, bf16),
            VMEM((nt,) + small, f32),
            VMEM((max(ne * block, 2 * erows, 2 * rows), width), f32),
            VMEM((max(ne * block, images * seqp), 1), f32),
            VMEM(slots, bf16),
            VMEM((nt, width, ffq), bf16),
            VMEM((nt, ffq, width), bf16),
            VMEM((nt, ADAPT, ffq), bf16),
            VMEM((nt, ffq, ADAPT), bf16),
            VMEM((erows, width), bf16),
            VMEM((erows, width), bf16),
            VMEM((2, erows, ADAPT), bf16),
            VMEM((ne, block, 2), f32),
            VMEM((ne, block), f32),
            VMEM((2, erows, ADAPT), f32),
            VMEM((ADAPT, width), f32),
            VMEM((nt, ADAPT, ffq), f32),
            VMEM((nt, ADAPT, ffq), f32),
            VMEM((ADAPT, width), f32),
            VMEM((nt, max(grows, la + lb), 128), bf16),
            VMEM((2, grows, 128), bf16),
            VMEM((max(grows, la + lb, 2 * la), 128), bf16),
            VMEM((grows, 128), bf16),
            VMEM((tok, width), bf16),
            VMEM((tok, width) if roomy else (8, 128), bf16),
            VMEM(spare, bf16),
            VMEM(spare, bf16),
            VMEM((2,) + one, bf16),
            VMEM((2,) + small, f32),
            VMEM((2,) + one, bf16),
            VMEM(one, bf16),
            VMEM(small, f32),
            VMEM(one, bf16),
            VMEM(small, f32),
            VMEM(one, bf16),
            VMEM((2, lb, 128), bf16),
            VMEM((lb, 128), bf16),
            VMEM((2, la, 128), bf16),
            VMEM((la, 128), bf16),
            VMEM((ne - 1, grows // ne, 128), bf16),
            VMEM((ne - 1, lb // ne, 128), bf16),
            VMEM((ne - 1, la // ne, 128), bf16),
            VMEM((rows, 3 * lw), bf16),
            VMEM((nt, rows, lw), bf16),
            VMEM((rows, ADAPT), f32),
            dma(3 * n_w),
            dma(3 * n_w),
            dma(3 * n_big),
            dma(3 * n_big),
            dma(ne),
            dma(ne),
            dma(6),
            dma(6),
            dma(chunks * ne),
            dma(chunks * ne),
            dma(chunks * ne),
            dma(chunks * ne),
            dma(ne),
            dma(ne),
            dma(9),
            dma(9),
            dma(9),
            dma(9),
            dma(2 * ne),
            dma(2 * ne),
            dma(2 * ne),
            dma(2 * ne),
            dma(2 * ne),
            dma(2 * ne),
            dma(12),
            dma(12),
            dma(3),
            dma(n_w),
            dma(n_big + 2),
            dma(2),
        ],
        compiler_params=pltpu.CompilerParams(
            collective_id=0, has_side_effects=True, vmem_limit_bytes=67000000
        ),
        name="block",
    )(
        adapter_index, priority, routes.T, cotangent, inputs, gain1, gain2,
        triple_weight.transpose(1, 0, 2), triple_up.transpose(1, 0, 2), project_weight,
        project_down, triple_down, project_up, rw, router_down, ru, first_down, second_up, *big,
    )

    outs = pl.pallas_call(
        functools.partial(write_kernel, (nt, seq, seqp, images, ffq, lw, grows)),
        out_shape=[
            shape((tok, width), bf16),
            shape((tok, width), bf16),
            shape((width, ADAPT), f32),
            shape((3, ADAPT, lw), f32),
            shape((lw, ADAPT), f32),
            shape((ADAPT, width), f32),
            shape((width, ADAPT), f32),
            shape((experts, ADAPT), f32),
            shape((width, ADAPT), f32),
            shape((ADAPT, ffq), f32),
            shape((ffq, ADAPT), f32),
            shape((ADAPT, width), f32),
        ],
        in_specs=whole(6),
        out_specs=whole(12),
        name="write",
    )(*finals[:6])
    outs = list(outs)
    outs[3] = outs[3].transpose(1, 0, 2)
    outs[7] = outs[7].T
    return tuple(outs)


def solution(mesh):
    return jax.shard_map(
        body,
        mesh=mesh,
        in_specs=(
            P("expert", None),
            P(),
            P(None, None, "tensor"),
            P("tensor", None),
            P(),
            P(),
            P("expert", None, "tensor"),
            P("expert", "tensor", None),
            P(),
            P(None, None, "tensor"),
            P("tensor", None),
            P(),
            P(),
            P(),
            P(),
            P(None, "tensor"),
            P("tensor", None),
            P(),
            P("expert"),
            P("expert", None),
            P("expert", None),
            P("expert", None),
        ),
        out_specs=(
            P("expert", None),
            P("expert", None),
            P(),
            P(None, None, "tensor"),
            P("tensor", None),
            P(),
            P(),
            P(),
            P(),
            P(None, "tensor"),
            P("tensor", None),
            P(),
        ),
        check_vma=False,
    )
```

```python
import functools

import jax
import jax.numpy as jnp
from jax import lax
from jax.experimental import pallas as pl
from jax.experimental.pallas import tpu as pltpu
from jax.sharding import PartitionSpec as P

HEAD_DIM = 64
TOP = 2
ADAPTERS = 8
RANK = 16
ADAPT = ADAPTERS * RANK
EPS = 1e-06

f32 = jnp.float32
bf16 = jnp.bfloat16
i32 = jnp.int32
MESH = pl.DeviceIdType.MESH
VMEM = pltpu.VMEM


def up(a, b):
    return -(-a // b) * b


def dot(a, b):
    return lax.dot_general(a, b, (((1,), (0,)), ((), ())), preferred_element_type=f32)


def dot_nt(a, b):
    return lax.dot_general(a, b, (((1,), (1,)), ((), ())), preferred_element_type=f32)


def dot_tn(a, b):
    return lax.dot_general(a, b, (((0,), (0,)), ((), ())), preferred_element_type=f32)


def split_high_low(a):
    high = a.astype(bf16)
    return high, (a - high.astype(f32)).astype(bf16)


def dot_fine(a, b):
    high, low = split_high_low(a)
    return dot(high, b) + dot(low, b)


def dot_nt_fine(a, b):
    high, low = split_high_low(a)
    return dot_nt(high, b) + dot_nt(low, b)


def iota(shape, axis):
    return lax.broadcasted_iota(i32, shape, axis)


def to_row(col):
    n = col.shape[0]
    return jnp.sum(jnp.where(iota((n, n), 0) == iota((n, n), 1), col, 0.0), axis=0, keepdims=True)


def to_col(row):
    n = row.shape[1]
    return jnp.sum(jnp.where(iota((n, n), 0) == iota((n, n), 1), row, 0.0), axis=1, keepdims=True)


def picks_of(adapters, base, per, seqp):
    lane = iota((seqp, ADAPT), 1) // RANK
    return jnp.concatenate(
        [(lane == adapters[base + li]).astype(f32) for li in range(per)], axis=0
    )


def whole(count):
    return [pl.BlockSpec(memory_space=VMEM) for _ in range(count)]


def norm_stats(x):
    centre = jnp.mean(x, axis=-1, keepdims=True)
    shifted = x - centre
    scale = lax.rsqrt(jnp.mean(shifted * shifted, axis=-1, keepdims=True) + EPS)
    return shifted * scale, scale


def norm_back(grad, gain, unit, scale):
    g = grad * gain
    return scale * (
        g - jnp.mean(g, axis=-1, keepdims=True) - unit * jnp.mean(g * unit, axis=-1, keepdims=True)
    )


def greet(peers):
    barrier = pltpu.get_barrier_semaphore()
    for peer in peers:
        pl.semaphore_signal(barrier, 1, device_id=peer, device_id_type=MESH)
    pl.semaphore_wait(barrier, len(peers))


def remote(src, dst, send, recv, peer):
    return pltpu.make_async_remote_copy(
        src_ref=src, dst_ref=dst, send_sem=send, recv_sem=recv, device_id=peer, device_id_type=MESH
    )


def where_am_i():
    e = lax.axis_index("expert")
    t = lax.axis_index("tensor")
    return e, t, jnp.bitwise_xor(t, 1), jnp.bitwise_xor(t, 2), jnp.bitwise_xor(t, 3)


def dma(n):
    return pltpu.SemaphoreType.DMA((n,))


def linked(ident):
    return pltpu.CompilerParams(collective_id=ident, has_side_effects=True)


def gates_of(mixed, r0, r1, pick, rw, rd, ru):
    low = dot(mixed, rd) * pick
    logits = dot_nt(mixed, rw) + dot_nt_fine(low, ru)
    lane = iota((1, rw.shape[0]), 1)
    first = jnp.sum(jnp.where(r0 == lane, logits, 0.0), axis=1, keepdims=True)
    second = jnp.sum(jnp.where(r1 == lane, logits, 0.0), axis=1, keepdims=True)
    top = jnp.maximum(first, second)
    a = jnp.exp(first - top)
    b = jnp.exp(second - top)
    return a / (a + b), b / (a + b), low


def own_images(ref, first, per, seq, seqp, put):
    tok = ref.shape[0]
    for li in range(per):
        row = iota((seqp, tok), 0)
        sel = (iota((seqp, tok), 1) == row + (first + li) * seq) & (row < seq)
        put(pl.ds(li * seqp, seqp), dot(sel.astype(f32).astype(bf16), ref[...]))


def erf_parts(pre):
    cdf = 0.5 * (1.0 + lax.erf(pre * 0.7071067811865476))
    return pre * cdf, cdf + pre * (jnp.exp(-0.5 * pre * pre) * 0.3989422804014327)


def chunk_of(ref, ne, p):
    size = ref.shape[0] // ne
    return pl.ds(pl.multiple_of(p * size, size), size)


def sum_copy(ne, src, parts, send, recv):
    e, t = where_am_i()[:2]

    def copy(d):
        p = lax.rem(e + d, ne)
        return remote(src.at[chunk_of(src, ne, p)], parts.at[d - 1], send.at[d], recv.at[d], (p, t))

    return copy


def start_all(ne, copy):
    def start(d, carry):
        copy(d).start()
        return carry

    lax.fori_loop(1, ne, start, 0)


def sum_share(ne, copy, src, parts, total, send, recv):
    e, t = where_am_i()[:2]
    mine = chunk_of(src, ne, e)

    def add(d, acc):
        copy(d).wait()
        return acc + parts[d - 1].astype(f32)

    total[mine, :] = lax.fori_loop(1, ne, add, src[mine, :].astype(f32)).astype(bf16)

    def share(d):
        p = lax.rem(e + d, ne)
        return remote(total.at[mine], total.at[mine], send.at[ne + d], recv.at[ne + d], (p, t))

    def start(d, carry):
        share(d).start()
        return carry

    lax.fori_loop(1, ne, start, 0)
    return share


def wait_all(ne, copy):
    def wait(d, carry):
        copy(d).wait()
        return carry

    lax.fori_loop(1, ne, wait, 0)


def block_kernel(
    dims, adapters, prio, routes, cot_in, x_in, gain1, gain2, wt_in, tup_in, pw_in, pd_in,
    tdn, pup, rw, rd, ru, fdn, sup, w1_in, w2_in, fup_in, sdn_in,
    etot, btot, atot, outs, rep_e, rep_a, back_out, res_out, *rest,
):
    nt, ne, seq, seqp, images, experts, cap, chunks, cp, held_e, grows, la, lb, roomy = dims
    (
        slotc, slotr, routec, xs, cot_own, mixed, middle, triple, attended, tlow, plow, attn_in,
        wt, tup, pw, pd, got, got_cot, cot_pad, one_s, cots, mall, gall, acc_s, gate_s, out_s,
        w1, w2, fup, sdn, sent_s, sg_s, low_s, gcol_s, gg_rows, acc_low,
        acc_fd, acc_fu, acc_sd, acc_su, gr_s, gin1, keep, gin2, cot, x_own,
        back_s, res_s, tin1, tin1k, tin1r, keep_g, keep_k, tin2, tin2k, tin2r,
        bin1, bin2, ain1, ain2, eparts, bparts, aparts, gt_s, ga_s, back_low, rank_r,
        wsend, wrecv, bsend, brecv, csend, crecv, tsend, trecv, send, recv, gsend, grecv, rsend, rrecv,
        ssend, srecv, usend, urecv, esend, erecv, b2send, b2recv, asend, arecv, osend, orecv,
        here, own_sem, load_sem, ret_sem,
    ) = rest
    back = back_s if roomy else back_out
    ebuf, bbuf = gin1.at[0], bin1.at[0]
    got_res = res_s if roomy else res_out
    e, t, near, far, cross = where_am_i()
    lw = pw_in.shape[0]
    width = x_in.shape[1]
    local = w1_in.shape[0]
    parts = nt // local
    n_out, block = cots.shape[0], cots.shape[1]
    peers = [(e, far), (e, near)] + [(lax.rem(e + d, ne), t) for d in range(1, ne)]
    barrier = pltpu.get_barrier_semaphore()
    for peer in peers:
        pl.semaphore_signal(barrier, 1, device_id=peer, device_id_type=MESH)

    def big_ref(k, to):
        return (fup_in, sdn_in)[k] if k < 2 else (w1_in, w2_in)[k - 2].at[lax.div(to, parts)]

    big = (fup, sdn, w1, w2)
    n_big = len(big)
    big_own = [
        pltpu.make_async_copy(big_ref(k, t), big[k].at[t], load_sem.at[k]) for k in range(n_big)
    ]
    big_far = [
        remote(big_ref(k, far), big[k].at[t], bsend.at[3 * k], brecv.at[3 * k], (e, far))
        for k in range(n_big)
    ]
    big_near = [
        remote(big_ref(k, near), big[k].at[t], bsend.at[3 * k + 1], brecv.at[3 * k + 1], (e, near))
        for k in range(n_big)
    ]
    big_relay = [
        remote(big[k].at[far], big[k].at[far], bsend.at[3 * k + 2], brecv.at[3 * k + 2], (e, near))
        for k in range(n_big)
    ]
    load_cot = pltpu.make_async_copy(cot_in, cot, load_sem.at[n_big])
    x_ref = x_own if roomy else cot
    load_x = pltpu.make_async_copy(x_in, x_ref, load_sem.at[n_big + 1])
    for copy in [load_cot] + big_own:
        copy.start()
    if roomy:
        load_x.start()

    moves = []
    for c in range(3):
        lanes = pl.ds(c * lw, lw)
        moves.append((wt_in.at[c], lambda q, lanes=lanes: wt.at[q, :, lanes]))
        moves.append((tup_in.at[c], lambda q, lanes=lanes: tup.at[q, :, lanes]))
    moves.append((pw_in, lambda q: pw.at[q]))
    moves.append((pd_in, lambda q: pd.at[q]))
    n_w = len(moves)
    fars = [
        remote(src, at(t), wsend.at[3 * i], wrecv.at[3 * i], (e, far))
        for i, (src, at) in enumerate(moves)
    ]
    nears = [
        remote(src, at(t), wsend.at[3 * i + 1], wrecv.at[3 * i + 1], (e, near))
        for i, (src, at) in enumerate(moves)
    ]
    relays = [
        remote(at(far), at(far), wsend.at[3 * i + 2], wrecv.at[3 * i + 2], (e, near))
        for i, (src, at) in enumerate(moves)
    ]
    owns = [
        pltpu.make_async_copy(src, at(t), own_sem.at[i]) for i, (src, at) in enumerate(moves)
    ]
    for copy in owns:
        copy.start()

    tok = prio.shape[1]
    per = images // nt
    rows = per * seqp
    total = nt * rows
    wide = one_s.shape[-1]
    order = iota((seqp, tok), 1).astype(f32)
    lane = iota((seqp, wide), 1)
    for i in range(images):
        if i == images // 2:
            pl.semaphore_wait(barrier, len(peers))
            for copy in fars + nears:
                copy.start()
        q, at = i // per, pl.ds(i % per * seqp, seqp)
        all_at = pl.ds(i * seqp, seqp)
        token = iota((seqp, 1), 0) + i * seq
        gate_s[all_at, :] = jnp.sum(
            jnp.where(prio[...] == token, order, 0.0), axis=1, keepdims=True
        )
        lane0 = i * seq // 128 * 128
        lane1 = min(lane0 + up(seq + 128, 128), tok)
        here_i = (iota((seqp, lane1 - lane0), 1) + lane0 == token) & (iota((seqp, lane1 - lane0), 0) < seq)
        r = [
            jnp.sum(
                jnp.where(here_i, routes[k : k + 1, lane0:lane1].astype(f32) + 1.0, 0.0),
                axis=1,
                keepdims=True,
            ).astype(i32)
            - 1
            for k in range(TOP)
        ]
        for k in range(TOP):
            routec[q, at, k : k + 1] = r[k]
        named = jnp.where(lane < experts, r[0], jnp.where(r[1] < 0, -1, r[1] + experts))
        one_s[all_at, :] = (named == lane).astype(f32).astype(bf16)
    totals = dot(jnp.ones((8, total), bf16), one_s[...])[0:1]
    for q in range(nt):
        rank_r[q : q + 1, :] = to_row(gate_s[pl.ds(q * rows, rows), :])
    lane = iota((rows, wide), 1)

    def slots_of(q, carry):
        at = pl.ds(pl.multiple_of(q * rows, 16), rows)
        mine = gate_s[at, :]
        counts = jnp.zeros((rows, wide), f32)
        for p in range(nt):
            before = (rank_r[p : p + 1, :] < mine).astype(f32).astype(bf16)
            counts = counts + dot(before, one_s[pl.ds(p * rows, rows), :])
        hot = one_s[at, :].astype(f32) * counts
        first = jnp.sum(jnp.where(lane < experts, hot, 0.0), axis=1, keepdims=True)
        second = jnp.sum(
            jnp.where(lane < experts, 0.0, hot)
            + jnp.where((lane < experts) & (routec[q, :, 1:2] == lane), totals, 0.0),
            axis=1,
            keepdims=True,
        )
        for k, pos in ((0, first), (1, second)):
            named = routec[q, :, k : k + 1]
            place = pos.astype(i32)
            kept = (named >= 0) & (place < cap)
            kept = kept & (lax.rem(named, local) == lax.div(t, parts))
            kept = kept & (lax.rem(place, parts) == lax.rem(t, parts))
            index = lax.div(place, parts)
            index = jnp.where(index < cp - 2, index, index + 2)
            slot = jnp.where(kept, lax.div(named, local) * block + index, -1)
            slotc[q, :, k : k + 1] = slot
            slotr[q, k : k + 1, :] = to_row(slot.astype(f32)).astype(i32)
        return carry

    lax.fori_loop(0, nt, slots_of, 0)

    load_cot.wait()
    for i in range(images):
        start = i * seq // 16 * 16
        stop = min(start + up(seq, 16) + 16, tok)
        src = iota((seqp, stop - start), 1) + start
        row = iota((seqp, stop - start), 0)
        sel = ((src == row + i * seq) & (row < seq)).astype(f32).astype(bf16)
        cot_pad[i // per, pl.ds(i % per * seqp, seqp), :] = dot(sel, cot[start:stop, :]).astype(bf16)
    step = max(1, 512 // block)
    image_of = iota((1, rows), 1) // seqp

    def pack(d, carry):
        s = iota((step * block, 1), 0) + d * (step * block)
        acc = jnp.zeros((step * block, width), f32)
        idc = jnp.zeros((step * block, 1), f32)
        for q in range(nt):
            ids = jnp.zeros((1, rows), f32)
            for li in range(per):
                ids = jnp.where(image_of == li, adapters[q * per + li].astype(f32), ids)
            g = (slotr[q, 0:1, :] == s) | (slotr[q, 1:2, :] == s)
            idc = idc + jnp.sum(jnp.where(g, ids, 0.0), axis=1, keepdims=True)
            acc = acc + dot(g.astype(f32).astype(bf16), cot_pad[q])
        row = iota((block, block), 0)
        for b in range(step):
            part = acc[b * block : (b + 1) * block]
            idr = to_row(idc[b * block : (b + 1) * block])
            head = jnp.where(row == cp - 2, idr, part[:, 0:block])
            cots[d * step + b, :, 0:block] = head.astype(bf16)
            cots[d * step + b, :, block:] = part[:, block:].astype(bf16)
        return carry

    lax.fori_loop(0, n_out // step, pack, 0)

    def cot_copy(d):
        p = lax.rem(e + d, ne)
        return remote(cots.at[p], got_cot.at[e], csend.at[d], crecv.at[d], (p, t))

    def cot_start(d, carry):
        cot_copy(d).start()
        return carry

    lax.fori_loop(1, ne, cot_start, 0)
    own_cot = pltpu.make_async_copy(cots.at[e], got_cot.at[e], here.at[0])
    own_cot.start()

    def put_x(at, value):
        xs[at, :] = value

    def put_cot(at, value):
        cot_own[at, :] = value.astype(bf16)

    if not roomy:
        own_images(cot, t * per, per, seq, seqp, put_cot)
        load_x.start()
    load_x.wait()
    own_images(x_ref, t * per, per, seq, seqp, put_x)
    pick = picks_of(adapters, t * per, per, seqp)
    unit, _ = norm_stats(xs[...])
    normed = (unit * gain1[...]).astype(bf16)
    attn_in[...] = normed
    low = (dot(normed, tdn[...]) * pick).astype(bf16)
    tlow[...] = low
    head_of = iota((1, lw), 1) // HEAD_DIM
    key_ok = iota((1, seqp), 1) < seq

    def piece(m, carry):
        p = jnp.bitwise_xor(t, m)

        @pl.when(m == 0)
        def _():
            for copy in owns:
                copy.wait()

        @pl.when(m == 1)
        def _():
            for copy in nears:
                copy.wait()

        @pl.when(m == 2)
        def _():
            for i in range(6):
                fars[i].wait_recv()
                relays[i].start()

        @pl.when(m == 3)
        def _():
            for i in range(6):
                relays[i].wait_recv()

        triple[p] = (dot(attn_in[...], wt[p]) + dot(tlow[...], tup[p])).astype(bf16)
        for li in range(per):
            at = pl.ds(li * seqp, seqp)
            q = triple[p, at, 0:lw]
            k = triple[p, at, lw : 2 * lw]
            v = triple[p, at, 2 * lw : 3 * lw]
            acc = jnp.zeros((seqp, lw), f32)
            for h in range(lw // HEAD_DIM):
                on = head_of == h
                s = dot_nt(jnp.where(on, q, 0.0).astype(bf16), k) * HEAD_DIM**-0.5
                s = jnp.where(key_ok, s, -jnp.inf)
                ex = jnp.exp(s - jnp.max(s, axis=1, keepdims=True))
                probs = (ex / jnp.sum(ex, axis=1, keepdims=True)).astype(bf16)
                acc = acc + dot(probs, jnp.where(on, v, 0.0).astype(bf16))
            attended[p, at, :] = acc.astype(bf16)
        return carry

    lax.fori_loop(0, nt, piece, 0)
    for copy in big_near:
        copy.start()
    for i in range(6, n_w):
        fars[i].wait_recv()
        relays[i].start()
    for i in range(6, n_w):
        relays[i].wait_recv()
    psum = jnp.zeros((rows, ADAPT), f32)
    branch = jnp.zeros((rows, width), f32)
    for p in range(nt):
        psum = psum + dot(attended[p], pd[p])
        branch = branch + dot(attended[p], pw[p])
    low2 = (psum * pick).astype(bf16)
    plow[...] = low2
    mid = xs[...] + branch + dot(low2, pup[...])
    middle[...] = mid
    unit2, _ = norm_stats(mid)
    mix = (unit2 * gain2[...]).astype(bf16)
    mixed[...] = mix
    mall[t] = mix

    mix_far = [
        remote(buf.at[t], buf.at[t], tsend.at[i], trecv.at[i], (e, far))
        for i, buf in enumerate((mall, gall))
    ]
    mix_near = [
        remote(buf.at[t], buf.at[t], tsend.at[2 + i], trecv.at[2 + i], (e, near))
        for i, buf in enumerate((mall, gall))
    ]
    mix_relay = [
        remote(buf.at[far], buf.at[far], tsend.at[4 + i], trecv.at[4 + i], (e, near))
        for i, buf in enumerate((mall, gall))
    ]
    mix_far[0].start()
    mix_near[0].start()
    r = routec[t]
    a, b, _ = gates_of(mix, r[:, 0:1], r[:, 1:2], pick, rw[...], rd[...], ru[...])
    gall[t] = jnp.zeros(gall.shape[1:], f32)
    gall[t, 0:1, :] = to_row(a)
    gall[t, 1:2, :] = to_row(b)
    for copy in [mix_far[1], mix_near[1]] + big_far:
        copy.start()
    step = max(1, 512 // block)

    def gather_rows(q, s):
        g0 = slotr[q, 0:1, :] == s
        g1 = slotr[q, 1:2, :] == s
        gate = jnp.sum(
            jnp.where(g0, gall[q, 0:1, :], jnp.where(g1, gall[q, 1:2, :], 0.0)), axis=1, keepdims=True
        )
        return dot((g0 | g1).astype(f32).astype(bf16), mall[q]), gate

    def add_quarter(q, fresh):
        def some(d, carry):
            at = pl.ds(pl.multiple_of(d * (step * block), step * block), step * block)
            s = iota((step * block, 1), 0) + d * (step * block)
            part, gate = gather_rows(q, s)
            acc_s[at, :] = part if fresh else acc_s[at, :] + part
            gate_s[at, :] = gate if fresh else gate_s[at, :] + gate
            return carry

        lax.fori_loop(0, n_out // step, some, 0)

    add_quarter(t, True)
    for copy in mix_near:
        copy.wait_recv()
    add_quarter(near, False)
    if roomy:
        own_images(cot, t * per, per, seq, seqp, put_cot)
    for copy in mix_far:
        copy.wait_recv()
    for copy in mix_relay:
        copy.start()
    add_quarter(far, False)
    for copy in mix_relay:
        copy.wait_recv()

    def finish(p):
        at = pl.ds(pl.multiple_of(p * block, block), block)
        part, gate = gather_rows(cross, iota((block, 1), 0) + p * block)
        part = acc_s[at, :] + part
        gate = to_row(gate_s[at, :] + gate)
        high = gate.astype(bf16).astype(f32)
        row = iota((block, block), 0)
        head = jnp.where(row == cp - 2, high, part[:, 0:block])
        head = jnp.where(row == cp - 1, gate - high, head)
        return head.astype(bf16), part[:, block:].astype(bf16)

    def chunk(h):
        return pl.ds(pl.multiple_of(h * cp, cp), cp)

    def out_copy(d, h):
        p = lax.rem(e + d, ne)
        k = d * chunks + h
        return remote(out_s.at[p, chunk(h)], got.at[e, chunk(h)], send.at[k], recv.at[k], (p, t))

    def send_one(d, carry):
        p = lax.rem(e + d, ne)
        head, tail = finish(p)
        out_s[p, :, 0:block] = head
        out_s[p, :, block:] = tail
        out_copy(d, 0).start()
        return carry

    lax.fori_loop(1, ne, send_one, 0)

    for h in range(1, chunks):

        def send_more(d, carry, h=h):
            out_copy(d, h).start()
            return carry

        lax.fori_loop(1, ne, send_more, 0)
    head, tail = finish(e)
    got[e, :, 0:block] = head
    got[e, :, block:] = tail

    n = ne
    erows = n * cp
    row_at = lax.rem(iota((erows, 1), 0), cp)
    res_at, gsent_at = pl.ds(0, erows), pl.ds(erows, erows)
    for buf in (acc_fd, acc_fu, acc_sd, acc_su):
        buf[...] = jnp.zeros_like(buf)
    for copy in big_own + big_near:
        copy.wait()

    def cot_wait(d, carry):
        cot_copy(d).wait()
        return carry

    lax.fori_loop(1, ne, cot_wait, 0)
    own_cot.wait()

    def grad_copy(d, h):
        p = lax.rem(e + d, ne)
        k = d * chunks + h
        return remote(cots.at[p, chunk(h)], back.at[e, chunk(h)], gsend.at[k], grecv.at[k], (p, t))

    def res_copy(d):
        p = lax.rem(e + d, ne)
        return remote(out_s.at[p], got_res.at[e], rsend.at[d], rrecv.at[d], (p, t))

    def experts_chunk(h, carry):
        at = chunk(h)

        def rows_wait(d, carry):
            out_copy(d, h).wait_recv()
            return carry

        lax.fori_loop(1, ne, rows_wait, 0)

        @pl.when(h == 0)
        def _():
            diag = iota((block, block), 0) == iota((block, block), 1)

            def headers(m, carry):
                idr = got_cot[m, cp - 2 : cp - 1, 0:block].astype(f32)
                gr = got[m, cp - 2 : cp - 1, 0:block].astype(f32) + got[
                    m, cp - 1 : cp, 0:block
                ].astype(f32)
                gcol_s[m, :, 0:1] = jnp.sum(jnp.where(diag, idr, 0.0), axis=1, keepdims=True)
                gcol_s[m, :, 1:2] = jnp.sum(jnp.where(diag, gr, 0.0), axis=1, keepdims=True)
                return carry

            lax.fori_loop(0, n, headers, 0)

        spare = jnp.where((h == 0) | (h == chunks - 1), cp - 2, cp)
        real = row_at < spare
        cols = gcol_s[:, at, :].reshape(erows, 2)
        sent = jnp.where(real, got[:, at, :].reshape(erows, width).astype(f32), 0.0).astype(bf16)
        cotf = jnp.where(real, got_cot[:, at, :].reshape(erows, width).astype(f32), 0.0)
        pick_e = (cols[:, 0:1] == (iota((1, ADAPT), 1) // RANK).astype(f32)).astype(f32)
        sent_s[...] = sent
        sgrad = (cols[:, 1:2] * cotf).astype(bf16)
        sg_s[...] = sgrad
        low_s[0] = (dot(sent, fdn[...]) * pick_e).astype(bf16)
        low_s[1] = (dot_nt(sgrad, sup[...]) * pick_e).astype(bf16)
        acc_low[...] = jnp.zeros_like(acc_low)
        acc_s[pl.ds(0, 2 * erows), :] = jnp.zeros((2 * erows, width), f32)

        def through(m, carry):
            c = jnp.bitwise_xor(t, m)

            @pl.when((h == 0) & (m == 2))
            def _():
                for far_copy, relay in zip(big_far, big_relay):
                    far_copy.wait_recv()
                    relay.start()

            @pl.when((h == 0) & (m == 3))
            def _():
                for relay in big_relay:
                    relay.wait_recv()

            span = min(erows, 512)
            for r0 in range(0, erows, span):
                rs = slice(r0, r0 + span)
                gs = slice(erows + r0, erows + r0 + span)
                pre = dot(sent_s[rs, :], w1[c]) + dot(low_s[0, rs, :], fup[c])
                act, slope = erf_parts(pre)
                hid = act.astype(bf16)
                acc_low[0, rs, :] += dot(hid, sdn[c])
                acc_s[rs, :] += dot(hid, w2[c])
                ghid = dot_nt(sg_s[rs, :], w2[c]) + dot_nt(low_s[1, rs, :], sdn[c])
                gpre = (ghid * slope).astype(bf16)
                acc_fu[c] += dot_tn(low_s[0, rs, :], gpre)
                acc_sd[c] += dot_tn(low_s[1, rs, :], hid)
                acc_low[1, rs, :] += dot_nt(gpre, fup[c])
                acc_s[gs, :] += dot_nt(gpre, w1[c])
            return carry

        lax.fori_loop(0, nt, through, 0)

        def sent_wait(d, carry):
            out_copy(d, h).wait_send()
            return carry

        lax.fori_loop(1, ne, sent_wait, 0)
        cols = gcol_s[:, at, :].reshape(erows, 2)
        pick_e = (cols[:, 0:1] == (iota((1, ADAPT), 1) // RANK).astype(f32)).astype(f32)
        second_low = (acc_low[0] * pick_e).astype(bf16)
        res = (acc_s[res_at, :] + dot(second_low, sup[...])).astype(bf16).astype(f32)
        cotf = got_cot[:, at, :].reshape(erows, width).astype(f32)
        acc_low[0, :, 0:1] = jnp.sum(res * cotf, axis=1, keepdims=True)
        g1low = (acc_low[1] * pick_e).astype(bf16)
        gsent = acc_s[gsent_at, :] + dot_nt(g1low, fdn[...])
        cots[:, at, :] = gsent.astype(bf16).reshape(n, cp, width)
        diag = iota((cp, block), 0) + h * cp == iota((cp, block), 1)

        def footers(m, carry):
            gg = jnp.sum(
                jnp.where(diag, acc_low[0, pl.ds(pl.multiple_of(m * cp, cp), cp), 0:1], 0.0),
                axis=0,
                keepdims=True,
            )
            total = jnp.where(h == 0, gg, gg_rows[pl.ds(m, 1), :] + gg)
            gg_rows[pl.ds(m, 1), :] = total

            @pl.when(h == chunks - 1)
            def _():
                high = total.astype(bf16).astype(f32)
                row = iota((16, block), 0)
                to = pl.ds(block - 16, 16)
                old = cots[m, to, 0:block].astype(f32)
                old = jnp.where(row == 14, high, jnp.where(row == 15, total - high, old))
                cots[m, to, 0:block] = old.astype(bf16)

            return carry

        lax.fori_loop(0, n, footers, 0)

        def grad_start(d, carry):
            grad_copy(d, h).start()
            return carry

        lax.fori_loop(1, ne, grad_start, 0)
        out_s[:, at, :] = (cols[:, 1:2] * res).astype(bf16).reshape(n, cp, width)
        acc_su[...] += dot_tn(second_low, sg_s[...])
        acc_fd[...] += dot_tn(g1low, sent_s[...])
        return carry

    gg_rows[...] = jnp.zeros_like(gg_rows)
    lax.fori_loop(0, chunks, experts_chunk, 0)
    locals_ = [
        pltpu.make_async_copy(cots.at[e], back.at[e], ret_sem.at[0]),
        pltpu.make_async_copy(out_s.at[e], got_res.at[e], ret_sem.at[1]),
    ]
    for copy in locals_:
        copy.start()

    def res_start(d, carry):
        res_copy(d).start()
        return carry

    ffq = w1.shape[2]
    quarter = width // nt
    share = ADAPT // nt
    for q in range(nt):
        off = 0
        for c in range(ffq // 128):
            gr_s[q, off : off + 128, :] = acc_fu[q, :, c * 128 : (c + 1) * 128].astype(bf16)
            off += 128
        gr_s[q, off : off + ffq, :] = acc_sd[q].T.astype(bf16)
        off += ffq
        gr_s[q, off : off + quarter, :] = acc_fd[:, q * quarter : (q + 1) * quarter].T.astype(bf16)
        off += quarter
        for c in range(width // 128):
            at = slice(q * share, (q + 1) * share)
            gr_s[q, off : off + share, :] = acc_su[at, c * 128 : (c + 1) * 128].astype(bf16)
            off += share
        if off < grows:
            gr_s[q, off:grows, :] = jnp.zeros((grows - off, 128), bf16)

    def tensor_sum(rows_at, in1, in2, k):
        a = remote(gr_s.at[cross, rows_at], in1.at[0], ssend.at[k], srecv.at[k], (e, near))
        b = remote(gr_s.at[near, rows_at], in1.at[1], ssend.at[k + 1], srecv.at[k + 1], (e, near))
        held = keep.at[rows_at]
        c = remote(held, in2, ssend.at[k + 2], srecv.at[k + 2], (e, far))

        def start():
            a.start()
            b.start()

        def cross_over():
            a.wait()
            held[...] = (gr_s[far, rows_at, :].astype(f32) + in1[0].astype(f32)).astype(bf16)
            c.start()

        def result():
            b.wait()
            c.wait()
            mine = gr_s[t, rows_at, :].astype(f32) + in1[1].astype(f32)
            return (mine + in2[...].astype(f32)).astype(bf16)

        return start, cross_over, result

    g_start, g_cross, g_result = tensor_sum(pl.ds(0, grows), gin1, gin2, 0)
    g_start()

    r = routec[t]
    prob0, prob1, rlow = gates_of(
        mixed[...], r[:, 0:1], r[:, 1:2], pick, rw[...], rd[...], ru[...]
    )
    g_cross()

    def softmax_of(qm, k):
        s = jnp.where(key_ok, dot_nt(qm, k) * HEAD_DIM**-0.5, -jnp.inf)
        ex = jnp.exp(s - jnp.max(s, axis=1, keepdims=True))
        return ex / jnp.sum(ex, axis=1, keepdims=True)

    def back_wait(d, carry):
        for h in range(chunks):
            grad_copy(d, h).wait()
        return carry

    lax.fori_loop(1, ne, back_wait, 0)
    lax.fori_loop(1, ne, res_start, 0)
    for copy in locals_:
        copy.wait()
    for copy in mix_far + mix_near + mix_relay:
        copy.wait_send()
    if not roomy:
        load = pltpu.make_async_copy(back, got, here.at[0])
        load.start()
        load.wait()
    rows_back = back if roomy else got
    slots = n * block
    grad_s, gg_s, tok_s = cot_pad, gall, mall

    def hot(q):
        s = iota((1, slots), 1)
        c = slotc[q]
        return ((c[:, 0:1] == s) | (c[:, 1:2] == s)).astype(f32).astype(bf16)

    def grad_tokens(q):
        grad_s[q] = dot(hot(q), rows_back[...].reshape(slots, width)).astype(bf16)

    def gate_tokens(q):
        sc = iota((slots, 1), 0)
        gg_s[q] = jnp.zeros(gg_s.shape[1:], f32)
        for k in range(TOP):
            gg_s[q, k : k + 1, :] = jnp.sum(
                jnp.where(slotr[q, k : k + 1, :] == sc, gate_s[0:slots, :], 0.0), axis=0, keepdims=True
            )

    stages = ((grad_s, tin1, keep_g, tin2), (gg_s, tin1k, keep_k, tin2k))
    first = {}
    for i, (src, dst, _, _) in enumerate(stages):
        if i == 1:


            def read_gates(d, carry):
                gr = rows_back[d, block - 2 : block - 1, 0:block].astype(f32)
                gr = gr + rows_back[d, block - 1 : block, 0:block].astype(f32)
                gate_s[pl.ds(pl.multiple_of(d * block, block), block), :] = to_col(gr)
                return carry

            lax.fori_loop(0, n, read_gates, 0)
        for j, q in enumerate((cross, near)):
            (grad_tokens, gate_tokens)[i](q)
            k = 3 * i + j
            first[i, j] = remote(src.at[q], dst.at[j], usend.at[k], urecv.at[k], (e, near))
            first[i, j].start()
        (grad_tokens, gate_tokens)[i](far)
    second = []
    for i, (src, one, held, two) in enumerate(stages):
        first[i, 0].wait()
        held[...] = (src[far].astype(f32) + one[0].astype(f32)).astype(held.dtype)
        copy = remote(held, two, usend.at[3 * i + 2], urecv.at[3 * i + 2], (e, far))
        copy.start()
        second.append(copy)
    grad_tokens(t)
    gate_tokens(t)
    ebuf[...] = g_result()
    e_first = sum_copy(ne, ebuf, eparts, esend, erecv)
    start_all(ne, e_first)
    unit2, scale2 = norm_stats(middle[...])
    sums = []
    for i, (src, one, _, two) in enumerate(stages):
        first[i, 1].wait()
        mine = src[t].astype(f32) + one[1].astype(f32)
        second[i].wait()
        sums.append(mine + two[...].astype(f32))
    gmix, ggate = sums
    gg0 = to_col(ggate[0:1, :])
    gg1 = to_col(ggate[1:2, :])
    inner = prob0 * gg0 + prob1 * gg1
    lane = iota((1, rw.shape[0]), 1)
    glog = jnp.where(r[:, 0:1] == lane, prob0 * (gg0 - inner), 0.0) + jnp.where(
        r[:, 1:2] == lane, prob1 * (gg1 - inner), 0.0
    )
    llow = dot_fine(glog, ru[...]) * pick
    gm = gmix + dot_fine(glog, rw[...]) + dot_nt_fine(llow, rd[...])
    router_up = dot_tn(glog.astype(bf16), rlow.astype(bf16))
    router_down = dot_tn(mixed[...], llow.astype(bf16))
    gmid = cot_own[...].astype(f32) + norm_back(gm, gain2[...], unit2, scale2)
    mid_at, in_at = pl.ds(0, rows), pl.ds(rows, rows)
    acc_s[mid_at, :] = gmid
    gbranch = gmid.astype(bf16)
    project_up = dot_tn(plow[...], gbranch)
    blow = (dot_nt(gbranch, pup[...]) * pick).astype(bf16)
    for p in range(nt):
        ga_s[p] = (dot_nt(gbranch, pw[p]) + dot_nt(blow, pd[p])).astype(bf16)

    for q in range(nt):
        off = la
        at = slice(q * share, (q + 1) * share)
        for c in range(width // 128):
            gr_s[q, off : off + share, :] = project_up[at, c * 128 : (c + 1) * 128].astype(bf16)
            off += share
        at = slice(q * quarter, (q + 1) * quarter)
        gr_s[q, off : off + quarter, :] = router_down[at].astype(bf16)
        off += quarter
        gr_s[q, off : la + lb - lw, :] = jnp.zeros((la + lb - lw - off, 128), bf16)
        gr_s[q, la + lb - lw : la + lb, :] = dot_tn(attended[q], blow).astype(bf16)
    off = la + ADAPT + quarter
    gr_s[0, off : off + experts, :] = router_up.astype(bf16)
    b_start, b_cross, b_result = tensor_sum(pl.ds(la, lb), bin1, bin2, 3)
    b_start()
    b_first = sum_copy(ne, bbuf, bparts, b2send, b2recv)

    acc_s[in_at, :] = jnp.zeros((rows, width), f32)
    back_low[...] = jnp.zeros_like(back_low)

    def piece_back(p, carry):
        for li in range(per):
            at = pl.ds(li * seqp, seqp)
            q = triple[p, at, 0:lw]
            k = triple[p, at, lw : 2 * lw]
            v = triple[p, at, 2 * lw : 3 * lw]
            ga = ga_s[p, at, :]
            gq = jnp.zeros((seqp, lw), f32)
            gk = jnp.zeros((seqp, lw), f32)
            gv = jnp.zeros((seqp, lw), f32)
            for h in range(lw // HEAD_DIM):
                on = head_of == h
                qm = jnp.where(on, q, 0.0).astype(bf16)
                km = jnp.where(on, k, 0.0).astype(bf16)
                gam = jnp.where(on, ga, 0.0).astype(bf16)
                probs = softmax_of(qm, k)
                gp = dot_nt(gam, v)
                ds = (probs * (gp - jnp.sum(probs * gp, axis=1, keepdims=True))).astype(bf16)
                gq = gq + dot(ds, km)
                gk = gk + dot_tn(ds, qm)
                gv = gv + dot_tn(probs.astype(bf16), gam)
            gt_s[at, 0:lw] = (gq * HEAD_DIM**-0.5).astype(bf16)
            gt_s[at, lw : 2 * lw] = (gk * HEAD_DIM**-0.5).astype(bf16)
            gt_s[at, 2 * lw : 3 * lw] = gv.astype(bf16)
        gt = gt_s[...]
        back_low[...] += dot_nt(gt, tup[p])
        acc_s[in_at, :] += dot_nt(gt, wt[p])
        tu = dot_tn(tlow[...], gt)
        for c in range(3 * lw // 128):
            gr_s[p, c * 128 : (c + 1) * 128, :] = tu[:, c * 128 : (c + 1) * 128].astype(bf16)

        @pl.when(p == 0)
        def _():
            b_cross()

        @pl.when(p == 2)
        def _():
            bbuf[...] = b_result()
            start_all(ne, b_first)

        return carry

    lax.fori_loop(0, nt, piece_back, 0)

    tglow = (back_low[...] * pick).astype(bf16)
    triple_down = dot_tn(attn_in[...], tglow)
    for q in range(nt):
        off = 3 * lw
        gr_s[q, off : off + quarter, :] = triple_down[q * quarter : (q + 1) * quarter].astype(bf16)
        if off + quarter < la:
            gr_s[q, off + quarter : la, :] = jnp.zeros((la - off - quarter, 128), bf16)
    a_start, a_cross, a_result = tensor_sum(pl.ds(0, la), ain1, ain2, 6)
    a_start()
    gin = acc_s[in_at, :] + dot_nt(tglow, tdn[...])
    a_cross()
    unit1, scale1 = norm_stats(xs[...])
    attn_in[...] = (acc_s[mid_at, :] + norm_back(gin, gain1[...], unit1, scale1)).astype(bf16)

    def share_out(j, src, k):
        return [
            remote(src, outs.at[t, j], osend.at[k], orecv.at[k], (e, far)),
            remote(src, outs.at[t, j], osend.at[k + 1], orecv.at[k + 1], (e, near)),
            remote(outs.at[far, j], outs.at[far, j], osend.at[k + 2], orecv.at[k + 2], (e, near)),
            pltpu.make_async_copy(src, outs.at[t, j], here.at[1 + j]),
        ]

    def share_rows(buf, k):
        return [
            remote(buf.at[t], buf.at[t], osend.at[k], orecv.at[k], (e, far)),
            remote(buf.at[t], buf.at[t], osend.at[k + 1], orecv.at[k + 1], (e, near)),
            remote(buf.at[far], buf.at[far], osend.at[k + 2], orecv.at[k + 2], (e, near)),
        ]

    igrad_out = share_out(1, attn_in, 0)
    for i in (0, 1, 3):
        igrad_out[i].start()
    def res_wait(d, carry):
        res_copy(d).wait()
        return carry

    lax.fori_loop(1, ne, res_wait, 0)
    if not roomy:
        load = pltpu.make_async_copy(got_res, got_cot, here.at[0])
        load.start()
        load.wait()
    res_rows = got_res if roomy else got_cot

    def res_tokens(q):
        tok_s[q] = dot(hot(q), res_rows[...].reshape(slots, width)).astype(bf16)

    res_first = []
    for j, q in enumerate((cross, near)):
        res_tokens(q)
        res_first.append(remote(tok_s.at[q], tin1r.at[j], usend.at[6 + j], urecv.at[6 + j], (e, near)))
        res_first[-1].start()
    res_tokens(far)
    res_first[0].wait()
    keep_g[...] = (tok_s[far].astype(f32) + tin1r[0].astype(f32)).astype(bf16)
    res_second = remote(keep_g, tin2r, usend.at[8], urecv.at[8], (e, far))
    res_second.start()
    res_tokens(t)
    abuf = keep.at[pl.ds(la, la)]
    abuf[...] = a_result()
    a_first = sum_copy(ne, abuf, aparts, asend, arecv)
    start_all(ne, a_first)
    e_second = sum_share(ne, e_first, ebuf, eparts, etot, esend, erecv)
    b_second = sum_share(ne, b_first, bbuf, bparts, btot, b2send, b2recv)
    a_second = sum_share(ne, a_first, abuf, aparts, atot, asend, arecv)
    wait_all(ne, e_second)
    wait_all(ne, b_second)
    ra = grows - held_e
    rep_e[t, 0:ra, :] = etot[held_e:grows, :]
    rep_e[t, ra:, :] = btot[0 : lb - lw, :]
    rep_out = share_rows(rep_e, 6)
    for i in (0, 1):
        rep_out[i].start()
    wait_all(ne, a_second)
    rep_a[t] = atot[3 * lw : 3 * lw + quarter, :]
    last_out = share_rows(rep_a, 9)
    for i in (0, 1):
        last_out[i].start()
    res_first[1].wait()
    res_second.wait()
    mixed[...] = (
        middle[...] + (tok_s[t].astype(f32) + tin1r[1].astype(f32)) + tin2r[...].astype(f32)
    ).astype(bf16)
    block_out = share_out(0, mixed, 3)
    for i in (0, 1, 3):
        block_out[i].start()
    igrad_out[0].wait_recv()
    igrad_out[2].start()
    for group in (block_out, rep_out, last_out):
        group[0].wait_recv()
        group[2].start()
    for group in (igrad_out, block_out, rep_out, last_out):
        group[0].wait_send()
        for copy in group[1:]:
            copy.wait()
    for copy in fars + relays + big_far + big_relay:
        copy.wait_send()


def write_kernel(
    dims, e_all, b_all, a_all, outs, rep_e, rep_a, block_output, input_grad, triple_down, triple_up, project_down,
    project_up, router_down, router_up, first_down, first_up, second_down, second_up,
):
    nt, seq, seqp, images, ffq, lw, grows = dims
    per = images // nt
    tok, width = block_output.shape
    flat = outs.shape[2]
    for j, out in enumerate((block_output, input_grad)):
        for a in range(0, tok, seqp):
            b = min(a + seqp, tok)
            i0, i1 = a // seq, (b - 1) // seq
            parts = []
            for i in range(i0, i1 + 1):
                row = iota((b - a, seqp), 0) + a
                sel = (iota((b - a, seqp), 1) == row - i * seq) & (row < (i + 1) * seq)
                src = outs[i // per, j, (i % per) * seqp : (i % per + 1) * seqp, :]
                parts.append(dot(sel.astype(f32).astype(bf16), src))
            whole_part = parts[0]
            for part in parts[1:]:
                whole_part = whole_part + part
            out[a:b, :] = whole_part.astype(bf16)
    for c in range(ffq // 128):
        first_up[:, c * 128 : (c + 1) * 128] = e_all[c * 128 : (c + 1) * 128].astype(f32)
    second_down[...] = e_all[ffq : 2 * ffq].astype(f32)
    for c in range(3):
        triple_up[c] = a_all[c * lw : (c + 1) * lw].astype(f32)
    last = b_all.shape[0]
    project_down[...] = b_all[last - lw : last].astype(f32)
    quarter = width // nt
    share = ADAPT // nt
    for q in range(nt):
        at = slice(q * quarter, (q + 1) * quarter)
        up_at = slice(q * share, (q + 1) * share)
        triple_down[at, :] = rep_a[q].astype(f32)
        first_down[at, :] = rep_e[q, 0:quarter, :].astype(f32)
        off = quarter
        for c in range(width // 128):
            second_up[up_at, c * 128 : (c + 1) * 128] = rep_e[q, off : off + share, :].astype(f32)
            off += share
        off = grows - 2 * ffq
        for c in range(width // 128):
            project_up[up_at, c * 128 : (c + 1) * 128] = rep_e[q, off : off + share, :].astype(f32)
            off += share
        router_down[at, :] = rep_e[q, off : off + quarter, :].astype(f32)
        off += quarter
    router_up[...] = rep_e[0, off : off + router_up.shape[0], :].astype(f32)


def body(
    inputs, gain_attend, triple_weight, project_weight, gain_mixture, router_weight, expert_first,
    expert_second, triple_down, triple_up, project_down, project_up, router_down, router_up,
    first_down, first_up, second_down, second_up, adapter_index, routes, priority, cotangent,
):
    ne = lax.axis_size("expert")
    nt = lax.axis_size("tensor")
    tok, width = inputs.shape
    images = adapter_index.shape[0]
    seq = tok // images
    seqp = up(seq, 16)
    per = images // nt
    rows = per * seqp
    experts = router_weight.shape[1]
    local = expert_first.shape[0]
    ffq = expert_first.shape[2]
    lw = triple_weight.shape[2]
    cap = nt * ((5 * tok * TOP + 4 * nt * experts - 1) // (4 * nt * experts))
    used = cap * local // nt
    chunks = 2
    block = up(used + 4, 16 * chunks)
    cp = block // chunks
    smem = pl.BlockSpec(memory_space=pltpu.SMEM)
    anywhere = pl.BlockSpec(memory_space=pl.ANY)
    shape = jax.ShapeDtypeStruct
    wide = up(2 * experts, 128)
    gain1 = gain_attend.reshape(1, width)
    gain2 = gain_mixture.reshape(1, width)
    rw = router_weight.T
    ru = router_up.T
    big = (expert_first, expert_second, first_up, second_down)
    n_w = 8
    erows = ne * cp
    quarter = width // nt
    held_e = 2 * ffq
    grows = up(held_e + quarter + (ADAPT // nt) * (width // 128), 16 * ne)
    one = (rows, width)
    small = (8, rows)
    la = up(3 * lw + quarter, 16 * ne)
    lb = up(ADAPT + quarter + experts + lw, 16 * ne)
    re = grows + lb - lw - held_e
    n_big = len(big)
    slots = (ne, block, width)
    roomy = ne * block <= 1024
    spare = slots if roomy else (8, 128)
    finals = pl.pallas_call(
        functools.partial(
            block_kernel,
            (nt, ne, seq, seqp, images, experts, cap, chunks, cp, held_e, grows, la, lb, roomy),
        ),
        out_shape=[
            shape((grows, 128), bf16),
            shape((lb, 128), bf16),
            shape((la, 128), bf16),
            shape((nt, 2) + one, bf16),
            shape((nt, re, 128), bf16),
            shape((nt, quarter, 128), bf16),
            shape((8, 128) if roomy else slots, bf16),
            shape((8, 128) if roomy else slots, bf16),
        ],
        in_specs=[smem] + whole(2) + [anywhere] * 2 + whole(13) + [anywhere] * 4,
        out_specs=whole(3) + [anywhere] + whole(2) + [anywhere] * 2,
        scratch_shapes=[
            VMEM((nt, rows, TOP), i32),
            VMEM((nt, TOP, rows), i32),
            VMEM((nt, rows, TOP), i32),
            VMEM(one, f32),
            VMEM(one, bf16),
            VMEM(one, bf16),
            VMEM(one, f32),
            VMEM((nt, rows, 3 * lw), bf16),
            VMEM((nt, rows, lw), bf16),
            VMEM((rows, ADAPT), bf16),
            VMEM((rows, ADAPT), bf16),
            VMEM(one, bf16),
            VMEM((nt, width, 3 * lw), bf16),
            VMEM((nt, ADAPT, 3 * lw), bf16),
            VMEM((nt, lw, width), bf16),
            VMEM((nt, lw, ADAPT), bf16),
            VMEM(slots, bf16),
            VMEM(slots, bf16),
            VMEM((nt,) + one, bf16),
            VMEM((images * seqp, wide), bf16),
            VMEM(slots, bf16),
            VMEM((nt,) + one, bf16),
            VMEM((nt,) + small, f32),
            VMEM((max(ne * block, 2 * erows, 2 * rows), width), f32),
            VMEM((max(ne * block, images * seqp), 1), f32),
            VMEM(slots, bf16),
            VMEM((nt, width, ffq), bf16),
            VMEM((nt, ffq, width), bf16),
            VMEM((nt, ADAPT, ffq), bf16),
            VMEM((nt, ffq, ADAPT), bf16),
            VMEM((erows, width), bf16),
            VMEM((erows, width), bf16),
            VMEM((2, erows, ADAPT), bf16),
            VMEM((ne, block, 2), f32),
            VMEM((ne, block), f32),
            VMEM((2, erows, ADAPT), f32),
            VMEM((ADAPT, width), f32),
            VMEM((nt, ADAPT, ffq), f32),
            VMEM((nt, ADAPT, ffq), f32),
            VMEM((ADAPT, width), f32),
            VMEM((nt, max(grows, la + lb), 128), bf16),
            VMEM((2, grows, 128), bf16),
            VMEM((max(grows, la + lb, 2 * la), 128), bf16),
            VMEM((grows, 128), bf16),
            VMEM((tok, width), bf16),
            VMEM((tok, width) if roomy else (8, 128), bf16),
            VMEM(spare, bf16),
            VMEM(spare, bf16),
            VMEM((2,) + one, bf16),
            VMEM((2,) + small, f32),
            VMEM((2,) + one, bf16),
            VMEM(one, bf16),
            VMEM(small, f32),
            VMEM(one, bf16),
            VMEM(small, f32),
            VMEM(one, bf16),
            VMEM((2, lb, 128), bf16),
            VMEM((lb, 128), bf16),
            VMEM((2, la, 128), bf16),
            VMEM((la, 128), bf16),
            VMEM((ne - 1, grows // ne, 128), bf16),
            VMEM((ne - 1, lb // ne, 128), bf16),
            VMEM((ne - 1, la // ne, 128), bf16),
            VMEM((rows, 3 * lw), bf16),
            VMEM((nt, rows, lw), bf16),
            VMEM((rows, ADAPT), f32),
            VMEM((nt, rows), f32),
            dma(3 * n_w),
            dma(3 * n_w),
            dma(3 * n_big),
            dma(3 * n_big),
            dma(ne),
            dma(ne),
            dma(6),
            dma(6),
            dma(chunks * ne),
            dma(chunks * ne),
            dma(chunks * ne),
            dma(chunks * ne),
            dma(ne),
            dma(ne),
            dma(9),
            dma(9),
            dma(9),
            dma(9),
            dma(2 * ne),
            dma(2 * ne),
            dma(2 * ne),
            dma(2 * ne),
            dma(2 * ne),
            dma(2 * ne),
            dma(12),
            dma(12),
            dma(3),
            dma(n_w),
            dma(n_big + 2),
            dma(2),
        ],
        compiler_params=pltpu.CompilerParams(
            collective_id=0, has_side_effects=True, vmem_limit_bytes=67000000
        ),
        name="block",
    )(
        adapter_index, priority, routes.T, cotangent, inputs, gain1, gain2,
        triple_weight.transpose(1, 0, 2), triple_up.transpose(1, 0, 2), project_weight,
        project_down, triple_down, project_up, rw, router_down, ru, first_down, second_up, *big,
    )

    outs = pl.pallas_call(
        functools.partial(write_kernel, (nt, seq, seqp, images, ffq, lw, grows)),
        out_shape=[
            shape((tok, width), bf16),
            shape((tok, width), bf16),
            shape((width, ADAPT), f32),
            shape((3, ADAPT, lw), f32),
            shape((lw, ADAPT), f32),
            shape((ADAPT, width), f32),
            shape((width, ADAPT), f32),
            shape((experts, ADAPT), f32),
            shape((width, ADAPT), f32),
            shape((ADAPT, ffq), f32),
            shape((ffq, ADAPT), f32),
            shape((ADAPT, width), f32),
        ],
        in_specs=whole(6),
        out_specs=whole(12),
        name="write",
    )(*finals[:6])
    outs = list(outs)
    outs[3] = outs[3].transpose(1, 0, 2)
    outs[7] = outs[7].T
    return tuple(outs)


def solution(mesh):
    return jax.shard_map(
        body,
        mesh=mesh,
        in_specs=(
            P("expert", None),
            P(),
            P(None, None, "tensor"),
            P("tensor", None),
            P(),
            P(),
            P("expert", None, "tensor"),
            P("expert", "tensor", None),
            P(),
            P(None, None, "tensor"),
            P("tensor", None),
            P(),
            P(),
            P(),
            P(),
            P(None, "tensor"),
            P("tensor", None),
            P(),
            P("expert"),
            P("expert", None),
            P("expert", None),
            P("expert", None),
        ),
        out_specs=(
            P("expert", None),
            P("expert", None),
            P(),
            P(None, None, "tensor"),
            P("tensor", None),
            P(),
            P(),
            P(),
            P(),
            P(None, "tensor"),
            P("tensor", None),
            P(),
        ),
        check_vma=False,
    )
```

```python
import functools

import jax
import jax.numpy as jnp
from jax import lax
from jax.experimental import pallas as pl
from jax.experimental.pallas import tpu as pltpu
from jax.sharding import PartitionSpec as P

HEAD_DIM = 64
TOP = 2
ADAPTERS = 8
RANK = 16
ADAPT = ADAPTERS * RANK
EPS = 1e-06

f32 = jnp.float32
bf16 = jnp.bfloat16
i32 = jnp.int32
MESH = pl.DeviceIdType.MESH
VMEM = pltpu.VMEM


def up(a, b):
    return -(-a // b) * b


def dot(a, b):
    return lax.dot_general(a, b, (((1,), (0,)), ((), ())), preferred_element_type=f32)


def dot_nt(a, b):
    return lax.dot_general(a, b, (((1,), (1,)), ((), ())), preferred_element_type=f32)


def dot_tn(a, b):
    return lax.dot_general(a, b, (((0,), (0,)), ((), ())), preferred_element_type=f32)


def split_high_low(a):
    high = a.astype(bf16)
    return high, (a - high.astype(f32)).astype(bf16)


def dot_fine(a, b):
    high, low = split_high_low(a)
    return dot(high, b) + dot(low, b)


def dot_nt_fine(a, b):
    high, low = split_high_low(a)
    return dot_nt(high, b) + dot_nt(low, b)


def iota(shape, axis):
    return lax.broadcasted_iota(i32, shape, axis)


def to_row(col):
    n = col.shape[0]
    return jnp.sum(jnp.where(iota((n, n), 0) == iota((n, n), 1), col, 0.0), axis=0, keepdims=True)


def to_col(row):
    n = row.shape[1]
    return jnp.sum(jnp.where(iota((n, n), 0) == iota((n, n), 1), row, 0.0), axis=1, keepdims=True)


def picks_of(adapters, base, per, seqp):
    lane = iota((seqp, ADAPT), 1) // RANK
    return jnp.concatenate(
        [(lane == adapters[base + li]).astype(f32) for li in range(per)], axis=0
    )


def whole(count):
    return [pl.BlockSpec(memory_space=VMEM) for _ in range(count)]


def norm_stats(x):
    centre = jnp.mean(x, axis=-1, keepdims=True)
    shifted = x - centre
    scale = lax.rsqrt(jnp.mean(shifted * shifted, axis=-1, keepdims=True) + EPS)
    return shifted * scale, scale


def norm_back(grad, gain, unit, scale):
    g = grad * gain
    return scale * (
        g - jnp.mean(g, axis=-1, keepdims=True) - unit * jnp.mean(g * unit, axis=-1, keepdims=True)
    )


def greet(peers):
    barrier = pltpu.get_barrier_semaphore()
    for peer in peers:
        pl.semaphore_signal(barrier, 1, device_id=peer, device_id_type=MESH)
    pl.semaphore_wait(barrier, len(peers))


def remote(src, dst, send, recv, peer):
    return pltpu.make_async_remote_copy(
        src_ref=src, dst_ref=dst, send_sem=send, recv_sem=recv, device_id=peer, device_id_type=MESH
    )


def where_am_i():
    e = lax.axis_index("expert")
    t = lax.axis_index("tensor")
    return e, t, jnp.bitwise_xor(t, 1), jnp.bitwise_xor(t, 2), jnp.bitwise_xor(t, 3)


def dma(n):
    return pltpu.SemaphoreType.DMA((n,))


def linked(ident):
    return pltpu.CompilerParams(collective_id=ident, has_side_effects=True)


def gates_of(mixed, r0, r1, pick, rw, rd, ru):
    low = dot(mixed, rd) * pick
    logits = dot_nt(mixed, rw) + dot_nt_fine(low, ru)
    lane = iota((1, rw.shape[0]), 1)
    first = jnp.sum(jnp.where(r0 == lane, logits, 0.0), axis=1, keepdims=True)
    second = jnp.sum(jnp.where(r1 == lane, logits, 0.0), axis=1, keepdims=True)
    top = jnp.maximum(first, second)
    a = jnp.exp(first - top)
    b = jnp.exp(second - top)
    return a / (a + b), b / (a + b), low


def own_images(ref, first, per, seq, seqp, put):
    tok = ref.shape[0]
    for li in range(per):
        row = iota((seqp, tok), 0)
        sel = (iota((seqp, tok), 1) == row + (first + li) * seq) & (row < seq)
        put(pl.ds(li * seqp, seqp), dot(sel.astype(f32).astype(bf16), ref[...]))


def erf_parts(pre):
    cdf = 0.5 * (1.0 + lax.erf(pre * 0.7071067811865476))
    return pre * cdf, cdf + pre * (jnp.exp(-0.5 * pre * pre) * 0.3989422804014327)


def chunk_of(ref, ne, p):
    size = ref.shape[0] // ne
    return pl.ds(pl.multiple_of(p * size, size), size)


def sum_copy(ne, src, parts, send, recv):
    e, t = where_am_i()[:2]

    def copy(d):
        p = lax.rem(e + d, ne)
        return remote(src.at[chunk_of(src, ne, p)], parts.at[d - 1], send.at[d], recv.at[d], (p, t))

    return copy


def start_all(ne, copy):
    def start(d, carry):
        copy(d).start()
        return carry

    lax.fori_loop(1, ne, start, 0)


def sum_share(ne, copy, src, parts, total, send, recv):
    e, t = where_am_i()[:2]
    mine = chunk_of(src, ne, e)

    def add(d, acc):
        copy(d).wait()
        return acc + parts[d - 1].astype(f32)

    total[mine, :] = lax.fori_loop(1, ne, add, src[mine, :].astype(f32)).astype(bf16)

    def share(d):
        p = lax.rem(e + d, ne)
        return remote(total.at[mine], total.at[mine], send.at[ne + d], recv.at[ne + d], (p, t))

    def start(d, carry):
        share(d).start()
        return carry

    lax.fori_loop(1, ne, start, 0)
    return share


def wait_all(ne, copy):
    def wait(d, carry):
        copy(d).wait()
        return carry

    lax.fori_loop(1, ne, wait, 0)


def block_kernel(
    dims, adapters, prio, routes, cot_in, x_in, gain1, gain2, wt_in, tup_in, pw_in, pd_in,
    tdn, pup, rw, rd, ru, fdn, sup, w1_in, w2_in, fup_in, sdn_in,
    etot, btot, atot, outs, rep_e, rep_a, back_out, res_out, *rest,
):
    nt, ne, seq, seqp, images, experts, cap, chunks, cp, held_e, grows, la, lb, roomy = dims
    (
        slotc, slotr, routec, xs, cot_own, mixed, middle, triple, attended, tlow, plow, attn_in,
        wt, tup, pw, pd, got, got_cot, cot_pad, one_s, cots, mall, gall, acc_s, gate_s, out_s,
        w1, w2, fup, sdn, sent_s, sg_s, low_s, gcol_s, gg_rows, acc_low,
        acc_fd, acc_fu, acc_sd, acc_su, gr_s, gin1, keep, gin2, cot, x_own,
        back_s, res_s, tin1, tin1k, tin1r, keep_g, keep_k, tin2, tin2k, tin2r,
        bin1, bin2, ain1, ain2, eparts, bparts, aparts, gt_s, ga_s, back_low, rank_r, probs_s,
        wsend, wrecv, bsend, brecv, csend, crecv, tsend, trecv, send, recv, gsend, grecv, rsend, rrecv,
        ssend, srecv, usend, urecv, esend, erecv, b2send, b2recv, asend, arecv, osend, orecv,
        here, own_sem, load_sem, ret_sem,
    ) = rest
    back = back_s if roomy else back_out
    ebuf, bbuf = gin1.at[0], bin1.at[0]
    got_res = res_s if roomy else res_out
    e, t, near, far, cross = where_am_i()
    lw = pw_in.shape[0]
    width = x_in.shape[1]
    local = w1_in.shape[0]
    parts = nt // local
    n_out, block = cots.shape[0], cots.shape[1]
    peers = [(e, far), (e, near)] + [(lax.rem(e + d, ne), t) for d in range(1, ne)]
    barrier = pltpu.get_barrier_semaphore()
    for peer in peers:
        pl.semaphore_signal(barrier, 1, device_id=peer, device_id_type=MESH)

    def big_ref(k, to):
        return (fup_in, sdn_in)[k] if k < 2 else (w1_in, w2_in)[k - 2].at[lax.div(to, parts)]

    big = (fup, sdn, w1, w2)
    n_big = len(big)
    big_own = [
        pltpu.make_async_copy(big_ref(k, t), big[k].at[t], load_sem.at[k]) for k in range(n_big)
    ]
    big_far = [
        remote(big_ref(k, far), big[k].at[t], bsend.at[3 * k], brecv.at[3 * k], (e, far))
        for k in range(n_big)
    ]
    big_near = [
        remote(big_ref(k, near), big[k].at[t], bsend.at[3 * k + 1], brecv.at[3 * k + 1], (e, near))
        for k in range(n_big)
    ]
    big_relay = [
        remote(big[k].at[far], big[k].at[far], bsend.at[3 * k + 2], brecv.at[3 * k + 2], (e, near))
        for k in range(n_big)
    ]
    load_cot = pltpu.make_async_copy(cot_in, cot, load_sem.at[n_big])
    x_ref = x_own if roomy else cot
    load_x = pltpu.make_async_copy(x_in, x_ref, load_sem.at[n_big + 1])
    for copy in [load_cot] + big_own:
        copy.start()
    if roomy:
        load_x.start()

    moves = []
    for c in range(3):
        lanes = pl.ds(c * lw, lw)
        moves.append((wt_in.at[c], lambda q, lanes=lanes: wt.at[q, :, lanes]))
        moves.append((tup_in.at[c], lambda q, lanes=lanes: tup.at[q, :, lanes]))
    moves.append((pw_in, lambda q: pw.at[q]))
    moves.append((pd_in, lambda q: pd.at[q]))
    n_w = len(moves)
    fars = [
        remote(src, at(t), wsend.at[3 * i], wrecv.at[3 * i], (e, far))
        for i, (src, at) in enumerate(moves)
    ]
    nears = [
        remote(src, at(t), wsend.at[3 * i + 1], wrecv.at[3 * i + 1], (e, near))
        for i, (src, at) in enumerate(moves)
    ]
    relays = [
        remote(at(far), at(far), wsend.at[3 * i + 2], wrecv.at[3 * i + 2], (e, near))
        for i, (src, at) in enumerate(moves)
    ]
    owns = [
        pltpu.make_async_copy(src, at(t), own_sem.at[i]) for i, (src, at) in enumerate(moves)
    ]
    for copy in owns:
        copy.start()

    tok = prio.shape[1]
    per = images // nt
    rows = per * seqp
    total = nt * rows
    wide = one_s.shape[-1]
    order = iota((seqp, tok), 1).astype(f32)
    lane = iota((seqp, wide), 1)
    for i in range(images):
        if i == images // 2:
            pl.semaphore_wait(barrier, len(peers))
            for copy in fars + nears:
                copy.start()
        q, at = i // per, pl.ds(i % per * seqp, seqp)
        all_at = pl.ds(i * seqp, seqp)
        token = iota((seqp, 1), 0) + i * seq
        gate_s[all_at, :] = jnp.sum(
            jnp.where(prio[...] == token, order, 0.0), axis=1, keepdims=True
        )
        lane0 = i * seq // 128 * 128
        lane1 = min(lane0 + up(seq + 128, 128), tok)
        here_i = (iota((seqp, lane1 - lane0), 1) + lane0 == token) & (iota((seqp, lane1 - lane0), 0) < seq)
        r = [
            jnp.sum(
                jnp.where(here_i, routes[k : k + 1, lane0:lane1].astype(f32) + 1.0, 0.0),
                axis=1,
                keepdims=True,
            ).astype(i32)
            - 1
            for k in range(TOP)
        ]
        for k in range(TOP):
            routec[q, at, k : k + 1] = r[k]
        named = jnp.where(lane < experts, r[0], jnp.where(r[1] < 0, -1, r[1] + experts))
        one_s[all_at, :] = (named == lane).astype(f32).astype(bf16)
    totals = dot(jnp.ones((8, total), bf16), one_s[...])[0:1]
    for q in range(nt):
        rank_r[q : q + 1, :] = to_row(gate_s[pl.ds(q * rows, rows), :])
    lane = iota((rows, wide), 1)

    def slots_of(q, carry):
        at = pl.ds(pl.multiple_of(q * rows, 16), rows)
        mine = gate_s[at, :]
        counts = jnp.zeros((rows, wide), f32)
        for p in range(nt):
            before = (rank_r[p : p + 1, :] < mine).astype(f32).astype(bf16)
            counts = counts + dot(before, one_s[pl.ds(p * rows, rows), :])
        hot = one_s[at, :].astype(f32) * counts
        first = jnp.sum(jnp.where(lane < experts, hot, 0.0), axis=1, keepdims=True)
        second = jnp.sum(
            jnp.where(lane < experts, 0.0, hot)
            + jnp.where((lane < experts) & (routec[q, :, 1:2] == lane), totals, 0.0),
            axis=1,
            keepdims=True,
        )
        for k, pos in ((0, first), (1, second)):
            named = routec[q, :, k : k + 1]
            place = pos.astype(i32)
            kept = (named >= 0) & (place < cap)
            kept = kept & (lax.rem(named, local) == lax.div(t, parts))
            kept = kept & (lax.rem(place, parts) == lax.rem(t, parts))
            index = lax.div(place, parts)
            index = jnp.where(index < cp - 2, index, index + 2)
            slot = jnp.where(kept, lax.div(named, local) * block + index, -1)
            slotc[q, :, k : k + 1] = slot
            slotr[q, k : k + 1, :] = to_row(slot.astype(f32)).astype(i32)
        return carry

    lax.fori_loop(0, nt, slots_of, 0)

    load_cot.wait()
    for i in range(images):
        start = i * seq // 16 * 16
        stop = min(start + up(seq, 16) + 16, tok)
        src = iota((seqp, stop - start), 1) + start
        row = iota((seqp, stop - start), 0)
        sel = ((src == row + i * seq) & (row < seq)).astype(f32).astype(bf16)
        cot_pad[i // per, pl.ds(i % per * seqp, seqp), :] = dot(sel, cot[start:stop, :]).astype(bf16)
    step = max(1, 512 // block)
    image_of = iota((1, rows), 1) // seqp

    def pack(d, carry):
        s = iota((step * block, 1), 0) + d * (step * block)
        acc = jnp.zeros((step * block, width), f32)
        idc = jnp.zeros((step * block, 1), f32)
        for q in range(nt):
            ids = jnp.zeros((1, rows), f32)
            for li in range(per):
                ids = jnp.where(image_of == li, adapters[q * per + li].astype(f32), ids)
            g = (slotr[q, 0:1, :] == s) | (slotr[q, 1:2, :] == s)
            idc = idc + jnp.sum(jnp.where(g, ids, 0.0), axis=1, keepdims=True)
            acc = acc + dot(g.astype(f32).astype(bf16), cot_pad[q])
        row = iota((block, block), 0)
        for b in range(step):
            part = acc[b * block : (b + 1) * block]
            idr = to_row(idc[b * block : (b + 1) * block])
            head = jnp.where(row == cp - 2, idr, part[:, 0:block])
            cots[d * step + b, :, 0:block] = head.astype(bf16)
            cots[d * step + b, :, block:] = part[:, block:].astype(bf16)
        return carry

    lax.fori_loop(0, n_out // step, pack, 0)

    def cot_copy(d):
        p = lax.rem(e + d, ne)
        return remote(cots.at[p], got_cot.at[e], csend.at[d], crecv.at[d], (p, t))

    def cot_start(d, carry):
        cot_copy(d).start()
        return carry

    lax.fori_loop(1, ne, cot_start, 0)
    own_cot = pltpu.make_async_copy(cots.at[e], got_cot.at[e], here.at[0])
    own_cot.start()

    def put_x(at, value):
        xs[at, :] = value

    def put_cot(at, value):
        cot_own[at, :] = value.astype(bf16)

    if not roomy:
        own_images(cot, t * per, per, seq, seqp, put_cot)
        load_x.start()
    load_x.wait()
    own_images(x_ref, t * per, per, seq, seqp, put_x)
    pick = picks_of(adapters, t * per, per, seqp)
    unit, _ = norm_stats(xs[...])
    normed = (unit * gain1[...]).astype(bf16)
    attn_in[...] = normed
    low = (dot(normed, tdn[...]) * pick).astype(bf16)
    tlow[...] = low
    head_of = iota((1, lw), 1) // HEAD_DIM
    key_ok = iota((1, seqp), 1) < seq

    def piece(m, carry):
        p = jnp.bitwise_xor(t, m)

        @pl.when(m == 0)
        def _():
            for copy in owns:
                copy.wait()

        @pl.when(m == 1)
        def _():
            for copy in nears:
                copy.wait()

        @pl.when(m == 2)
        def _():
            for i in range(6):
                fars[i].wait_recv()
                relays[i].start()

        @pl.when(m == 3)
        def _():
            for i in range(6):
                relays[i].wait_recv()

        triple[p] = (dot(attn_in[...], wt[p]) + dot(tlow[...], tup[p])).astype(bf16)
        for li in range(per):
            at = pl.ds(li * seqp, seqp)
            q = triple[p, at, 0:lw]
            k = triple[p, at, lw : 2 * lw]
            v = triple[p, at, 2 * lw : 3 * lw]
            acc = jnp.zeros((seqp, lw), f32)
            for h in range(lw // HEAD_DIM):
                on = head_of == h
                qm = jnp.where(on, q * HEAD_DIM**-0.5, 0.0).astype(bf16)
                s = jnp.where(key_ok, dot_nt(qm, k), -jnp.inf)
                ex = jnp.exp(s - jnp.max(s, axis=1, keepdims=True))
                probs = (ex * (1.0 / jnp.sum(ex, axis=1, keepdims=True))).astype(bf16)
                acc = acc + dot(probs, jnp.where(on, v, 0.0).astype(bf16))
            attended[p, at, :] = acc.astype(bf16)
        return carry

    lax.fori_loop(0, nt, piece, 0)
    for copy in big_near:
        copy.start()
    for i in range(6, n_w):
        fars[i].wait_recv()
        relays[i].start()
    for i in range(6, n_w):
        relays[i].wait_recv()
    psum = jnp.zeros((rows, ADAPT), f32)
    branch = jnp.zeros((rows, width), f32)
    for p in range(nt):
        psum = psum + dot(attended[p], pd[p])
        branch = branch + dot(attended[p], pw[p])
    low2 = (psum * pick).astype(bf16)
    plow[...] = low2
    mid = xs[...] + branch + dot(low2, pup[...])
    middle[...] = mid
    unit2, _ = norm_stats(mid)
    mix = (unit2 * gain2[...]).astype(bf16)
    mixed[...] = mix
    mall[t] = mix

    mix_far = [
        remote(buf.at[t], buf.at[t], tsend.at[i], trecv.at[i], (e, far))
        for i, buf in enumerate((mall, gall))
    ]
    mix_near = [
        remote(buf.at[t], buf.at[t], tsend.at[2 + i], trecv.at[2 + i], (e, near))
        for i, buf in enumerate((mall, gall))
    ]
    mix_relay = [
        remote(buf.at[far], buf.at[far], tsend.at[4 + i], trecv.at[4 + i], (e, near))
        for i, buf in enumerate((mall, gall))
    ]
    mix_far[0].start()
    mix_near[0].start()
    r = routec[t]
    a, b, _ = gates_of(mix, r[:, 0:1], r[:, 1:2], pick, rw[...], rd[...], ru[...])
    gall[t] = jnp.zeros(gall.shape[1:], f32)
    gall[t, 0:1, :] = to_row(a)
    gall[t, 1:2, :] = to_row(b)
    for copy in [mix_far[1], mix_near[1]] + big_far:
        copy.start()
    step = max(1, 512 // block)

    def gather_rows(q, s):
        g0 = slotr[q, 0:1, :] == s
        g1 = slotr[q, 1:2, :] == s
        gate = jnp.sum(
            jnp.where(g0, gall[q, 0:1, :], jnp.where(g1, gall[q, 1:2, :], 0.0)), axis=1, keepdims=True
        )
        return dot((g0 | g1).astype(f32).astype(bf16), mall[q]), gate

    def add_quarter(q, fresh):
        def some(d, carry):
            at = pl.ds(pl.multiple_of(d * (step * block), step * block), step * block)
            s = iota((step * block, 1), 0) + d * (step * block)
            part, gate = gather_rows(q, s)
            acc_s[at, :] = part if fresh else acc_s[at, :] + part
            gate_s[at, :] = gate if fresh else gate_s[at, :] + gate
            return carry

        lax.fori_loop(0, n_out // step, some, 0)

    add_quarter(t, True)
    for copy in mix_near:
        copy.wait_recv()
    add_quarter(near, False)
    if roomy:
        own_images(cot, t * per, per, seq, seqp, put_cot)
    for copy in mix_far:
        copy.wait_recv()
    for copy in mix_relay:
        copy.start()
    add_quarter(far, False)
    for copy in mix_relay:
        copy.wait_recv()

    def finish(p):
        at = pl.ds(pl.multiple_of(p * block, block), block)
        part, gate = gather_rows(cross, iota((block, 1), 0) + p * block)
        part = acc_s[at, :] + part
        gate = to_row(gate_s[at, :] + gate)
        high = gate.astype(bf16).astype(f32)
        row = iota((block, block), 0)
        head = jnp.where(row == cp - 2, high, part[:, 0:block])
        head = jnp.where(row == cp - 1, gate - high, head)
        return head.astype(bf16), part[:, block:].astype(bf16)

    def chunk(h):
        return pl.ds(pl.multiple_of(h * cp, cp), cp)

    def out_copy(d, h):
        p = lax.rem(e + d, ne)
        k = d * chunks + h
        return remote(out_s.at[p, chunk(h)], got.at[e, chunk(h)], send.at[k], recv.at[k], (p, t))

    def send_one(d, carry):
        p = lax.rem(e + d, ne)
        head, tail = finish(p)
        out_s[p, :, 0:block] = head
        out_s[p, :, block:] = tail
        out_copy(d, 0).start()
        return carry

    lax.fori_loop(1, ne, send_one, 0)

    for h in range(1, chunks):

        def send_more(d, carry, h=h):
            out_copy(d, h).start()
            return carry

        lax.fori_loop(1, ne, send_more, 0)
    head, tail = finish(e)
    got[e, :, 0:block] = head
    got[e, :, block:] = tail

    n = ne
    erows = n * cp
    row_at = lax.rem(iota((erows, 1), 0), cp)
    res_at, gsent_at = pl.ds(0, erows), pl.ds(erows, erows)
    for buf in (acc_fd, acc_fu, acc_sd, acc_su):
        buf[...] = jnp.zeros_like(buf)
    for copy in big_own + big_near:
        copy.wait()

    def cot_wait(d, carry):
        cot_copy(d).wait()
        return carry

    lax.fori_loop(1, ne, cot_wait, 0)
    own_cot.wait()

    def grad_copy(d, h):
        p = lax.rem(e + d, ne)
        k = d * chunks + h
        return remote(cots.at[p, chunk(h)], back.at[e, chunk(h)], gsend.at[k], grecv.at[k], (p, t))

    def res_copy(d):
        p = lax.rem(e + d, ne)
        return remote(out_s.at[p], got_res.at[e], rsend.at[d], rrecv.at[d], (p, t))

    def experts_chunk(h, carry):
        at = chunk(h)

        def rows_wait(d, carry):
            out_copy(d, h).wait_recv()
            return carry

        lax.fori_loop(1, ne, rows_wait, 0)

        @pl.when(h == 0)
        def _():
            diag = iota((block, block), 0) == iota((block, block), 1)

            def headers(m, carry):
                idr = got_cot[m, cp - 2 : cp - 1, 0:block].astype(f32)
                gr = got[m, cp - 2 : cp - 1, 0:block].astype(f32) + got[
                    m, cp - 1 : cp, 0:block
                ].astype(f32)
                gcol_s[m, :, 0:1] = jnp.sum(jnp.where(diag, idr, 0.0), axis=1, keepdims=True)
                gcol_s[m, :, 1:2] = jnp.sum(jnp.where(diag, gr, 0.0), axis=1, keepdims=True)
                return carry

            lax.fori_loop(0, n, headers, 0)

        spare = jnp.where((h == 0) | (h == chunks - 1), cp - 2, cp)
        real = row_at < spare
        cols = gcol_s[:, at, :].reshape(erows, 2)
        sent = jnp.where(real, got[:, at, :].reshape(erows, width).astype(f32), 0.0).astype(bf16)
        cotf = jnp.where(real, got_cot[:, at, :].reshape(erows, width).astype(f32), 0.0)
        pick_e = (cols[:, 0:1] == (iota((1, ADAPT), 1) // RANK).astype(f32)).astype(f32)
        sent_s[...] = sent
        sgrad = (cols[:, 1:2] * cotf).astype(bf16)
        sg_s[...] = sgrad
        low_s[0] = (dot(sent, fdn[...]) * pick_e).astype(bf16)
        low_s[1] = (dot_nt(sgrad, sup[...]) * pick_e).astype(bf16)
        acc_low[...] = jnp.zeros_like(acc_low)
        acc_s[pl.ds(0, 2 * erows), :] = jnp.zeros((2 * erows, width), f32)

        def through(m, carry):
            c = jnp.bitwise_xor(t, m)

            @pl.when((h == 0) & (m == 2))
            def _():
                for far_copy, relay in zip(big_far, big_relay):
                    far_copy.wait_recv()
                    relay.start()

            @pl.when((h == 0) & (m == 3))
            def _():
                for relay in big_relay:
                    relay.wait_recv()

            span = min(erows, 512)
            for r0 in range(0, erows, span):
                rs = slice(r0, r0 + span)
                gs = slice(erows + r0, erows + r0 + span)
                pre = dot(sent_s[rs, :], w1[c]) + dot(low_s[0, rs, :], fup[c])
                act, slope = erf_parts(pre)
                hid = act.astype(bf16)
                acc_low[0, rs, :] += dot(hid, sdn[c])
                acc_s[rs, :] += dot(hid, w2[c])
                ghid = dot_nt(sg_s[rs, :], w2[c]) + dot_nt(low_s[1, rs, :], sdn[c])
                gpre = (ghid * slope).astype(bf16)
                acc_fu[c] += dot_tn(low_s[0, rs, :], gpre)
                acc_sd[c] += dot_tn(low_s[1, rs, :], hid)
                acc_low[1, rs, :] += dot_nt(gpre, fup[c])
                acc_s[gs, :] += dot_nt(gpre, w1[c])
            return carry

        lax.fori_loop(0, nt, through, 0)

        def sent_wait(d, carry):
            out_copy(d, h).wait_send()
            return carry

        lax.fori_loop(1, ne, sent_wait, 0)
        cols = gcol_s[:, at, :].reshape(erows, 2)
        pick_e = (cols[:, 0:1] == (iota((1, ADAPT), 1) // RANK).astype(f32)).astype(f32)
        second_low = (acc_low[0] * pick_e).astype(bf16)
        res = (acc_s[res_at, :] + dot(second_low, sup[...])).astype(bf16).astype(f32)
        cotf = got_cot[:, at, :].reshape(erows, width).astype(f32)
        acc_low[0, :, 0:1] = jnp.sum(res * cotf, axis=1, keepdims=True)
        g1low = (acc_low[1] * pick_e).astype(bf16)
        gsent = acc_s[gsent_at, :] + dot_nt(g1low, fdn[...])
        cots[:, at, :] = gsent.astype(bf16).reshape(n, cp, width)
        diag = iota((cp, block), 0) + h * cp == iota((cp, block), 1)

        def footers(m, carry):
            gg = jnp.sum(
                jnp.where(diag, acc_low[0, pl.ds(pl.multiple_of(m * cp, cp), cp), 0:1], 0.0),
                axis=0,
                keepdims=True,
            )
            total = jnp.where(h == 0, gg, gg_rows[pl.ds(m, 1), :] + gg)
            gg_rows[pl.ds(m, 1), :] = total

            @pl.when(h == chunks - 1)
            def _():
                high = total.astype(bf16).astype(f32)
                row = iota((16, block), 0)
                to = pl.ds(block - 16, 16)
                old = cots[m, to, 0:block].astype(f32)
                old = jnp.where(row == 14, high, jnp.where(row == 15, total - high, old))
                cots[m, to, 0:block] = old.astype(bf16)

            return carry

        lax.fori_loop(0, n, footers, 0)

        def grad_start(d, carry):
            grad_copy(d, h).start()
            return carry

        lax.fori_loop(1, ne, grad_start, 0)
        out_s[:, at, :] = (cols[:, 1:2] * res).astype(bf16).reshape(n, cp, width)
        acc_su[...] += dot_tn(second_low, sg_s[...])
        acc_fd[...] += dot_tn(g1low, sent_s[...])
        return carry

    gg_rows[...] = jnp.zeros_like(gg_rows)
    lax.fori_loop(0, chunks, experts_chunk, 0)
    locals_ = [
        pltpu.make_async_copy(cots.at[e], back.at[e], ret_sem.at[0]),
        pltpu.make_async_copy(out_s.at[e], got_res.at[e], ret_sem.at[1]),
    ]
    for copy in locals_:
        copy.start()

    def res_start(d, carry):
        res_copy(d).start()
        return carry

    ffq = w1.shape[2]
    quarter = width // nt
    share = ADAPT // nt
    for q in range(nt):
        off = 0
        for c in range(ffq // 128):
            gr_s[q, off : off + 128, :] = acc_fu[q, :, c * 128 : (c + 1) * 128].astype(bf16)
            off += 128
        gr_s[q, off : off + ffq, :] = acc_sd[q].T.astype(bf16)
        off += ffq
        gr_s[q, off : off + quarter, :] = acc_fd[:, q * quarter : (q + 1) * quarter].T.astype(bf16)
        off += quarter
        for c in range(width // 128):
            at = slice(q * share, (q + 1) * share)
            gr_s[q, off : off + share, :] = acc_su[at, c * 128 : (c + 1) * 128].astype(bf16)
            off += share
        if off < grows:
            gr_s[q, off:grows, :] = jnp.zeros((grows - off, 128), bf16)

    def tensor_sum(rows_at, in1, in2, k):
        a = remote(gr_s.at[cross, rows_at], in1.at[0], ssend.at[k], srecv.at[k], (e, near))
        b = remote(gr_s.at[near, rows_at], in1.at[1], ssend.at[k + 1], srecv.at[k + 1], (e, near))
        held = keep.at[rows_at]
        c = remote(held, in2, ssend.at[k + 2], srecv.at[k + 2], (e, far))

        def start():
            a.start()
            b.start()

        def cross_over():
            a.wait()
            held[...] = (gr_s[far, rows_at, :].astype(f32) + in1[0].astype(f32)).astype(bf16)
            c.start()

        def result():
            b.wait()
            c.wait()
            mine = gr_s[t, rows_at, :].astype(f32) + in1[1].astype(f32)
            return (mine + in2[...].astype(f32)).astype(bf16)

        return start, cross_over, result

    g_start, g_cross, g_result = tensor_sum(pl.ds(0, grows), gin1, gin2, 0)
    g_start()

    r = routec[t]
    prob0, prob1, rlow = gates_of(
        mixed[...], r[:, 0:1], r[:, 1:2], pick, rw[...], rd[...], ru[...]
    )
    g_cross()

    key_row = iota((seqp, 1), 0) < seq
    heads = lw // HEAD_DIM

    def softmax_of(qm, k):
        s = jnp.where(key_row, dot_nt(k, qm), -jnp.inf)
        ex = jnp.exp(s - jnp.max(s, axis=0, keepdims=True))
        return ex * (1.0 / jnp.sum(ex, axis=0, keepdims=True))

    def softmax_piece(p, carry):
        for li in range(per):
            at = pl.ds(li * seqp, seqp)
            q = triple[p, at, 0:lw] * HEAD_DIM**-0.5
            k = triple[p, at, lw : 2 * lw]
            for h in range(heads):
                qm = jnp.where(head_of == h, q, 0.0).astype(bf16)
                probs_s[(p * per + li) * heads + h] = softmax_of(qm, k).astype(bf16)
        return carry

    if roomy:
        lax.fori_loop(0, nt, softmax_piece, 0)

    def back_wait(d, carry):
        for h in range(chunks):
            grad_copy(d, h).wait()
        return carry

    lax.fori_loop(1, ne, back_wait, 0)
    lax.fori_loop(1, ne, res_start, 0)
    for copy in locals_:
        copy.wait()
    for copy in mix_far + mix_near + mix_relay:
        copy.wait_send()
    if not roomy:
        load = pltpu.make_async_copy(back, got, here.at[0])
        load.start()
        load.wait()
    rows_back = back if roomy else got
    slots = n * block
    grad_s, gg_s, tok_s = cot_pad, gall, mall

    def hot(q):
        s = iota((1, slots), 1)
        c = slotc[q]
        return ((c[:, 0:1] == s) | (c[:, 1:2] == s)).astype(f32).astype(bf16)

    def grad_tokens(q):
        grad_s[q] = dot(hot(q), rows_back[...].reshape(slots, width)).astype(bf16)

    def gate_tokens(q):
        sc = iota((slots, 1), 0)
        gg_s[q] = jnp.zeros(gg_s.shape[1:], f32)
        for k in range(TOP):
            gg_s[q, k : k + 1, :] = jnp.sum(
                jnp.where(slotr[q, k : k + 1, :] == sc, gate_s[0:slots, :], 0.0), axis=0, keepdims=True
            )

    stages = ((grad_s, tin1, keep_g, tin2), (gg_s, tin1k, keep_k, tin2k))
    first, second = {}, []
    for i, (src, dst, held, two) in enumerate(stages):
        if i == 1:


            def read_gates(d, carry):
                gr = rows_back[d, block - 2 : block - 1, 0:block].astype(f32)
                gr = gr + rows_back[d, block - 1 : block, 0:block].astype(f32)
                gate_s[pl.ds(pl.multiple_of(d * block, block), block), :] = to_col(gr)
                return carry

            lax.fori_loop(0, n, read_gates, 0)
        for j, q in enumerate((cross, near)):
            (grad_tokens, gate_tokens)[i](q)
            k = 3 * i + j
            first[i, j] = remote(src.at[q], dst.at[j], usend.at[k], urecv.at[k], (e, near))
            first[i, j].start()
        (grad_tokens, gate_tokens)[i](far)
        first[i, 0].wait()
        held[...] = (src[far].astype(f32) + dst[0].astype(f32)).astype(held.dtype)
        second.append(remote(held, two, usend.at[3 * i + 2], urecv.at[3 * i + 2], (e, far)))
        second[-1].start()
    grad_tokens(t)
    gate_tokens(t)
    ebuf[...] = g_result()
    e_first = sum_copy(ne, ebuf, eparts, esend, erecv)
    start_all(ne, e_first)
    unit2, scale2 = norm_stats(middle[...])
    sums = []
    for i, (src, one, _, two) in enumerate(stages):
        first[i, 1].wait()
        mine = src[t].astype(f32) + one[1].astype(f32)
        second[i].wait()
        sums.append(mine + two[...].astype(f32))
    gmix, ggate = sums
    gg0 = to_col(ggate[0:1, :])
    gg1 = to_col(ggate[1:2, :])
    inner = prob0 * gg0 + prob1 * gg1
    lane = iota((1, rw.shape[0]), 1)
    glog = jnp.where(r[:, 0:1] == lane, prob0 * (gg0 - inner), 0.0) + jnp.where(
        r[:, 1:2] == lane, prob1 * (gg1 - inner), 0.0
    )
    llow = dot_fine(glog, ru[...]) * pick
    gm = gmix + dot_fine(glog, rw[...]) + dot_nt_fine(llow, rd[...])
    router_up = dot_tn(glog.astype(bf16), rlow.astype(bf16))
    router_down = dot_tn(mixed[...], llow.astype(bf16))
    gmid = cot_own[...].astype(f32) + norm_back(gm, gain2[...], unit2, scale2)
    mid_at, in_at = pl.ds(0, rows), pl.ds(rows, rows)
    acc_s[mid_at, :] = gmid
    gbranch = gmid.astype(bf16)
    project_up = dot_tn(plow[...], gbranch)
    blow = (dot_nt(gbranch, pup[...]) * pick).astype(bf16)
    for p in range(nt):
        ga_s[p] = (dot_nt(gbranch, pw[p]) + dot_nt(blow, pd[p])).astype(bf16)

    for q in range(nt):
        off = la
        at = slice(q * share, (q + 1) * share)
        for c in range(width // 128):
            gr_s[q, off : off + share, :] = project_up[at, c * 128 : (c + 1) * 128].astype(bf16)
            off += share
        at = slice(q * quarter, (q + 1) * quarter)
        gr_s[q, off : off + quarter, :] = router_down[at].astype(bf16)
        off += quarter
        gr_s[q, off : la + lb - lw, :] = jnp.zeros((la + lb - lw - off, 128), bf16)
        gr_s[q, la + lb - lw : la + lb, :] = dot_tn(attended[q], blow).astype(bf16)
    off = la + ADAPT + quarter
    gr_s[0, off : off + experts, :] = router_up.astype(bf16)
    b_start, b_cross, b_result = tensor_sum(pl.ds(la, lb), bin1, bin2, 3)
    b_start()
    b_first = sum_copy(ne, bbuf, bparts, b2send, b2recv)

    acc_s[in_at, :] = jnp.zeros((rows, width), f32)
    back_low[...] = jnp.zeros_like(back_low)

    def piece_back(p, carry):
        for li in range(per):
            at = pl.ds(li * seqp, seqp)
            q = triple[p, at, 0:lw] * HEAD_DIM**-0.5
            k = triple[p, at, lw : 2 * lw]
            v = triple[p, at, 2 * lw : 3 * lw]
            ga = ga_s[p, at, :]
            gq = jnp.zeros((seqp, lw), f32)
            gk = jnp.zeros((seqp, lw), f32)
            gv = jnp.zeros((seqp, lw), f32)
            for h in range(heads):
                on = head_of == h
                qm = jnp.where(on, q, 0.0).astype(bf16)
                km = jnp.where(on, k, 0.0).astype(bf16)
                gam = jnp.where(on, ga, 0.0).astype(bf16)
                if roomy:
                    half = probs_s[(p * per + li) * heads + h]
                    probs = half.astype(f32)
                else:
                    probs = softmax_of(qm, k)
                    half = probs.astype(bf16)
                weighted = probs * dot_nt(v, gam)
                ds = (weighted - probs * jnp.sum(weighted, axis=0, keepdims=True)).astype(bf16)
                gq = gq + dot_tn(ds, km)
                gk = gk + dot(ds, qm)
                gv = gv + dot(half, gam)
            gt_s[at, 0:lw] = (gq * HEAD_DIM**-0.5).astype(bf16)
            gt_s[at, lw : 2 * lw] = gk.astype(bf16)
            gt_s[at, 2 * lw : 3 * lw] = gv.astype(bf16)
        gt = gt_s[...]
        back_low[...] += dot_nt(gt, tup[p])
        acc_s[in_at, :] += dot_nt(gt, wt[p])
        tu = dot_tn(tlow[...], gt)
        for c in range(3 * lw // 128):
            gr_s[p, c * 128 : (c + 1) * 128, :] = tu[:, c * 128 : (c + 1) * 128].astype(bf16)

        @pl.when(p == 0)
        def _():
            b_cross()

        @pl.when(p == 2)
        def _():
            bbuf[...] = b_result()
            start_all(ne, b_first)

        return carry

    lax.fori_loop(0, nt, piece_back, 0)

    tglow = (back_low[...] * pick).astype(bf16)
    triple_down = dot_tn(attn_in[...], tglow)
    for q in range(nt):
        off = 3 * lw
        gr_s[q, off : off + quarter, :] = triple_down[q * quarter : (q + 1) * quarter].astype(bf16)
        if off + quarter < la:
            gr_s[q, off + quarter : la, :] = jnp.zeros((la - off - quarter, 128), bf16)
    a_start, a_cross, a_result = tensor_sum(pl.ds(0, la), ain1, ain2, 6)
    a_start()
    gin = acc_s[in_at, :] + dot_nt(tglow, tdn[...])
    a_cross()
    unit1, scale1 = norm_stats(xs[...])
    attn_in[...] = (acc_s[mid_at, :] + norm_back(gin, gain1[...], unit1, scale1)).astype(bf16)

    def share_out(j, src, k):
        return [
            remote(src, outs.at[t, j], osend.at[k], orecv.at[k], (e, far)),
            remote(src, outs.at[t, j], osend.at[k + 1], orecv.at[k + 1], (e, near)),
            remote(outs.at[far, j], outs.at[far, j], osend.at[k + 2], orecv.at[k + 2], (e, near)),
            pltpu.make_async_copy(src, outs.at[t, j], here.at[1 + j]),
        ]

    def share_rows(buf, k):
        return [
            remote(buf.at[t], buf.at[t], osend.at[k], orecv.at[k], (e, far)),
            remote(buf.at[t], buf.at[t], osend.at[k + 1], orecv.at[k + 1], (e, near)),
            remote(buf.at[far], buf.at[far], osend.at[k + 2], orecv.at[k + 2], (e, near)),
        ]

    igrad_out = share_out(1, attn_in, 0)
    for i in (0, 1, 3):
        igrad_out[i].start()
    def res_wait(d, carry):
        res_copy(d).wait()
        return carry

    lax.fori_loop(1, ne, res_wait, 0)
    if not roomy:
        load = pltpu.make_async_copy(got_res, got_cot, here.at[0])
        load.start()
        load.wait()
    res_rows = got_res if roomy else got_cot

    def res_tokens(q):
        tok_s[q] = dot(hot(q), res_rows[...].reshape(slots, width)).astype(bf16)

    res_first = []
    for j, q in enumerate((cross, near)):
        res_tokens(q)
        res_first.append(remote(tok_s.at[q], tin1r.at[j], usend.at[6 + j], urecv.at[6 + j], (e, near)))
        res_first[-1].start()
    res_tokens(far)
    res_first[0].wait()
    keep_g[...] = (tok_s[far].astype(f32) + tin1r[0].astype(f32)).astype(bf16)
    res_second = remote(keep_g, tin2r, usend.at[8], urecv.at[8], (e, far))
    res_second.start()
    res_tokens(t)
    abuf = keep.at[pl.ds(la, la)]
    abuf[...] = a_result()
    a_first = sum_copy(ne, abuf, aparts, asend, arecv)
    start_all(ne, a_first)
    e_second = sum_share(ne, e_first, ebuf, eparts, etot, esend, erecv)
    b_second = sum_share(ne, b_first, bbuf, bparts, btot, b2send, b2recv)
    a_second = sum_share(ne, a_first, abuf, aparts, atot, asend, arecv)
    wait_all(ne, e_second)
    wait_all(ne, b_second)
    ra = grows - held_e
    rep_e[t, 0:ra, :] = etot[held_e:grows, :]
    rep_e[t, ra:, :] = btot[0 : rep_e.shape[1] - ra, :]
    rep_out = share_rows(rep_e, 6)
    for i in (0, 1):
        rep_out[i].start()
    wait_all(ne, a_second)
    rep_a[t] = atot[3 * lw : 3 * lw + quarter, :]
    last_out = share_rows(rep_a, 9)
    for i in (0, 1):
        last_out[i].start()
    res_first[1].wait()
    res_second.wait()
    mixed[...] = (
        middle[...] + (tok_s[t].astype(f32) + tin1r[1].astype(f32)) + tin2r[...].astype(f32)
    ).astype(bf16)
    block_out = share_out(0, mixed, 3)
    for i in (0, 1, 3):
        block_out[i].start()
    igrad_out[0].wait_recv()
    igrad_out[2].start()
    for group in (block_out, rep_out, last_out):
        group[0].wait_recv()
        group[2].start()
    for group in (igrad_out, block_out, rep_out, last_out):
        group[0].wait_send()
        for copy in group[1:]:
            copy.wait()
    for copy in fars + relays + big_far + big_relay:
        copy.wait_send()


def write_kernel(
    dims, e_all, b_all, a_all, outs, rep_e, rep_a, block_output, input_grad, triple_down, triple_up, project_down,
    project_up, router_down, router_up, first_down, first_up, second_down, second_up,
):
    nt, seq, seqp, images, ffq, lw, grows = dims
    per = images // nt
    tok, width = block_output.shape
    flat = outs.shape[2]
    for j, out in enumerate((block_output, input_grad)):
        for a in range(0, tok, seqp):
            b = min(a + seqp, tok)
            i0, i1 = a // seq, (b - 1) // seq
            parts = []
            for i in range(i0, i1 + 1):
                row = iota((b - a, seqp), 0) + a
                sel = (iota((b - a, seqp), 1) == row - i * seq) & (row < (i + 1) * seq)
                src = outs[i // per, j, (i % per) * seqp : (i % per + 1) * seqp, :]
                parts.append(dot(sel.astype(f32).astype(bf16), src))
            whole_part = parts[0]
            for part in parts[1:]:
                whole_part = whole_part + part
            out[a:b, :] = whole_part.astype(bf16)
    for c in range(ffq // 128):
        first_up[:, c * 128 : (c + 1) * 128] = e_all[c * 128 : (c + 1) * 128].astype(f32)
    second_down[...] = e_all[ffq : 2 * ffq].astype(f32)
    for c in range(3):
        triple_up[c] = a_all[c * lw : (c + 1) * lw].astype(f32)
    last = b_all.shape[0]
    project_down[...] = b_all[last - lw : last].astype(f32)
    quarter = width // nt
    share = ADAPT // nt
    for q in range(nt):
        at = slice(q * quarter, (q + 1) * quarter)
        up_at = slice(q * share, (q + 1) * share)
        triple_down[at, :] = rep_a[q].astype(f32)
        first_down[at, :] = rep_e[q, 0:quarter, :].astype(f32)
        off = quarter
        for c in range(width // 128):
            second_up[up_at, c * 128 : (c + 1) * 128] = rep_e[q, off : off + share, :].astype(f32)
            off += share
        off = grows - 2 * ffq
        for c in range(width // 128):
            project_up[up_at, c * 128 : (c + 1) * 128] = rep_e[q, off : off + share, :].astype(f32)
            off += share
        router_down[at, :] = rep_e[q, off : off + quarter, :].astype(f32)
        off += quarter
    router_up[...] = rep_e[0, off : off + router_up.shape[0], :].astype(f32)


def body(
    inputs, gain_attend, triple_weight, project_weight, gain_mixture, router_weight, expert_first,
    expert_second, triple_down, triple_up, project_down, project_up, router_down, router_up,
    first_down, first_up, second_down, second_up, adapter_index, routes, priority, cotangent,
):
    ne = lax.axis_size("expert")
    nt = lax.axis_size("tensor")
    tok, width = inputs.shape
    images = adapter_index.shape[0]
    seq = tok // images
    seqp = up(seq, 16)
    per = images // nt
    rows = per * seqp
    experts = router_weight.shape[1]
    local = expert_first.shape[0]
    ffq = expert_first.shape[2]
    lw = triple_weight.shape[2]
    cap = nt * ((5 * tok * TOP + 4 * nt * experts - 1) // (4 * nt * experts))
    used = cap * local // nt
    chunks = 2
    block = up(used + 4, 16 * chunks)
    cp = block // chunks
    smem = pl.BlockSpec(memory_space=pltpu.SMEM)
    anywhere = pl.BlockSpec(memory_space=pl.ANY)
    shape = jax.ShapeDtypeStruct
    wide = up(2 * experts, 128)
    gain1 = gain_attend.reshape(1, width)
    gain2 = gain_mixture.reshape(1, width)
    rw = router_weight.T
    ru = router_up.T
    big = (expert_first, expert_second, first_up, second_down)
    n_w = 8
    erows = ne * cp
    quarter = width // nt
    held_e = 2 * ffq
    grows = up(held_e + quarter + (ADAPT // nt) * (width // 128), 16 * ne)
    one = (rows, width)
    small = (8, rows)
    la = up(3 * lw + quarter, 16 * ne)
    lb = up(ADAPT + quarter + experts + lw, 16 * ne)
    re = grows - held_e + ADAPT + quarter + experts
    n_big = len(big)
    slots = (ne, block, width)
    roomy = ne * block <= 1024
    spare = slots if roomy else (8, 128)
    finals = pl.pallas_call(
        functools.partial(
            block_kernel,
            (nt, ne, seq, seqp, images, experts, cap, chunks, cp, held_e, grows, la, lb, roomy),
        ),
        out_shape=[
            shape((grows, 128), bf16),
            shape((lb, 128), bf16),
            shape((la, 128), bf16),
            shape((nt, 2) + one, bf16),
            shape((nt, re, 128), bf16),
            shape((nt, quarter, 128), bf16),
            shape((8, 128) if roomy else slots, bf16),
            shape((8, 128) if roomy else slots, bf16),
        ],
        in_specs=[smem] + whole(2) + [anywhere] * 2 + whole(13) + [anywhere] * 4,
        out_specs=whole(3) + [anywhere] + whole(2) + [anywhere] * 2,
        scratch_shapes=[
            VMEM((nt, rows, TOP), i32),
            VMEM((nt, TOP, rows), i32),
            VMEM((nt, rows, TOP), i32),
            VMEM(one, f32),
            VMEM(one, bf16),
            VMEM(one, bf16),
            VMEM(one, f32),
            VMEM((nt, rows, 3 * lw), bf16),
            VMEM((nt, rows, lw), bf16),
            VMEM((rows, ADAPT), bf16),
            VMEM((rows, ADAPT), bf16),
            VMEM(one, bf16),
            VMEM((nt, width, 3 * lw), bf16),
            VMEM((nt, ADAPT, 3 * lw), bf16),
            VMEM((nt, lw, width), bf16),
            VMEM((nt, lw, ADAPT), bf16),
            VMEM(slots, bf16),
            VMEM(slots, bf16),
            VMEM((nt,) + one, bf16),
            VMEM((images * seqp, wide), bf16),
            VMEM(slots, bf16),
            VMEM((nt,) + one, bf16),
            VMEM((nt,) + small, f32),
            VMEM((max(ne * block, 2 * erows, 2 * rows), width), f32),
            VMEM((max(ne * block, images * seqp), 1), f32),
            VMEM(slots, bf16),
            VMEM((nt, width, ffq), bf16),
            VMEM((nt, ffq, width), bf16),
            VMEM((nt, ADAPT, ffq), bf16),
            VMEM((nt, ffq, ADAPT), bf16),
            VMEM((erows, width), bf16),
            VMEM((erows, width), bf16),
            VMEM((2, erows, ADAPT), bf16),
            VMEM((ne, block, 2), f32),
            VMEM((ne, block), f32),
            VMEM((2, erows, ADAPT), f32),
            VMEM((ADAPT, width), f32),
            VMEM((nt, ADAPT, ffq), f32),
            VMEM((nt, ADAPT, ffq), f32),
            VMEM((ADAPT, width), f32),
            VMEM((nt, max(grows, la + lb), 128), bf16),
            VMEM((2, grows, 128), bf16),
            VMEM((max(grows, la + lb, 2 * la), 128), bf16),
            VMEM((grows, 128), bf16),
            VMEM((tok, width), bf16),
            VMEM((tok, width) if roomy else (8, 128), bf16),
            VMEM(spare, bf16),
            VMEM(spare, bf16),
            VMEM((2,) + one, bf16),
            VMEM((2,) + small, f32),
            VMEM((2,) + one, bf16),
            VMEM(one, bf16),
            VMEM(small, f32),
            VMEM(one, bf16),
            VMEM(small, f32),
            VMEM(one, bf16),
            VMEM((2, lb, 128), bf16),
            VMEM((lb, 128), bf16),
            VMEM((2, la, 128), bf16),
            VMEM((la, 128), bf16),
            VMEM((ne - 1, grows // ne, 128), bf16),
            VMEM((ne - 1, lb // ne, 128), bf16),
            VMEM((ne - 1, la // ne, 128), bf16),
            VMEM((rows, 3 * lw), bf16),
            VMEM((nt, rows, lw), bf16),
            VMEM((rows, ADAPT), f32),
            VMEM((nt, rows), f32),
            VMEM((nt * per * lw // HEAD_DIM, seqp, seqp) if roomy else (1, 16, 128), bf16),
            dma(3 * n_w),
            dma(3 * n_w),
            dma(3 * n_big),
            dma(3 * n_big),
            dma(ne),
            dma(ne),
            dma(6),
            dma(6),
            dma(chunks * ne),
            dma(chunks * ne),
            dma(chunks * ne),
            dma(chunks * ne),
            dma(ne),
            dma(ne),
            dma(9),
            dma(9),
            dma(9),
            dma(9),
            dma(2 * ne),
            dma(2 * ne),
            dma(2 * ne),
            dma(2 * ne),
            dma(2 * ne),
            dma(2 * ne),
            dma(12),
            dma(12),
            dma(3),
            dma(n_w),
            dma(n_big + 2),
            dma(2),
        ],
        compiler_params=pltpu.CompilerParams(
            collective_id=0, has_side_effects=True, vmem_limit_bytes=67000000
        ),
        name="block",
    )(
        adapter_index, priority, routes.T, cotangent, inputs, gain1, gain2,
        triple_weight.transpose(1, 0, 2), triple_up.transpose(1, 0, 2), project_weight,
        project_down, triple_down, project_up, rw, router_down, ru, first_down, second_up, *big,
    )

    outs = pl.pallas_call(
        functools.partial(write_kernel, (nt, seq, seqp, images, ffq, lw, grows)),
        out_shape=[
            shape((tok, width), bf16),
            shape((tok, width), bf16),
            shape((width, ADAPT), f32),
            shape((3, ADAPT, lw), f32),
            shape((lw, ADAPT), f32),
            shape((ADAPT, width), f32),
            shape((width, ADAPT), f32),
            shape((experts, ADAPT), f32),
            shape((width, ADAPT), f32),
            shape((ADAPT, ffq), f32),
            shape((ffq, ADAPT), f32),
            shape((ADAPT, width), f32),
        ],
        in_specs=whole(6),
        out_specs=whole(12),
        name="write",
    )(*finals[:6])
    outs = list(outs)
    outs[3] = outs[3].transpose(1, 0, 2)
    outs[7] = outs[7].T
    return tuple(outs)


def solution(mesh):
    return jax.shard_map(
        body,
        mesh=mesh,
        in_specs=(
            P("expert", None),
            P(),
            P(None, None, "tensor"),
            P("tensor", None),
            P(),
            P(),
            P("expert", None, "tensor"),
            P("expert", "tensor", None),
            P(),
            P(None, None, "tensor"),
            P("tensor", None),
            P(),
            P(),
            P(),
            P(),
            P(None, "tensor"),
            P("tensor", None),
            P(),
            P("expert"),
            P("expert", None),
            P("expert", None),
            P("expert", None),
        ),
        out_specs=(
            P("expert", None),
            P("expert", None),
            P(),
            P(None, None, "tensor"),
            P("tensor", None),
            P(),
            P(),
            P(),
            P(),
            P(None, "tensor"),
            P("tensor", None),
            P(),
        ),
        check_vma=False,
    )
```

```python
import functools

import jax
import jax.numpy as jnp
from jax import lax
from jax.experimental import pallas as pl
from jax.experimental.pallas import tpu as pltpu
from jax.sharding import PartitionSpec as P

HEAD_DIM = 64
TOP = 2
ADAPTERS = 8
RANK = 16
ADAPT = ADAPTERS * RANK
EPS = 1e-06

f32 = jnp.float32
bf16 = jnp.bfloat16
i32 = jnp.int32
MESH = pl.DeviceIdType.MESH
VMEM = pltpu.VMEM


def up(a, b):
    return -(-a // b) * b


def dot(a, b):
    return lax.dot_general(a, b, (((1,), (0,)), ((), ())), preferred_element_type=f32)


def dot_nt(a, b):
    return lax.dot_general(a, b, (((1,), (1,)), ((), ())), preferred_element_type=f32)


def dot_tn(a, b):
    return lax.dot_general(a, b, (((0,), (0,)), ((), ())), preferred_element_type=f32)


def split_high_low(a):
    high = a.astype(bf16)
    return high, (a - high.astype(f32)).astype(bf16)


def dot_fine(a, b):
    high, low = split_high_low(a)
    return dot(high, b) + dot(low, b)


def dot_nt_fine(a, b):
    high, low = split_high_low(a)
    return dot_nt(high, b) + dot_nt(low, b)


def iota(shape, axis):
    return lax.broadcasted_iota(i32, shape, axis)


def to_row(col):
    n = col.shape[0]
    return jnp.sum(jnp.where(iota((n, n), 0) == iota((n, n), 1), col, 0.0), axis=0, keepdims=True)


def to_col(row):
    n = row.shape[1]
    return jnp.sum(jnp.where(iota((n, n), 0) == iota((n, n), 1), row, 0.0), axis=1, keepdims=True)


def picks_of(adapters, base, per, seqp):
    lane = iota((seqp, ADAPT), 1) // RANK
    return jnp.concatenate(
        [(lane == adapters[base + li]).astype(f32) for li in range(per)], axis=0
    )


def whole(count):
    return [pl.BlockSpec(memory_space=VMEM) for _ in range(count)]


def norm_stats(x):
    centre = jnp.mean(x, axis=-1, keepdims=True)
    shifted = x - centre
    scale = lax.rsqrt(jnp.mean(shifted * shifted, axis=-1, keepdims=True) + EPS)
    return shifted * scale, scale


def norm_back(grad, gain, unit, scale):
    g = grad * gain
    return scale * (
        g - jnp.mean(g, axis=-1, keepdims=True) - unit * jnp.mean(g * unit, axis=-1, keepdims=True)
    )


def greet(peers):
    barrier = pltpu.get_barrier_semaphore()
    for peer in peers:
        pl.semaphore_signal(barrier, 1, device_id=peer, device_id_type=MESH)
    pl.semaphore_wait(barrier, len(peers))


def remote(src, dst, send, recv, peer):
    return pltpu.make_async_remote_copy(
        src_ref=src, dst_ref=dst, send_sem=send, recv_sem=recv, device_id=peer, device_id_type=MESH
    )


def where_am_i():
    e = lax.axis_index("expert")
    t = lax.axis_index("tensor")
    return e, t, jnp.bitwise_xor(t, 1), jnp.bitwise_xor(t, 2), jnp.bitwise_xor(t, 3)


def dma(n):
    return pltpu.SemaphoreType.DMA((n,))


def linked(ident):
    return pltpu.CompilerParams(collective_id=ident, has_side_effects=True)


def gates_of(mixed, r0, r1, pick, rw, rd, ru):
    low = dot(mixed, rd) * pick
    logits = dot_nt(mixed, rw) + dot_nt_fine(low, ru)
    lane = iota((1, rw.shape[0]), 1)
    first = jnp.sum(jnp.where(r0 == lane, logits, 0.0), axis=1, keepdims=True)
    second = jnp.sum(jnp.where(r1 == lane, logits, 0.0), axis=1, keepdims=True)
    top = jnp.maximum(first, second)
    a = jnp.exp(first - top)
    b = jnp.exp(second - top)
    return a / (a + b), b / (a + b), low


def own_images(ref, first, per, seq, seqp, put):
    tok = ref.shape[0]
    for li in range(per):
        row = iota((seqp, tok), 0)
        sel = (iota((seqp, tok), 1) == row + (first + li) * seq) & (row < seq)
        put(pl.ds(li * seqp, seqp), dot(sel.astype(f32).astype(bf16), ref[...]))


def erf_parts(pre):
    cdf = 0.5 * (1.0 + lax.erf(pre * 0.7071067811865476))
    return pre * cdf, cdf + pre * (jnp.exp(-0.5 * pre * pre) * 0.3989422804014327)


def chunk_of(ref, ne, p):
    size = ref.shape[0] // ne
    return pl.ds(pl.multiple_of(p * size, size), size)


def sum_copy(ne, src, parts, send, recv):
    e, t = where_am_i()[:2]

    def copy(d):
        p = lax.rem(e + 3 * d, ne)
        return remote(src.at[chunk_of(src, ne, p)], parts.at[d - 1], send.at[d], recv.at[d], (p, t))

    return copy


def start_all(ne, copy):
    def start(d, carry):
        copy(d).start()
        return carry

    lax.fori_loop(1, ne, start, 0)


def sum_share(ne, copy, src, parts, total, send, recv):
    e, t = where_am_i()[:2]
    mine = chunk_of(src, ne, e)

    def add(d, acc):
        copy(d).wait()
        return acc + parts[d - 1].astype(f32)

    total[mine, :] = lax.fori_loop(1, ne, add, src[mine, :].astype(f32)).astype(bf16)

    def share(d):
        p = lax.rem(e + 3 * d, ne)
        return remote(total.at[mine], total.at[mine], send.at[ne + d], recv.at[ne + d], (p, t))

    def start(d, carry):
        share(d).start()
        return carry

    lax.fori_loop(1, ne, start, 0)
    return share


def wait_all(ne, copy):
    def wait(d, carry):
        copy(d).wait()
        return carry

    lax.fori_loop(1, ne, wait, 0)


def block_kernel(
    dims, adapters, prio, routes, cot_in, x_in, gain1, gain2, wt_in, tup_in, pw_in, pd_in,
    tdn, pup, rw, rd, ru, fdn, sup, w1_in, w2_in, fup_in, sdn_in,
    etot, btot, atot, outs, rep_e, rep_a, back_out, res_out, *rest,
):
    nt, ne, seq, seqp, images, experts, cap, chunks, cp, held_e, grows, la, lb, roomy = dims
    (
        slotc, slotr, routec, xs, cot_own, mixed, middle, triple, attended, tlow, plow, attn_in,
        wt, tup, pw, pd, got, got_cot, cot_pad, one_s, cots, mall, gall, acc_s, gate_s, out_s,
        w1, w2, fup, sdn, sent_s, sg_s, low_s, gcol_s, gg_rows, acc_low,
        acc_fd, acc_fu, acc_sd, acc_su, gr_s, gin1, keep, gin2, cot, x_own,
        back_s, res_s, tin1, tin1k, tin1r, keep_g, keep_k, tin2, tin2k, tin2r,
        bin1, bin2, ain1, ain2, eparts, bparts, aparts, gt_s, ga_s, back_low, rank_r, probs_s,
        wsend, wrecv, bsend, brecv, csend, crecv, tsend, trecv, send, recv, gsend, grecv, rsend, rrecv,
        ssend, srecv, usend, urecv, esend, erecv, b2send, b2recv, asend, arecv, osend, orecv,
        here, own_sem, load_sem, ret_sem,
    ) = rest
    back = back_s if roomy else back_out
    ebuf, bbuf = gin1.at[0], bin1.at[0]
    got_res = res_s if roomy else res_out
    e, t, near, far, cross = where_am_i()
    lw = pw_in.shape[0]
    width = x_in.shape[1]
    local = w1_in.shape[0]
    parts = nt // local
    n_out, block = cots.shape[0], cots.shape[1]
    peers = [(e, far), (e, near)] + [(lax.rem(e + 3 * d, ne), t) for d in range(1, ne)]
    barrier = pltpu.get_barrier_semaphore()
    for peer in peers:
        pl.semaphore_signal(barrier, 1, device_id=peer, device_id_type=MESH)

    def big_ref(k, to):
        return (fup_in, sdn_in)[k] if k < 2 else (w1_in, w2_in)[k - 2].at[lax.div(to, parts)]

    big = (fup, sdn, w1, w2)
    n_big = len(big)
    big_own = [
        pltpu.make_async_copy(big_ref(k, t), big[k].at[t], load_sem.at[k]) for k in range(n_big)
    ]
    big_far = [
        remote(big_ref(k, far), big[k].at[t], bsend.at[3 * k], brecv.at[3 * k], (e, far))
        for k in range(n_big)
    ]
    big_near = [
        remote(big_ref(k, near), big[k].at[t], bsend.at[3 * k + 1], brecv.at[3 * k + 1], (e, near))
        for k in range(n_big)
    ]
    big_relay = [
        remote(big[k].at[far], big[k].at[far], bsend.at[3 * k + 2], brecv.at[3 * k + 2], (e, near))
        for k in range(n_big)
    ]
    load_cot = pltpu.make_async_copy(cot_in, cot, load_sem.at[n_big])
    x_ref = x_own if roomy else cot
    load_x = pltpu.make_async_copy(x_in, x_ref, load_sem.at[n_big + 1])
    for copy in [load_cot] + big_own:
        copy.start()
    if roomy:
        load_x.start()

    moves = []
    for c in range(3):
        lanes = pl.ds(c * lw, lw)
        moves.append((wt_in.at[c], lambda q, lanes=lanes: wt.at[q, :, lanes]))
        moves.append((tup_in.at[c], lambda q, lanes=lanes: tup.at[q, :, lanes]))
    moves.append((pw_in, lambda q: pw.at[q]))
    moves.append((pd_in, lambda q: pd.at[q]))
    n_w = len(moves)
    fars = [
        remote(src, at(t), wsend.at[3 * i], wrecv.at[3 * i], (e, far))
        for i, (src, at) in enumerate(moves)
    ]
    nears = [
        remote(src, at(t), wsend.at[3 * i + 1], wrecv.at[3 * i + 1], (e, near))
        for i, (src, at) in enumerate(moves)
    ]
    relays = [
        remote(at(far), at(far), wsend.at[3 * i + 2], wrecv.at[3 * i + 2], (e, near))
        for i, (src, at) in enumerate(moves)
    ]
    owns = [
        pltpu.make_async_copy(src, at(t), own_sem.at[i]) for i, (src, at) in enumerate(moves)
    ]
    for copy in owns:
        copy.start()

    tok = prio.shape[1]
    per = images // nt
    rows = per * seqp
    total = nt * rows
    wide = one_s.shape[-1]
    order = iota((seqp, tok), 1).astype(f32)
    lane = iota((seqp, wide), 1)
    for i in range(images):
        if i == images // 2:
            pl.semaphore_wait(barrier, len(peers))
            for copy in fars + nears:
                copy.start()
        q, at = i // per, pl.ds(i % per * seqp, seqp)
        all_at = pl.ds(i * seqp, seqp)
        token = iota((seqp, 1), 0) + i * seq
        gate_s[all_at, :] = jnp.sum(
            jnp.where(prio[...] == token, order, 0.0), axis=1, keepdims=True
        )
        lane0 = i * seq // 128 * 128
        lane1 = min(lane0 + up(seq + 128, 128), tok)
        here_i = (iota((seqp, lane1 - lane0), 1) + lane0 == token) & (iota((seqp, lane1 - lane0), 0) < seq)
        r = [
            jnp.sum(
                jnp.where(here_i, routes[k : k + 1, lane0:lane1].astype(f32) + 1.0, 0.0),
                axis=1,
                keepdims=True,
            ).astype(i32)
            - 1
            for k in range(TOP)
        ]
        for k in range(TOP):
            routec[q, at, k : k + 1] = r[k]
        named = jnp.where(lane < experts, r[0], jnp.where(r[1] < 0, -1, r[1] + experts))
        one_s[all_at, :] = (named == lane).astype(f32).astype(bf16)
    totals = dot(jnp.ones((8, total), bf16), one_s[...])[0:1]
    for q in range(nt):
        rank_r[q : q + 1, :] = to_row(gate_s[pl.ds(q * rows, rows), :])
    lane = iota((rows, wide), 1)

    def slots_of(q, carry):
        at = pl.ds(pl.multiple_of(q * rows, 16), rows)
        mine = gate_s[at, :]
        counts = jnp.zeros((rows, wide), f32)
        for p in range(nt):
            before = (rank_r[p : p + 1, :] < mine).astype(f32).astype(bf16)
            counts = counts + dot(before, one_s[pl.ds(p * rows, rows), :])
        hot = one_s[at, :].astype(f32) * counts
        first = jnp.sum(jnp.where(lane < experts, hot, 0.0), axis=1, keepdims=True)
        second = jnp.sum(
            jnp.where(lane < experts, 0.0, hot)
            + jnp.where((lane < experts) & (routec[q, :, 1:2] == lane), totals, 0.0),
            axis=1,
            keepdims=True,
        )
        for k, pos in ((0, first), (1, second)):
            named = routec[q, :, k : k + 1]
            place = pos.astype(i32)
            kept = (named >= 0) & (place < cap)
            kept = kept & (lax.rem(named, local) == lax.div(t, parts))
            kept = kept & (lax.rem(place, parts) == lax.rem(t, parts))
            index = lax.div(place, parts)
            index = jnp.where(index < cp - 2, index, index + 2)
            slot = jnp.where(kept, lax.div(named, local) * block + index, -1)
            slotc[q, :, k : k + 1] = slot
            slotr[q, k : k + 1, :] = to_row(slot.astype(f32)).astype(i32)
        return carry

    lax.fori_loop(0, nt, slots_of, 0)

    load_cot.wait()
    for i in range(images):
        start = i * seq // 16 * 16
        stop = min(start + up(seq, 16) + 16, tok)
        src = iota((seqp, stop - start), 1) + start
        row = iota((seqp, stop - start), 0)
        sel = ((src == row + i * seq) & (row < seq)).astype(f32).astype(bf16)
        cot_pad[i // per, pl.ds(i % per * seqp, seqp), :] = dot(sel, cot[start:stop, :]).astype(bf16)
    step = max(1, 512 // block)
    image_of = iota((1, rows), 1) // seqp

    def pack(d, carry):
        s = iota((step * block, 1), 0) + d * (step * block)
        acc = jnp.zeros((step * block, width), f32)
        idc = jnp.zeros((step * block, 1), f32)
        for q in range(nt):
            ids = jnp.zeros((1, rows), f32)
            for li in range(per):
                ids = jnp.where(image_of == li, adapters[q * per + li].astype(f32), ids)
            g = (slotr[q, 0:1, :] == s) | (slotr[q, 1:2, :] == s)
            idc = idc + jnp.sum(jnp.where(g, ids, 0.0), axis=1, keepdims=True)
            acc = acc + dot(g.astype(f32).astype(bf16), cot_pad[q])
        row = iota((block, block), 0)
        for b in range(step):
            part = acc[b * block : (b + 1) * block]
            idr = to_row(idc[b * block : (b + 1) * block])
            head = jnp.where(row == cp - 2, idr, part[:, 0:block])
            cots[d * step + b, :, 0:block] = head.astype(bf16)
            cots[d * step + b, :, block:] = part[:, block:].astype(bf16)
        return carry

    lax.fori_loop(0, n_out // step, pack, 0)

    def cot_copy(d):
        p = lax.rem(e + 3 * d, ne)
        return remote(cots.at[p], got_cot.at[e], csend.at[d], crecv.at[d], (p, t))

    def cot_start(d, carry):
        cot_copy(d).start()
        return carry

    lax.fori_loop(1, ne, cot_start, 0)
    own_cot = pltpu.make_async_copy(cots.at[e], got_cot.at[e], here.at[0])
    own_cot.start()

    def put_x(at, value):
        xs[at, :] = value

    def put_cot(at, value):
        cot_own[at, :] = value.astype(bf16)

    if not roomy:
        own_images(cot, t * per, per, seq, seqp, put_cot)
        load_x.start()
    load_x.wait()
    own_images(x_ref, t * per, per, seq, seqp, put_x)
    pick = picks_of(adapters, t * per, per, seqp)
    unit, _ = norm_stats(xs[...])
    normed = (unit * gain1[...]).astype(bf16)
    attn_in[...] = normed
    low = (dot(normed, tdn[...]) * pick).astype(bf16)
    tlow[...] = low
    head_of = iota((1, lw), 1) // HEAD_DIM
    key_ok = iota((1, seqp), 1) < seq

    def piece(m, carry):
        p = jnp.bitwise_xor(t, m)

        @pl.when(m == 0)
        def _():
            for copy in owns:
                copy.wait()

        @pl.when(m == 1)
        def _():
            for copy in nears:
                copy.wait()

        @pl.when(m == 2)
        def _():
            for i in range(6):
                fars[i].wait_recv()
                relays[i].start()

        @pl.when(m == 3)
        def _():
            for i in range(6):
                relays[i].wait_recv()

        triple[p] = (dot(attn_in[...], wt[p]) + dot(tlow[...], tup[p])).astype(bf16)
        for li in range(per):
            at = pl.ds(li * seqp, seqp)
            q = triple[p, at, 0:lw]
            k = triple[p, at, lw : 2 * lw]
            v = triple[p, at, 2 * lw : 3 * lw]
            acc = jnp.zeros((seqp, lw), f32)
            for h in range(lw // HEAD_DIM):
                on = head_of == h
                qm = jnp.where(on, q * HEAD_DIM**-0.5, 0.0).astype(bf16)
                s = jnp.where(key_ok, dot_nt(qm, k), -jnp.inf)
                ex = jnp.exp(s - jnp.max(s, axis=1, keepdims=True))
                probs = (ex * (1.0 / jnp.sum(ex, axis=1, keepdims=True))).astype(bf16)
                acc = acc + dot(probs, jnp.where(on, v, 0.0).astype(bf16))
            attended[p, at, :] = acc.astype(bf16)
        return carry

    lax.fori_loop(0, nt, piece, 0)
    for copy in big_near:
        copy.start()
    for i in range(6, n_w):
        fars[i].wait_recv()
        relays[i].start()
    for i in range(6, n_w):
        relays[i].wait_recv()
    psum = jnp.zeros((rows, ADAPT), f32)
    branch = jnp.zeros((rows, width), f32)
    for p in range(nt):
        psum = psum + dot(attended[p], pd[p])
        branch = branch + dot(attended[p], pw[p])
    low2 = (psum * pick).astype(bf16)
    plow[...] = low2
    mid = xs[...] + branch + dot(low2, pup[...])
    middle[...] = mid
    unit2, _ = norm_stats(mid)
    mix = (unit2 * gain2[...]).astype(bf16)
    mixed[...] = mix
    mall[t] = mix

    mix_far = [
        remote(buf.at[t], buf.at[t], tsend.at[i], trecv.at[i], (e, far))
        for i, buf in enumerate((mall, gall))
    ]
    mix_near = [
        remote(buf.at[t], buf.at[t], tsend.at[2 + i], trecv.at[2 + i], (e, near))
        for i, buf in enumerate((mall, gall))
    ]
    mix_relay = [
        remote(buf.at[far], buf.at[far], tsend.at[4 + i], trecv.at[4 + i], (e, near))
        for i, buf in enumerate((mall, gall))
    ]
    mix_far[0].start()
    mix_near[0].start()
    r = routec[t]
    a, b, _ = gates_of(mix, r[:, 0:1], r[:, 1:2], pick, rw[...], rd[...], ru[...])
    gall[t] = jnp.zeros(gall.shape[1:], f32)
    gall[t, 0:1, :] = to_row(a)
    gall[t, 1:2, :] = to_row(b)
    for copy in [mix_far[1], mix_near[1]] + big_far:
        copy.start()
    step = max(1, 512 // block)

    def gather_rows(q, s):
        g0 = slotr[q, 0:1, :] == s
        g1 = slotr[q, 1:2, :] == s
        gate = jnp.sum(
            jnp.where(g0, gall[q, 0:1, :], jnp.where(g1, gall[q, 1:2, :], 0.0)), axis=1, keepdims=True
        )
        return dot((g0 | g1).astype(f32).astype(bf16), mall[q]), gate

    def add_quarter(q, fresh):
        def some(d, carry):
            at = pl.ds(pl.multiple_of(d * (step * block), step * block), step * block)
            s = iota((step * block, 1), 0) + d * (step * block)
            part, gate = gather_rows(q, s)
            acc_s[at, :] = part if fresh else acc_s[at, :] + part
            gate_s[at, :] = gate if fresh else gate_s[at, :] + gate
            return carry

        lax.fori_loop(0, n_out // step, some, 0)

    add_quarter(t, True)
    for copy in mix_near:
        copy.wait_recv()
    add_quarter(near, False)
    if roomy:
        own_images(cot, t * per, per, seq, seqp, put_cot)
    for copy in mix_far:
        copy.wait_recv()
    for copy in mix_relay:
        copy.start()
    add_quarter(far, False)
    for copy in mix_relay:
        copy.wait_recv()

    def finish(p):
        at = pl.ds(pl.multiple_of(p * block, block), block)
        part, gate = gather_rows(cross, iota((block, 1), 0) + p * block)
        part = acc_s[at, :] + part
        gate = to_row(gate_s[at, :] + gate)
        high = gate.astype(bf16).astype(f32)
        row = iota((block, block), 0)
        head = jnp.where(row == cp - 2, high, part[:, 0:block])
        head = jnp.where(row == cp - 1, gate - high, head)
        return head.astype(bf16), part[:, block:].astype(bf16)

    def chunk(h):
        return pl.ds(pl.multiple_of(h * cp, cp), cp)

    def out_copy(d, h):
        p = lax.rem(e + 3 * d, ne)
        k = d * chunks + h
        return remote(out_s.at[p, chunk(h)], got.at[e, chunk(h)], send.at[k], recv.at[k], (p, t))

    def send_one(d, carry):
        p = lax.rem(e + 3 * d, ne)
        head, tail = finish(p)
        out_s[p, :, 0:block] = head
        out_s[p, :, block:] = tail
        out_copy(d, 0).start()
        return carry

    lax.fori_loop(1, ne, send_one, 0)

    for h in range(1, chunks):

        def send_more(d, carry, h=h):
            out_copy(d, h).start()
            return carry

        lax.fori_loop(1, ne, send_more, 0)
    head, tail = finish(e)
    got[e, :, 0:block] = head
    got[e, :, block:] = tail

    n = ne
    erows = n * cp
    row_at = lax.rem(iota((erows, 1), 0), cp)
    res_at, gsent_at = pl.ds(0, erows), pl.ds(erows, erows)
    for buf in (acc_fd, acc_fu, acc_sd, acc_su):
        buf[...] = jnp.zeros_like(buf)
    for copy in big_own + big_near:
        copy.wait()

    def cot_wait(d, carry):
        cot_copy(d).wait()
        return carry

    lax.fori_loop(1, ne, cot_wait, 0)
    own_cot.wait()

    def grad_copy(d, h):
        p = lax.rem(e + 3 * d, ne)
        k = d * chunks + h
        return remote(cots.at[p, chunk(h)], back.at[e, chunk(h)], gsend.at[k], grecv.at[k], (p, t))

    def res_copy(d):
        p = lax.rem(e + 3 * d, ne)
        return remote(out_s.at[p], got_res.at[e], rsend.at[d], rrecv.at[d], (p, t))

    def experts_chunk(h, carry):
        at = chunk(h)

        def rows_wait(d, carry):
            out_copy(d, h).wait_recv()
            return carry

        lax.fori_loop(1, ne, rows_wait, 0)

        @pl.when(h == 0)
        def _():
            diag = iota((block, block), 0) == iota((block, block), 1)

            def headers(m, carry):
                idr = got_cot[m, cp - 2 : cp - 1, 0:block].astype(f32)
                gr = got[m, cp - 2 : cp - 1, 0:block].astype(f32) + got[
                    m, cp - 1 : cp, 0:block
                ].astype(f32)
                gcol_s[m, :, 0:1] = jnp.sum(jnp.where(diag, idr, 0.0), axis=1, keepdims=True)
                gcol_s[m, :, 1:2] = jnp.sum(jnp.where(diag, gr, 0.0), axis=1, keepdims=True)
                return carry

            lax.fori_loop(0, n, headers, 0)

        spare = jnp.where((h == 0) | (h == chunks - 1), cp - 2, cp)
        real = row_at < spare
        cols = gcol_s[:, at, :].reshape(erows, 2)
        sent = jnp.where(real, got[:, at, :].reshape(erows, width).astype(f32), 0.0).astype(bf16)
        cotf = jnp.where(real, got_cot[:, at, :].reshape(erows, width).astype(f32), 0.0)
        pick_e = (cols[:, 0:1] == (iota((1, ADAPT), 1) // RANK).astype(f32)).astype(f32)
        sent_s[...] = sent
        sgrad = (cols[:, 1:2] * cotf).astype(bf16)
        sg_s[...] = sgrad
        low_s[0] = (dot(sent, fdn[...]) * pick_e).astype(bf16)
        low_s[1] = (dot_nt(sgrad, sup[...]) * pick_e).astype(bf16)
        acc_low[...] = jnp.zeros_like(acc_low)
        acc_s[pl.ds(0, 2 * erows), :] = jnp.zeros((2 * erows, width), f32)

        def through(m, carry):
            c = jnp.bitwise_xor(t, m)

            @pl.when((h == 0) & (m == 2))
            def _():
                for far_copy, relay in zip(big_far, big_relay):
                    far_copy.wait_recv()
                    relay.start()

            @pl.when((h == 0) & (m == 3))
            def _():
                for relay in big_relay:
                    relay.wait_recv()

            span = min(erows, 512)
            for r0 in range(0, erows, span):
                rs = slice(r0, r0 + span)
                gs = slice(erows + r0, erows + r0 + span)
                pre = dot(sent_s[rs, :], w1[c]) + dot(low_s[0, rs, :], fup[c])
                act, slope = erf_parts(pre)
                hid = act.astype(bf16)
                acc_low[0, rs, :] += dot(hid, sdn[c])
                acc_s[rs, :] += dot(hid, w2[c])
                ghid = dot_nt(sg_s[rs, :], w2[c]) + dot_nt(low_s[1, rs, :], sdn[c])
                gpre = (ghid * slope).astype(bf16)
                acc_fu[c] += dot_tn(low_s[0, rs, :], gpre)
                acc_sd[c] += dot_tn(low_s[1, rs, :], hid)
                acc_low[1, rs, :] += dot_nt(gpre, fup[c])
                acc_s[gs, :] += dot_nt(gpre, w1[c])
            return carry

        lax.fori_loop(0, nt, through, 0)

        def sent_wait(d, carry):
            out_copy(d, h).wait_send()
            return carry

        lax.fori_loop(1, ne, sent_wait, 0)
        cols = gcol_s[:, at, :].reshape(erows, 2)
        pick_e = (cols[:, 0:1] == (iota((1, ADAPT), 1) // RANK).astype(f32)).astype(f32)
        second_low = (acc_low[0] * pick_e).astype(bf16)
        res = (acc_s[res_at, :] + dot(second_low, sup[...])).astype(bf16).astype(f32)
        cotf = got_cot[:, at, :].reshape(erows, width).astype(f32)
        acc_low[0, :, 0:1] = jnp.sum(res * cotf, axis=1, keepdims=True)
        g1low = (acc_low[1] * pick_e).astype(bf16)
        gsent = acc_s[gsent_at, :] + dot_nt(g1low, fdn[...])
        cots[:, at, :] = gsent.astype(bf16).reshape(n, cp, width)
        diag = iota((cp, block), 0) + h * cp == iota((cp, block), 1)

        def footers(m, carry):
            gg = jnp.sum(
                jnp.where(diag, acc_low[0, pl.ds(pl.multiple_of(m * cp, cp), cp), 0:1], 0.0),
                axis=0,
                keepdims=True,
            )
            total = jnp.where(h == 0, gg, gg_rows[pl.ds(m, 1), :] + gg)
            gg_rows[pl.ds(m, 1), :] = total

            @pl.when(h == chunks - 1)
            def _():
                high = total.astype(bf16).astype(f32)
                row = iota((16, block), 0)
                to = pl.ds(block - 16, 16)
                old = cots[m, to, 0:block].astype(f32)
                old = jnp.where(row == 14, high, jnp.where(row == 15, total - high, old))
                cots[m, to, 0:block] = old.astype(bf16)

            return carry

        lax.fori_loop(0, n, footers, 0)

        def grad_start(d, carry):
            grad_copy(d, h).start()
            return carry

        lax.fori_loop(1, ne, grad_start, 0)
        out_s[:, at, :] = (cols[:, 1:2] * res).astype(bf16).reshape(n, cp, width)
        acc_su[...] += dot_tn(second_low, sg_s[...])
        acc_fd[...] += dot_tn(g1low, sent_s[...])
        return carry

    gg_rows[...] = jnp.zeros_like(gg_rows)
    lax.fori_loop(0, chunks, experts_chunk, 0)
    locals_ = [
        pltpu.make_async_copy(cots.at[e], back.at[e], ret_sem.at[0]),
        pltpu.make_async_copy(out_s.at[e], got_res.at[e], ret_sem.at[1]),
    ]
    for copy in locals_:
        copy.start()

    def res_start(d, carry):
        res_copy(d).start()
        return carry

    ffq = w1.shape[2]
    quarter = width // nt
    share = ADAPT // nt
    for q in range(nt):
        off = 0
        for c in range(ffq // 128):
            gr_s[q, off : off + 128, :] = acc_fu[q, :, c * 128 : (c + 1) * 128].astype(bf16)
            off += 128
        gr_s[q, off : off + ffq, :] = acc_sd[q].T.astype(bf16)
        off += ffq
        gr_s[q, off : off + quarter, :] = acc_fd[:, q * quarter : (q + 1) * quarter].T.astype(bf16)
        off += quarter
        for c in range(width // 128):
            at = slice(q * share, (q + 1) * share)
            gr_s[q, off : off + share, :] = acc_su[at, c * 128 : (c + 1) * 128].astype(bf16)
            off += share
        if off < grows:
            gr_s[q, off:grows, :] = jnp.zeros((grows - off, 128), bf16)

    def tensor_sum(rows_at, in1, in2, k):
        a = remote(gr_s.at[cross, rows_at], in1.at[0], ssend.at[k], srecv.at[k], (e, near))
        b = remote(gr_s.at[near, rows_at], in1.at[1], ssend.at[k + 1], srecv.at[k + 1], (e, near))
        held = keep.at[rows_at]
        c = remote(held, in2, ssend.at[k + 2], srecv.at[k + 2], (e, far))

        def start():
            a.start()
            b.start()

        def cross_over():
            a.wait()
            held[...] = (gr_s[far, rows_at, :].astype(f32) + in1[0].astype(f32)).astype(bf16)
            c.start()

        def result():
            b.wait()
            c.wait()
            mine = gr_s[t, rows_at, :].astype(f32) + in1[1].astype(f32)
            return (mine + in2[...].astype(f32)).astype(bf16)

        return start, cross_over, result

    g_start, g_cross, g_result = tensor_sum(pl.ds(0, grows), gin1, gin2, 0)
    g_start()

    r = routec[t]
    prob0, prob1, rlow = gates_of(
        mixed[...], r[:, 0:1], r[:, 1:2], pick, rw[...], rd[...], ru[...]
    )
    g_cross()

    key_row = iota((seqp, 1), 0) < seq
    heads = lw // HEAD_DIM

    def softmax_of(qm, k):
        s = jnp.where(key_row, dot_nt(k, qm), -jnp.inf)
        ex = jnp.exp(s - jnp.max(s, axis=0, keepdims=True))
        return ex * (1.0 / jnp.sum(ex, axis=0, keepdims=True))

    def softmax_piece(p, carry):
        for li in range(per):
            at = pl.ds(li * seqp, seqp)
            q = triple[p, at, 0:lw] * HEAD_DIM**-0.5
            k = triple[p, at, lw : 2 * lw]
            for h in range(heads):
                qm = jnp.where(head_of == h, q, 0.0).astype(bf16)
                probs_s[(p * per + li) * heads + h] = softmax_of(qm, k).astype(bf16)
        return carry

    if roomy:
        lax.fori_loop(0, nt, softmax_piece, 0)

    def back_wait(d, carry):
        for h in range(chunks):
            grad_copy(d, h).wait()
        return carry

    lax.fori_loop(1, ne, back_wait, 0)
    lax.fori_loop(1, ne, res_start, 0)
    for copy in locals_:
        copy.wait()
    for copy in mix_far + mix_near + mix_relay:
        copy.wait_send()
    if not roomy:
        load = pltpu.make_async_copy(back, got, here.at[0])
        load.start()
        load.wait()
    rows_back = back if roomy else got
    slots = n * block
    grad_s, gg_s, tok_s = cot_pad, gall, mall

    def hot(q):
        s = iota((1, slots), 1)
        c = slotc[q]
        return ((c[:, 0:1] == s) | (c[:, 1:2] == s)).astype(f32).astype(bf16)

    def grad_tokens(q):
        grad_s[q] = dot(hot(q), rows_back[...].reshape(slots, width)).astype(bf16)

    def gate_tokens(q):
        sc = iota((slots, 1), 0)
        gg_s[q] = jnp.zeros(gg_s.shape[1:], f32)
        for k in range(TOP):
            gg_s[q, k : k + 1, :] = jnp.sum(
                jnp.where(slotr[q, k : k + 1, :] == sc, gate_s[0:slots, :], 0.0), axis=0, keepdims=True
            )

    stages = ((grad_s, tin1, keep_g, tin2), (gg_s, tin1k, keep_k, tin2k))
    first, second = {}, []
    for i, (src, dst, held, two) in enumerate(stages):
        if i == 1:


            def read_gates(d, carry):
                gr = rows_back[d, block - 2 : block - 1, 0:block].astype(f32)
                gr = gr + rows_back[d, block - 1 : block, 0:block].astype(f32)
                gate_s[pl.ds(pl.multiple_of(d * block, block), block), :] = to_col(gr)
                return carry

            lax.fori_loop(0, n, read_gates, 0)
        for j, q in enumerate((cross, near)):
            (grad_tokens, gate_tokens)[i](q)
            k = 3 * i + j
            first[i, j] = remote(src.at[q], dst.at[j], usend.at[k], urecv.at[k], (e, near))
            first[i, j].start()
        (grad_tokens, gate_tokens)[i](far)
        first[i, 0].wait()
        held[...] = (src[far].astype(f32) + dst[0].astype(f32)).astype(held.dtype)
        second.append(remote(held, two, usend.at[3 * i + 2], urecv.at[3 * i + 2], (e, far)))
        second[-1].start()
    grad_tokens(t)
    gate_tokens(t)
    ebuf[...] = g_result()
    e_first = sum_copy(ne, ebuf, eparts, esend, erecv)
    start_all(ne, e_first)
    unit2, scale2 = norm_stats(middle[...])
    sums = []
    for i, (src, one, _, two) in enumerate(stages):
        first[i, 1].wait()
        mine = src[t].astype(f32) + one[1].astype(f32)
        second[i].wait()
        sums.append(mine + two[...].astype(f32))
    gmix, ggate = sums
    gg0 = to_col(ggate[0:1, :])
    gg1 = to_col(ggate[1:2, :])
    inner = prob0 * gg0 + prob1 * gg1
    lane = iota((1, rw.shape[0]), 1)
    glog = jnp.where(r[:, 0:1] == lane, prob0 * (gg0 - inner), 0.0) + jnp.where(
        r[:, 1:2] == lane, prob1 * (gg1 - inner), 0.0
    )
    llow = dot_fine(glog, ru[...]) * pick
    gm = gmix + dot_fine(glog, rw[...]) + dot_nt_fine(llow, rd[...])
    router_up = dot_tn(glog.astype(bf16), rlow.astype(bf16))
    router_down = dot_tn(mixed[...], llow.astype(bf16))
    gmid = cot_own[...].astype(f32) + norm_back(gm, gain2[...], unit2, scale2)
    mid_at, in_at = pl.ds(0, rows), pl.ds(rows, rows)
    acc_s[mid_at, :] = gmid
    gbranch = gmid.astype(bf16)
    project_up = dot_tn(plow[...], gbranch)
    blow = (dot_nt(gbranch, pup[...]) * pick).astype(bf16)
    for p in range(nt):
        ga_s[p] = (dot_nt(gbranch, pw[p]) + dot_nt(blow, pd[p])).astype(bf16)

    for q in range(nt):
        off = la
        at = slice(q * share, (q + 1) * share)
        for c in range(width // 128):
            gr_s[q, off : off + share, :] = project_up[at, c * 128 : (c + 1) * 128].astype(bf16)
            off += share
        at = slice(q * quarter, (q + 1) * quarter)
        gr_s[q, off : off + quarter, :] = router_down[at].astype(bf16)
        off += quarter
        gr_s[q, off : la + lb - lw, :] = jnp.zeros((la + lb - lw - off, 128), bf16)
        gr_s[q, la + lb - lw : la + lb, :] = dot_tn(attended[q], blow).astype(bf16)
    off = la + ADAPT + quarter
    gr_s[0, off : off + experts, :] = router_up.astype(bf16)
    b_start, b_cross, b_result = tensor_sum(pl.ds(la, lb), bin1, bin2, 3)
    b_start()
    b_first = sum_copy(ne, bbuf, bparts, b2send, b2recv)

    acc_s[in_at, :] = jnp.zeros((rows, width), f32)
    back_low[...] = jnp.zeros_like(back_low)

    def piece_back(p, carry):
        for li in range(per):
            at = pl.ds(li * seqp, seqp)
            q = triple[p, at, 0:lw] * HEAD_DIM**-0.5
            k = triple[p, at, lw : 2 * lw]
            v = triple[p, at, 2 * lw : 3 * lw]
            ga = ga_s[p, at, :]
            gq = jnp.zeros((seqp, lw), f32)
            gk = jnp.zeros((seqp, lw), f32)
            gv = jnp.zeros((seqp, lw), f32)
            for h in range(heads):
                on = head_of == h
                qm = jnp.where(on, q, 0.0).astype(bf16)
                km = jnp.where(on, k, 0.0).astype(bf16)
                gam = jnp.where(on, ga, 0.0).astype(bf16)
                if roomy:
                    half = probs_s[(p * per + li) * heads + h]
                    probs = half.astype(f32)
                else:
                    probs = softmax_of(qm, k)
                    half = probs.astype(bf16)
                weighted = probs * dot_nt(v, gam)
                ds = (weighted - probs * jnp.sum(weighted, axis=0, keepdims=True)).astype(bf16)
                gq = gq + dot_tn(ds, km)
                gk = gk + dot(ds, qm)
                gv = gv + dot(half, gam)
            gt_s[at, 0:lw] = (gq * HEAD_DIM**-0.5).astype(bf16)
            gt_s[at, lw : 2 * lw] = gk.astype(bf16)
            gt_s[at, 2 * lw : 3 * lw] = gv.astype(bf16)
        gt = gt_s[...]
        back_low[...] += dot_nt(gt, tup[p])
        acc_s[in_at, :] += dot_nt(gt, wt[p])
        tu = dot_tn(tlow[...], gt)
        for c in range(3 * lw // 128):
            gr_s[p, c * 128 : (c + 1) * 128, :] = tu[:, c * 128 : (c + 1) * 128].astype(bf16)

        @pl.when(p == 0)
        def _():
            b_cross()

        @pl.when(p == 2)
        def _():
            bbuf[...] = b_result()
            start_all(ne, b_first)

        return carry

    lax.fori_loop(0, nt, piece_back, 0)

    tglow = (back_low[...] * pick).astype(bf16)
    triple_down = dot_tn(attn_in[...], tglow)
    for q in range(nt):
        off = 3 * lw
        gr_s[q, off : off + quarter, :] = triple_down[q * quarter : (q + 1) * quarter].astype(bf16)
        if off + quarter < la:
            gr_s[q, off + quarter : la, :] = jnp.zeros((la - off - quarter, 128), bf16)
    a_start, a_cross, a_result = tensor_sum(pl.ds(0, la), ain1, ain2, 6)
    a_start()
    gin = acc_s[in_at, :] + dot_nt(tglow, tdn[...])
    a_cross()
    unit1, scale1 = norm_stats(xs[...])
    attn_in[...] = (acc_s[mid_at, :] + norm_back(gin, gain1[...], unit1, scale1)).astype(bf16)

    def share_out(j, src, k):
        return [
            remote(src, outs.at[t, j], osend.at[k], orecv.at[k], (e, far)),
            remote(src, outs.at[t, j], osend.at[k + 1], orecv.at[k + 1], (e, near)),
            remote(outs.at[far, j], outs.at[far, j], osend.at[k + 2], orecv.at[k + 2], (e, near)),
            pltpu.make_async_copy(src, outs.at[t, j], here.at[1 + j]),
        ]

    def share_rows(buf, k):
        return [
            remote(buf.at[t], buf.at[t], osend.at[k], orecv.at[k], (e, far)),
            remote(buf.at[t], buf.at[t], osend.at[k + 1], orecv.at[k + 1], (e, near)),
            remote(buf.at[far], buf.at[far], osend.at[k + 2], orecv.at[k + 2], (e, near)),
        ]

    igrad_out = share_out(1, attn_in, 0)
    for i in (0, 1, 3):
        igrad_out[i].start()
    def res_wait(d, carry):
        res_copy(d).wait()
        return carry

    lax.fori_loop(1, ne, res_wait, 0)
    if not roomy:
        load = pltpu.make_async_copy(got_res, got_cot, here.at[0])
        load.start()
        load.wait()
    res_rows = got_res if roomy else got_cot

    def res_tokens(q):
        tok_s[q] = dot(hot(q), res_rows[...].reshape(slots, width)).astype(bf16)

    res_first = []
    for j, q in enumerate((cross, near)):
        res_tokens(q)
        res_first.append(remote(tok_s.at[q], tin1r.at[j], usend.at[6 + j], urecv.at[6 + j], (e, near)))
        res_first[-1].start()
    res_tokens(far)
    res_first[0].wait()
    keep_g[...] = (tok_s[far].astype(f32) + tin1r[0].astype(f32)).astype(bf16)
    res_second = remote(keep_g, tin2r, usend.at[8], urecv.at[8], (e, far))
    res_second.start()
    res_tokens(t)
    abuf = keep.at[pl.ds(la, la)]
    abuf[...] = a_result()
    a_first = sum_copy(ne, abuf, aparts, asend, arecv)
    start_all(ne, a_first)
    e_second = sum_share(ne, e_first, ebuf, eparts, etot, esend, erecv)
    b_second = sum_share(ne, b_first, bbuf, bparts, btot, b2send, b2recv)
    a_second = sum_share(ne, a_first, abuf, aparts, atot, asend, arecv)
    wait_all(ne, e_second)
    wait_all(ne, b_second)
    ra = grows - held_e
    rep_e[t, 0:ra, :] = etot[held_e:grows, :]
    rep_e[t, ra:, :] = btot[0 : rep_e.shape[1] - ra, :]
    rep_out = share_rows(rep_e, 6)
    for i in (0, 1):
        rep_out[i].start()
    wait_all(ne, a_second)
    rep_a[t] = atot[3 * lw : 3 * lw + quarter, :]
    last_out = share_rows(rep_a, 9)
    for i in (0, 1):
        last_out[i].start()
    res_first[1].wait()
    res_second.wait()
    mixed[...] = (
        middle[...] + (tok_s[t].astype(f32) + tin1r[1].astype(f32)) + tin2r[...].astype(f32)
    ).astype(bf16)
    block_out = share_out(0, mixed, 3)
    for i in (0, 1, 3):
        block_out[i].start()
    igrad_out[0].wait_recv()
    igrad_out[2].start()
    for group in (block_out, rep_out, last_out):
        group[0].wait_recv()
        group[2].start()
    for group in (igrad_out, block_out, rep_out, last_out):
        group[0].wait_send()
        for copy in group[1:]:
            copy.wait()
    for copy in fars + relays + big_far + big_relay:
        copy.wait_send()


def write_kernel(
    dims, e_all, b_all, a_all, outs, rep_e, rep_a, block_output, input_grad, triple_down, triple_up, project_down,
    project_up, router_down, router_up, first_down, first_up, second_down, second_up,
):
    nt, seq, seqp, images, ffq, lw, grows = dims
    per = images // nt
    tok, width = block_output.shape
    flat = outs.shape[2]
    for j, out in enumerate((block_output, input_grad)):
        for a in range(0, tok, seqp):
            b = min(a + seqp, tok)
            i0, i1 = a // seq, (b - 1) // seq
            parts = []
            for i in range(i0, i1 + 1):
                row = iota((b - a, seqp), 0) + a
                sel = (iota((b - a, seqp), 1) == row - i * seq) & (row < (i + 1) * seq)
                src = outs[i // per, j, (i % per) * seqp : (i % per + 1) * seqp, :]
                parts.append(dot(sel.astype(f32).astype(bf16), src))
            whole_part = parts[0]
            for part in parts[1:]:
                whole_part = whole_part + part
            out[a:b, :] = whole_part.astype(bf16)
    for c in range(ffq // 128):
        first_up[:, c * 128 : (c + 1) * 128] = e_all[c * 128 : (c + 1) * 128].astype(f32)
    second_down[...] = e_all[ffq : 2 * ffq].astype(f32)
    for c in range(3):
        triple_up[c] = a_all[c * lw : (c + 1) * lw].astype(f32)
    last = b_all.shape[0]
    project_down[...] = b_all[last - lw : last].astype(f32)
    quarter = width // nt
    share = ADAPT // nt
    for q in range(nt):
        at = slice(q * quarter, (q + 1) * quarter)
        up_at = slice(q * share, (q + 1) * share)
        triple_down[at, :] = rep_a[q].astype(f32)
        first_down[at, :] = rep_e[q, 0:quarter, :].astype(f32)
        off = quarter
        for c in range(width // 128):
            second_up[up_at, c * 128 : (c + 1) * 128] = rep_e[q, off : off + share, :].astype(f32)
            off += share
        off = grows - 2 * ffq
        for c in range(width // 128):
            project_up[up_at, c * 128 : (c + 1) * 128] = rep_e[q, off : off + share, :].astype(f32)
            off += share
        router_down[at, :] = rep_e[q, off : off + quarter, :].astype(f32)
        off += quarter
    router_up[...] = rep_e[0, off : off + router_up.shape[0], :].astype(f32)


def body(
    inputs, gain_attend, triple_weight, project_weight, gain_mixture, router_weight, expert_first,
    expert_second, triple_down, triple_up, project_down, project_up, router_down, router_up,
    first_down, first_up, second_down, second_up, adapter_index, routes, priority, cotangent,
):
    ne = lax.axis_size("expert")
    nt = lax.axis_size("tensor")
    tok, width = inputs.shape
    images = adapter_index.shape[0]
    seq = tok // images
    seqp = up(seq, 16)
    per = images // nt
    rows = per * seqp
    experts = router_weight.shape[1]
    local = expert_first.shape[0]
    ffq = expert_first.shape[2]
    lw = triple_weight.shape[2]
    cap = nt * ((5 * tok * TOP + 4 * nt * experts - 1) // (4 * nt * experts))
    used = cap * local // nt
    chunks = 2
    block = up(used + 4, 16 * chunks)
    cp = block // chunks
    smem = pl.BlockSpec(memory_space=pltpu.SMEM)
    anywhere = pl.BlockSpec(memory_space=pl.ANY)
    shape = jax.ShapeDtypeStruct
    wide = up(2 * experts, 128)
    gain1 = gain_attend.reshape(1, width)
    gain2 = gain_mixture.reshape(1, width)
    rw = router_weight.T
    ru = router_up.T
    big = (expert_first, expert_second, first_up, second_down)
    n_w = 8
    erows = ne * cp
    quarter = width // nt
    held_e = 2 * ffq
    grows = up(held_e + quarter + (ADAPT // nt) * (width // 128), 16 * ne)
    one = (rows, width)
    small = (8, rows)
    la = up(3 * lw + quarter, 16 * ne)
    lb = up(ADAPT + quarter + experts + lw, 16 * ne)
    re = grows - held_e + ADAPT + quarter + experts
    n_big = len(big)
    slots = (ne, block, width)
    roomy = ne * block <= 1024
    spare = slots if roomy else (8, 128)
    finals = pl.pallas_call(
        functools.partial(
            block_kernel,
            (nt, ne, seq, seqp, images, experts, cap, chunks, cp, held_e, grows, la, lb, roomy),
        ),
        out_shape=[
            shape((grows, 128), bf16),
            shape((lb, 128), bf16),
            shape((la, 128), bf16),
            shape((nt, 2) + one, bf16),
            shape((nt, re, 128), bf16),
            shape((nt, quarter, 128), bf16),
            shape((8, 128) if roomy else slots, bf16),
            shape((8, 128) if roomy else slots, bf16),
        ],
        in_specs=[smem] + whole(2) + [anywhere] * 2 + whole(13) + [anywhere] * 4,
        out_specs=whole(3) + [anywhere] + whole(2) + [anywhere] * 2,
        scratch_shapes=[
            VMEM((nt, rows, TOP), i32),
            VMEM((nt, TOP, rows), i32),
            VMEM((nt, rows, TOP), i32),
            VMEM(one, f32),
            VMEM(one, bf16),
            VMEM(one, bf16),
            VMEM(one, f32),
            VMEM((nt, rows, 3 * lw), bf16),
            VMEM((nt, rows, lw), bf16),
            VMEM((rows, ADAPT), bf16),
            VMEM((rows, ADAPT), bf16),
            VMEM(one, bf16),
            VMEM((nt, width, 3 * lw), bf16),
            VMEM((nt, ADAPT, 3 * lw), bf16),
            VMEM((nt, lw, width), bf16),
            VMEM((nt, lw, ADAPT), bf16),
            VMEM(slots, bf16),
            VMEM(slots, bf16),
            VMEM((nt,) + one, bf16),
            VMEM((images * seqp, wide), bf16),
            VMEM(slots, bf16),
            VMEM((nt,) + one, bf16),
            VMEM((nt,) + small, f32),
            VMEM((max(ne * block, 2 * erows, 2 * rows), width), f32),
            VMEM((max(ne * block, images * seqp), 1), f32),
            VMEM(slots, bf16),
            VMEM((nt, width, ffq), bf16),
            VMEM((nt, ffq, width), bf16),
            VMEM((nt, ADAPT, ffq), bf16),
            VMEM((nt, ffq, ADAPT), bf16),
            VMEM((erows, width), bf16),
            VMEM((erows, width), bf16),
            VMEM((2, erows, ADAPT), bf16),
            VMEM((ne, block, 2), f32),
            VMEM((ne, block), f32),
            VMEM((2, erows, ADAPT), f32),
            VMEM((ADAPT, width), f32),
            VMEM((nt, ADAPT, ffq), f32),
            VMEM((nt, ADAPT, ffq), f32),
            VMEM((ADAPT, width), f32),
            VMEM((nt, max(grows, la + lb), 128), bf16),
            VMEM((2, grows, 128), bf16),
            VMEM((max(grows, la + lb, 2 * la), 128), bf16),
            VMEM((grows, 128), bf16),
            VMEM((tok, width), bf16),
            VMEM((tok, width) if roomy else (8, 128), bf16),
            VMEM(spare, bf16),
            VMEM(spare, bf16),
            VMEM((2,) + one, bf16),
            VMEM((2,) + small, f32),
            VMEM((2,) + one, bf16),
            VMEM(one, bf16),
            VMEM(small, f32),
            VMEM(one, bf16),
            VMEM(small, f32),
            VMEM(one, bf16),
            VMEM((2, lb, 128), bf16),
            VMEM((lb, 128), bf16),
            VMEM((2, la, 128), bf16),
            VMEM((la, 128), bf16),
            VMEM((ne - 1, grows // ne, 128), bf16),
            VMEM((ne - 1, lb // ne, 128), bf16),
            VMEM((ne - 1, la // ne, 128), bf16),
            VMEM((rows, 3 * lw), bf16),
            VMEM((nt, rows, lw), bf16),
            VMEM((rows, ADAPT), f32),
            VMEM((nt, rows), f32),
            VMEM((nt * per * lw // HEAD_DIM, seqp, seqp) if roomy else (1, 16, 128), bf16),
            dma(3 * n_w),
            dma(3 * n_w),
            dma(3 * n_big),
            dma(3 * n_big),
            dma(ne),
            dma(ne),
            dma(6),
            dma(6),
            dma(chunks * ne),
            dma(chunks * ne),
            dma(chunks * ne),
            dma(chunks * ne),
            dma(ne),
            dma(ne),
            dma(9),
            dma(9),
            dma(9),
            dma(9),
            dma(2 * ne),
            dma(2 * ne),
            dma(2 * ne),
            dma(2 * ne),
            dma(2 * ne),
            dma(2 * ne),
            dma(12),
            dma(12),
            dma(3),
            dma(n_w),
            dma(n_big + 2),
            dma(2),
        ],
        compiler_params=pltpu.CompilerParams(
            collective_id=0, has_side_effects=True, vmem_limit_bytes=67000000
        ),
        name="block",
    )(
        adapter_index, priority, routes.T, cotangent, inputs, gain1, gain2,
        triple_weight.transpose(1, 0, 2), triple_up.transpose(1, 0, 2), project_weight,
        project_down, triple_down, project_up, rw, router_down, ru, first_down, second_up, *big,
    )

    outs = pl.pallas_call(
        functools.partial(write_kernel, (nt, seq, seqp, images, ffq, lw, grows)),
        out_shape=[
            shape((tok, width), bf16),
            shape((tok, width), bf16),
            shape((width, ADAPT), f32),
            shape((3, ADAPT, lw), f32),
            shape((lw, ADAPT), f32),
            shape((ADAPT, width), f32),
            shape((width, ADAPT), f32),
            shape((experts, ADAPT), f32),
            shape((width, ADAPT), f32),
            shape((ADAPT, ffq), f32),
            shape((ffq, ADAPT), f32),
            shape((ADAPT, width), f32),
        ],
        in_specs=whole(6),
        out_specs=whole(12),
        name="write",
    )(*finals[:6])
    outs = list(outs)
    outs[3] = outs[3].transpose(1, 0, 2)
    outs[7] = outs[7].T
    return tuple(outs)


def solution(mesh):
    return jax.shard_map(
        body,
        mesh=mesh,
        in_specs=(
            P("expert", None),
            P(),
            P(None, None, "tensor"),
            P("tensor", None),
            P(),
            P(),
            P("expert", None, "tensor"),
            P("expert", "tensor", None),
            P(),
            P(None, None, "tensor"),
            P("tensor", None),
            P(),
            P(),
            P(),
            P(),
            P(None, "tensor"),
            P("tensor", None),
            P(),
            P("expert"),
            P("expert", None),
            P("expert", None),
            P("expert", None),
        ),
        out_specs=(
            P("expert", None),
            P("expert", None),
            P(),
            P(None, None, "tensor"),
            P("tensor", None),
            P(),
            P(),
            P(),
            P(),
            P(None, "tensor"),
            P("tensor", None),
            P(),
        ),
        check_vma=False,
    )
```
